32 devices in a mesh: panel: 2 (over x), lat: 4 (over z), lon: 4 (over y, core).
Axes of the slice: x: 2, y: 2, z: 4, core: 2. Of those that a mesh axis runs over, the one named last changes fastest.
Arguments:
- state: float32 [2, 64, 64, 8, 128], P('panel', 'lat', 'lon'), may hold values from -6 to 6
- rim_base: int32 [2, 512, 2], P('panel', ('lat', 'lon')), may hold values from 1 to 61, as said below
- rim_weight: float32 [2, 512, 16], P('panel', ('lat', 'lon')), may hold values from -0.1 to 0.2
- rim_angle: float32 [2, 512], P('panel', ('lat', 'lon')), may hold values from -3 to 3
- rim_target: int32 [2, 512, 2], P('panel'), may hold values from -2 to 65, as said below
Outputs:
- change: float32 [2, 64, 64, 8, 128], P('panel', 'lat', 'lon')
The draws below stay inside these ranges and needn't reach their ends.
Inputs may be any that keep to these rules, and one draw needn't show every extreme that they name: `rim_base`: entry e of panel p names a base cell (row, column) of panel p whose 4 x 4 donor stencil, rows and columns from base - 1 to base + 2, lies inside the panel; the base cell lies in block e // 32 of 16 x 16 cells, blocks numbered row by row with 4 blocks to a row. `rim_target`: the rim of panel q is a loop of 512 positions: rows -2 and -1 at columns 0 to 64 - 1 (column by column, row -2 first), then columns 64 and 65 at rows 0 to 64 - 1 (row by row), then rows 64 and 65 at columns 63 down to 0, then columns -2 and -1 at rows 63 down to 0. Entry e, with b = e // 32 and i = e % 32, fills loop position (i * 16 + b + o_q) mod 512, for one offset o_q per panel.
All inputs are finite; a program needn't handle non-finite values.
Results may differ from the reference program's by a relative error of at most 0.00015.
Values sent between devices are 32-bit elements; how exact they have to be, the bound alone decides.
No kernel may reach another device: no remote copies, remote signals or barrier semaphores. Data moves between devices by JAX's collectives and lax.ppermute only.
A program may use at most 64 MiB of HBM per device.

```python
import math
import jax
import jax.numpy as jnp
from jax import lax

CT = 16
CP = 16
NR = 128
FIELDS = 8
NTH = 64
NPH = 64
RIM_DEV = 32
NRIM = 512
N_LAT = 4


def draw_rim_base(key, part):
    lat_blocks = NTH // CT
    lon_blocks = NPH // CP
    entry = jnp.arange(NRIM, dtype=jnp.int32)
    block_id = entry // RIM_DEV
    block_row = block_id // lon_blocks
    block_col = block_id % lon_blocks
    low_row = jnp.where(block_row == 0, 1, 0)
    high_row = jnp.where(block_row == lat_blocks - 1, CT - 2, CT)
    low_col = jnp.where(block_col == 0, 1, 0)
    high_col = jnp.where(block_col == lon_blocks - 1, CP - 2, CP)
    key_row, key_col = jax.random.split(jax.random.fold_in(key, 11))
    row_pick = jax.random.randint(key_row, (2, NRIM), low_row, high_row, dtype=jnp.int32)
    col_pick = jax.random.randint(key_col, (2, NRIM), low_col, high_col, dtype=jnp.int32)
    return jnp.stack([block_row * CT + row_pick, block_col * CP + col_pick], axis=-1).astype(jnp.int32)


def loop_order():
    entry = jnp.arange(NRIM, dtype=jnp.int32)
    block_total = NRIM // RIM_DEV
    return entry % RIM_DEV * block_total + entry // RIM_DEV


def draw_rim_angle(key, part):
    loop_pos = loop_order().astype(jnp.float32)
    key_phase, key_rough = jax.random.split(jax.random.fold_in(key, 31))
    phase = jax.random.uniform(key_phase, (2, 1), jnp.float32, 0.0, 2.0 * math.pi)
    smooth = 2.5 * jnp.sin(2.0 * math.pi * loop_pos[None, :] / NRIM + phase)
    rough = jnp.clip(0.15 * jax.random.normal(key_rough, (2, NRIM), jnp.float32), -0.4, 0.4)
    return (smooth + rough).astype(jnp.float32)


def draw_rim_target(key, part):
    loop_pos = loop_order()
    offset = jax.random.randint(jax.random.fold_in(key, 23), (2, 1), 0, NRIM, dtype=jnp.int32)
    place = (loop_pos[None, :] + offset) % NRIM
    top_band = place < 2 * NPH
    right_ids = place - 2 * NPH
    right_band = (right_ids >= 0) & (right_ids < 2 * NTH)
    bottom_ids = right_ids - 2 * NTH
    bottom_band = (bottom_ids >= 0) & (bottom_ids < 2 * NPH)
    left_ids = bottom_ids - 2 * NPH
    row_ids = jnp.where(top_band, place % 2 - 2, jnp.where(right_band, right_ids // 2, jnp.where(bottom_band, NTH + bottom_ids % 2, NTH - 1 - left_ids // 2)))
    col_ids = jnp.where(top_band, place // 2, jnp.where(right_band, NPH + right_ids % 2, jnp.where(bottom_band, NPH - 1 - bottom_ids // 2, left_ids % 2 - 2)))
    return jnp.stack([row_ids, col_ids], axis=-1).astype(jnp.int32)


def level_of(stream_key, dims, cuts, least, top_value):
    level = 1.0
    for position, shards_of in cuts:
        draws = jax.random.uniform(jax.random.fold_in(jax.random.fold_in(stream_key, 6), position), (shards_of,), jnp.float32, least / len(cuts), top_value / len(cuts))
        level = level * jnp.repeat(jnp.exp(draws), dims[position] // shards_of).reshape((-1,) + (1,) * (len(dims) - 1 - position))
    return level


def gaussian(key, shape, scale, most, pieces=(), kind=jnp.bfloat16):
    gain = level_of(key, shape, pieces, -0.22, 0.18) if pieces else 1.0
    array = jax.random.normal(key, shape, jnp.float32) * scale * gain
    return jnp.minimum(jnp.maximum(array, -most), most).astype(kind)


def setup_inputs(seed: int = 0) -> dict:
    streams_of = jax.random.split(jax.random.key(seed), 6)
    state = gaussian(streams_of[0], (2, NTH, NPH, FIELDS, NR), 1.0, 6.0, ((0, 2), (1, 4), (2, 4)), jnp.float32)
    rim_base = draw_rim_base(jax.random.fold_in(streams_of[5], 71), 0)
    rim_weight = jnp.clip(-0.1 + 0.3 * jax.random.uniform(streams_of[2], (2, NRIM, 16), jnp.float32) ** level_of(streams_of[2], (2, NRIM, 16), ((0, 2), (1, 16)), -0.2, 0.2), -0.1, 0.2)
    rim_angle = draw_rim_angle(jax.random.fold_in(streams_of[5], 71), 0)
    rim_target = draw_rim_target(jax.random.fold_in(streams_of[5], 71), 0)
    return dict(state=state, rim_base=rim_base, rim_weight=rim_weight, rim_angle=rim_angle, rim_target=rim_target)


ETA_COEF = 0.2
NU_COEF = 0.2
KAPPA_COEF = 0.3
SOUND_SQ = 1.0
ARCHIMEDES_LIFT = 0.5
TIME_STEP = 0.2


def grid_geometry(levels, theta_count, phi_count):
    radius_scale = 2.0 * theta_count / math.pi
    radial_step = 0.65 * radius_scale / levels
    radius = 0.35 * radius_scale + (jnp.arange(levels, dtype=jnp.int32).astype(jnp.float32) + 0.5) * radial_step
    return radius, radial_step, math.pi / (2 * theta_count), 1.5 * math.pi / phi_count


def theta_sine(first_row, count, theta_count):
    row_index = first_row + jnp.arange(count, dtype=jnp.int32)
    colatitude = math.pi / 4 + (row_index.astype(jnp.float32) + 0.5) * (math.pi / (2 * theta_count))
    return jnp.sin(colatitude)


def inner_volumes(quantity):
    return quantity[1:-1, 1:-1]


def diff_theta(quantity, spacing):
    return (quantity[2:, 1:-1] - quantity[:-2, 1:-1]) * (0.5 / spacing)


def diff_phi(quantity, spacing):
    return (quantity[1:-1, 2:] - quantity[1:-1, :-2]) * (0.5 / spacing)


def diff_radius(quantity, spacing):
    zero_layer = jnp.zeros(quantity.shape[:-1] + (1,), quantity.dtype)
    upper_part = jnp.concatenate([quantity[..., 1:], zero_layer], axis=-1)
    lower_part = jnp.concatenate([zero_layer, quantity[..., :-1]], axis=-1)
    return (upper_part - lower_part) * (0.5 / spacing)


def curl_of(directional_components, colatitude_factor_list, spherical_layout):
    radius, radial_step, polar_step, azimuth_step = spherical_layout
    radial_part, polar_part, azimuth_part = directional_components
    polar_factor_halfway = colatitude_factor_list[1:-1]
    out_radial = (diff_theta(colatitude_factor_list * azimuth_part, polar_step) - diff_phi(polar_part, azimuth_step)) / (radius * polar_factor_halfway)
    out_polar = (diff_phi(radial_part, azimuth_step) / polar_factor_halfway - diff_radius(inner_volumes(radius * azimuth_part), radial_step)) / radius
    out_azimuth = (diff_radius(inner_volumes(radius * polar_part), radial_step) - diff_theta(radial_part, polar_step)) / radius
    return (out_radial, out_polar, out_azimuth)


def slope_quantity(quantity, colatitude_factor_list, spherical_layout):
    radius, radial_step, polar_step, azimuth_step = spherical_layout
    polar_factor_halfway = colatitude_factor_list[1:-1]
    return (diff_radius(inner_volumes(quantity), radial_step), diff_theta(quantity, polar_step) / radius, diff_phi(quantity, azimuth_step) / (radius * polar_factor_halfway))


def outflow_density(directional_components, colatitude_factor_list, spherical_layout):
    radius, radial_step, polar_step, azimuth_step = spherical_layout
    radial_part, polar_part, azimuth_part = directional_components
    polar_factor_halfway = colatitude_factor_list[1:-1]
    radial_term = diff_radius(inner_volumes(radius * radius * radial_part), radial_step) / (radius * radius)
    return radial_term + (diff_theta(colatitude_factor_list * polar_part, polar_step) + diff_phi(azimuth_part, azimuth_step)) / (radius * polar_factor_halfway)


def cross_product(left, right):
    return (left[1] * right[2] - left[2] * right[1], left[2] * right[0] - left[0] * right[2], left[0] * right[1] - left[1] * right[0])


def dot_product(left, right):
    return left[0] * right[0] + left[1] * right[1] + left[2] * right[2]


def tendency(padded, colatitude_factor_list, spherical_layout):
    directional_components = [padded[:, :, number, :] for number in range(8)]
    velocity = tuple(directional_components[0:3])
    magnetic = tuple(directional_components[3:6])
    warmth_state = directional_components[6]
    pressure = directional_components[7]
    polar_factor_halfway = colatitude_factor_list[1:-1]
    current = curl_of(magnetic, colatitude_factor_list, spherical_layout)
    vorticity = curl_of(velocity, colatitude_factor_list, spherical_layout)
    warmth_slope = slope_quantity(warmth_state, colatitude_factor_list, spherical_layout)
    velocity_mid = tuple(inner_volumes(part) for part in velocity)
    magnetic_mid = tuple(inner_volumes(part) for part in magnetic)
    induced = cross_product(velocity_mid, magnetic_mid)
    electric = tuple(induced[number] - ETA_COEF * current[number] for number in range(3))
    magnetic_rate = curl_of(electric, polar_factor_halfway, spherical_layout)
    vorticity_curl = curl_of(vorticity, polar_factor_halfway, spherical_layout)
    thermal_flux = outflow_density(warmth_slope, polar_factor_halfway, spherical_layout)
    total_head = inner_volumes(pressure) + 0.5 * dot_product(velocity_mid, velocity_mid)
    head_grad = slope_quantity(total_head, polar_factor_halfway, spherical_layout)
    pressure_rate = -SOUND_SQ * outflow_density(velocity_mid, polar_factor_halfway, spherical_layout)
    velocity_in = tuple(inner_volumes(part) for part in velocity_mid)
    magnetic_in = tuple(inner_volumes(part) for part in magnetic_mid)
    current_in = tuple(inner_volumes(part) for part in current)
    vorticity_in = tuple(inner_volumes(part) for part in vorticity)
    slope_heat_entering = tuple(inner_volumes(part) for part in warmth_slope)
    warmth_entering = inner_volumes(inner_volumes(warmth_state))
    lorentz = cross_product(current_in, magnetic_in)
    advect = cross_product(velocity_in, vorticity_in)
    flow_acceleration = [advect[number] + lorentz[number] - head_grad[number] - NU_COEF * vorticity_curl[number] for number in range(3)]
    flow_acceleration[0] = flow_acceleration[0] + ARCHIMEDES_LIFT * warmth_entering
    temp_rate = KAPPA_COEF * thermal_flux - dot_product(velocity_in, slope_heat_entering)
    return jnp.stack(flow_acceleration + list(magnetic_rate) + [temp_rate, pressure_rate], axis=2)


def interpolate(donors, weights, turning):
    mixed = jnp.einsum("ek,ekfr->efr", weights, donors, precision=lax.Precision.HIGHEST)
    cosine = jnp.cos(turning)[:, None]
    sine_turn = jnp.sin(turning)[:, None]
    return jnp.stack([mixed[:, 0], cosine * mixed[:, 1] - sine_turn * mixed[:, 2], sine_turn * mixed[:, 1] + cosine * mixed[:, 2], mixed[:, 3], cosine * mixed[:, 4] - sine_turn * mixed[:, 5], sine_turn * mixed[:, 4] + cosine * mixed[:, 5], mixed[:, 6], mixed[:, 7]], axis=1)


def rim_values(fields, rim_base, rim_weight, rim_angle, donor_panel):
    base_cell = rim_base[donor_panel]
    steps_row = jnp.arange(4, dtype=jnp.int32)
    offsets = ((steps_row[:, None] - 1) * NPH + steps_row[None, :] - 1).reshape(1, 16)
    donor_ids = (base_cell[:, 0] * NPH + base_cell[:, 1])[:, None] + offsets
    flat_cells = fields[donor_panel].reshape(NTH * NPH, fields.shape[3], fields.shape[4])
    return interpolate(flat_cells[donor_ids], rim_weight[donor_panel], rim_angle[donor_panel])


def padded_panel(fields, values, rim_target, panel_id):
    wide_cols = NPH + 4
    frame = jnp.zeros((NTH + 4, wide_cols) + fields.shape[3:], fields.dtype)
    frame = frame.at[2:-2, 2:-2].set(fields[panel_id])
    target = rim_target[panel_id]
    spots = (target[:, 0] + 2) * wide_cols + target[:, 1] + 2
    flat_frame = frame.reshape(((NTH + 4) * wide_cols,) + fields.shape[3:]).at[spots].set(values)
    return flat_frame.reshape((NTH + 4, wide_cols) + fields.shape[3:])


def panel_rate(frame, spherical_layout):
    def one_slab(slab_id):
        first_row = slab_id * CT
        row_slab = lax.dynamic_slice_in_dim(frame, first_row, CT + 4, 0)
        colatitude_factor_list = theta_sine(first_row - 2, CT + 4, NTH)[:, None, None]
        return tendency(row_slab, colatitude_factor_list, spherical_layout)

    slabs = lax.map(one_slab, jnp.arange(N_LAT, dtype=jnp.int32))
    return slabs.reshape((NTH, NPH) + frame.shape[2:])


def rates(fields, rim_base, rim_weight, rim_angle, rim_target, spherical_layout):
    results = []
    for panel_id in range(2):
        values = rim_values(fields, rim_base, rim_weight, rim_angle, 1 - panel_id)
        frame = padded_panel(fields, values, rim_target, panel_id)
        results.append(panel_rate(frame, spherical_layout))
    return jnp.stack(results)


def reference(state, rim_base, rim_weight, rim_angle, rim_target):
    spherical_layout = grid_geometry(NR, NTH, NPH)
    first_rate = rates(state, rim_base, rim_weight, rim_angle, rim_target, spherical_layout)
    middle = state + TIME_STEP * first_rate
    second_rate = rates(middle, rim_base, rim_weight, rim_angle, rim_target, spherical_layout)
    return 0.5 * TIME_STEP * (first_rate + second_rate)
```

```python
import math

import jax
import jax.numpy as jnp
import numpy as np
from jax import lax
from jax.experimental import pallas as pl
from jax.experimental.pallas import tpu as pltpu
from jax.sharding import PartitionSpec as P

ETA_COEF = 0.2
NU_COEF = 0.2
KAPPA_COEF = 0.3
SOUND_SQ = 1.0
ARCHIMEDES_LIFT = 0.5
TIME_STEP = 0.2

HALO = 4
PAD = 8
TILE = 8


def is_power_of_two(count):
    return count & (count - 1) == 0


def to_device(index, step, count):
    return index ^ step if is_power_of_two(count) else (index + step) % count


def from_device(index, step, count):
    return index ^ step if is_power_of_two(count) else (index + count - step) % count


def even_pairs(count):
    return [(i, i ^ 1) for i in range(count) if i ^ 1 < count]


def odd_pairs(count):
    route = []
    for low in range(1, count - 1, 2):
        route += [(low, low + 1), (low + 1, low)]
    return route


def lon_route(step, count):
    return [(i, to_device(i, step, count)) for i in range(count)]


def lat_route(step, count):
    return [
        (side * count + i, (1 - side) * count + to_device(i, step, count))
        for side in range(2)
        for i in range(count)
    ]


class Loop:
    def __init__(self, rows, cols, lat_count, lon_count):
        self.rows, self.cols = rows, cols
        self.lat_count, self.lon_count = lat_count, lon_count
        self.nth, self.nph = rows * lat_count, cols * lon_count
        self.total = 4 * (self.nth + self.nph)
        self.blocks = lat_count * lon_count
        longest = max(
            2 * (rows + cols + 2 * HALO), 2 * (rows + 2 * HALO), 2 * (cols + 2 * HALO)
        )
        self.slots = -(-longest // self.blocks)

    def position(self, row, col):
        nth, nph = self.nth, self.nph
        top = 2 * col + row + 2
        right = 2 * nph + 2 * row + col - nph
        bottom = 2 * nph + 2 * nth + 2 * (nph - 1 - col) + row - nth
        left = 4 * nph + 2 * nth + 2 * (nth - 1 - row) + col + 2
        return jnp.where(
            row < 0, top, jnp.where(row >= nth, bottom, jnp.where(col >= nph, right, left))
        )

    def cell(self, place):
        nth, nph = self.nth, self.nph
        right = place - 2 * nph
        bottom = right - 2 * nth
        left = bottom - 2 * nph
        on_top, on_right, on_bottom = right < 0, bottom < 0, left < 0
        row = jnp.where(
            on_top,
            place % 2 - 2,
            jnp.where(
                on_right, right // 2, jnp.where(on_bottom, nth + bottom % 2, nth - 1 - left // 2)
            ),
        )
        col = jnp.where(
            on_top,
            place // 2,
            jnp.where(
                on_right, nph + right % 2, jnp.where(on_bottom, nph - 1 - bottom // 2, left % 2 - 2)
            ),
        )
        return row, col

    def stretch(self, lat, lon):
        nth, nph = self.nth, self.nph
        row_low = jnp.maximum(lat * self.rows - HALO, 0)
        row_high = jnp.minimum(lat * self.rows + self.rows + HALO, nth)
        col_low = jnp.maximum(lon * self.cols - HALO, 0)
        col_high = jnp.minimum(lon * self.cols + self.cols + HALO, nph)
        top, bottom = lat == 0, lat == self.lat_count - 1
        left, right = lon == 0, lon == self.lon_count - 1
        left_start = 4 * nph + 2 * nth + 2 * (nth - row_high)
        bottom_start = 2 * nph + 2 * nth + 2 * (nph - col_high)
        start = jnp.where(
            top & left,
            left_start,
            jnp.where(
                top,
                2 * col_low,
                jnp.where(
                    right, 2 * nph + 2 * row_low, jnp.where(bottom, bottom_start, left_start)
                ),
            ),
        )
        span = jnp.where(top | bottom, 2 * (col_high - col_low), 0) + jnp.where(
            left | right, 2 * (row_high - row_low), 0
        )
        return start, span

    def first_entry(self, start, donor, offset):
        lead = 2 * self.total
        return (start - donor - offset + lead + self.blocks - 1) // self.blocks - (
            lead // self.blocks
        )


def whole(count):
    return [pl.BlockSpec(memory_space=pltpu.VMEM)] * count


def scalars(count):
    return [pl.BlockSpec(memory_space=pltpu.SMEM)] * count


def tiles(index, count):
    if isinstance(index, int):
        return pl.ds(index * TILE, count * TILE)
    return pl.ds(pl.multiple_of(index * TILE, TILE), count * TILE)


def strip_kernel(rows, cols, flag_ref, state_ref, even_ref, odd_ref, send_even_ref, send_odd_ref):
    lat_even = flag_ref[0] == 0
    lon_even = flag_ref[1] == 0

    def copy_rows(first, count, source):
        for out_ref, last in ((send_even_ref, lon_even), (send_odd_ref, jnp.logical_not(lon_even))):
            low = jnp.where(last, cols - HALO, 0)
            for row in range(count):
                out_ref[tiles((first + row) * HALO, HALO), :] = source[
                    tiles(row * cols + low, HALO), :
                ]

    copy_rows(HALO, rows, state_ref)

    @pl.when(lat_even)
    def _():
        copy_rows(0, HALO, odd_ref)
        copy_rows(HALO + rows, HALO, even_ref)

    @pl.when(jnp.logical_not(lat_even))
    def _():
        copy_rows(0, HALO, even_ref)
        copy_rows(HALO + rows, HALO, odd_ref)


def mix_and_pack(entries, wide, table, float_ref, int_ref, frame_ref, value_ref, send_refs, picks):
    field = lax.broadcasted_iota(jnp.int32, (TILE, 128), 0)
    takes_next = (field == 1) | (field == 4)
    turned = takes_next | (field == 2) | (field == 5)

    def one_entry(entry, carry):
        base = int_ref[table["base"] + entry]
        total = None
        for a in range(4):
            for b in range(4):
                weight = float_ref[table["weight"] + entry * 16 + 4 * a + b]
                part = weight * frame_ref[tiles(base + a * wide + b, 1), :]
                total = part if total is None else total + part
        cosine = float_ref[table["cosine"] + entry]
        sine = float_ref[table["sine"] + entry]
        other = jnp.where(
            takes_next, pltpu.roll(total, TILE - 1, 0), pltpu.roll(total, 1, 0)
        )
        mixed = cosine * total + jnp.where(takes_next, -sine, sine) * other
        value_ref[tiles(entry, 1), :] = jnp.where(turned, mixed, total)
        return carry

    lax.fori_loop(0, entries, one_entry, 0, unroll=4)
    for step, send_ref in enumerate(send_refs):
        for place in range(picks):
            entry = int_ref[table["send"] + step * picks + place]
            send_ref[tiles(place, 1), :] = value_ref[tiles(entry, 1), :]


def frame_kernel(
    rows, cols, entries, table, picks, steps,
    flag_ref, int_ref, float_ref, state_ref, lat_even_ref, lat_odd_ref, lon_even_ref, lon_odd_ref,
    frame_ref, *rest,
):
    send_refs, value_ref = rest[:steps], rest[steps]
    wide = cols + 2 * HALO
    lat_even = flag_ref[0] == 0
    lon_even = flag_ref[1] == 0

    def copy_rows(first, count, source, left, width):
        for row in range(count):
            frame_ref[tiles((first + row) * wide + left, width), :] = source[
                tiles(row * width, width), :
            ]

    copy_rows(HALO, rows, state_ref, HALO, cols)

    @pl.when(lat_even)
    def _():
        copy_rows(0, HALO, lat_odd_ref, HALO, cols)
        copy_rows(HALO + rows, HALO, lat_even_ref, HALO, cols)

    @pl.when(jnp.logical_not(lat_even))
    def _():
        copy_rows(0, HALO, lat_even_ref, HALO, cols)
        copy_rows(HALO + rows, HALO, lat_odd_ref, HALO, cols)

    @pl.when(lon_even)
    def _():
        copy_rows(0, rows + 2 * HALO, lon_odd_ref, 0, HALO)
        copy_rows(0, rows + 2 * HALO, lon_even_ref, HALO + cols, HALO)

    @pl.when(jnp.logical_not(lon_even))
    def _():
        copy_rows(0, rows + 2 * HALO, lon_even_ref, 0, HALO)
        copy_rows(0, rows + 2 * HALO, lon_odd_ref, HALO + cols, HALO)

    mix_and_pack(
        entries, wide, table, float_ref, int_ref, frame_ref, value_ref, send_refs, picks
    )


def swap_kernel(lat_count, lon_count, slots, *refs):
    got_refs, out_refs = refs[:lon_count], refs[lon_count:]
    for lat_step in range(lat_count):
        for lon_step in range(lon_count):
            out_refs[lat_step][tiles(lon_step * slots, slots), :] = got_refs[lon_step][
                tiles(lat_step * slots, slots), :
            ]


def section(
    rows, cols, table, arrivals, lat_count, radial_ref, int_ref, float_ref, frame_ref, got_refs,
    plane_ref, work_ref, rate_rows, rate_chunks, emit,
):
    tall, wide = rows + 2 * HALO, cols + 2 * HALO
    pitch = wide + 2 * PAD

    def spread_row(row, carry):
        for chunk in range(0, wide, 8):
            for f in range(TILE):
                start = (row * wide + chunk) * TILE + f
                plane_ref[pl.ds((f * tall + row) * pitch + PAD + chunk, 8), :] = frame_ref[
                    pl.ds(start, 8, stride=TILE), :
                ]
        return carry

    first_row, last_row = rate_rows
    lax.fori_loop(first_row - 2, last_row + 2, spread_row, 0)
    for lat_step in range(lat_count):
        for place in range(arrivals):
            spot = int_ref[table["receive"] + lat_step * arrivals + place]
            plane_ref[pl.ds(spot, TILE, stride=tall * pitch), :] = got_refs[lat_step][
                tiles(place, 1), :
            ]

    levels = radial_ref.shape[-1]
    inverse_radius, ru, rl, du, dl, qu, ql = [radial_ref[n] for n in range(7)]

    def up(x):
        return pltpu.roll(x, levels - 1, 1)

    def down(x):
        return pltpu.roll(x, 1, 1)

    half_theta = table["half_theta"]

    def row_factors(row):
        return (
            float_ref[table["theta_up"] + row],
            float_ref[table["theta_down"] + row],
            float_ref[table["phi"] + row],
        )

    def reader(ref, row, col):
        def at(number, row_step=0, col_step=0):
            return ref[
                pl.ds((number * tall + row + row_step) * pitch + PAD + col + col_step, 8), :
            ]

        return at

    def curl(at, first, factors, with_phi, with_theta):
        tu, td, ph = factors
        a, b, c = first, first + 1, first + 2
        mid_b, mid_c = at(b), at(c)
        radial = inverse_radius * (
            (tu * at(c, 1) - td * at(c, -1)) - ph * (at(b, 0, 1) - at(b, 0, -1))
        )
        polar = with_phi * (at(a, 0, 1) - at(a, 0, -1)) - (ru * up(mid_c) - rl * down(mid_c))
        azimuth = (ru * up(mid_b) - rl * down(mid_b)) - with_theta * (at(a, 1) - at(a, -1))
        return radial, polar, azimuth

    def slope(at, number, with_phi, with_theta):
        mid = at(number)
        return (
            du * up(mid) - dl * down(mid),
            with_theta * (at(number, 1) - at(number, -1)),
            with_phi * (at(number, 0, 1) - at(number, 0, -1)),
        )

    def outflow(at, first, factors):
        tu, td, ph = factors
        mid = at(first)
        return (qu * up(mid) - ql * down(mid)) + inverse_radius * (
            (tu * at(first + 1, 1) - td * at(first + 1, -1))
            + ph * (at(first + 2, 0, 1) - at(first + 2, 0, -1))
        )

    def cross(x, y):
        return (
            x[1] * y[2] - x[2] * y[1],
            x[2] * y[0] - x[0] * y[2],
            x[0] * y[1] - x[1] * y[0],
        )

    def dot(x, y):
        return x[0] * y[0] + x[1] * y[1] + x[2] * y[2]

    with_theta = inverse_radius * half_theta

    def first_pass(row, carry):
        factors = row_factors(row)
        with_phi = inverse_radius * factors[2]
        for chunk in range(0, wide, 8):
            at = reader(plane_ref, row, chunk)

            def put(number, value):
                work_ref[pl.ds((number * tall + row) * pitch + PAD + chunk, 8), :] = value

            flow = [at(n) for n in range(3)]
            field = [at(n) for n in range(3, 6)]
            current = curl(at, 3, factors, with_phi, with_theta)
            spin = curl(at, 0, factors, with_phi, with_theta)
            induced = cross(flow, field)
            warm = slope(at, 6, with_phi, with_theta)
            for n in range(3):
                put(n, current[n])
                put(3 + n, spin[n])
                put(6 + n, induced[n] - ETA_COEF * current[n])
                put(9 + n, warm[n])
            put(12, at(7) + 0.5 * dot(flow, flow))
        return carry

    lax.fori_loop(first_row - 1, last_row + 1, first_pass, 0)

    def second_pass(row, carry):
        factors = row_factors(row)
        with_phi = inverse_radius * factors[2]
        for chunk in rate_chunks:
            at = reader(plane_ref, row, chunk)
            work = reader(work_ref, row, chunk)
            flow = [at(n) for n in range(3)]
            field = [at(n) for n in range(3, 6)]
            current = [work(n) for n in range(3)]
            spin = [work(3 + n) for n in range(3)]
            warm = [work(9 + n) for n in range(3)]
            field_rate = curl(work, 6, factors, with_phi, with_theta)
            spin_curl = curl(work, 3, factors, with_phi, with_theta)
            head = slope(work, 12, with_phi, with_theta)
            lorentz = cross(current, field)
            advect = cross(flow, spin)
            speed = [
                advect[n] + lorentz[n] - head[n] - NU_COEF * spin_curl[n] for n in range(3)
            ]
            speed[0] = speed[0] + ARCHIMEDES_LIFT * at(6)
            heat = KAPPA_COEF * outflow(work, 9, factors) - dot(flow, warm)
            squeeze = -SOUND_SQ * outflow(at, 0, factors)
            emit(row, chunk, at, speed + list(field_rate) + [heat, squeeze])
        return carry

    lax.fori_loop(first_row, last_row, second_pass, 0)


def first_section_kernel(
    rows, cols, entries, table, picks, steps, arrivals, lat_count, nth, nph,
    int_ref, float_ref, radial_ref, frame_in_ref, *rest,
):
    got_refs, rest = rest[:lat_count], rest[lat_count:]
    frame_ref, rate_ref, rest = rest[0], rest[1], rest[2:]
    send_refs, (value_ref, plane_ref, work_ref) = rest[:steps], rest[steps:]
    tall, wide = rows + 2 * HALO, cols + 2 * HALO
    first_row = int_ref[table["corner"]]
    first_col = int_ref[table["corner"] + 1]

    def emit(row, chunk, at, rate):
        in_row = (row + first_row >= 0) & (row + first_row < nth)
        col = lax.broadcasted_iota(jnp.int32, (8, 128), 0) + (chunk + first_col)
        inside = (col >= jnp.where(in_row, 0, nph)) & (col < nph)
        for f in range(TILE):
            rate_ref[f, row, pl.ds(chunk, 8), :] = rate[f]
            start = (row * wide + chunk) * TILE + f
            frame_ref[pl.ds(start, 8, stride=TILE), :] = jnp.where(
                inside, at(f) + TIME_STEP * rate[f], 0.0
            )

    section(
        rows, cols, table, arrivals, lat_count, radial_ref, int_ref, float_ref, frame_in_ref,
        got_refs, plane_ref, work_ref, (2, tall - 2), range(0, wide, 8), emit,
    )
    mix_and_pack(
        entries, wide, table, float_ref, int_ref, frame_ref, value_ref, send_refs, picks
    )


def second_section_kernel(
    rows, cols, table, arrivals, lat_count,
    int_ref, float_ref, radial_ref, frame_in_ref, rate_ref, *rest,
):
    got_refs, rest = rest[:lat_count], rest[lat_count:]
    change_ref, plane_ref, work_ref = rest

    def emit(row, chunk, at, rate):
        for f in range(TILE):
            start = ((row - HALO) * cols + chunk - HALO) * TILE + f
            change_ref[pl.ds(start, 8, stride=TILE), :] = (0.5 * TIME_STEP) * (
                rate_ref[f, row, pl.ds(chunk, 8), :] + rate[f]
            )

    section(
        rows, cols, table, arrivals, lat_count, radial_ref, int_ref, float_ref, frame_in_ref,
        got_refs, plane_ref, work_ref, (HALO, HALO + rows), range(HALO, HALO + cols, 8), emit,
    )


def radial_factors(levels, theta_count):
    scale = 2.0 * theta_count / math.pi
    step = 0.65 * scale / levels
    radius = 0.35 * scale + (np.arange(levels) + 0.5) * step
    half = 0.5 / step
    above = np.append(radius[1:], 0.0)
    below = np.append(0.0, radius[:-1])
    ones_above = np.append(np.ones(levels - 1), 0.0)
    ones_below = np.append(0.0, np.ones(levels - 1))
    rows = np.stack(
        [
            1.0 / radius,
            half * above / radius,
            half * below / radius,
            half * ones_above,
            half * ones_below,
            half * above**2 / radius**2,
            half * below**2 / radius**2,
        ]
    )
    return np.repeat(rows[:, None, :], 8, axis=1).astype(np.float32)


def per_device(state, rim_base, rim_weight, rim_angle, rim_target):
    _, rows, cols, fields, levels = state.shape
    lat_count, lon_count = lax.axis_size("lat"), lax.axis_size("lon")
    loop = Loop(rows, cols, lat_count, lon_count)
    nth, nph, slots = loop.nth, loop.nph, loop.slots
    entries = rim_base.shape[1]
    tall, wide = rows + 2 * HALO, cols + 2 * HALO
    pitch = wide + 2 * PAD
    lat, lon = lax.axis_index("lat"), lax.axis_index("lon")
    first_row, first_col = lat * rows - HALO, lon * cols - HALO
    block = state[0].reshape(rows * cols * fields, levels)
    f32 = jnp.float32

    def tile_array(count):
        return jax.ShapeDtypeStruct((count * TILE, levels), f32)

    mine = loop.position(rim_target[0, 0:1, 0], rim_target[0, 0:1, 1]) % loop.total
    other = lax.ppermute(mine, "panel", [(0, 1), (1, 0)])

    flags = jnp.stack([lat % 2, lon % 2]).astype(jnp.int32)
    cells = state[0]
    last_first = lat % 2 == 0
    head, tail = cells[:HALO], cells[rows - HALO :]
    send_even = jnp.where(last_first, tail, head).reshape(HALO * cols * fields, levels)
    send_odd = jnp.where(last_first, head, tail).reshape(HALO * cols * fields, levels)
    lat_even = lax.ppermute(send_even, "lat", even_pairs(lat_count))
    lat_odd = lax.ppermute(send_odd, "lat", odd_pairs(lat_count))

    strip_even, strip_odd = pl.pallas_call(
        lambda *refs: strip_kernel(rows, cols, *refs),
        out_shape=[tile_array(tall * HALO)] * 2,
        in_specs=scalars(1) + whole(3),
        out_specs=whole(2),
        name="strips",
    )(flags, block, lat_even, lat_odd)
    lon_even = lax.ppermute(strip_even, "lon", even_pairs(lon_count))
    lon_odd = lax.ppermute(strip_odd, "lon", odd_pairs(lon_count))

    base_cell = rim_base[0]
    base = (base_cell[:, 0] - first_row - 1) * wide + (base_cell[:, 1] - first_col - 1)
    lat_step = jnp.arange(lat_count, dtype=jnp.int32)
    lon_step = jnp.arange(lon_count, dtype=jnp.int32)
    slot = jnp.arange(slots, dtype=jnp.int32)
    start, _ = loop.stretch(
        to_device(lat, lat_step, lat_count)[None, :], to_device(lon, lon_step, lon_count)[:, None]
    )
    lead = loop.first_entry(start, lat * lon_count + lon, other)
    send = (lead[:, :, None] + slot) % entries
    donor = (
        from_device(lat, lat_step, lat_count)[:, None] * lon_count
        + from_device(lon, lon_step, lon_count)[None, :]
    )
    start, span = loop.stretch(lat, lon)
    lead = loop.first_entry(start, donor, mine)
    place = (lead[:, :, None] + slot) * loop.blocks + donor[:, :, None] + mine
    row, col = loop.cell(place % loop.total)
    receive = jnp.where(
        place < start + span, (row - first_row) * pitch + PAD + (col - first_col), 0
    )
    ints = jnp.concatenate(
        [
            base.reshape(-1),
            send.reshape(-1),
            receive.reshape(-1),
            first_row[None],
            first_col[None],
        ]
    ).astype(jnp.int32)
    picks = lat_count * slots
    arrivals = lon_count * slots

    polar_step, azimuth_step = math.pi / (2 * nth), 1.5 * math.pi / nph
    row_ids = first_row - 1 + jnp.arange(tall + 2, dtype=jnp.int32)
    sines = jnp.sin(math.pi / 4 + (row_ids.astype(f32) + 0.5) * (math.pi / (2 * nth)))
    middle = sines[1:-1]
    floats = jnp.concatenate(
        [
            sines[2:] / middle * (0.5 / polar_step),
            sines[:-2] / middle * (0.5 / polar_step),
            (0.5 / azimuth_step) / middle,
            jnp.cos(rim_angle[0]),
            jnp.sin(rim_angle[0]),
            rim_weight[0].reshape(-1),
        ]
    )
    table = {
        "base": 0,
        "send": entries,
        "receive": entries + lon_count * picks,
        "corner": entries + lon_count * picks + lat_count * arrivals,
        "theta_up": 0,
        "theta_down": tall,
        "phi": 2 * tall,
        "cosine": 3 * tall,
        "sine": 3 * tall + entries,
        "weight": 3 * tall + 2 * entries,
        "half_theta": 0.5 / polar_step,
    }
    radial = jnp.asarray(radial_factors(levels, nth))

    frame, *packed = pl.pallas_call(
        lambda *refs: frame_kernel(rows, cols, entries, table, picks, lon_count, *refs),
        out_shape=[tile_array(tall * wide)] + [tile_array(picks)] * lon_count,
        in_specs=scalars(3) + whole(5),
        out_specs=whole(1 + lon_count),
        scratch_shapes=[pltpu.VMEM((entries * TILE, levels), f32)],
        name="frame",
    )(flags, ints, floats, block, lat_even, lat_odd, lon_even, lon_odd)

    def exchange(packed):
        got = [packed[0]] + [
            lax.ppermute(packed[step], "lon", lon_route(step, lon_count))
            for step in range(1, lon_count)
        ]
        turned = pl.pallas_call(
            lambda *refs: swap_kernel(lat_count, lon_count, slots, *refs),
            out_shape=[tile_array(arrivals)] * lat_count,
            in_specs=whole(lon_count),
            out_specs=whole(lat_count),
            name="swap",
        )(*got)
        return [
            lax.ppermute(turned[step], ("panel", "lat"), lat_route(step, lat_count))
            for step in range(lat_count)
        ]

    got = exchange(packed)
    planes = [
        pltpu.VMEM((fields * tall * (wide + 2 * PAD), levels), f32),
        pltpu.VMEM((13 * tall * (wide + 2 * PAD), levels), f32),
    ]
    frame, rate, *packed = pl.pallas_call(
        lambda *refs: first_section_kernel(
            rows, cols, entries, table, picks, lon_count, arrivals, lat_count, nth, nph, *refs
        ),
        out_shape=[tile_array(tall * wide), jax.ShapeDtypeStruct((fields, tall, wide, levels), f32)]
        + [tile_array(picks)] * lon_count,
        in_specs=scalars(2) + whole(2 + lat_count),
        out_specs=whole(2 + lon_count),
        scratch_shapes=[pltpu.VMEM((entries * TILE, levels), f32)] + planes,
        name="first_section",
    )(ints, floats, radial, frame, *got)

    got = exchange(packed)
    change = pl.pallas_call(
        lambda *refs: second_section_kernel(rows, cols, table, arrivals, lat_count, *refs),
        out_shape=tile_array(rows * cols),
        in_specs=scalars(2) + whole(3 + lat_count),
        out_specs=whole(1)[0],
        scratch_shapes=planes,
        name="second_section",
    )(ints, floats, radial, frame, rate, *got)
    return change.reshape(1, rows, cols, fields, levels)


def solution(mesh):
    return jax.shard_map(
        per_device,
        mesh=mesh,
        in_specs=(
            P("panel", "lat", "lon", None, None),
            P("panel", ("lat", "lon"), None),
            P("panel", ("lat", "lon"), None),
            P("panel", ("lat", "lon")),
            P("panel", None, None),
        ),
        out_specs=P("panel", "lat", "lon", None, None),
        check_vma=False,
    )
```

```python
import math

import jax
import jax.numpy as jnp
import numpy as np
from jax import lax
from jax.experimental import pallas as pl
from jax.experimental.pallas import tpu as pltpu
from jax.sharding import PartitionSpec as P

ETA_COEF = 0.2
NU_COEF = 0.2
KAPPA_COEF = 0.3
SOUND_SQ = 1.0
ARCHIMEDES_LIFT = 0.5
TIME_STEP = 0.2

HALO = 4
PAD = 8
TILE = 8


def is_power_of_two(count):
    return count & (count - 1) == 0


def to_device(index, step, count):
    return index ^ step if is_power_of_two(count) else (index + step) % count


def from_device(index, step, count):
    return index ^ step if is_power_of_two(count) else (index + count - step) % count


def even_pairs(count):
    return [(i, i ^ 1) for i in range(count) if i ^ 1 < count]


def odd_pairs(count):
    route = []
    for low in range(1, count - 1, 2):
        route += [(low, low + 1), (low + 1, low)]
    return route


def lon_route(step, count):
    return [(i, to_device(i, step, count)) for i in range(count)]


def lat_route(step, count):
    return [
        (side * count + i, (1 - side) * count + to_device(i, step, count))
        for side in range(2)
        for i in range(count)
    ]


class Loop:
    def __init__(self, rows, cols, lat_count, lon_count):
        self.rows, self.cols = rows, cols
        self.lat_count, self.lon_count = lat_count, lon_count
        self.nth, self.nph = rows * lat_count, cols * lon_count
        self.total = 4 * (self.nth + self.nph)
        self.blocks = lat_count * lon_count
        longest = max(
            2 * (rows + cols + 2 * HALO), 2 * (rows + 2 * HALO), 2 * (cols + 2 * HALO)
        )
        self.slots = -(-longest // self.blocks)

    def position(self, row, col):
        nth, nph = self.nth, self.nph
        top = 2 * col + row + 2
        right = 2 * nph + 2 * row + col - nph
        bottom = 2 * nph + 2 * nth + 2 * (nph - 1 - col) + row - nth
        left = 4 * nph + 2 * nth + 2 * (nth - 1 - row) + col + 2
        return jnp.where(
            row < 0, top, jnp.where(row >= nth, bottom, jnp.where(col >= nph, right, left))
        )

    def cell(self, place):
        nth, nph = self.nth, self.nph
        right = place - 2 * nph
        bottom = right - 2 * nth
        left = bottom - 2 * nph
        on_top, on_right, on_bottom = right < 0, bottom < 0, left < 0
        row = jnp.where(
            on_top,
            place % 2 - 2,
            jnp.where(
                on_right, right // 2, jnp.where(on_bottom, nth + bottom % 2, nth - 1 - left // 2)
            ),
        )
        col = jnp.where(
            on_top,
            place // 2,
            jnp.where(
                on_right, nph + right % 2, jnp.where(on_bottom, nph - 1 - bottom // 2, left % 2 - 2)
            ),
        )
        return row, col

    def stretch(self, lat, lon):
        nth, nph = self.nth, self.nph
        row_low = jnp.maximum(lat * self.rows - HALO, 0)
        row_high = jnp.minimum(lat * self.rows + self.rows + HALO, nth)
        col_low = jnp.maximum(lon * self.cols - HALO, 0)
        col_high = jnp.minimum(lon * self.cols + self.cols + HALO, nph)
        top, bottom = lat == 0, lat == self.lat_count - 1
        left, right = lon == 0, lon == self.lon_count - 1
        left_start = 4 * nph + 2 * nth + 2 * (nth - row_high)
        bottom_start = 2 * nph + 2 * nth + 2 * (nph - col_high)
        start = jnp.where(
            top & left,
            left_start,
            jnp.where(
                top,
                2 * col_low,
                jnp.where(
                    right, 2 * nph + 2 * row_low, jnp.where(bottom, bottom_start, left_start)
                ),
            ),
        )
        span = jnp.where(top | bottom, 2 * (col_high - col_low), 0) + jnp.where(
            left | right, 2 * (row_high - row_low), 0
        )
        return start, span

    def first_entry(self, start, donor, offset):
        lead = 2 * self.total
        return (start - donor - offset + lead + self.blocks - 1) // self.blocks - (
            lead // self.blocks
        )


def whole(count):
    return [pl.BlockSpec(memory_space=pltpu.VMEM)] * count


def scalars(count):
    return [pl.BlockSpec(memory_space=pltpu.SMEM)] * count


def grant(mebibytes):
    return pltpu.CompilerParams(vmem_limit_bytes=mebibytes << 20)


def tiles(index, count):
    if isinstance(index, int):
        return pl.ds(index * TILE, count * TILE)
    return pl.ds(pl.multiple_of(index * TILE, TILE), count * TILE)


def strip_kernel(rows, cols, flag_ref, state_ref, even_ref, odd_ref, send_even_ref, send_odd_ref):
    lat_even = flag_ref[0] == 0
    lon_even = flag_ref[1] == 0

    def copy_rows(first, count, source):
        for out_ref, last in ((send_even_ref, lon_even), (send_odd_ref, jnp.logical_not(lon_even))):
            low = jnp.where(last, cols - HALO, 0)
            for row in range(count):
                out_ref[tiles((first + row) * HALO, HALO), :] = source[
                    tiles(row * cols + low, HALO), :
                ]

    copy_rows(HALO, rows, state_ref)

    @pl.when(lat_even)
    def _():
        copy_rows(0, HALO, odd_ref)
        copy_rows(HALO + rows, HALO, even_ref)

    @pl.when(jnp.logical_not(lat_even))
    def _():
        copy_rows(0, HALO, even_ref)
        copy_rows(HALO + rows, HALO, odd_ref)


def mix_and_pack(entries, wide, table, float_ref, int_ref, frame_ref, value_ref, send_refs, picks):
    field = lax.broadcasted_iota(jnp.int32, (TILE, 128), 0)
    takes_next = (field == 1) | (field == 4)
    turned = takes_next | (field == 2) | (field == 5)

    def one_entry(entry, carry):
        base = int_ref[table["base"] + entry]
        total = None
        for a in range(4):
            for b in range(4):
                weight = float_ref[table["weight"] + entry * 16 + 4 * a + b]
                part = weight * frame_ref[tiles(base + a * wide + b, 1), :]
                total = part if total is None else total + part
        cosine = float_ref[table["cosine"] + entry]
        sine = float_ref[table["sine"] + entry]
        other = jnp.where(
            takes_next, pltpu.roll(total, TILE - 1, 0), pltpu.roll(total, 1, 0)
        )
        mixed = cosine * total + jnp.where(takes_next, -sine, sine) * other
        value_ref[tiles(entry, 1), :] = jnp.where(turned, mixed, total)
        return carry

    lax.fori_loop(0, entries, one_entry, 0, unroll=4)
    for step, send_ref in enumerate(send_refs):
        for place in range(picks):
            entry = int_ref[table["send"] + step * picks + place]
            send_ref[tiles(place, 1), :] = value_ref[tiles(entry, 1), :]


def frame_kernel(
    rows, cols, entries, table, picks, steps,
    flag_ref, int_ref, float_ref, state_ref, lat_even_ref, lat_odd_ref, lon_even_ref, lon_odd_ref,
    frame_ref, *rest,
):
    send_refs, value_ref = rest[:steps], rest[steps]
    wide = cols + 2 * HALO
    lat_even = flag_ref[0] == 0
    lon_even = flag_ref[1] == 0

    def copy_rows(first, count, source, left, width):
        for row in range(count):
            frame_ref[tiles((first + row) * wide + left, width), :] = source[
                tiles(row * width, width), :
            ]

    copy_rows(HALO, rows, state_ref, HALO, cols)

    @pl.when(lat_even)
    def _():
        copy_rows(0, HALO, lat_odd_ref, HALO, cols)
        copy_rows(HALO + rows, HALO, lat_even_ref, HALO, cols)

    @pl.when(jnp.logical_not(lat_even))
    def _():
        copy_rows(0, HALO, lat_even_ref, HALO, cols)
        copy_rows(HALO + rows, HALO, lat_odd_ref, HALO, cols)

    @pl.when(lon_even)
    def _():
        copy_rows(0, rows + 2 * HALO, lon_odd_ref, 0, HALO)
        copy_rows(0, rows + 2 * HALO, lon_even_ref, HALO + cols, HALO)

    @pl.when(jnp.logical_not(lon_even))
    def _():
        copy_rows(0, rows + 2 * HALO, lon_even_ref, 0, HALO)
        copy_rows(0, rows + 2 * HALO, lon_odd_ref, HALO + cols, HALO)

    mix_and_pack(
        entries, wide, table, float_ref, int_ref, frame_ref, value_ref, send_refs, picks
    )


def swap_kernel(lat_count, lon_count, slots, *refs):
    got_refs, out_refs = refs[:lon_count], refs[lon_count:]
    for lat_step in range(lat_count):
        for lon_step in range(lon_count):
            out_refs[lat_step][tiles(lon_step * slots, slots), :] = got_refs[lon_step][
                tiles(lat_step * slots, slots), :
            ]


def section(
    rows, cols, table, arrivals, lat_count, radial_ref, int_ref, float_ref, frame_ref, got_refs,
    plane_ref, work_ref, rate_rows, rate_chunks, emit,
):
    tall, wide = rows + 2 * HALO, cols + 2 * HALO
    pitch = wide + 2 * PAD

    def spread_row(row, carry):
        for chunk in range(0, wide, 8):
            for f in range(TILE):
                start = (row * wide + chunk) * TILE + f
                plane_ref[pl.ds((f * tall + row) * pitch + PAD + chunk, 8), :] = frame_ref[
                    pl.ds(start, 8, stride=TILE), :
                ]
        return carry

    first_row, last_row = rate_rows
    lax.fori_loop(first_row - 2, last_row + 2, spread_row, 0)
    for lat_step in range(lat_count):
        for place in range(arrivals):
            spot = int_ref[table["receive"] + lat_step * arrivals + place]
            plane_ref[pl.ds(spot, TILE, stride=tall * pitch), :] = got_refs[lat_step][
                tiles(place, 1), :
            ]

    levels = radial_ref.shape[-1]
    inverse_radius, ru, rl, du, dl, qu, ql = [radial_ref[n] for n in range(7)]

    def up(x):
        return pltpu.roll(x, levels - 1, 1)

    def down(x):
        return pltpu.roll(x, 1, 1)

    half_theta = table["half_theta"]

    def row_factors(row):
        return (
            float_ref[table["theta_up"] + row],
            float_ref[table["theta_down"] + row],
            float_ref[table["phi"] + row],
        )

    def reader(ref, row, col):
        def at(number, row_step=0, col_step=0):
            return ref[
                pl.ds((number * tall + row + row_step) * pitch + PAD + col + col_step, 8), :
            ]

        return at

    def curl(at, first, factors, with_phi, with_theta):
        tu, td, ph = factors
        a, b, c = first, first + 1, first + 2
        mid_b, mid_c = at(b), at(c)
        radial = inverse_radius * (
            (tu * at(c, 1) - td * at(c, -1)) - ph * (at(b, 0, 1) - at(b, 0, -1))
        )
        polar = with_phi * (at(a, 0, 1) - at(a, 0, -1)) - (ru * up(mid_c) - rl * down(mid_c))
        azimuth = (ru * up(mid_b) - rl * down(mid_b)) - with_theta * (at(a, 1) - at(a, -1))
        return radial, polar, azimuth

    def slope(at, number, with_phi, with_theta):
        mid = at(number)
        return (
            du * up(mid) - dl * down(mid),
            with_theta * (at(number, 1) - at(number, -1)),
            with_phi * (at(number, 0, 1) - at(number, 0, -1)),
        )

    def outflow(at, first, factors):
        tu, td, ph = factors
        mid = at(first)
        return (qu * up(mid) - ql * down(mid)) + inverse_radius * (
            (tu * at(first + 1, 1) - td * at(first + 1, -1))
            + ph * (at(first + 2, 0, 1) - at(first + 2, 0, -1))
        )

    def cross(x, y):
        return (
            x[1] * y[2] - x[2] * y[1],
            x[2] * y[0] - x[0] * y[2],
            x[0] * y[1] - x[1] * y[0],
        )

    def dot(x, y):
        return x[0] * y[0] + x[1] * y[1] + x[2] * y[2]

    with_theta = inverse_radius * half_theta

    def first_pass(row, carry):
        factors = row_factors(row)
        with_phi = inverse_radius * factors[2]
        for chunk in range(0, wide, 8):
            at = reader(plane_ref, row, chunk)

            def put(number, value):
                work_ref[pl.ds((number * tall + row) * pitch + PAD + chunk, 8), :] = value

            flow = [at(n) for n in range(3)]
            field = [at(n) for n in range(3, 6)]
            current = curl(at, 3, factors, with_phi, with_theta)
            spin = curl(at, 0, factors, with_phi, with_theta)
            induced = cross(flow, field)
            warm = slope(at, 6, with_phi, with_theta)
            for n in range(3):
                put(n, current[n])
                put(3 + n, spin[n])
                put(6 + n, induced[n] - ETA_COEF * current[n])
                put(9 + n, warm[n])
            put(12, at(7) + 0.5 * dot(flow, flow))
        return carry

    lax.fori_loop(first_row - 1, last_row + 1, first_pass, 0)

    def second_pass(row, carry):
        factors = row_factors(row)
        with_phi = inverse_radius * factors[2]
        for chunk in rate_chunks:
            at = reader(plane_ref, row, chunk)
            work = reader(work_ref, row, chunk)
            flow = [at(n) for n in range(3)]
            field = [at(n) for n in range(3, 6)]
            current = [work(n) for n in range(3)]
            spin = [work(3 + n) for n in range(3)]
            warm = [work(9 + n) for n in range(3)]
            field_rate = curl(work, 6, factors, with_phi, with_theta)
            spin_curl = curl(work, 3, factors, with_phi, with_theta)
            head = slope(work, 12, with_phi, with_theta)
            lorentz = cross(current, field)
            advect = cross(flow, spin)
            speed = [
                advect[n] + lorentz[n] - head[n] - NU_COEF * spin_curl[n] for n in range(3)
            ]
            speed[0] = speed[0] + ARCHIMEDES_LIFT * at(6)
            heat = KAPPA_COEF * outflow(work, 9, factors) - dot(flow, warm)
            squeeze = -SOUND_SQ * outflow(at, 0, factors)
            emit(row, chunk, at, speed + list(field_rate) + [heat, squeeze])
        return carry

    lax.fori_loop(first_row, last_row, second_pass, 0)


def first_section_kernel(
    rows, cols, entries, table, picks, steps, arrivals, lat_count, nth, nph,
    int_ref, float_ref, radial_ref, frame_in_ref, *rest,
):
    got_refs, rest = rest[:lat_count], rest[lat_count:]
    frame_ref, rate_ref, rest = rest[0], rest[1], rest[2:]
    send_refs, (value_ref, plane_ref, work_ref) = rest[:steps], rest[steps:]
    tall, wide = rows + 2 * HALO, cols + 2 * HALO
    first_row = int_ref[table["corner"]]
    first_col = int_ref[table["corner"] + 1]

    def emit(row, chunk, at, rate):
        in_row = (row + first_row >= 0) & (row + first_row < nth)
        col = lax.broadcasted_iota(jnp.int32, (8, 128), 0) + (chunk + first_col)
        inside = (col >= jnp.where(in_row, 0, nph)) & (col < nph)
        for f in range(TILE):
            rate_ref[f, row, pl.ds(chunk, 8), :] = rate[f]
            start = (row * wide + chunk) * TILE + f
            frame_ref[pl.ds(start, 8, stride=TILE), :] = jnp.where(
                inside, at(f) + TIME_STEP * rate[f], 0.0
            )

    section(
        rows, cols, table, arrivals, lat_count, radial_ref, int_ref, float_ref, frame_in_ref,
        got_refs, plane_ref, work_ref, (2, tall - 2), range(0, wide, 8), emit,
    )
    mix_and_pack(
        entries, wide, table, float_ref, int_ref, frame_ref, value_ref, send_refs, picks
    )


def second_section_kernel(
    rows, cols, table, arrivals, lat_count,
    int_ref, float_ref, radial_ref, frame_in_ref, rate_ref, *rest,
):
    got_refs, rest = rest[:lat_count], rest[lat_count:]
    change_ref, plane_ref, work_ref = rest

    def emit(row, chunk, at, rate):
        for f in range(TILE):
            start = ((row - HALO) * cols + chunk - HALO) * TILE + f
            change_ref[pl.ds(start, 8, stride=TILE), :] = (0.5 * TIME_STEP) * (
                rate_ref[f, row, pl.ds(chunk, 8), :] + rate[f]
            )

    section(
        rows, cols, table, arrivals, lat_count, radial_ref, int_ref, float_ref, frame_in_ref,
        got_refs, plane_ref, work_ref, (HALO, HALO + rows), range(HALO, HALO + cols, 8), emit,
    )


def radial_factors(levels, theta_count):
    scale = 2.0 * theta_count / math.pi
    step = 0.65 * scale / levels
    radius = 0.35 * scale + (np.arange(levels) + 0.5) * step
    half = 0.5 / step
    above = np.append(radius[1:], 0.0)
    below = np.append(0.0, radius[:-1])
    ones_above = np.append(np.ones(levels - 1), 0.0)
    ones_below = np.append(0.0, np.ones(levels - 1))
    rows = np.stack(
        [
            1.0 / radius,
            half * above / radius,
            half * below / radius,
            half * ones_above,
            half * ones_below,
            half * above**2 / radius**2,
            half * below**2 / radius**2,
        ]
    )
    return np.repeat(rows[:, None, :], 8, axis=1).astype(np.float32)


def per_device(state, rim_base, rim_weight, rim_angle, rim_target):
    _, rows, cols, fields, levels = state.shape
    lat_count, lon_count = lax.axis_size("lat"), lax.axis_size("lon")
    loop = Loop(rows, cols, lat_count, lon_count)
    nth, nph, slots = loop.nth, loop.nph, loop.slots
    entries = rim_base.shape[1]
    tall, wide = rows + 2 * HALO, cols + 2 * HALO
    pitch = wide + 2 * PAD
    lat, lon = lax.axis_index("lat"), lax.axis_index("lon")
    first_row, first_col = lat * rows - HALO, lon * cols - HALO
    block = state[0].reshape(rows * cols * fields, levels)
    f32 = jnp.float32

    def tile_array(count):
        return jax.ShapeDtypeStruct((count * TILE, levels), f32)

    first_cell = rim_target[0, 0]
    other_cell = lax.ppermute(first_cell, "panel", [(0, 1), (1, 0)])
    mine = loop.position(first_cell[0], first_cell[1])
    other = loop.position(other_cell[0], other_cell[1])

    flags = jnp.stack([lat % 2, lon % 2]).astype(jnp.int32)
    cells = state[0]
    last_first = lat % 2 == 0
    head, tail = cells[:HALO], cells[rows - HALO :]
    send_even = jnp.where(last_first, tail, head).reshape(HALO * cols * fields, levels)
    send_odd = jnp.where(last_first, head, tail).reshape(HALO * cols * fields, levels)
    lat_even = lax.ppermute(send_even, "lat", even_pairs(lat_count))
    lat_odd = lax.ppermute(send_odd, "lat", odd_pairs(lat_count))

    strip_even, strip_odd = pl.pallas_call(
        lambda *refs: strip_kernel(rows, cols, *refs),
        out_shape=[tile_array(tall * HALO)] * 2,
        in_specs=scalars(1) + whole(3),
        out_specs=whole(2),
        compiler_params=grant(4),
        name="strips",
    )(flags, block, lat_even, lat_odd)
    lon_even = lax.ppermute(strip_even, "lon", even_pairs(lon_count))
    lon_odd = lax.ppermute(strip_odd, "lon", odd_pairs(lon_count))

    base_cell = rim_base[0]
    base = (base_cell[:, 0] - first_row - 1) * wide + (base_cell[:, 1] - first_col - 1)
    lat_step = jnp.arange(lat_count, dtype=jnp.int32)
    lon_step = jnp.arange(lon_count, dtype=jnp.int32)
    slot = jnp.arange(slots, dtype=jnp.int32)
    start, _ = loop.stretch(
        to_device(lat, lat_step, lat_count)[None, :], to_device(lon, lon_step, lon_count)[:, None]
    )
    lead = loop.first_entry(start, lat * lon_count + lon, other)
    send = (lead[:, :, None] + slot) % entries
    donor = (
        from_device(lat, lat_step, lat_count)[:, None] * lon_count
        + from_device(lon, lon_step, lon_count)[None, :]
    )
    start, span = loop.stretch(lat, lon)
    lead = loop.first_entry(start, donor, mine)
    place = (lead[:, :, None] + slot) * loop.blocks + donor[:, :, None] + mine
    row, col = loop.cell(place % loop.total)
    receive = jnp.where(
        place < start + span, (row - first_row) * pitch + PAD + (col - first_col), 0
    )
    ints = jnp.concatenate(
        [
            base.reshape(-1),
            send.reshape(-1),
            receive.reshape(-1),
            first_row[None],
            first_col[None],
        ]
    ).astype(jnp.int32)
    picks = lat_count * slots
    arrivals = lon_count * slots

    polar_step, azimuth_step = math.pi / (2 * nth), 1.5 * math.pi / nph
    row_ids = first_row - 1 + jnp.arange(tall + 2, dtype=jnp.int32)
    sines = jnp.sin(math.pi / 4 + (row_ids.astype(f32) + 0.5) * (math.pi / (2 * nth)))
    middle = sines[1:-1]
    floats = jnp.concatenate(
        [
            sines[2:] / middle * (0.5 / polar_step),
            sines[:-2] / middle * (0.5 / polar_step),
            (0.5 / azimuth_step) / middle,
            jnp.cos(rim_angle[0]),
            jnp.sin(rim_angle[0]),
            rim_weight[0].reshape(-1),
        ]
    )
    table = {
        "base": 0,
        "send": entries,
        "receive": entries + lon_count * picks,
        "corner": entries + lon_count * picks + lat_count * arrivals,
        "theta_up": 0,
        "theta_down": tall,
        "phi": 2 * tall,
        "cosine": 3 * tall,
        "sine": 3 * tall + entries,
        "weight": 3 * tall + 2 * entries,
        "half_theta": 0.5 / polar_step,
    }
    radial = jnp.asarray(radial_factors(levels, nth))

    frame, *packed = pl.pallas_call(
        lambda *refs: frame_kernel(rows, cols, entries, table, picks, lon_count, *refs),
        out_shape=[tile_array(tall * wide)] + [tile_array(picks)] * lon_count,
        in_specs=scalars(3) + whole(5),
        out_specs=whole(1 + lon_count),
        scratch_shapes=[pltpu.VMEM((entries * TILE, levels), f32)],
        compiler_params=grant(8),
        name="frame",
    )(flags, ints, floats, block, lat_even, lat_odd, lon_even, lon_odd)

    def exchange(packed):
        got = [packed[0]] + [
            lax.ppermute(packed[step], "lon", lon_route(step, lon_count))
            for step in range(1, lon_count)
        ]
        turned = pl.pallas_call(
            lambda *refs: swap_kernel(lat_count, lon_count, slots, *refs),
            out_shape=[tile_array(arrivals)] * lat_count,
            in_specs=whole(lon_count),
            out_specs=whole(lat_count),
            compiler_params=grant(4),
        name="swap",
        )(*got)
        return [
            lax.ppermute(turned[step], ("panel", "lat"), lat_route(step, lat_count))
            for step in range(lat_count)
        ]

    got = exchange(packed)
    planes = [
        pltpu.VMEM((fields * tall * (wide + 2 * PAD), levels), f32),
        pltpu.VMEM((13 * tall * (wide + 2 * PAD), levels), f32),
    ]
    frame, rate, *packed = pl.pallas_call(
        lambda *refs: first_section_kernel(
            rows, cols, entries, table, picks, lon_count, arrivals, lat_count, nth, nph, *refs
        ),
        out_shape=[tile_array(tall * wide), jax.ShapeDtypeStruct((fields, tall, wide, levels), f32)]
        + [tile_array(picks)] * lon_count,
        in_specs=scalars(2) + whole(2 + lat_count),
        out_specs=whole(2 + lon_count),
        scratch_shapes=[pltpu.VMEM((entries * TILE, levels), f32)] + planes,
        compiler_params=grant(24),
        name="first_section",
    )(ints, floats, radial, frame, *got)

    got = exchange(packed)
    change = pl.pallas_call(
        lambda *refs: second_section_kernel(rows, cols, table, arrivals, lat_count, *refs),
        out_shape=tile_array(rows * cols),
        in_specs=scalars(2) + whole(3 + lat_count),
        out_specs=whole(1)[0],
        scratch_shapes=planes,
        compiler_params=grant(24),
        name="second_section",
    )(ints, floats, radial, frame, rate, *got)
    return change.reshape(1, rows, cols, fields, levels)


def solution(mesh):
    return jax.shard_map(
        per_device,
        mesh=mesh,
        in_specs=(
            P("panel", "lat", "lon", None, None),
            P("panel", ("lat", "lon"), None),
            P("panel", ("lat", "lon"), None),
            P("panel", ("lat", "lon")),
            P("panel", None, None),
        ),
        out_specs=P("panel", "lat", "lon", None, None),
        check_vma=False,
    )
```

```python
import math

import jax
import jax.numpy as jnp
import numpy as np
from jax import lax
from jax.experimental import pallas as pl
from jax.experimental.pallas import tpu as pltpu
from jax.sharding import PartitionSpec as P

ETA_COEF = 0.2
NU_COEF = 0.2
KAPPA_COEF = 0.3
SOUND_SQ = 1.0
ARCHIMEDES_LIFT = 0.5
TIME_STEP = 0.2

HALO = 4
PAD = 8
TILE = 8


def is_power_of_two(count):
    return count & (count - 1) == 0


def to_device(index, step, count):
    return index ^ step if is_power_of_two(count) else (index + step) % count


def from_device(index, step, count):
    return index ^ step if is_power_of_two(count) else (index + count - step) % count


def even_pairs(count):
    return [(i, i ^ 1) for i in range(count) if i ^ 1 < count]


def odd_pairs(count):
    route = []
    for low in range(1, count - 1, 2):
        route += [(low, low + 1), (low + 1, low)]
    return route


def lon_route(step, count):
    return [(i, to_device(i, step, count)) for i in range(count)]


def lat_route(step, lat_count, lon_count):
    route = []
    for side in range(2):
        for lat in range(lat_count):
            for lon in range(lon_count):
                target = to_device(lat, step, lat_count)
                if 0 < target < lat_count - 1 and 0 < lon < lon_count - 1:
                    continue
                here = (side * lat_count + lat) * lon_count + lon
                there = ((1 - side) * lat_count + target) * lon_count + lon
                route.append((here, there))
    return route


class Loop:
    def __init__(self, rows, cols, lat_count, lon_count, entries):
        self.rows, self.cols = rows, cols
        self.lat_count, self.lon_count = lat_count, lon_count
        self.nth, self.nph = rows * lat_count, cols * lon_count
        self.total = 4 * (self.nth + self.nph)
        self.blocks = lat_count * lon_count
        self.entries = entries
        one_row = 2 * (cols + 2 * HALO)
        one_col = 2 * (rows + 2 * HALO)
        corner = 2 * (rows + cols + 2 * HALO)
        self.slots = -(-max(corner, one_row, one_col) // self.blocks)
        self.half = -(-one_row // self.blocks)
        side = 4 * (cols + HALO) + 2 * self.nth
        self.column_slots = max(-(-side // self.blocks), 2 * self.half)

    def position(self, row, col):
        nth, nph = self.nth, self.nph
        top = 2 * col + row + 2
        right = 2 * nph + 2 * row + col - nph
        bottom = 2 * nph + 2 * nth + 2 * (nph - 1 - col) + row - nth
        left = 4 * nph + 2 * nth + 2 * (nth - 1 - row) + col + 2
        return jnp.where(
            row < 0, top, jnp.where(row >= nth, bottom, jnp.where(col >= nph, right, left))
        )

    def cell(self, place):
        nth, nph = self.nth, self.nph
        right = place - 2 * nph
        bottom = right - 2 * nth
        left = bottom - 2 * nph
        on_top, on_right, on_bottom = right < 0, bottom < 0, left < 0
        row = jnp.where(
            on_top,
            (place & 1) - 2,
            jnp.where(
                on_right,
                right >> 1,
                jnp.where(on_bottom, nth + (bottom & 1), nth - 1 - (left >> 1)),
            ),
        )
        col = jnp.where(
            on_top,
            place >> 1,
            jnp.where(
                on_right,
                nph + (right & 1),
                jnp.where(on_bottom, nph - 1 - (bottom >> 1), (left & 1) - 2),
            ),
        )
        return row, col

    def top_start(self, lon):
        return 2 * jnp.maximum(lon * self.cols - HALO, 0)

    def bottom_start(self, lon):
        high = jnp.minimum(lon * self.cols + self.cols + HALO, self.nph)
        return 2 * self.nph + 2 * self.nth + 2 * (self.nph - high)

    def stretch(self, lat, lon):
        nth, nph = self.nth, self.nph
        row_low = jnp.maximum(lat * self.rows - HALO, 0)
        row_high = jnp.minimum(lat * self.rows + self.rows + HALO, nth)
        col_low = jnp.maximum(lon * self.cols - HALO, 0)
        col_high = jnp.minimum(lon * self.cols + self.cols + HALO, nph)
        top, bottom = lat == 0, lat == self.lat_count - 1
        left, right = lon == 0, lon == self.lon_count - 1
        left_start = 4 * nph + 2 * nth + 2 * (nth - row_high)
        start = jnp.where(
            top & left,
            left_start,
            jnp.where(
                top,
                self.top_start(lon),
                jnp.where(
                    right,
                    2 * nph + 2 * row_low,
                    jnp.where(bottom, self.bottom_start(lon), left_start),
                ),
            ),
        )
        span = jnp.where(top | bottom, 2 * (col_high - col_low), 0) + jnp.where(
            left | right, 2 * (row_high - row_low), 0
        )
        return start, span

    def first_entry(self, start, donor, offset):
        lead = -(-2 * self.total // self.blocks)
        raised = start - donor - offset + lead * self.blocks + self.blocks - 1
        if is_power_of_two(self.blocks):
            return (raised >> (self.blocks.bit_length() - 1)) - lead
        return lax.div(raised, jnp.full_like(raised, self.blocks)) - lead

    def wrap(self, entry):
        for bound in (8, 4, 2, 1):
            entry = jnp.where(entry < 0, entry + self.entries * bound, entry)
        for bound in (8, 4, 2, 1):
            over = entry - self.entries * bound
            entry = jnp.where(over >= 0, over, entry)
        return entry

    def column_entry(self, lon, donor, offset, slot):
        side = (lon == 0) | (lon == self.lon_count - 1)
        top = self.first_entry(self.top_start(lon), donor, offset)
        bottom = self.first_entry(self.bottom_start(lon), donor, offset)
        lower = (lon == 0) | jnp.logical_not(side) & (slot >= self.half)
        skipped = jnp.where(jnp.logical_not(side) & (slot >= self.half), self.half, 0)
        return jnp.where(lower, bottom, top) + slot - skipped

    def column_slot(self, lat, lon, donor, offset):
        side = (lon == 0) | (lon == self.lon_count - 1)
        start, _ = self.stretch(lat, lon)
        ahead = self.first_entry(start, donor, offset) - self.first_entry(
            jnp.where(lon == 0, self.bottom_start(lon), self.top_start(lon)), donor, offset
        )
        middle = jnp.where(lat == self.lat_count - 1, self.half, 0)
        return jnp.where(side, jnp.maximum(ahead, 0), middle)


def padded_rows(count):
    return -(-count // 1024) * 8


def table_ids(outer, inner, slots):
    rows = padded_rows(outer * inner * slots)
    flat = np.minimum(np.arange(rows * 128), outer * inner * slots - 1)
    return np.stack(
        [flat // (inner * slots), flat // slots % inner, flat % slots]
    ).reshape(3, rows, 128).astype(np.int32)


def whole(count):
    return [pl.BlockSpec(memory_space=pltpu.VMEM)] * count


def scalars(count):
    return [pl.BlockSpec(memory_space=pltpu.SMEM)] * count


def lookup(table_ref, index):
    return table_ref[index // 128, index % 128]


def grant(mebibytes):
    return pltpu.CompilerParams(vmem_limit_bytes=mebibytes << 20)


def tiles(index, count):
    if isinstance(index, int):
        return pl.ds(index * TILE, count * TILE)
    return pl.ds(pl.multiple_of(index * TILE, TILE), count * TILE)


def table_kernel(
    loop, pitch, cell_ref, other_ref, send_id_ref, swap_id_ref, got_id_ref,
    send_ref, swap_ref, receive_ref,
):
    lat, lon = lax.axis_index("lat"), lax.axis_index("lon")
    lat_count, lon_count = loop.lat_count, loop.lon_count
    mine = loop.position(cell_ref[0], cell_ref[1])
    other = loop.position(other_ref[0], other_ref[1])

    step, _, slot = [send_id_ref[n] for n in range(3)]
    entry = loop.column_entry(
        to_device(lon, step, lon_count), lat * lon_count + lon, other, slot
    )
    send_ref[...] = loop.wrap(entry)

    lat_step, lon_step, slot = [swap_id_ref[n] for n in range(3)]
    donor = lat * lon_count + from_device(lon, lon_step, lon_count)
    here = jnp.full_like(slot, lon)
    ahead = loop.column_slot(to_device(lat, lat_step, lat_count), here, donor, other)
    swap_ref[...] = jnp.minimum(ahead + slot, loop.column_slots - 1)

    lat_step, lon_step, slot = [got_id_ref[n] for n in range(3)]
    donor = from_device(lat, lat_step, lat_count) * lon_count + from_device(
        lon, lon_step, lon_count
    )
    start, span = loop.stretch(jnp.full_like(slot, lat), jnp.full_like(slot, lon))
    entry = loop.first_entry(start, donor, mine) + slot
    place = entry * loop.blocks + donor + mine
    wrapped = jnp.where(place >= loop.total, place - loop.total, place)
    row, col = loop.cell(wrapped)
    spot = (row - lat * loop.rows + HALO) * pitch + PAD + (col - lon * loop.cols + HALO)
    receive_ref[...] = jnp.where(place < start + span, spot, 0)


def strip_kernel(rows, cols, state_ref, even_ref, odd_ref, send_even_ref, send_odd_ref):
    lat_even = lax.rem(lax.axis_index("lat"), 2) == 0
    lon_even = lax.rem(lax.axis_index("lon"), 2) == 0

    def copy_rows(first, count, source):
        for out_ref, last in ((send_even_ref, lon_even), (send_odd_ref, jnp.logical_not(lon_even))):
            low = jnp.where(last, cols - HALO, 0)
            for row in range(count):
                out_ref[tiles((first + row) * HALO, HALO), :] = source[
                    tiles(row * cols + low, HALO), :
                ]

    copy_rows(HALO, rows, state_ref)

    @pl.when(lat_even)
    def _():
        copy_rows(0, HALO, odd_ref)
        copy_rows(HALO + rows, HALO, even_ref)

    @pl.when(jnp.logical_not(lat_even))
    def _():
        copy_rows(0, HALO, even_ref)
        copy_rows(HALO + rows, HALO, odd_ref)


def mix_and_pack(loop, wide, rim, frame_ref, value_ref, send_refs):
    send_table_ref, base_ref, weight_ref, cosine_ref, sine_ref = rim
    field = lax.broadcasted_iota(jnp.int32, (TILE, 128), 0)
    takes_next = (field == 1) | (field == 4)
    turned = takes_next | (field == 2) | (field == 5)
    first_row = lax.axis_index("lat") * loop.rows - HALO + 1
    first_col = lax.axis_index("lon") * loop.cols - HALO + 1

    def one_entry(entry, carry):
        base = (base_ref[entry, 0] - first_row) * wide + (base_ref[entry, 1] - first_col)
        total = None
        for a in range(4):
            for b in range(4):
                weight = weight_ref[entry, 4 * a + b]
                part = weight * frame_ref[tiles(base + a * wide + b, 1), :]
                total = part if total is None else total + part
        cosine, sine = cosine_ref[entry], sine_ref[entry]
        other = jnp.where(
            takes_next, pltpu.roll(total, TILE - 1, 0), pltpu.roll(total, 1, 0)
        )
        mixed = cosine * total + jnp.where(takes_next, -sine, sine) * other
        value_ref[tiles(entry, 1), :] = jnp.where(turned, mixed, total)
        return carry

    lax.fori_loop(0, loop.entries, one_entry, 0, unroll=4)
    for step, send_ref in enumerate(send_refs):
        for slot in range(loop.column_slots):
            entry = lookup(send_table_ref, step * loop.column_slots + slot)
            send_ref[tiles(slot, 1), :] = value_ref[tiles(entry, 1), :]


def frame_kernel(loop, *refs):
    rim, refs = refs[:5], refs[5:]
    state_ref, lat_even_ref, lat_odd_ref, lon_even_ref, lon_odd_ref, frame_ref = refs[:6]
    send_refs, value_ref = refs[6:-1], refs[-1]
    rows, cols = loop.rows, loop.cols
    wide = cols + 2 * HALO
    lat_even = lax.rem(lax.axis_index("lat"), 2) == 0
    lon_even = lax.rem(lax.axis_index("lon"), 2) == 0

    def copy_rows(first, count, source, left, width):
        for row in range(count):
            frame_ref[tiles((first + row) * wide + left, width), :] = source[
                tiles(row * width, width), :
            ]

    copy_rows(HALO, rows, state_ref, HALO, cols)

    @pl.when(lat_even)
    def _():
        copy_rows(0, HALO, lat_odd_ref, HALO, cols)
        copy_rows(HALO + rows, HALO, lat_even_ref, HALO, cols)

    @pl.when(jnp.logical_not(lat_even))
    def _():
        copy_rows(0, HALO, lat_even_ref, HALO, cols)
        copy_rows(HALO + rows, HALO, lat_odd_ref, HALO, cols)

    @pl.when(lon_even)
    def _():
        copy_rows(0, rows + 2 * HALO, lon_odd_ref, 0, HALO)
        copy_rows(0, rows + 2 * HALO, lon_even_ref, HALO + cols, HALO)

    @pl.when(jnp.logical_not(lon_even))
    def _():
        copy_rows(0, rows + 2 * HALO, lon_even_ref, 0, HALO)
        copy_rows(0, rows + 2 * HALO, lon_odd_ref, HALO + cols, HALO)

    mix_and_pack(loop, wide, rim, frame_ref, value_ref, send_refs)


def swap_kernel(loop, table_ref, *refs):
    got_refs, out_refs = refs[: loop.lon_count], refs[loop.lon_count :]
    for lat_step in range(loop.lat_count):
        for lon_step in range(loop.lon_count):
            for slot in range(loop.slots):
                place = lon_step * loop.slots + slot
                source = lookup(table_ref, lat_step * loop.lon_count * loop.slots + place)
                out_refs[lat_step][tiles(place, 1), :] = got_refs[lon_step][tiles(source, 1), :]


def section(
    loop, receive_ref, factor_ref, radial_ref, frame_ref, got_refs, plane_ref, work_ref,
    rate_rows, rate_chunks, emit,
):
    tall, wide = loop.rows + 2 * HALO, loop.cols + 2 * HALO
    pitch = wide + 2 * PAD
    arrivals = loop.lon_count * loop.slots

    def spread_row(row, carry):
        for chunk in range(0, wide, 8):
            for f in range(TILE):
                start = (row * wide + chunk) * TILE + f
                plane_ref[pl.ds((f * tall + row) * pitch + PAD + chunk, 8), :] = frame_ref[
                    pl.ds(start, 8, stride=TILE), :
                ]
        return carry

    first_row, last_row = rate_rows
    lax.fori_loop(first_row - 2, last_row + 2, spread_row, 0)
    for lat_step in range(loop.lat_count):
        for place in range(arrivals):
            spot = lookup(receive_ref, lat_step * arrivals + place)
            plane_ref[pl.ds(spot, TILE, stride=tall * pitch), :] = got_refs[lat_step][
                tiles(place, 1), :
            ]

    levels = radial_ref.shape[-1]
    inverse_radius, ru, rl, du, dl, qu, ql = [radial_ref[n] for n in range(7)]

    def up(x):
        return pltpu.roll(x, levels - 1, 1)

    def down(x):
        return pltpu.roll(x, 1, 1)

    half_theta = loop.nth / math.pi
    lat = lax.axis_index("lat")

    def row_factors(row):
        return [factor_ref[(lat * 3 + n) * tall + row] for n in range(3)]

    def reader(ref, row, col):
        def at(number, row_step=0, col_step=0):
            return ref[
                pl.ds((number * tall + row + row_step) * pitch + PAD + col + col_step, 8), :
            ]

        return at

    def curl(at, first, factors, with_phi, with_theta):
        tu, td, ph = factors
        a, b, c = first, first + 1, first + 2
        mid_b, mid_c = at(b), at(c)
        radial = inverse_radius * (
            (tu * at(c, 1) - td * at(c, -1)) - ph * (at(b, 0, 1) - at(b, 0, -1))
        )
        polar = with_phi * (at(a, 0, 1) - at(a, 0, -1)) - (ru * up(mid_c) - rl * down(mid_c))
        azimuth = (ru * up(mid_b) - rl * down(mid_b)) - with_theta * (at(a, 1) - at(a, -1))
        return radial, polar, azimuth

    def slope(at, number, with_phi, with_theta):
        mid = at(number)
        return (
            du * up(mid) - dl * down(mid),
            with_theta * (at(number, 1) - at(number, -1)),
            with_phi * (at(number, 0, 1) - at(number, 0, -1)),
        )

    def outflow(at, first, factors):
        tu, td, ph = factors
        mid = at(first)
        return (qu * up(mid) - ql * down(mid)) + inverse_radius * (
            (tu * at(first + 1, 1) - td * at(first + 1, -1))
            + ph * (at(first + 2, 0, 1) - at(first + 2, 0, -1))
        )

    def cross(x, y):
        return (
            x[1] * y[2] - x[2] * y[1],
            x[2] * y[0] - x[0] * y[2],
            x[0] * y[1] - x[1] * y[0],
        )

    def dot(x, y):
        return x[0] * y[0] + x[1] * y[1] + x[2] * y[2]

    with_theta = inverse_radius * half_theta

    def first_pass(row, carry):
        factors = row_factors(row)
        with_phi = inverse_radius * factors[2]
        for chunk in range(0, wide, 8):
            at = reader(plane_ref, row, chunk)

            def put(number, value):
                work_ref[pl.ds((number * tall + row) * pitch + PAD + chunk, 8), :] = value

            flow = [at(n) for n in range(3)]
            field = [at(n) for n in range(3, 6)]
            current = curl(at, 3, factors, with_phi, with_theta)
            spin = curl(at, 0, factors, with_phi, with_theta)
            induced = cross(flow, field)
            warm = slope(at, 6, with_phi, with_theta)
            for n in range(3):
                put(n, current[n])
                put(3 + n, spin[n])
                put(6 + n, induced[n] - ETA_COEF * current[n])
                put(9 + n, warm[n])
            put(12, at(7) + 0.5 * dot(flow, flow))
        return carry

    lax.fori_loop(first_row - 1, last_row + 1, first_pass, 0)

    def second_pass(row, carry):
        factors = row_factors(row)
        with_phi = inverse_radius * factors[2]
        for chunk in rate_chunks:
            at = reader(plane_ref, row, chunk)
            work = reader(work_ref, row, chunk)
            flow = [at(n) for n in range(3)]
            field = [at(n) for n in range(3, 6)]
            current = [work(n) for n in range(3)]
            spin = [work(3 + n) for n in range(3)]
            warm = [work(9 + n) for n in range(3)]
            field_rate = curl(work, 6, factors, with_phi, with_theta)
            spin_curl = curl(work, 3, factors, with_phi, with_theta)
            head = slope(work, 12, with_phi, with_theta)
            lorentz = cross(current, field)
            advect = cross(flow, spin)
            speed = [
                advect[n] + lorentz[n] - head[n] - NU_COEF * spin_curl[n] for n in range(3)
            ]
            speed[0] = speed[0] + ARCHIMEDES_LIFT * at(6)
            heat = KAPPA_COEF * outflow(work, 9, factors) - dot(flow, warm)
            squeeze = -SOUND_SQ * outflow(at, 0, factors)
            emit(row, chunk, at, speed + list(field_rate) + [heat, squeeze])
        return carry

    lax.fori_loop(first_row, last_row, second_pass, 0)


def first_section_kernel(loop, *refs):
    rim, refs = refs[:5], refs[5:]
    receive_ref, factor_ref, radial_ref, frame_in_ref = refs[:4]
    got_refs, refs = refs[4 : 4 + loop.lat_count], refs[4 + loop.lat_count :]
    frame_ref, rate_ref = refs[:2]
    send_refs, (value_ref, plane_ref, work_ref) = refs[2:-3], refs[-3:]
    tall, wide = loop.rows + 2 * HALO, loop.cols + 2 * HALO
    first_row = lax.axis_index("lat") * loop.rows - HALO
    first_col = lax.axis_index("lon") * loop.cols - HALO

    def emit(row, chunk, at, rate):
        in_row = (row + first_row >= 0) & (row + first_row < loop.nth)
        col = lax.broadcasted_iota(jnp.int32, (8, 128), 0) + (chunk + first_col)
        inside = (col >= jnp.where(in_row, 0, loop.nph)) & (col < loop.nph)
        for f in range(TILE):
            rate_ref[f, row, pl.ds(chunk, 8), :] = rate[f]
            start = (row * wide + chunk) * TILE + f
            frame_ref[pl.ds(start, 8, stride=TILE), :] = jnp.where(
                inside, at(f) + TIME_STEP * rate[f], 0.0
            )

    section(
        loop, receive_ref, factor_ref, radial_ref, frame_in_ref, got_refs, plane_ref, work_ref,
        (2, tall - 2), range(0, wide, 8), emit,
    )
    mix_and_pack(loop, wide, rim, frame_ref, value_ref, send_refs)


def second_section_kernel(loop, receive_ref, factor_ref, radial_ref, frame_ref, rate_ref, *refs):
    got_refs, (change_ref, plane_ref, work_ref) = refs[: loop.lat_count], refs[loop.lat_count :]
    rows, cols = loop.rows, loop.cols

    def emit(row, chunk, at, rate):
        for f in range(TILE):
            start = ((row - HALO) * cols + chunk - HALO) * TILE + f
            change_ref[pl.ds(start, 8, stride=TILE), :] = (0.5 * TIME_STEP) * (
                rate_ref[f, row, pl.ds(chunk, 8), :] + rate[f]
            )

    section(
        loop, receive_ref, factor_ref, radial_ref, frame_ref, got_refs, plane_ref, work_ref,
        (HALO, HALO + rows), range(HALO, HALO + cols, 8), emit,
    )


def radial_factors(levels, theta_count):
    scale = 2.0 * theta_count / math.pi
    step = 0.65 * scale / levels
    radius = 0.35 * scale + (np.arange(levels) + 0.5) * step
    half = 0.5 / step
    above = np.append(radius[1:], 0.0)
    below = np.append(0.0, radius[:-1])
    ones_above = np.append(np.ones(levels - 1), 0.0)
    ones_below = np.append(0.0, np.ones(levels - 1))
    rows = np.stack(
        [
            1.0 / radius,
            half * above / radius,
            half * below / radius,
            half * ones_above,
            half * ones_below,
            half * above**2 / radius**2,
            half * below**2 / radius**2,
        ]
    )
    return np.repeat(rows[:, None, :], 8, axis=1).astype(np.float32)


def row_factors(rows, lat_count, nth, nph):
    polar_step, azimuth_step = math.pi / (2 * nth), 1.5 * math.pi / nph
    tall = rows + 2 * HALO
    parts = []
    for lat in range(lat_count):
        row = lat * rows - HALO - 1 + np.arange(tall + 2)
        sines = np.sin(math.pi / 4 + (row + 0.5) * polar_step)
        middle = sines[1:-1]
        parts += [
            sines[2:] / middle * (0.5 / polar_step),
            sines[:-2] / middle * (0.5 / polar_step),
            (0.5 / azimuth_step) / middle,
        ]
    return np.concatenate(parts).astype(np.float32)


def per_device(state, rim_base, rim_weight, rim_angle, rim_target):
    _, rows, cols, fields, levels = state.shape
    lat_count, lon_count = lax.axis_size("lat"), lax.axis_size("lon")
    entries = rim_base.shape[1]
    loop = Loop(rows, cols, lat_count, lon_count, entries)
    tall, wide = rows + 2 * HALO, cols + 2 * HALO
    pitch = wide + 2 * PAD
    block = state[0].reshape(rows * cols * fields, levels)
    f32 = jnp.float32

    def tile_array(count):
        return jax.ShapeDtypeStruct((count * TILE, levels), f32)

    first_cell = rim_target[0, 0]
    other_cell = lax.ppermute(first_cell, "panel", [(0, 1), (1, 0)])

    cells = state[0]
    last_first = lax.axis_index("lat") % 2 == 0
    head, tail = cells[:HALO], cells[rows - HALO :]
    send_even = jnp.where(last_first, tail, head).reshape(HALO * cols * fields, levels)
    send_odd = jnp.where(last_first, head, tail).reshape(HALO * cols * fields, levels)
    lat_even = lax.ppermute(send_even, "lat", even_pairs(lat_count))
    lat_odd = lax.ppermute(send_odd, "lat", odd_pairs(lat_count))

    send_ids = table_ids(1, lon_count, loop.column_slots)[[1, 0, 2]]
    got_ids = table_ids(lat_count, lon_count, loop.slots)
    send_table, swap_table, receive_table = pl.pallas_call(
        lambda *refs: table_kernel(loop, pitch, *refs),
        out_shape=[
            jax.ShapeDtypeStruct(ids.shape[1:], jnp.int32) for ids in (send_ids, got_ids, got_ids)
        ],
        in_specs=scalars(2) + whole(3),
        out_specs=whole(3),
        compiler_params=grant(4),
        name="tables",
    )(first_cell, other_cell, jnp.asarray(send_ids), jnp.asarray(got_ids), jnp.asarray(got_ids))
    angle = rim_angle[0]
    rim = (send_table, rim_base[0], rim_weight[0], jnp.cos(angle), jnp.sin(angle))
    factors = jnp.asarray(row_factors(rows, lat_count, loop.nth, loop.nph))
    radial = jnp.asarray(radial_factors(levels, loop.nth))

    strip_even, strip_odd = pl.pallas_call(
        lambda *refs: strip_kernel(rows, cols, *refs),
        out_shape=[tile_array(tall * HALO)] * 2,
        in_specs=whole(3),
        out_specs=whole(2),
        compiler_params=grant(4),
        name="strips",
    )(block, lat_even, lat_odd)
    lon_even = lax.ppermute(strip_even, "lon", even_pairs(lon_count))
    lon_odd = lax.ppermute(strip_odd, "lon", odd_pairs(lon_count))

    packed_shapes = [tile_array(loop.column_slots)] * lon_count
    frame, *packed = pl.pallas_call(
        lambda *refs: frame_kernel(loop, *refs),
        out_shape=[tile_array(tall * wide)] + packed_shapes,
        in_specs=scalars(5) + whole(5),
        out_specs=whole(1 + lon_count),
        scratch_shapes=[pltpu.VMEM((entries * TILE, levels), f32)],
        compiler_params=grant(8),
        name="frame",
    )(*rim, block, lat_even, lat_odd, lon_even, lon_odd)

    def exchange(packed):
        got = [packed[0]] + [
            lax.ppermute(packed[step], "lon", lon_route(step, lon_count))
            for step in range(1, lon_count)
        ]
        turned = pl.pallas_call(
            lambda *refs: swap_kernel(loop, *refs),
            out_shape=[tile_array(lon_count * loop.slots)] * lat_count,
            in_specs=scalars(1) + whole(lon_count),
            out_specs=whole(lat_count),
            compiler_params=grant(4),
            name="swap",
        )(swap_table, *got)
        return [
            lax.ppermute(
                turned[step], ("panel", "lat", "lon"), lat_route(step, lat_count, lon_count)
            )
            for step in range(lat_count)
        ]

    got = exchange(packed)
    planes = [
        pltpu.VMEM((fields * tall * pitch, levels), f32),
        pltpu.VMEM((13 * tall * pitch, levels), f32),
    ]
    frame, rate, *packed = pl.pallas_call(
        lambda *refs: first_section_kernel(loop, *refs),
        out_shape=[tile_array(tall * wide), jax.ShapeDtypeStruct((fields, tall, wide, levels), f32)]
        + packed_shapes,
        in_specs=scalars(7) + whole(2 + lat_count),
        out_specs=whole(2 + lon_count),
        scratch_shapes=[pltpu.VMEM((entries * TILE, levels), f32)] + planes,
        compiler_params=grant(24),
        name="first_section",
    )(*rim, receive_table, factors, radial, frame, *got)

    got = exchange(packed)
    change = pl.pallas_call(
        lambda *refs: second_section_kernel(loop, *refs),
        out_shape=tile_array(rows * cols),
        in_specs=scalars(2) + whole(3 + lat_count),
        out_specs=whole(1)[0],
        scratch_shapes=planes,
        compiler_params=grant(24),
        name="second_section",
    )(receive_table, factors, radial, frame, rate, *got)
    return change.reshape(1, rows, cols, fields, levels)


def solution(mesh):
    return jax.shard_map(
        per_device,
        mesh=mesh,
        in_specs=(
            P("panel", "lat", "lon", None, None),
            P("panel", ("lat", "lon"), None),
            P("panel", ("lat", "lon"), None),
            P("panel", ("lat", "lon")),
            P("panel", None, None),
        ),
        out_specs=P("panel", "lat", "lon", None, None),
        check_vma=False,
    )
```

```python
import math

import jax
import jax.numpy as jnp
import numpy as np
from jax import lax
from jax.experimental import pallas as pl
from jax.experimental.pallas import tpu as pltpu
from jax.sharding import PartitionSpec as P

ETA_COEF = 0.2
NU_COEF = 0.2
KAPPA_COEF = 0.3
SOUND_SQ = 1.0
ARCHIMEDES_LIFT = 0.5
TIME_STEP = 0.2

HALO = 4
PAD = 8
TILE = 8


def is_power_of_two(count):
    return count & (count - 1) == 0


def to_device(index, step, count):
    return index ^ step if is_power_of_two(count) else (index + step) % count


def from_device(index, step, count):
    return index ^ step if is_power_of_two(count) else (index + count - step) % count


def even_pairs(count):
    return [(i, i ^ 1) for i in range(count) if i ^ 1 < count]


def odd_pairs(count):
    route = []
    for low in range(1, count - 1, 2):
        route += [(low, low + 1), (low + 1, low)]
    return route


def lon_route(step, count):
    return [(i, to_device(i, step, count)) for i in range(count)]


def lat_route(step, count):
    return [
        (side * count + i, (1 - side) * count + to_device(i, step, count))
        for side in range(2)
        for i in range(count)
    ]


class Loop:
    def __init__(self, rows, cols, lat_count, lon_count, entries):
        self.rows, self.cols = rows, cols
        self.lat_count, self.lon_count = lat_count, lon_count
        self.nth, self.nph = rows * lat_count, cols * lon_count
        self.total = 4 * (self.nth + self.nph)
        self.blocks = lat_count * lon_count
        self.entries = entries
        one_row = 2 * (cols + 2 * HALO)
        one_col = 2 * (rows + 2 * HALO)
        corner = 2 * (rows + cols + 2 * HALO)
        self.slots = -(-max(corner, one_row, one_col) // self.blocks)
        self.half = -(-one_row // self.blocks)
        side = 4 * (cols + HALO) + 2 * self.nth
        self.column_slots = max(-(-side // self.blocks), 2 * self.half)

    def position(self, row, col):
        nth, nph = self.nth, self.nph
        top = 2 * col + row + 2
        right = 2 * nph + 2 * row + col - nph
        bottom = 2 * nph + 2 * nth + 2 * (nph - 1 - col) + row - nth
        left = 4 * nph + 2 * nth + 2 * (nth - 1 - row) + col + 2
        return jnp.where(
            row < 0, top, jnp.where(row >= nth, bottom, jnp.where(col >= nph, right, left))
        )

    def cell(self, place):
        nth, nph = self.nth, self.nph
        right = place - 2 * nph
        bottom = right - 2 * nth
        left = bottom - 2 * nph
        on_top, on_right, on_bottom = right < 0, bottom < 0, left < 0
        row = jnp.where(
            on_top,
            (place & 1) - 2,
            jnp.where(
                on_right,
                right >> 1,
                jnp.where(on_bottom, nth + (bottom & 1), nth - 1 - (left >> 1)),
            ),
        )
        col = jnp.where(
            on_top,
            place >> 1,
            jnp.where(
                on_right,
                nph + (right & 1),
                jnp.where(on_bottom, nph - 1 - (bottom >> 1), (left & 1) - 2),
            ),
        )
        return row, col

    def top_start(self, lon):
        return 2 * jnp.maximum(lon * self.cols - HALO, 0)

    def bottom_start(self, lon):
        high = jnp.minimum(lon * self.cols + self.cols + HALO, self.nph)
        return 2 * self.nph + 2 * self.nth + 2 * (self.nph - high)

    def stretch(self, lat, lon):
        nth, nph = self.nth, self.nph
        row_low = jnp.maximum(lat * self.rows - HALO, 0)
        row_high = jnp.minimum(lat * self.rows + self.rows + HALO, nth)
        col_low = jnp.maximum(lon * self.cols - HALO, 0)
        col_high = jnp.minimum(lon * self.cols + self.cols + HALO, nph)
        top, bottom = lat == 0, lat == self.lat_count - 1
        left, right = lon == 0, lon == self.lon_count - 1
        left_start = 4 * nph + 2 * nth + 2 * (nth - row_high)
        start = jnp.where(
            top & left,
            left_start,
            jnp.where(
                top,
                self.top_start(lon),
                jnp.where(
                    right,
                    2 * nph + 2 * row_low,
                    jnp.where(bottom, self.bottom_start(lon), left_start),
                ),
            ),
        )
        span = jnp.where(top | bottom, 2 * (col_high - col_low), 0) + jnp.where(
            left | right, 2 * (row_high - row_low), 0
        )
        return start, span

    def first_entry(self, start, donor, offset):
        lead = -(-2 * self.total // self.blocks)
        raised = start - donor - offset + lead * self.blocks + self.blocks - 1
        if is_power_of_two(self.blocks):
            return (raised >> (self.blocks.bit_length() - 1)) - lead
        return lax.div(raised, jnp.full_like(raised, self.blocks)) - lead

    def wrap(self, entry):
        for bound in (8, 4, 2, 1):
            entry = jnp.where(entry < 0, entry + self.entries * bound, entry)
        for bound in (8, 4, 2, 1):
            over = entry - self.entries * bound
            entry = jnp.where(over >= 0, over, entry)
        return entry

    def column_entry(self, lon, donor, offset, slot):
        side = (lon == 0) | (lon == self.lon_count - 1)
        top = self.first_entry(self.top_start(lon), donor, offset)
        bottom = self.first_entry(self.bottom_start(lon), donor, offset)
        lower = (lon == 0) | jnp.logical_not(side) & (slot >= self.half)
        skipped = jnp.where(jnp.logical_not(side) & (slot >= self.half), self.half, 0)
        return jnp.where(lower, bottom, top) + slot - skipped

    def column_slot(self, lat, lon, donor, offset):
        side = (lon == 0) | (lon == self.lon_count - 1)
        start, _ = self.stretch(lat, lon)
        ahead = self.first_entry(start, donor, offset) - self.first_entry(
            jnp.where(lon == 0, self.bottom_start(lon), self.top_start(lon)), donor, offset
        )
        middle = jnp.where(lat == self.lat_count - 1, self.half, 0)
        return jnp.where(side, jnp.maximum(ahead, 0), middle)


def padded_rows(count):
    return -(-count // 1024) * 8


def table_ids(outer, inner, slots):
    rows = padded_rows(outer * inner * slots)
    flat = np.minimum(np.arange(rows * 128), outer * inner * slots - 1)
    return np.stack(
        [flat // (inner * slots), flat // slots % inner, flat % slots]
    ).reshape(3, rows, 128).astype(np.int32)


def whole(count):
    return [pl.BlockSpec(memory_space=pltpu.VMEM)] * count


def scalars(count):
    return [pl.BlockSpec(memory_space=pltpu.SMEM)] * count


def lookup(table_ref, index):
    return table_ref[index // 128, index % 128]


def grant(mebibytes):
    return pltpu.CompilerParams(vmem_limit_bytes=mebibytes << 20)


def tiles(index, count):
    if isinstance(index, int):
        return pl.ds(index * TILE, count * TILE)
    return pl.ds(pl.multiple_of(index * TILE, TILE), count * TILE)


def table_kernel(
    loop, pitch, cell_ref, other_ref, send_id_ref, swap_id_ref, got_id_ref,
    send_ref, swap_ref, receive_ref,
):
    lat, lon = lax.axis_index("lat"), lax.axis_index("lon")
    lat_count, lon_count = loop.lat_count, loop.lon_count
    mine = loop.position(cell_ref[0], cell_ref[1])
    other = loop.position(other_ref[0], other_ref[1])

    step, _, slot = [send_id_ref[n] for n in range(3)]
    entry = loop.column_entry(
        to_device(lon, step, lon_count), lat * lon_count + lon, other, slot
    )
    send_ref[...] = loop.wrap(entry)

    lat_step, lon_step, slot = [swap_id_ref[n] for n in range(3)]
    donor = lat * lon_count + from_device(lon, lon_step, lon_count)
    here = jnp.full_like(slot, lon)
    ahead = loop.column_slot(to_device(lat, lat_step, lat_count), here, donor, other)
    swap_ref[...] = jnp.minimum(ahead + slot, loop.column_slots - 1)

    lat_step, lon_step, slot = [got_id_ref[n] for n in range(3)]
    donor = from_device(lat, lat_step, lat_count) * lon_count + from_device(
        lon, lon_step, lon_count
    )
    start, span = loop.stretch(jnp.full_like(slot, lat), jnp.full_like(slot, lon))
    entry = loop.first_entry(start, donor, mine) + slot
    place = entry * loop.blocks + donor + mine
    wrapped = jnp.where(place >= loop.total, place - loop.total, place)
    row, col = loop.cell(wrapped)
    spot = (row - lat * loop.rows + HALO) * pitch + PAD + (col - lon * loop.cols + HALO)
    receive_ref[...] = jnp.where(place < start + span, spot, 0)


def strip_kernel(rows, cols, own_even_ref, own_odd_ref, even_ref, odd_ref, *send_refs):
    lat_even = lax.rem(lax.axis_index("lat"), 2) == 0
    lon_even = lax.rem(lax.axis_index("lon"), 2) == 0
    high = cols - HALO
    lows = (jnp.where(lon_even, high, 0), jnp.where(lon_even, 0, high))

    def copy_halo(first, source):
        for send_ref, low in zip(send_refs, lows):
            for row in range(HALO):
                send_ref[tiles((first + row) * HALO, HALO), :] = source[
                    tiles(row * cols + low, HALO), :
                ]

    for send_ref, own_ref in zip(send_refs, (own_even_ref, own_odd_ref)):
        send_ref[tiles(HALO * HALO, rows * HALO), :] = own_ref[...]

    @pl.when(lat_even)
    def _():
        copy_halo(0, odd_ref)
        copy_halo(HALO + rows, even_ref)

    @pl.when(jnp.logical_not(lat_even))
    def _():
        copy_halo(0, even_ref)
        copy_halo(HALO + rows, odd_ref)


def mix_and_pack(loop, wide, rim, frame_ref, value_ref, send_refs):
    send_table_ref, base_ref, weight_ref, cosine_ref, sine_ref = rim
    field = lax.broadcasted_iota(jnp.int32, (TILE, 128), 0)
    takes_next = (field == 1) | (field == 4)
    turned = takes_next | (field == 2) | (field == 5)
    first_row = lax.axis_index("lat") * loop.rows - HALO + 1
    first_col = lax.axis_index("lon") * loop.cols - HALO + 1

    def one_entry(entry, carry):
        base = (base_ref[entry, 0] - first_row) * wide + (base_ref[entry, 1] - first_col)
        total = None
        for a in range(4):
            for b in range(4):
                weight = weight_ref[entry, 4 * a + b]
                part = weight * frame_ref[tiles(base + a * wide + b, 1), :]
                total = part if total is None else total + part
        cosine, sine = cosine_ref[entry], sine_ref[entry]
        other = jnp.where(
            takes_next, pltpu.roll(total, TILE - 1, 0), pltpu.roll(total, 1, 0)
        )
        mixed = cosine * total + jnp.where(takes_next, -sine, sine) * other
        value_ref[tiles(entry, 1), :] = jnp.where(turned, mixed, total)
        return carry

    lax.fori_loop(0, loop.entries, one_entry, 0, unroll=4)
    for step, send_ref in enumerate(send_refs):
        for slot in range(loop.column_slots):
            entry = lookup(send_table_ref, step * loop.column_slots + slot)
            send_ref[tiles(slot, 1), :] = value_ref[tiles(entry, 1), :]


def frame_kernel(loop, *refs):
    rim, refs = refs[:5], refs[5:]
    state_ref, lat_even_ref, lat_odd_ref, lon_even_ref, lon_odd_ref, frame_ref = refs[:6]
    send_refs, value_ref = refs[6:-1], refs[-1]
    rows, cols = loop.rows, loop.cols
    wide = cols + 2 * HALO
    lat_even = lax.rem(lax.axis_index("lat"), 2) == 0
    lon_even = lax.rem(lax.axis_index("lon"), 2) == 0

    def copy_rows(first, count, source, left, width):
        for row in range(count):
            frame_ref[tiles((first + row) * wide + left, width), :] = source[
                tiles(row * width, width), :
            ]

    copy_rows(HALO, rows, state_ref, HALO, cols)

    @pl.when(lat_even)
    def _():
        copy_rows(0, HALO, lat_odd_ref, HALO, cols)
        copy_rows(HALO + rows, HALO, lat_even_ref, HALO, cols)

    @pl.when(jnp.logical_not(lat_even))
    def _():
        copy_rows(0, HALO, lat_even_ref, HALO, cols)
        copy_rows(HALO + rows, HALO, lat_odd_ref, HALO, cols)

    @pl.when(lon_even)
    def _():
        copy_rows(0, rows + 2 * HALO, lon_odd_ref, 0, HALO)
        copy_rows(0, rows + 2 * HALO, lon_even_ref, HALO + cols, HALO)

    @pl.when(jnp.logical_not(lon_even))
    def _():
        copy_rows(0, rows + 2 * HALO, lon_even_ref, 0, HALO)
        copy_rows(0, rows + 2 * HALO, lon_odd_ref, HALO + cols, HALO)

    mix_and_pack(loop, wide, rim, frame_ref, value_ref, send_refs)


def swap_kernel(loop, table_ref, *refs):
    got_refs, out_refs = refs[: loop.lon_count], refs[loop.lon_count :]
    for lat_step in range(loop.lat_count):
        for lon_step in range(loop.lon_count):
            for slot in range(loop.slots):
                place = lon_step * loop.slots + slot
                source = lookup(table_ref, lat_step * loop.lon_count * loop.slots + place)
                out_refs[lat_step][tiles(place, 1), :] = got_refs[lon_step][tiles(source, 1), :]


def section(
    loop, receive_ref, factor_ref, radial_ref, frame_ref, got_refs, plane_ref, work_ref,
    rate_rows, rate_chunks, emit,
):
    tall, wide = loop.rows + 2 * HALO, loop.cols + 2 * HALO
    pitch = wide + 2 * PAD
    arrivals = loop.lon_count * loop.slots

    def spread_row(row, carry):
        for chunk in range(0, wide, 8):
            for f in range(TILE):
                start = (row * wide + chunk) * TILE + f
                plane_ref[pl.ds((f * tall + row) * pitch + PAD + chunk, 8), :] = frame_ref[
                    pl.ds(start, 8, stride=TILE), :
                ]
        return carry

    first_row, last_row = rate_rows
    lax.fori_loop(first_row - 2, last_row + 2, spread_row, 0)
    for lat_step in range(loop.lat_count):
        for place in range(arrivals):
            spot = lookup(receive_ref, lat_step * arrivals + place)
            plane_ref[pl.ds(spot, TILE, stride=tall * pitch), :] = got_refs[lat_step][
                tiles(place, 1), :
            ]

    levels = radial_ref.shape[-1]
    inverse_radius, ru, rl, du, dl, qu, ql = [radial_ref[n] for n in range(7)]

    def up(x):
        return pltpu.roll(x, levels - 1, 1)

    def down(x):
        return pltpu.roll(x, 1, 1)

    half_theta = loop.nth / math.pi
    lat = lax.axis_index("lat")

    def row_factors(row):
        return [factor_ref[(lat * 3 + n) * tall + row] for n in range(3)]

    def reader(ref, row, col):
        def at(number, row_step=0, col_step=0):
            return ref[
                pl.ds((number * tall + row + row_step) * pitch + PAD + col + col_step, 8), :
            ]

        return at

    def curl(at, first, factors, with_phi, with_theta):
        tu, td, ph = factors
        a, b, c = first, first + 1, first + 2
        mid_b, mid_c = at(b), at(c)
        radial = inverse_radius * (
            (tu * at(c, 1) - td * at(c, -1)) - ph * (at(b, 0, 1) - at(b, 0, -1))
        )
        polar = with_phi * (at(a, 0, 1) - at(a, 0, -1)) - (ru * up(mid_c) - rl * down(mid_c))
        azimuth = (ru * up(mid_b) - rl * down(mid_b)) - with_theta * (at(a, 1) - at(a, -1))
        return radial, polar, azimuth

    def slope(at, number, with_phi, with_theta):
        mid = at(number)
        return (
            du * up(mid) - dl * down(mid),
            with_theta * (at(number, 1) - at(number, -1)),
            with_phi * (at(number, 0, 1) - at(number, 0, -1)),
        )

    def outflow(at, first, factors):
        tu, td, ph = factors
        mid = at(first)
        return (qu * up(mid) - ql * down(mid)) + inverse_radius * (
            (tu * at(first + 1, 1) - td * at(first + 1, -1))
            + ph * (at(first + 2, 0, 1) - at(first + 2, 0, -1))
        )

    def cross(x, y):
        return (
            x[1] * y[2] - x[2] * y[1],
            x[2] * y[0] - x[0] * y[2],
            x[0] * y[1] - x[1] * y[0],
        )

    def dot(x, y):
        return x[0] * y[0] + x[1] * y[1] + x[2] * y[2]

    with_theta = inverse_radius * half_theta

    def first_pass(row, carry):
        factors = row_factors(row)
        with_phi = inverse_radius * factors[2]
        for chunk in range(0, wide, 8):
            at = reader(plane_ref, row, chunk)

            def put(number, value):
                work_ref[pl.ds((number * tall + row) * pitch + PAD + chunk, 8), :] = value

            flow = [at(n) for n in range(3)]
            field = [at(n) for n in range(3, 6)]
            current = curl(at, 3, factors, with_phi, with_theta)
            spin = curl(at, 0, factors, with_phi, with_theta)
            induced = cross(flow, field)
            warm = slope(at, 6, with_phi, with_theta)
            for n in range(3):
                put(n, current[n])
                put(3 + n, spin[n])
                put(6 + n, induced[n] - ETA_COEF * current[n])
                put(9 + n, warm[n])
            put(12, at(7) + 0.5 * dot(flow, flow))
        return carry

    lax.fori_loop(first_row - 1, last_row + 1, first_pass, 0)

    def second_pass(row, carry):
        factors = row_factors(row)
        with_phi = inverse_radius * factors[2]
        for chunk in rate_chunks:
            at = reader(plane_ref, row, chunk)
            work = reader(work_ref, row, chunk)
            flow = [at(n) for n in range(3)]
            field = [at(n) for n in range(3, 6)]
            current = [work(n) for n in range(3)]
            spin = [work(3 + n) for n in range(3)]
            warm = [work(9 + n) for n in range(3)]
            field_rate = curl(work, 6, factors, with_phi, with_theta)
            spin_curl = curl(work, 3, factors, with_phi, with_theta)
            head = slope(work, 12, with_phi, with_theta)
            lorentz = cross(current, field)
            advect = cross(flow, spin)
            speed = [
                advect[n] + lorentz[n] - head[n] - NU_COEF * spin_curl[n] for n in range(3)
            ]
            speed[0] = speed[0] + ARCHIMEDES_LIFT * at(6)
            heat = KAPPA_COEF * outflow(work, 9, factors) - dot(flow, warm)
            squeeze = -SOUND_SQ * outflow(at, 0, factors)
            emit(row, chunk, at, speed + list(field_rate) + [heat, squeeze])
        return carry

    lax.fori_loop(first_row, last_row, second_pass, 0)


def first_section_kernel(loop, *refs):
    rim, refs = refs[:5], refs[5:]
    receive_ref, factor_ref, radial_ref, frame_in_ref = refs[:4]
    got_refs, refs = refs[4 : 4 + loop.lat_count], refs[4 + loop.lat_count :]
    frame_ref, rate_ref = refs[:2]
    send_refs, (value_ref, plane_ref, work_ref) = refs[2:-3], refs[-3:]
    tall, wide = loop.rows + 2 * HALO, loop.cols + 2 * HALO
    first_row = lax.axis_index("lat") * loop.rows - HALO
    first_col = lax.axis_index("lon") * loop.cols - HALO

    def emit(row, chunk, at, rate):
        in_row = (row + first_row >= 0) & (row + first_row < loop.nth)
        col = lax.broadcasted_iota(jnp.int32, (8, 128), 0) + (chunk + first_col)
        inside = (col >= jnp.where(in_row, 0, loop.nph)) & (col < loop.nph)
        for f in range(TILE):
            rate_ref[f, row, pl.ds(chunk, 8), :] = rate[f]
            start = (row * wide + chunk) * TILE + f
            frame_ref[pl.ds(start, 8, stride=TILE), :] = jnp.where(
                inside, at(f) + TIME_STEP * rate[f], 0.0
            )

    section(
        loop, receive_ref, factor_ref, radial_ref, frame_in_ref, got_refs, plane_ref, work_ref,
        (2, tall - 2), range(0, wide, 8), emit,
    )
    mix_and_pack(loop, wide, rim, frame_ref, value_ref, send_refs)


def second_section_kernel(loop, receive_ref, factor_ref, radial_ref, frame_ref, rate_ref, *refs):
    got_refs, (change_ref, plane_ref, work_ref) = refs[: loop.lat_count], refs[loop.lat_count :]
    rows, cols = loop.rows, loop.cols

    def emit(row, chunk, at, rate):
        for f in range(TILE):
            start = ((row - HALO) * cols + chunk - HALO) * TILE + f
            change_ref[pl.ds(start, 8, stride=TILE), :] = (0.5 * TIME_STEP) * (
                rate_ref[f, row, pl.ds(chunk, 8), :] + rate[f]
            )

    section(
        loop, receive_ref, factor_ref, radial_ref, frame_ref, got_refs, plane_ref, work_ref,
        (HALO, HALO + rows), range(HALO, HALO + cols, 8), emit,
    )


def radial_factors(levels, theta_count):
    scale = 2.0 * theta_count / math.pi
    step = 0.65 * scale / levels
    radius = 0.35 * scale + (np.arange(levels) + 0.5) * step
    half = 0.5 / step
    above = np.append(radius[1:], 0.0)
    below = np.append(0.0, radius[:-1])
    ones_above = np.append(np.ones(levels - 1), 0.0)
    ones_below = np.append(0.0, np.ones(levels - 1))
    rows = np.stack(
        [
            1.0 / radius,
            half * above / radius,
            half * below / radius,
            half * ones_above,
            half * ones_below,
            half * above**2 / radius**2,
            half * below**2 / radius**2,
        ]
    )
    return np.repeat(rows[:, None, :], 8, axis=1).astype(np.float32)


def row_factors(rows, lat_count, nth, nph):
    polar_step, azimuth_step = math.pi / (2 * nth), 1.5 * math.pi / nph
    tall = rows + 2 * HALO
    parts = []
    for lat in range(lat_count):
        row = lat * rows - HALO - 1 + np.arange(tall + 2)
        sines = np.sin(math.pi / 4 + (row + 0.5) * polar_step)
        middle = sines[1:-1]
        parts += [
            sines[2:] / middle * (0.5 / polar_step),
            sines[:-2] / middle * (0.5 / polar_step),
            (0.5 / azimuth_step) / middle,
        ]
    return np.concatenate(parts).astype(np.float32)


def per_device(state, rim_base, rim_weight, rim_angle, rim_target):
    _, rows, cols, fields, levels = state.shape
    lat_count, lon_count = lax.axis_size("lat"), lax.axis_size("lon")
    entries = rim_base.shape[1]
    loop = Loop(rows, cols, lat_count, lon_count, entries)
    tall, wide = rows + 2 * HALO, cols + 2 * HALO
    pitch = wide + 2 * PAD
    block = state[0].reshape(rows * cols * fields, levels)
    f32 = jnp.float32

    def tile_array(count):
        return jax.ShapeDtypeStruct((count * TILE, levels), f32)

    first_cell = rim_target[0, 0]
    other_cell = lax.ppermute(first_cell, "panel", [(0, 1), (1, 0)])

    cells = state[0]
    last_first = lax.axis_index("lat") % 2 == 0
    head, tail = cells[:HALO], cells[rows - HALO :]
    send_even = jnp.where(last_first, tail, head).reshape(HALO * cols * fields, levels)
    send_odd = jnp.where(last_first, head, tail).reshape(HALO * cols * fields, levels)
    lat_even = lax.ppermute(send_even, "lat", even_pairs(lat_count))
    lat_odd = lax.ppermute(send_odd, "lat", odd_pairs(lat_count))

    send_ids = table_ids(1, lon_count, loop.column_slots)[[1, 0, 2]]
    got_ids = table_ids(lat_count, lon_count, loop.slots)
    send_table, swap_table, receive_table = pl.pallas_call(
        lambda *refs: table_kernel(loop, pitch, *refs),
        out_shape=[
            jax.ShapeDtypeStruct(ids.shape[1:], jnp.int32) for ids in (send_ids, got_ids, got_ids)
        ],
        in_specs=scalars(2) + whole(3),
        out_specs=whole(3),
        compiler_params=grant(4),
        name="tables",
    )(first_cell, other_cell, jnp.asarray(send_ids), jnp.asarray(got_ids), jnp.asarray(got_ids))
    angle = rim_angle[0]
    rim = (send_table, rim_base[0], rim_weight[0], jnp.cos(angle), jnp.sin(angle))
    factors = jnp.asarray(row_factors(rows, lat_count, loop.nth, loop.nph))
    radial = jnp.asarray(radial_factors(levels, loop.nth))

    east_first = lax.axis_index("lon") % 2 == 0
    head, tail = cells[:, :HALO], cells[:, cols - HALO :]
    own_even = jnp.where(east_first, tail, head).reshape(rows * HALO * fields, levels)
    own_odd = jnp.where(east_first, head, tail).reshape(rows * HALO * fields, levels)
    strip_even, strip_odd = pl.pallas_call(
        lambda *refs: strip_kernel(rows, cols, *refs),
        out_shape=[tile_array(tall * HALO)] * 2,
        in_specs=whole(4),
        out_specs=whole(2),
        compiler_params=grant(4),
        name="strips",
    )(own_even, own_odd, lat_even, lat_odd)
    lon_even = lax.ppermute(strip_even, "lon", even_pairs(lon_count))
    lon_odd = lax.ppermute(strip_odd, "lon", odd_pairs(lon_count))

    packed_shapes = [tile_array(loop.column_slots)] * lon_count
    frame, *packed = pl.pallas_call(
        lambda *refs: frame_kernel(loop, *refs),
        out_shape=[tile_array(tall * wide)] + packed_shapes,
        in_specs=scalars(5) + whole(5),
        out_specs=whole(1 + lon_count),
        scratch_shapes=[pltpu.VMEM((entries * TILE, levels), f32)],
        compiler_params=grant(8),
        name="frame",
    )(*rim, block, lat_even, lat_odd, lon_even, lon_odd)

    def exchange(packed):
        got = [packed[0]] + [
            lax.ppermute(packed[step], "lon", lon_route(step, lon_count))
            for step in range(1, lon_count)
        ]
        turned = pl.pallas_call(
            lambda *refs: swap_kernel(loop, *refs),
            out_shape=[tile_array(lon_count * loop.slots)] * lat_count,
            in_specs=scalars(1) + whole(lon_count),
            out_specs=whole(lat_count),
            compiler_params=grant(4),
            name="swap",
        )(swap_table, *got)
        return [
            lax.ppermute(turned[step], ("panel", "lat"), lat_route(step, lat_count))
            for step in range(lat_count)
        ]

    got = exchange(packed)
    planes = [
        pltpu.VMEM((fields * tall * pitch, levels), f32),
        pltpu.VMEM((13 * tall * pitch, levels), f32),
    ]
    frame, rate, *packed = pl.pallas_call(
        lambda *refs: first_section_kernel(loop, *refs),
        out_shape=[tile_array(tall * wide), jax.ShapeDtypeStruct((fields, tall, wide, levels), f32)]
        + packed_shapes,
        in_specs=scalars(7) + whole(2 + lat_count),
        out_specs=whole(2 + lon_count),
        scratch_shapes=[pltpu.VMEM((entries * TILE, levels), f32)] + planes,
        compiler_params=grant(24),
        name="first_section",
    )(*rim, receive_table, factors, radial, frame, *got)

    got = exchange(packed)
    change = pl.pallas_call(
        lambda *refs: second_section_kernel(loop, *refs),
        out_shape=tile_array(rows * cols),
        in_specs=scalars(2) + whole(3 + lat_count),
        out_specs=whole(1)[0],
        scratch_shapes=planes,
        compiler_params=grant(24),
        name="second_section",
    )(receive_table, factors, radial, frame, rate, *got)
    return change.reshape(1, rows, cols, fields, levels)


def solution(mesh):
    return jax.shard_map(
        per_device,
        mesh=mesh,
        in_specs=(
            P("panel", "lat", "lon", None, None),
            P("panel", ("lat", "lon"), None),
            P("panel", ("lat", "lon"), None),
            P("panel", ("lat", "lon")),
            P("panel", None, None),
        ),
        out_specs=P("panel", "lat", "lon", None, None),
        check_vma=False,
    )
```

```python
import math

import jax
import jax.numpy as jnp
import numpy as np
from jax import lax
from jax.experimental import pallas as pl
from jax.experimental.pallas import tpu as pltpu
from jax.sharding import PartitionSpec as P

ETA_COEF = 0.2
NU_COEF = 0.2
KAPPA_COEF = 0.3
SOUND_SQ = 1.0
ARCHIMEDES_LIFT = 0.5
TIME_STEP = 0.2

HALO = 4
PAD = 8
TILE = 8


def is_power_of_two(count):
    return count & (count - 1) == 0


def to_device(index, step, count):
    return index ^ step if is_power_of_two(count) else (index + step) % count


def from_device(index, step, count):
    return index ^ step if is_power_of_two(count) else (index + count - step) % count


def even_pairs(count):
    return [(i, i ^ 1) for i in range(count) if i ^ 1 < count]


def odd_pairs(count):
    route = []
    for low in range(1, count - 1, 2):
        route += [(low, low + 1), (low + 1, low)]
    return route


def lon_route(step, count):
    return [(i, to_device(i, step, count)) for i in range(count)]


def lat_route(step, count):
    return [
        (side * count + i, (1 - side) * count + to_device(i, step, count))
        for side in range(2)
        for i in range(count)
    ]


class Loop:
    def __init__(self, rows, cols, lat_count, lon_count, entries):
        self.rows, self.cols = rows, cols
        self.lat_count, self.lon_count = lat_count, lon_count
        self.nth, self.nph = rows * lat_count, cols * lon_count
        self.total = 4 * (self.nth + self.nph)
        self.blocks = lat_count * lon_count
        self.entries = entries
        one_row = 2 * (cols + 2 * HALO)
        one_col = 2 * (rows + 2 * HALO)
        corner = 2 * (rows + cols + 2 * HALO)
        self.slots = -(-max(corner, one_row, one_col) // self.blocks)
        self.half = -(-one_row // self.blocks)
        side = 4 * (cols + HALO) + 2 * self.nth
        self.column_slots = max(-(-side // self.blocks), 2 * self.half)

    def position(self, row, col):
        nth, nph = self.nth, self.nph
        top = 2 * col + row + 2
        right = 2 * nph + 2 * row + col - nph
        bottom = 2 * nph + 2 * nth + 2 * (nph - 1 - col) + row - nth
        left = 4 * nph + 2 * nth + 2 * (nth - 1 - row) + col + 2
        return jnp.where(
            row < 0, top, jnp.where(row >= nth, bottom, jnp.where(col >= nph, right, left))
        )

    def cell(self, place):
        nth, nph = self.nth, self.nph
        right = place - 2 * nph
        bottom = right - 2 * nth
        left = bottom - 2 * nph
        on_top, on_right, on_bottom = right < 0, bottom < 0, left < 0
        row = jnp.where(
            on_top,
            (place & 1) - 2,
            jnp.where(
                on_right,
                right >> 1,
                jnp.where(on_bottom, nth + (bottom & 1), nth - 1 - (left >> 1)),
            ),
        )
        col = jnp.where(
            on_top,
            place >> 1,
            jnp.where(
                on_right,
                nph + (right & 1),
                jnp.where(on_bottom, nph - 1 - (bottom >> 1), (left & 1) - 2),
            ),
        )
        return row, col

    def top_start(self, lon):
        return 2 * jnp.maximum(lon * self.cols - HALO, 0)

    def bottom_start(self, lon):
        high = jnp.minimum(lon * self.cols + self.cols + HALO, self.nph)
        return 2 * self.nph + 2 * self.nth + 2 * (self.nph - high)

    def stretch(self, lat, lon):
        nth, nph = self.nth, self.nph
        row_low = jnp.maximum(lat * self.rows - HALO, 0)
        row_high = jnp.minimum(lat * self.rows + self.rows + HALO, nth)
        col_low = jnp.maximum(lon * self.cols - HALO, 0)
        col_high = jnp.minimum(lon * self.cols + self.cols + HALO, nph)
        top, bottom = lat == 0, lat == self.lat_count - 1
        left, right = lon == 0, lon == self.lon_count - 1
        left_start = 4 * nph + 2 * nth + 2 * (nth - row_high)
        start = jnp.where(
            top & left,
            left_start,
            jnp.where(
                top,
                self.top_start(lon),
                jnp.where(
                    right,
                    2 * nph + 2 * row_low,
                    jnp.where(bottom, self.bottom_start(lon), left_start),
                ),
            ),
        )
        span = jnp.where(top | bottom, 2 * (col_high - col_low), 0) + jnp.where(
            left | right, 2 * (row_high - row_low), 0
        )
        return start, span

    def first_entry(self, start, donor, offset):
        lead = -(-2 * self.total // self.blocks)
        raised = start - donor - offset + lead * self.blocks + self.blocks - 1
        if is_power_of_two(self.blocks):
            return (raised >> (self.blocks.bit_length() - 1)) - lead
        return lax.div(raised, jnp.full_like(raised, self.blocks)) - lead

    def wrap(self, entry):
        for bound in (8, 4, 2, 1):
            entry = jnp.where(entry < 0, entry + self.entries * bound, entry)
        for bound in (8, 4, 2, 1):
            over = entry - self.entries * bound
            entry = jnp.where(over >= 0, over, entry)
        return entry

    def column_entry(self, lon, donor, offset, slot):
        side = (lon == 0) | (lon == self.lon_count - 1)
        top = self.first_entry(self.top_start(lon), donor, offset)
        bottom = self.first_entry(self.bottom_start(lon), donor, offset)
        lower = (lon == 0) | jnp.logical_not(side) & (slot >= self.half)
        skipped = jnp.where(jnp.logical_not(side) & (slot >= self.half), self.half, 0)
        return jnp.where(lower, bottom, top) + slot - skipped

    def column_slot(self, lat, lon, donor, offset):
        side = (lon == 0) | (lon == self.lon_count - 1)
        start, _ = self.stretch(lat, lon)
        ahead = self.first_entry(start, donor, offset) - self.first_entry(
            jnp.where(lon == 0, self.bottom_start(lon), self.top_start(lon)), donor, offset
        )
        middle = jnp.where(lat == self.lat_count - 1, self.half, 0)
        return jnp.where(side, jnp.maximum(ahead, 0), middle)


def padded_rows(count):
    return -(-count // 1024) * 8


def table_ids(outer, inner, slots):
    rows = padded_rows(outer * inner * slots)
    flat = np.minimum(np.arange(rows * 128), outer * inner * slots - 1)
    return np.stack(
        [flat // (inner * slots), flat // slots % inner, flat % slots]
    ).reshape(3, rows, 128).astype(np.int32)


def whole(count):
    return [pl.BlockSpec(memory_space=pltpu.VMEM)] * count


def scalars(count):
    return [pl.BlockSpec(memory_space=pltpu.SMEM)] * count


def lookup(table_ref, index):
    return table_ref[index // 128, index % 128]


def grant(mebibytes):
    return pltpu.CompilerParams(vmem_limit_bytes=mebibytes << 20)


def tiles(index, count):
    if isinstance(index, int):
        return pl.ds(index * TILE, count * TILE)
    return pl.ds(pl.multiple_of(index * TILE, TILE), count * TILE)


def table_kernel(
    loop, pitch, cell_ref, other_ref, send_id_ref, swap_id_ref, got_id_ref,
    send_ref, swap_ref, receive_ref,
):
    lat, lon = lax.axis_index("lat"), lax.axis_index("lon")
    lat_count, lon_count = loop.lat_count, loop.lon_count
    mine = loop.position(cell_ref[0], cell_ref[1])
    other = loop.position(other_ref[0], other_ref[1])

    step, _, slot = [send_id_ref[n] for n in range(3)]
    entry = loop.column_entry(
        to_device(lon, step, lon_count), lat * lon_count + lon, other, slot
    )
    send_ref[...] = loop.wrap(entry)

    lat_step, lon_step, slot = [swap_id_ref[n] for n in range(3)]
    donor = lat * lon_count + from_device(lon, lon_step, lon_count)
    here = jnp.full_like(slot, lon)
    ahead = loop.column_slot(to_device(lat, lat_step, lat_count), here, donor, other)
    swap_ref[...] = jnp.minimum(ahead + slot, loop.column_slots - 1)

    lat_step, lon_step, slot = [got_id_ref[n] for n in range(3)]
    donor = from_device(lat, lat_step, lat_count) * lon_count + from_device(
        lon, lon_step, lon_count
    )
    start, span = loop.stretch(jnp.full_like(slot, lat), jnp.full_like(slot, lon))
    entry = loop.first_entry(start, donor, mine) + slot
    place = entry * loop.blocks + donor + mine
    wrapped = jnp.where(place >= loop.total, place - loop.total, place)
    row, col = loop.cell(wrapped)
    spot = (row - lat * loop.rows + HALO) * pitch + PAD + (col - lon * loop.cols + HALO)
    receive_ref[...] = jnp.where(place < start + span, spot, 0)


def strip_kernel(rows, cols, own_even_ref, own_odd_ref, even_ref, odd_ref, *send_refs):
    lat_even = lax.rem(lax.axis_index("lat"), 2) == 0
    lon_even = lax.rem(lax.axis_index("lon"), 2) == 0
    high = cols - HALO
    lows = (jnp.where(lon_even, high, 0), jnp.where(lon_even, 0, high))

    def copy_halo(first, source):
        for send_ref, low in zip(send_refs, lows):
            for row in range(HALO):
                send_ref[tiles((first + row) * HALO, HALO), :] = source[
                    tiles(row * cols + low, HALO), :
                ]

    for send_ref, own_ref in zip(send_refs, (own_even_ref, own_odd_ref)):
        send_ref[tiles(HALO * HALO, rows * HALO), :] = own_ref[...]

    @pl.when(lat_even)
    def _():
        copy_halo(0, odd_ref)
        copy_halo(HALO + rows, even_ref)

    @pl.when(jnp.logical_not(lat_even))
    def _():
        copy_halo(0, even_ref)
        copy_halo(HALO + rows, odd_ref)


def mix_and_pack(loop, wide, rim, frame_ref, value_ref, send_refs):
    send_table_ref, base_ref, weight_ref, cosine_ref, sine_ref = rim
    field = lax.broadcasted_iota(jnp.int32, (TILE, 128), 0)
    takes_next = (field == 1) | (field == 4)
    turned = takes_next | (field == 2) | (field == 5)
    first_row = lax.axis_index("lat") * loop.rows - HALO + 1
    first_col = lax.axis_index("lon") * loop.cols - HALO + 1

    def one_entry(entry, carry):
        base = (base_ref[entry, 0] - first_row) * wide + (base_ref[entry, 1] - first_col)
        total = None
        for a in range(4):
            for b in range(4):
                weight = weight_ref[entry, 4 * a + b]
                part = weight * frame_ref[tiles(base + a * wide + b, 1), :]
                total = part if total is None else total + part
        cosine, sine = cosine_ref[entry], sine_ref[entry]
        other = jnp.where(
            takes_next, pltpu.roll(total, TILE - 1, 0), pltpu.roll(total, 1, 0)
        )
        mixed = cosine * total + jnp.where(takes_next, -sine, sine) * other
        value_ref[tiles(entry, 1), :] = jnp.where(turned, mixed, total)
        return carry

    lax.fori_loop(0, loop.entries, one_entry, 0, unroll=4)
    for step, send_ref in enumerate(send_refs):
        for slot in range(loop.column_slots):
            entry = lookup(send_table_ref, step * loop.column_slots + slot)
            send_ref[tiles(slot, 1), :] = value_ref[tiles(entry, 1), :]


def frame_kernel(loop, *refs):
    rim, refs = refs[:5], refs[5:]
    state_ref, lat_even_ref, lat_odd_ref, lon_even_ref, lon_odd_ref, frame_ref = refs[:6]
    send_refs, value_ref = refs[6:-1], refs[-1]
    rows, cols = loop.rows, loop.cols
    wide = cols + 2 * HALO
    lat_even = lax.rem(lax.axis_index("lat"), 2) == 0
    lon_even = lax.rem(lax.axis_index("lon"), 2) == 0

    def copy_rows(first, count, source, left, width):
        for row in range(count):
            frame_ref[tiles((first + row) * wide + left, width), :] = source[
                tiles(row * width, width), :
            ]

    copy_rows(HALO, rows, state_ref, HALO, cols)

    @pl.when(lat_even)
    def _():
        copy_rows(0, HALO, lat_odd_ref, HALO, cols)
        copy_rows(HALO + rows, HALO, lat_even_ref, HALO, cols)

    @pl.when(jnp.logical_not(lat_even))
    def _():
        copy_rows(0, HALO, lat_even_ref, HALO, cols)
        copy_rows(HALO + rows, HALO, lat_odd_ref, HALO, cols)

    @pl.when(lon_even)
    def _():
        copy_rows(0, rows + 2 * HALO, lon_odd_ref, 0, HALO)
        copy_rows(0, rows + 2 * HALO, lon_even_ref, HALO + cols, HALO)

    @pl.when(jnp.logical_not(lon_even))
    def _():
        copy_rows(0, rows + 2 * HALO, lon_even_ref, 0, HALO)
        copy_rows(0, rows + 2 * HALO, lon_odd_ref, HALO + cols, HALO)

    mix_and_pack(loop, wide, rim, frame_ref, value_ref, send_refs)


def swap_kernel(loop, table_ref, *refs):
    got_refs, out_refs = refs[: loop.lon_count], refs[loop.lon_count :]
    for lat_step in range(loop.lat_count):
        for lon_step in range(loop.lon_count):
            for slot in range(loop.slots):
                place = lon_step * loop.slots + slot
                source = lookup(table_ref, lat_step * loop.lon_count * loop.slots + place)
                out_refs[lat_step][tiles(place, 1), :] = got_refs[lon_step][tiles(source, 1), :]


class Section:
    def __init__(self, loop, factor_ref, radial_ref, plane_ref, work_ref):
        self.loop = loop
        self.tall, self.wide = loop.rows + 2 * HALO, loop.cols + 2 * HALO
        self.pitch = self.wide + 2 * PAD
        self.factor_ref, self.radial_ref = factor_ref, radial_ref
        self.plane_ref, self.work_ref = plane_ref, work_ref
        lat, lon = lax.axis_index("lat"), lax.axis_index("lon")
        self.lat = lat
        self.at_top, self.at_left = lat == 0, lon == 0
        self.on_row_edge = self.at_top | (lat == loop.lat_count - 1)
        self.on_col_edge = self.at_left | (lon == loop.lon_count - 1)

    def spread(self, frame_ref, rows):
        def one_row(row, carry):
            for chunk in range(0, self.wide, 8):
                for f in range(TILE):
                    start = (row * self.wide + chunk) * TILE + f
                    self.plane_ref[self.at(f, row, chunk), :] = frame_ref[
                        pl.ds(start, 8, stride=TILE), :
                    ]
            return carry

        lax.fori_loop(*rows, one_row, 0)

    def scatter(self, receive_ref, got_refs):
        arrivals = self.loop.lon_count * self.loop.slots
        for lat_step in range(self.loop.lat_count):
            for place in range(arrivals):
                spot = lookup(receive_ref, lat_step * arrivals + place)
                self.plane_ref[pl.ds(spot, TILE, stride=self.tall * self.pitch), :] = got_refs[
                    lat_step
                ][tiles(place, 1), :]

    def at(self, number, row, col):
        return pl.ds((number * self.tall + row) * self.pitch + PAD + col, 8)

    def reader(self, ref, row, col):
        def read(number, row_step=0, col_step=0):
            return ref[self.at(number, row + row_step, col + col_step), :]

        return read

    def prepare(self, row):
        factors = [self.factor_ref[(self.lat * 3 + n) * self.tall + row] for n in range(3)]
        inverse_radius = self.radial_ref[0]
        with_theta = inverse_radius * (self.loop.nth / math.pi)
        return factors, inverse_radius * factors[2], with_theta

    def up(self, x):
        return pltpu.roll(x, x.shape[-1] - 1, 1)

    def down(self, x):
        return pltpu.roll(x, 1, 1)

    def curl(self, read, first, prepared):
        (tu, td, ph), with_phi, with_theta = prepared
        ru, rl = self.radial_ref[1], self.radial_ref[2]
        a, b, c = first, first + 1, first + 2
        mid_b, mid_c = read(b), read(c)
        radial = self.radial_ref[0] * (
            (tu * read(c, 1) - td * read(c, -1)) - ph * (read(b, 0, 1) - read(b, 0, -1))
        )
        polar = with_phi * (read(a, 0, 1) - read(a, 0, -1)) - (
            ru * self.up(mid_c) - rl * self.down(mid_c)
        )
        azimuth = (ru * self.up(mid_b) - rl * self.down(mid_b)) - with_theta * (
            read(a, 1) - read(a, -1)
        )
        return radial, polar, azimuth

    def slope(self, read, number, prepared):
        _, with_phi, with_theta = prepared
        mid = read(number)
        return (
            self.radial_ref[3] * self.up(mid) - self.radial_ref[4] * self.down(mid),
            with_theta * (read(number, 1) - read(number, -1)),
            with_phi * (read(number, 0, 1) - read(number, 0, -1)),
        )

    def outflow(self, read, first, prepared):
        (tu, td, ph), _, _ = prepared
        mid = read(first)
        return (
            self.radial_ref[5] * self.up(mid) - self.radial_ref[6] * self.down(mid)
        ) + self.radial_ref[0] * (
            (tu * read(first + 1, 1) - td * read(first + 1, -1))
            + ph * (read(first + 2, 0, 1) - read(first + 2, 0, -1))
        )

    def first_pass(self, row, chunk):
        prepared = self.prepare(row)
        read = self.reader(self.plane_ref, row, chunk)

        def put(number, value):
            self.work_ref[self.at(number, row, chunk), :] = value

        flow = [read(n) for n in range(3)]
        field = [read(n) for n in range(3, 6)]
        current = self.curl(read, 3, prepared)
        spin = self.curl(read, 0, prepared)
        induced = cross(flow, field)
        warm = self.slope(read, 6, prepared)
        for n in range(3):
            put(n, current[n])
            put(3 + n, spin[n])
            put(6 + n, induced[n] - ETA_COEF * current[n])
            put(9 + n, warm[n])
        put(12, read(7) + 0.5 * dot(flow, flow))

    def second_pass(self, row, chunk, emit):
        prepared = self.prepare(row)
        read = self.reader(self.plane_ref, row, chunk)
        work = self.reader(self.work_ref, row, chunk)
        flow = [read(n) for n in range(3)]
        field = [read(n) for n in range(3, 6)]
        current = [work(n) for n in range(3)]
        spin = [work(3 + n) for n in range(3)]
        warm = [work(9 + n) for n in range(3)]
        field_rate = self.curl(work, 6, prepared)
        spin_curl = self.curl(work, 3, prepared)
        head = self.slope(work, 12, prepared)
        lorentz = cross(current, field)
        advect = cross(flow, spin)
        speed = [advect[n] + lorentz[n] - head[n] - NU_COEF * spin_curl[n] for n in range(3)]
        speed[0] = speed[0] + ARCHIMEDES_LIFT * read(6)
        heat = KAPPA_COEF * self.outflow(work, 9, prepared) - dot(flow, warm)
        squeeze = -SOUND_SQ * self.outflow(read, 0, prepared)
        emit(row, chunk, read, speed + list(field_rate) + [heat, squeeze])

    def over(self, rows, one_row, unroll):
        def step(row, carry):
            one_row(row)
            return carry

        lax.fori_loop(*rows, step, 0, unroll=unroll)

    def everywhere(self, rows, chunks, emit):
        def first(row):
            for chunk in range(0, self.wide, 8):
                self.first_pass(row, chunk)

        def second(row):
            for chunk in chunks:
                self.second_pass(row, chunk, emit)

        self.over((rows[0] - 1, rows[1] + 1), first, 2)
        self.over(rows, second, 2)

    def along_edges(self, rows, chunks, emit):
        tall, wide = self.tall, self.wide
        low_chunk, high_chunk = chunks[0], chunks[-1]

        @pl.when(self.on_row_edge)
        def _():
            row = jnp.where(self.at_top, HALO - 1, tall - HALO - 1)
            for step in range(2):
                for chunk in range(0, wide, 8):
                    self.first_pass(row + step, chunk)

        @pl.when(self.on_col_edge)
        def _():
            chunk = pl.multiple_of(jnp.where(self.at_left, 0, wide - 8), 8)
            self.over(
                (rows[0] - 1, rows[1] + 1), lambda row: self.first_pass(row, chunk), 2
            )

        @pl.when(self.on_row_edge)
        def _():
            row = jnp.where(self.at_top, HALO, tall - HALO - 2)
            for step in range(2):
                for chunk in chunks:
                    self.second_pass(row + step, chunk, emit)

        @pl.when(self.on_col_edge)
        def _():
            chunk = jnp.where(self.at_left, low_chunk, high_chunk)
            self.over(rows, lambda row: self.second_pass(row, chunk, emit), 2)


def cross(x, y):
    return (
        x[1] * y[2] - x[2] * y[1],
        x[2] * y[0] - x[0] * y[2],
        x[0] * y[1] - x[1] * y[0],
    )


def dot(x, y):
    return x[0] * y[0] + x[1] * y[1] + x[2] * y[2]


def middle_state(loop, frame_ref, rate_ref):
    wide = loop.cols + 2 * HALO
    first_row = lax.axis_index("lat") * loop.rows - HALO
    first_col = lax.axis_index("lon") * loop.cols - HALO

    def emit(row, chunk, read, rate):
        in_row = (row + first_row >= 0) & (row + first_row < loop.nth)
        col = lax.broadcasted_iota(jnp.int32, (8, 128), 0) + (chunk + first_col)
        inside = (col >= jnp.where(in_row, 0, loop.nph)) & (col < loop.nph)
        for f in range(TILE):
            rate_ref[f, row, pl.ds(chunk, 8), :] = rate[f]
            start = (row * wide + chunk) * TILE + f
            frame_ref[pl.ds(start, 8, stride=TILE), :] = jnp.where(
                inside, read(f) + TIME_STEP * rate[f], 0.0
            )

    return emit


def total_change(loop, change_ref, rate_ref):
    def emit(row, chunk, read, rate):
        for f in range(TILE):
            start = ((row - HALO) * loop.cols + chunk - HALO) * TILE + f
            change_ref[pl.ds(start, 8, stride=TILE), :] = (0.5 * TIME_STEP) * (
                rate_ref[f, row, pl.ds(chunk, 8), :] + rate[f]
            )

    return emit


def first_inner_kernel(
    loop, factor_ref, radial_ref, frame_in_ref, after_ref, frame_ref, rate_ref, plane_ref, work_ref
):
    del after_ref
    part = Section(loop, factor_ref, radial_ref, plane_ref, work_ref)
    part.spread(frame_in_ref, (0, part.tall))
    part.everywhere(
        (2, part.tall - 2), range(0, part.wide, 8), middle_state(loop, frame_ref, rate_ref)
    )


def first_edge_kernel(loop, *refs):
    rim, refs = refs[:5], refs[5:]
    receive_ref, factor_ref, radial_ref = refs[:3]
    got_refs, refs = refs[7 : 7 + loop.lat_count], refs[7 + loop.lat_count :]
    frame_ref, rate_ref, plane_ref, work_ref = refs[:4]
    send_refs, value_ref = refs[4:-1], refs[-1]
    part = Section(loop, factor_ref, radial_ref, plane_ref, work_ref)
    part.scatter(receive_ref, got_refs)
    part.along_edges(
        (2, part.tall - 2), range(0, part.wide, 8), middle_state(loop, frame_ref, rate_ref)
    )
    mix_and_pack(loop, part.wide, rim, frame_ref, value_ref, send_refs)


def second_inner_kernel(
    loop, factor_ref, radial_ref, frame_ref, rate_ref, after_ref, change_ref, plane_ref, work_ref
):
    del after_ref
    part = Section(loop, factor_ref, radial_ref, plane_ref, work_ref)
    part.spread(frame_ref, (2, part.tall - 2))
    part.everywhere(
        (HALO, HALO + loop.rows),
        range(HALO, HALO + loop.cols, 8),
        total_change(loop, change_ref, rate_ref),
    )


def second_edge_kernel(loop, receive_ref, factor_ref, radial_ref, rate_ref, inner_ref, *refs):
    got_refs, refs = refs[2 : 2 + loop.lat_count], refs[2 + loop.lat_count :]
    plane_ref, work_ref, change_ref = refs
    part = Section(loop, factor_ref, radial_ref, plane_ref, work_ref)
    for row in range(loop.rows):
        here = tiles(row * loop.cols, loop.cols)
        change_ref[here, :] = inner_ref[here, :]
    part.scatter(receive_ref, got_refs)
    part.along_edges(
        (HALO, HALO + loop.rows),
        range(HALO, HALO + loop.cols, 8),
        total_change(loop, change_ref, rate_ref),
    )


def radial_factors(levels, theta_count):
    scale = 2.0 * theta_count / math.pi
    step = 0.65 * scale / levels
    radius = 0.35 * scale + (np.arange(levels) + 0.5) * step
    half = 0.5 / step
    above = np.append(radius[1:], 0.0)
    below = np.append(0.0, radius[:-1])
    ones_above = np.append(np.ones(levels - 1), 0.0)
    ones_below = np.append(0.0, np.ones(levels - 1))
    rows = np.stack(
        [
            1.0 / radius,
            half * above / radius,
            half * below / radius,
            half * ones_above,
            half * ones_below,
            half * above**2 / radius**2,
            half * below**2 / radius**2,
        ]
    )
    return np.repeat(rows[:, None, :], 8, axis=1).astype(np.float32)


def row_factors(rows, lat_count, nth, nph):
    polar_step, azimuth_step = math.pi / (2 * nth), 1.5 * math.pi / nph
    tall = rows + 2 * HALO
    parts = []
    for lat in range(lat_count):
        row = lat * rows - HALO - 1 + np.arange(tall + 2)
        sines = np.sin(math.pi / 4 + (row + 0.5) * polar_step)
        middle = sines[1:-1]
        parts += [
            sines[2:] / middle * (0.5 / polar_step),
            sines[:-2] / middle * (0.5 / polar_step),
            (0.5 / azimuth_step) / middle,
        ]
    return np.concatenate(parts).astype(np.float32)


def per_device(state, rim_base, rim_weight, rim_angle, rim_target):
    _, rows, cols, fields, levels = state.shape
    lat_count, lon_count = lax.axis_size("lat"), lax.axis_size("lon")
    entries = rim_base.shape[1]
    loop = Loop(rows, cols, lat_count, lon_count, entries)
    tall, wide = rows + 2 * HALO, cols + 2 * HALO
    pitch = wide + 2 * PAD
    block = state[0].reshape(rows * cols * fields, levels)
    f32 = jnp.float32

    def tile_array(count):
        return jax.ShapeDtypeStruct((count * TILE, levels), f32)

    first_cell = rim_target[0, 0]
    other_cell = lax.ppermute(first_cell, "panel", [(0, 1), (1, 0)])

    cells = state[0]
    last_first = lax.axis_index("lat") % 2 == 0
    head, tail = cells[:HALO], cells[rows - HALO :]
    send_even = jnp.where(last_first, tail, head).reshape(HALO * cols * fields, levels)
    send_odd = jnp.where(last_first, head, tail).reshape(HALO * cols * fields, levels)
    lat_even = lax.ppermute(send_even, "lat", even_pairs(lat_count))
    lat_odd = lax.ppermute(send_odd, "lat", odd_pairs(lat_count))

    send_ids = table_ids(1, lon_count, loop.column_slots)[[1, 0, 2]]
    got_ids = table_ids(lat_count, lon_count, loop.slots)
    send_table, swap_table, receive_table = pl.pallas_call(
        lambda *refs: table_kernel(loop, pitch, *refs),
        out_shape=[
            jax.ShapeDtypeStruct(ids.shape[1:], jnp.int32) for ids in (send_ids, got_ids, got_ids)
        ],
        in_specs=scalars(2) + whole(3),
        out_specs=whole(3),
        compiler_params=grant(4),
        name="tables",
    )(first_cell, other_cell, jnp.asarray(send_ids), jnp.asarray(got_ids), jnp.asarray(got_ids))
    angle = rim_angle[0]
    rim = (send_table, rim_base[0], rim_weight[0], jnp.cos(angle), jnp.sin(angle))
    factors = jnp.asarray(row_factors(rows, lat_count, loop.nth, loop.nph))
    radial = jnp.asarray(radial_factors(levels, loop.nth))

    east_first = lax.axis_index("lon") % 2 == 0
    head, tail = cells[:, :HALO], cells[:, cols - HALO :]
    own_even = jnp.where(east_first, tail, head).reshape(rows * HALO * fields, levels)
    own_odd = jnp.where(east_first, head, tail).reshape(rows * HALO * fields, levels)
    strip_even, strip_odd = pl.pallas_call(
        lambda *refs: strip_kernel(rows, cols, *refs),
        out_shape=[tile_array(tall * HALO)] * 2,
        in_specs=whole(4),
        out_specs=whole(2),
        compiler_params=grant(4),
        name="strips",
    )(own_even, own_odd, lat_even, lat_odd)
    lon_even = lax.ppermute(strip_even, "lon", even_pairs(lon_count))
    lon_odd = lax.ppermute(strip_odd, "lon", odd_pairs(lon_count))

    packed_shapes = [tile_array(loop.column_slots)] * lon_count
    frame, *packed = pl.pallas_call(
        lambda *refs: frame_kernel(loop, *refs),
        out_shape=[tile_array(tall * wide)] + packed_shapes,
        in_specs=scalars(5) + whole(5),
        out_specs=whole(1 + lon_count),
        scratch_shapes=[pltpu.VMEM((entries * TILE, levels), f32)],
        compiler_params=grant(8),
        name="frame",
    )(*rim, block, lat_even, lat_odd, lon_even, lon_odd)

    def first_round(packed):
        got = [packed[0]] + [
            lax.ppermute(packed[step], "lon", lon_route(step, lon_count))
            for step in range(1, lon_count)
        ]
        return pl.pallas_call(
            lambda *refs: swap_kernel(loop, *refs),
            out_shape=[tile_array(lon_count * loop.slots)] * lat_count,
            in_specs=scalars(1) + whole(lon_count),
            out_specs=whole(lat_count),
            compiler_params=grant(4),
            name="swap",
        )(swap_table, *got)

    def second_round(turned):
        return [
            lax.ppermute(turned[step], ("panel", "lat"), lat_route(step, lat_count))
            for step in range(lat_count)
        ]

    planes = [
        jax.ShapeDtypeStruct((fields * tall * pitch, levels), f32),
        jax.ShapeDtypeStruct((13 * tall * pitch, levels), f32),
    ]
    rates = jax.ShapeDtypeStruct((fields, tall, wide, levels), f32)

    turned = first_round(packed)
    got = second_round(turned)
    frame, rate, plane, work = pl.pallas_call(
        lambda *refs: first_inner_kernel(loop, *refs),
        out_shape=[tile_array(tall * wide), rates] + planes,
        in_specs=scalars(1) + whole(3),
        out_specs=whole(4),
        compiler_params=grant(4),
        name="first_inner",
    )(factors, radial, frame, turned[-1])
    frame, rate, _, _, *packed = pl.pallas_call(
        lambda *refs: first_edge_kernel(loop, *refs),
        out_shape=[tile_array(tall * wide), rates] + planes + packed_shapes,
        in_specs=scalars(7) + whole(5 + lat_count),
        out_specs=whole(4 + lon_count),
        scratch_shapes=[pltpu.VMEM((entries * TILE, levels), f32)],
        input_output_aliases={8: 0, 9: 1, 10: 2, 11: 3},
        compiler_params=grant(4),
        name="first_edge",
    )(*rim, receive_table, factors, radial, frame, rate, plane, work, *got)

    turned = first_round(packed)
    got = second_round(turned)
    inner, plane, work = pl.pallas_call(
        lambda *refs: second_inner_kernel(loop, *refs),
        out_shape=[tile_array(rows * cols)] + planes,
        in_specs=scalars(1) + whole(4),
        out_specs=whole(3),
        compiler_params=grant(4),
        name="second_inner",
    )(factors, radial, frame, rate, turned[-1])
    _, _, change = pl.pallas_call(
        lambda *refs: second_edge_kernel(loop, *refs),
        out_shape=planes + [tile_array(rows * cols)],
        in_specs=scalars(2) + whole(5 + lat_count),
        out_specs=whole(3),
        input_output_aliases={5: 0, 6: 1},
        compiler_params=grant(4),
        name="second_edge",
    )(receive_table, factors, radial, rate, inner, plane, work, *got)
    return change.reshape(1, rows, cols, fields, levels)


def solution(mesh):
    return jax.shard_map(
        per_device,
        mesh=mesh,
        in_specs=(
            P("panel", "lat", "lon", None, None),
            P("panel", ("lat", "lon"), None),
            P("panel", ("lat", "lon"), None),
            P("panel", ("lat", "lon")),
            P("panel", None, None),
        ),
        out_specs=P("panel", "lat", "lon", None, None),
        check_vma=False,
    )
```

```python
import math

import jax
import jax.numpy as jnp
import numpy as np
from jax import lax
from jax.experimental import pallas as pl
from jax.experimental.pallas import tpu as pltpu
from jax.sharding import PartitionSpec as P

ETA_COEF = 0.2
NU_COEF = 0.2
KAPPA_COEF = 0.3
SOUND_SQ = 1.0
ARCHIMEDES_LIFT = 0.5
TIME_STEP = 0.2

HALO = 4
PAD = 8
TILE = 8


def is_power_of_two(count):
    return count & (count - 1) == 0


def to_device(index, step, count):
    return index ^ step if is_power_of_two(count) else (index + step) % count


def from_device(index, step, count):
    return index ^ step if is_power_of_two(count) else (index + count - step) % count


def swap_route(parity, count):
    mate = list(range(count))
    for low in range(parity, count - 1, 2):
        mate[low], mate[low + 1] = low + 1, low
    return [
        (side * count + i, (side if mate[i] != i else 1 - side) * count + mate[i])
        for side in range(2)
        for i in range(count)
    ]


def lon_route(step, count):
    return [(i, to_device(i, step, count)) for i in range(count)]


def lat_route(step, count):
    return [
        (side * count + i, (1 - side) * count + to_device(i, step, count))
        for side in range(2)
        for i in range(count)
    ]


class Loop:
    def __init__(self, rows, cols, lat_count, lon_count, entries):
        self.rows, self.cols = rows, cols
        self.lat_count, self.lon_count = lat_count, lon_count
        self.nth, self.nph = rows * lat_count, cols * lon_count
        self.total = 4 * (self.nth + self.nph)
        self.blocks = lat_count * lon_count
        self.entries = entries
        one_row = 2 * (cols + 2 * HALO)
        one_col = 2 * (rows + 2 * HALO)
        corner = 2 * (rows + cols + 2 * HALO)
        self.slots = -(-max(corner, one_row, one_col) // self.blocks)
        self.half = -(-one_row // self.blocks)
        side = 4 * (cols + HALO) + 2 * self.nth
        self.column_slots = max(-(-side // self.blocks), 2 * self.half)

    def position(self, row, col):
        nth, nph = self.nth, self.nph
        top = 2 * col + row + 2
        right = 2 * nph + 2 * row + col - nph
        bottom = 2 * nph + 2 * nth + 2 * (nph - 1 - col) + row - nth
        left = 4 * nph + 2 * nth + 2 * (nth - 1 - row) + col + 2
        return jnp.where(
            row < 0, top, jnp.where(row >= nth, bottom, jnp.where(col >= nph, right, left))
        )

    def cell(self, place):
        nth, nph = self.nth, self.nph
        right = place - 2 * nph
        bottom = right - 2 * nth
        left = bottom - 2 * nph
        on_top, on_right, on_bottom = right < 0, bottom < 0, left < 0
        row = jnp.where(
            on_top,
            (place & 1) - 2,
            jnp.where(
                on_right,
                right >> 1,
                jnp.where(on_bottom, nth + (bottom & 1), nth - 1 - (left >> 1)),
            ),
        )
        col = jnp.where(
            on_top,
            place >> 1,
            jnp.where(
                on_right,
                nph + (right & 1),
                jnp.where(on_bottom, nph - 1 - (bottom >> 1), (left & 1) - 2),
            ),
        )
        return row, col

    def top_start(self, lon):
        return 2 * jnp.maximum(lon * self.cols - HALO, 0)

    def bottom_start(self, lon):
        high = jnp.minimum(lon * self.cols + self.cols + HALO, self.nph)
        return 2 * self.nph + 2 * self.nth + 2 * (self.nph - high)

    def stretch(self, lat, lon):
        nth, nph = self.nth, self.nph
        row_low = jnp.maximum(lat * self.rows - HALO, 0)
        row_high = jnp.minimum(lat * self.rows + self.rows + HALO, nth)
        col_low = jnp.maximum(lon * self.cols - HALO, 0)
        col_high = jnp.minimum(lon * self.cols + self.cols + HALO, nph)
        top, bottom = lat == 0, lat == self.lat_count - 1
        left, right = lon == 0, lon == self.lon_count - 1
        left_start = 4 * nph + 2 * nth + 2 * (nth - row_high)
        start = jnp.where(
            top & left,
            left_start,
            jnp.where(
                top,
                self.top_start(lon),
                jnp.where(
                    right,
                    2 * nph + 2 * row_low,
                    jnp.where(bottom, self.bottom_start(lon), left_start),
                ),
            ),
        )
        span = jnp.where(top | bottom, 2 * (col_high - col_low), 0) + jnp.where(
            left | right, 2 * (row_high - row_low), 0
        )
        return start, span

    def first_entry(self, start, donor, offset):
        lead = -(-2 * self.total // self.blocks)
        raised = start - donor - offset + lead * self.blocks + self.blocks - 1
        if is_power_of_two(self.blocks):
            return (raised >> (self.blocks.bit_length() - 1)) - lead
        return lax.div(raised, jnp.full_like(raised, self.blocks)) - lead

    def wrap(self, entry):
        for bound in (8, 4, 2, 1):
            entry = jnp.where(entry < 0, entry + self.entries * bound, entry)
        for bound in (8, 4, 2, 1):
            over = entry - self.entries * bound
            entry = jnp.where(over >= 0, over, entry)
        return entry

    def column_entry(self, lon, donor, offset, slot):
        side = (lon == 0) | (lon == self.lon_count - 1)
        top = self.first_entry(self.top_start(lon), donor, offset)
        bottom = self.first_entry(self.bottom_start(lon), donor, offset)
        lower = (lon == 0) | jnp.logical_not(side) & (slot >= self.half)
        skipped = jnp.where(jnp.logical_not(side) & (slot >= self.half), self.half, 0)
        return jnp.where(lower, bottom, top) + slot - skipped

    def column_slot(self, lat, lon, donor, offset):
        side = (lon == 0) | (lon == self.lon_count - 1)
        start, _ = self.stretch(lat, lon)
        ahead = self.first_entry(start, donor, offset) - self.first_entry(
            jnp.where(lon == 0, self.bottom_start(lon), self.top_start(lon)), donor, offset
        )
        middle = jnp.where(lat == self.lat_count - 1, self.half, 0)
        return jnp.where(side, jnp.maximum(ahead, 0), middle)


def padded_rows(count):
    return -(-count // 1024) * 8


def table_ids(outer, inner, slots):
    rows = padded_rows(outer * inner * slots)
    flat = np.minimum(np.arange(rows * 128), outer * inner * slots - 1)
    return np.stack(
        [flat // (inner * slots), flat // slots % inner, flat % slots]
    ).reshape(3, rows, 128).astype(np.int32)


def whole(count):
    return [pl.BlockSpec(memory_space=pltpu.VMEM)] * count


def scalars(count):
    return [pl.BlockSpec(memory_space=pltpu.SMEM)] * count


def lookup(table_ref, index):
    return table_ref[index // 128, index % 128]


def grant(mebibytes):
    return pltpu.CompilerParams(vmem_limit_bytes=mebibytes << 20)


def tiles(index, count):
    if isinstance(index, int):
        return pl.ds(index * TILE, count * TILE)
    return pl.ds(pl.multiple_of(index * TILE, TILE), count * TILE)


def table_kernel(
    loop, pitch, cell_ref, other_ref, send_id_ref, swap_id_ref, got_id_ref,
    send_ref, swap_ref, receive_ref,
):
    lat, lon = lax.axis_index("lat"), lax.axis_index("lon")
    lat_count, lon_count = loop.lat_count, loop.lon_count
    mine = loop.position(cell_ref[0], cell_ref[1])
    other = loop.position(other_ref[0], other_ref[1])

    step, _, slot = [send_id_ref[n] for n in range(3)]
    entry = loop.column_entry(
        to_device(lon, step, lon_count), lat * lon_count + lon, other, slot
    )
    send_ref[...] = loop.wrap(entry)

    lat_step, lon_step, slot = [swap_id_ref[n] for n in range(3)]
    donor = lat * lon_count + from_device(lon, lon_step, lon_count)
    here = jnp.full_like(slot, lon)
    ahead = loop.column_slot(to_device(lat, lat_step, lat_count), here, donor, other)
    swap_ref[...] = jnp.minimum(ahead + slot, loop.column_slots - 1)

    lat_step, lon_step, slot = [got_id_ref[n] for n in range(3)]
    donor = from_device(lat, lat_step, lat_count) * lon_count + from_device(
        lon, lon_step, lon_count
    )
    start, span = loop.stretch(jnp.full_like(slot, lat), jnp.full_like(slot, lon))
    entry = loop.first_entry(start, donor, mine) + slot
    place = entry * loop.blocks + donor + mine
    wrapped = jnp.where(place >= loop.total, place - loop.total, place)
    row, col = loop.cell(wrapped)
    spot = (row - lat * loop.rows + HALO) * pitch + PAD + (col - lon * loop.cols + HALO)
    receive_ref[...] = jnp.where(place < start + span, spot, 0)


def strip_kernel(rows, cols, own_even_ref, own_odd_ref, even_ref, odd_ref, *send_refs):
    lat_even = lax.rem(lax.axis_index("lat"), 2) == 0
    lon_even = lax.rem(lax.axis_index("lon"), 2) == 0
    high = cols - HALO
    lows = (jnp.where(lon_even, high, 0), jnp.where(lon_even, 0, high))

    def copy_halo(first, source):
        for send_ref, low in zip(send_refs, lows):
            for row in range(HALO):
                send_ref[tiles((first + row) * HALO, HALO), :] = source[
                    tiles(row * cols + low, HALO), :
                ]

    for send_ref, own_ref in zip(send_refs, (own_even_ref, own_odd_ref)):
        send_ref[tiles(HALO * HALO, rows * HALO), :] = own_ref[...]

    @pl.when(lat_even)
    def _():
        copy_halo(0, odd_ref)
        copy_halo(HALO + rows, even_ref)

    @pl.when(jnp.logical_not(lat_even))
    def _():
        copy_halo(0, even_ref)
        copy_halo(HALO + rows, odd_ref)


def mix_and_pack(loop, wide, rim, frame_ref, value_ref, send_refs):
    send_table_ref, base_ref, weight_ref, cosine_ref, sine_ref = rim
    field = lax.broadcasted_iota(jnp.int32, (TILE, 128), 0)
    takes_next = (field == 1) | (field == 4)
    turned = takes_next | (field == 2) | (field == 5)
    first_row = lax.axis_index("lat") * loop.rows - HALO + 1
    first_col = lax.axis_index("lon") * loop.cols - HALO + 1

    def one_entry(entry, carry):
        base = (base_ref[0, entry] - first_row) * wide + (base_ref[1, entry] - first_col)
        total = None
        for a in range(4):
            for b in range(4):
                weight = weight_ref[4 * a + b, entry]
                part = weight * frame_ref[tiles(base + a * wide + b, 1), :]
                total = part if total is None else total + part
        cosine, sine = cosine_ref[entry], sine_ref[entry]
        other = jnp.where(
            takes_next, pltpu.roll(total, TILE - 1, 0), pltpu.roll(total, 1, 0)
        )
        mixed = cosine * total + jnp.where(takes_next, -sine, sine) * other
        value_ref[tiles(entry, 1), :] = jnp.where(turned, mixed, total)
        return carry

    lax.fori_loop(0, loop.entries, one_entry, 0, unroll=4)
    for step, send_ref in enumerate(send_refs):
        for slot in range(loop.column_slots):
            entry = lookup(send_table_ref, step * loop.column_slots + slot)
            send_ref[tiles(slot, 1), :] = value_ref[tiles(entry, 1), :]


def frame_kernel(loop, *refs):
    rim, refs = refs[:5], refs[5:]
    state_ref, lat_even_ref, lat_odd_ref, lon_even_ref, lon_odd_ref, frame_ref = refs[:6]
    send_refs, value_ref = refs[6:-1], refs[-1]
    rows, cols = loop.rows, loop.cols
    wide = cols + 2 * HALO
    lat_even = lax.rem(lax.axis_index("lat"), 2) == 0
    lon_even = lax.rem(lax.axis_index("lon"), 2) == 0

    def copy_rows(first, count, source, left, width):
        for row in range(count):
            frame_ref[tiles((first + row) * wide + left, width), :] = source[
                tiles(row * width, width), :
            ]

    copy_rows(HALO, rows, state_ref, HALO, cols)

    @pl.when(lat_even)
    def _():
        copy_rows(0, HALO, lat_odd_ref, HALO, cols)
        copy_rows(HALO + rows, HALO, lat_even_ref, HALO, cols)

    @pl.when(jnp.logical_not(lat_even))
    def _():
        copy_rows(0, HALO, lat_even_ref, HALO, cols)
        copy_rows(HALO + rows, HALO, lat_odd_ref, HALO, cols)

    @pl.when(lon_even)
    def _():
        copy_rows(0, rows + 2 * HALO, lon_odd_ref, 0, HALO)
        copy_rows(0, rows + 2 * HALO, lon_even_ref, HALO + cols, HALO)

    @pl.when(jnp.logical_not(lon_even))
    def _():
        copy_rows(0, rows + 2 * HALO, lon_even_ref, 0, HALO)
        copy_rows(0, rows + 2 * HALO, lon_odd_ref, HALO + cols, HALO)

    lat, lon = lax.axis_index("lat"), lax.axis_index("lon")
    zeros = jnp.zeros((HALO * TILE, frame_ref.shape[1]), jnp.float32)
    for at_row, top in ((lat == 0, 0), (lat == loop.lat_count - 1, HALO + rows)):
        for at_col, left in ((lon == 0, 0), (lon == loop.lon_count - 1, HALO + cols)):

            @pl.when(at_row & at_col)
            def _():
                for row in range(HALO):
                    frame_ref[tiles((top + row) * wide + left, HALO), :] = zeros

    mix_and_pack(loop, wide, rim, frame_ref, value_ref, send_refs)


def swap_kernel(loop, table_ref, *refs):
    got_refs, out_refs = refs[: loop.lon_count], refs[loop.lon_count :]
    for lat_step in range(loop.lat_count):
        for lon_step in range(loop.lon_count):
            for slot in range(loop.slots):
                place = lon_step * loop.slots + slot
                source = lookup(table_ref, lat_step * loop.lon_count * loop.slots + place)
                out_refs[lat_step][tiles(place, 1), :] = got_refs[lon_step][tiles(source, 1), :]


class Section:
    def __init__(self, loop, factor_ref, radial_ref, plane_ref, work_ref):
        self.loop = loop
        self.tall, self.wide = loop.rows + 2 * HALO, loop.cols + 2 * HALO
        self.pitch = self.wide + 2 * PAD
        self.factor_ref, self.radial_ref = factor_ref, radial_ref
        self.plane_ref, self.work_ref = plane_ref, work_ref
        lat, lon = lax.axis_index("lat"), lax.axis_index("lon")
        self.lat = lat
        self.at_top, self.at_left = lat == 0, lon == 0
        self.on_row_edge = self.at_top | (lat == loop.lat_count - 1)
        self.on_col_edge = self.at_left | (lon == loop.lon_count - 1)

    def spread(self, frame_ref, rows):
        def one_row(row, carry):
            for chunk in range(0, self.wide, 8):
                for f in range(TILE):
                    start = (row * self.wide + chunk) * TILE + f
                    self.plane_ref[self.at(f, row, chunk), :] = frame_ref[
                        pl.ds(start, 8, stride=TILE), :
                    ]
            return carry

        lax.fori_loop(*rows, one_row, 0)

    def scatter(self, receive_ref, got_refs):
        arrivals = self.loop.lon_count * self.loop.slots
        for lat_step in range(self.loop.lat_count):
            for place in range(arrivals):
                spot = lookup(receive_ref, lat_step * arrivals + place)
                self.plane_ref[pl.ds(spot, TILE, stride=self.tall * self.pitch), :] = got_refs[
                    lat_step
                ][tiles(place, 1), :]

    def at(self, number, row, col):
        return pl.ds((number * self.tall + row) * self.pitch + PAD + col, 8)

    def reader(self, ref, row, col):
        def read(number, row_step=0, col_step=0):
            return ref[self.at(number, row + row_step, col + col_step), :]

        return read

    def prepare(self, row):
        factors = [self.factor_ref[(self.lat * 3 + n) * self.tall + row] for n in range(3)]
        inverse_radius = self.radial_ref[0]
        with_theta = inverse_radius * (self.loop.nth / math.pi)
        return factors, inverse_radius * factors[2], with_theta

    def up(self, x):
        return pltpu.roll(x, x.shape[-1] - 1, 1)

    def down(self, x):
        return pltpu.roll(x, 1, 1)

    def curl(self, read, first, prepared):
        (tu, td, ph), with_phi, with_theta = prepared
        ru, rl = self.radial_ref[1], self.radial_ref[2]
        a, b, c = first, first + 1, first + 2
        mid_b, mid_c = read(b), read(c)
        radial = self.radial_ref[0] * (
            (tu * read(c, 1) - td * read(c, -1)) - ph * (read(b, 0, 1) - read(b, 0, -1))
        )
        polar = with_phi * (read(a, 0, 1) - read(a, 0, -1)) - (
            ru * self.up(mid_c) - rl * self.down(mid_c)
        )
        azimuth = (ru * self.up(mid_b) - rl * self.down(mid_b)) - with_theta * (
            read(a, 1) - read(a, -1)
        )
        return radial, polar, azimuth

    def slope(self, read, number, prepared):
        _, with_phi, with_theta = prepared
        mid = read(number)
        return (
            self.radial_ref[3] * self.up(mid) - self.radial_ref[4] * self.down(mid),
            with_theta * (read(number, 1) - read(number, -1)),
            with_phi * (read(number, 0, 1) - read(number, 0, -1)),
        )

    def outflow(self, read, first, prepared):
        (tu, td, ph), _, _ = prepared
        mid = read(first)
        return (
            self.radial_ref[5] * self.up(mid) - self.radial_ref[6] * self.down(mid)
        ) + self.radial_ref[0] * (
            (tu * read(first + 1, 1) - td * read(first + 1, -1))
            + ph * (read(first + 2, 0, 1) - read(first + 2, 0, -1))
        )

    def first_pass(self, row, chunk):
        prepared = self.prepare(row)
        read = self.reader(self.plane_ref, row, chunk)

        def put(number, value):
            self.work_ref[self.at(number, row, chunk), :] = value

        flow = [read(n) for n in range(3)]
        field = [read(n) for n in range(3, 6)]
        current = self.curl(read, 3, prepared)
        spin = self.curl(read, 0, prepared)
        induced = cross(flow, field)
        warm = self.slope(read, 6, prepared)
        for n in range(3):
            put(n, current[n])
            put(3 + n, spin[n])
            put(6 + n, induced[n] - ETA_COEF * current[n])
            put(9 + n, warm[n])
        put(12, read(7) + 0.5 * dot(flow, flow))

    def second_pass(self, row, chunk, emit):
        prepared = self.prepare(row)
        read = self.reader(self.plane_ref, row, chunk)
        work = self.reader(self.work_ref, row, chunk)
        flow = [read(n) for n in range(3)]
        field = [read(n) for n in range(3, 6)]
        current = [work(n) for n in range(3)]
        spin = [work(3 + n) for n in range(3)]
        warm = [work(9 + n) for n in range(3)]
        field_rate = self.curl(work, 6, prepared)
        spin_curl = self.curl(work, 3, prepared)
        head = self.slope(work, 12, prepared)
        lorentz = cross(current, field)
        advect = cross(flow, spin)
        speed = [advect[n] + lorentz[n] - head[n] - NU_COEF * spin_curl[n] for n in range(3)]
        speed[0] = speed[0] + ARCHIMEDES_LIFT * read(6)
        heat = KAPPA_COEF * self.outflow(work, 9, prepared) - dot(flow, warm)
        squeeze = -SOUND_SQ * self.outflow(read, 0, prepared)
        emit(row, chunk, read, speed + list(field_rate) + [heat, squeeze])

    def over(self, rows, one_row, unroll):
        def step(row, carry):
            one_row(row)
            return carry

        lax.fori_loop(*rows, step, 0, unroll=unroll)

    def everywhere(self, rows, chunks, emit):
        def first(row):
            for chunk in range(0, self.wide, 8):
                self.first_pass(row, chunk)

        def second(row):
            for chunk in chunks:
                self.second_pass(row, chunk, emit)

        self.over((rows[0] - 1, rows[1] + 1), first, 2)
        self.over(rows, second, 2)

    def along_edges(self, rows, chunks, emit):
        tall, wide = self.tall, self.wide
        low_chunk, high_chunk = chunks[0], chunks[-1]

        @pl.when(self.on_row_edge)
        def _():
            row = jnp.where(self.at_top, HALO - 1, tall - HALO - 1)
            for step in range(2):
                for chunk in range(0, wide, 8):
                    self.first_pass(row + step, chunk)

        @pl.when(self.on_col_edge)
        def _():
            chunk = pl.multiple_of(jnp.where(self.at_left, 0, wide - 8), 8)
            count = rows[1] - rows[0]
            self.over(
                (rows[0] - 1, rows[1] + 1), lambda row: self.first_pass(row, chunk), count // 2 + 1
            )

        @pl.when(self.on_row_edge)
        def _():
            row = jnp.where(self.at_top, HALO, tall - HALO - 2)
            for step in range(2):
                for chunk in chunks:
                    self.second_pass(row + step, chunk, emit)

        @pl.when(self.on_col_edge)
        def _():
            chunk = jnp.where(self.at_left, low_chunk, high_chunk)
            count = rows[1] - rows[0]
            self.over(rows, lambda row: self.second_pass(row, chunk, emit), count // 2)


def cross(x, y):
    return (
        x[1] * y[2] - x[2] * y[1],
        x[2] * y[0] - x[0] * y[2],
        x[0] * y[1] - x[1] * y[0],
    )


def dot(x, y):
    return x[0] * y[0] + x[1] * y[1] + x[2] * y[2]


def middle_state(loop, frame_ref, rate_ref):
    wide = loop.cols + 2 * HALO
    first_row = lax.axis_index("lat") * loop.rows - HALO
    first_col = lax.axis_index("lon") * loop.cols - HALO

    def emit(row, chunk, read, rate):
        in_row = (row + first_row >= 0) & (row + first_row < loop.nth)
        col = lax.broadcasted_iota(jnp.int32, (8, 128), 0) + (chunk + first_col)
        inside = (col >= jnp.where(in_row, 0, loop.nph)) & (col < loop.nph)
        for f in range(TILE):
            rate_ref[f, row, pl.ds(chunk, 8), :] = rate[f]
            start = (row * wide + chunk) * TILE + f
            frame_ref[pl.ds(start, 8, stride=TILE), :] = jnp.where(
                inside, read(f) + TIME_STEP * rate[f], 0.0
            )

    return emit


def total_change(loop, change_ref, rate_ref):
    def emit(row, chunk, read, rate):
        for f in range(TILE):
            start = ((row - HALO) * loop.cols + chunk - HALO) * TILE + f
            change_ref[pl.ds(start, 8, stride=TILE), :] = (0.5 * TIME_STEP) * (
                rate_ref[f, row, pl.ds(chunk, 8), :] + rate[f]
            )

    return emit


def first_inner_kernel(
    loop, factor_ref, radial_ref, frame_in_ref, after_ref, frame_ref, rate_ref, plane_ref, work_ref
):
    del after_ref
    part = Section(loop, factor_ref, radial_ref, plane_ref, work_ref)
    part.spread(frame_in_ref, (0, part.tall))
    part.everywhere(
        (2, part.tall - 2), range(0, part.wide, 8), middle_state(loop, frame_ref, rate_ref)
    )


def first_edge_kernel(loop, *refs):
    rim, refs = refs[:5], refs[5:]
    receive_ref, factor_ref, radial_ref = refs[:3]
    got_refs, refs = refs[7 : 7 + loop.lat_count], refs[7 + loop.lat_count :]
    frame_ref, rate_ref, plane_ref, work_ref = refs[:4]
    send_refs, value_ref = refs[4:-1], refs[-1]
    part = Section(loop, factor_ref, radial_ref, plane_ref, work_ref)
    part.scatter(receive_ref, got_refs)
    part.along_edges(
        (2, part.tall - 2), range(0, part.wide, 8), middle_state(loop, frame_ref, rate_ref)
    )
    mix_and_pack(loop, part.wide, rim, frame_ref, value_ref, send_refs)


def second_inner_kernel(
    loop, factor_ref, radial_ref, frame_ref, rate_ref, after_ref, change_ref, plane_ref, work_ref
):
    del after_ref
    part = Section(loop, factor_ref, radial_ref, plane_ref, work_ref)
    part.spread(frame_ref, (2, part.tall - 2))
    part.everywhere(
        (HALO, HALO + loop.rows),
        range(HALO, HALO + loop.cols, 8),
        total_change(loop, change_ref, rate_ref),
    )


def second_edge_kernel(loop, receive_ref, factor_ref, radial_ref, rate_ref, inner_ref, *refs):
    got_refs, refs = refs[2 : 2 + loop.lat_count], refs[2 + loop.lat_count :]
    plane_ref, work_ref, change_ref = refs
    part = Section(loop, factor_ref, radial_ref, plane_ref, work_ref)
    for row in range(loop.rows):
        here = tiles(row * loop.cols, loop.cols)
        change_ref[here, :] = inner_ref[here, :]
    part.scatter(receive_ref, got_refs)
    part.along_edges(
        (HALO, HALO + loop.rows),
        range(HALO, HALO + loop.cols, 8),
        total_change(loop, change_ref, rate_ref),
    )


def radial_factors(levels, theta_count):
    scale = 2.0 * theta_count / math.pi
    step = 0.65 * scale / levels
    radius = 0.35 * scale + (np.arange(levels) + 0.5) * step
    half = 0.5 / step
    above = np.append(radius[1:], 0.0)
    below = np.append(0.0, radius[:-1])
    ones_above = np.append(np.ones(levels - 1), 0.0)
    ones_below = np.append(0.0, np.ones(levels - 1))
    rows = np.stack(
        [
            1.0 / radius,
            half * above / radius,
            half * below / radius,
            half * ones_above,
            half * ones_below,
            half * above**2 / radius**2,
            half * below**2 / radius**2,
        ]
    )
    return np.repeat(rows[:, None, :], 8, axis=1).astype(np.float32)


def row_factors(rows, lat_count, nth, nph):
    polar_step, azimuth_step = math.pi / (2 * nth), 1.5 * math.pi / nph
    tall = rows + 2 * HALO
    parts = []
    for lat in range(lat_count):
        row = lat * rows - HALO - 1 + np.arange(tall + 2)
        sines = np.sin(math.pi / 4 + (row + 0.5) * polar_step)
        middle = sines[1:-1]
        parts += [
            sines[2:] / middle * (0.5 / polar_step),
            sines[:-2] / middle * (0.5 / polar_step),
            (0.5 / azimuth_step) / middle,
        ]
    return np.concatenate(parts).astype(np.float32)


def per_device(state, rim_base, rim_weight, rim_angle, rim_target):
    _, rows, cols, fields, levels = state.shape
    lat_count, lon_count = lax.axis_size("lat"), lax.axis_size("lon")
    entries = rim_base.shape[1]
    loop = Loop(rows, cols, lat_count, lon_count, entries)
    tall, wide = rows + 2 * HALO, cols + 2 * HALO
    pitch = wide + 2 * PAD
    block = state[0].reshape(rows * cols * fields, levels)
    f32 = jnp.float32

    def tile_array(count):
        return jax.ShapeDtypeStruct((count * TILE, levels), f32)

    first_cell = rim_target[0, 0]
    other_cell = lax.ppermute(first_cell, "panel", [(0, 1), (1, 0)])

    cells = state[0]
    last_first = lax.axis_index("lat") % 2 == 0
    head, tail = cells[:HALO], cells[rows - HALO :]
    send_even = jnp.where(last_first, tail, head).reshape(HALO * cols * fields, levels)
    send_odd = jnp.where(last_first, head, tail).reshape(HALO * cols * fields, levels)
    lat_even = lax.ppermute(send_even, ("panel", "lat"), swap_route(0, lat_count))
    lat_odd = lax.ppermute(send_odd, ("panel", "lat"), swap_route(1, lat_count))

    send_ids = table_ids(1, lon_count, loop.column_slots)[[1, 0, 2]]
    got_ids = table_ids(lat_count, lon_count, loop.slots)
    send_table, swap_table, receive_table = pl.pallas_call(
        lambda *refs: table_kernel(loop, pitch, *refs),
        out_shape=[
            jax.ShapeDtypeStruct(ids.shape[1:], jnp.int32) for ids in (send_ids, got_ids, got_ids)
        ],
        in_specs=scalars(2) + whole(3),
        out_specs=whole(3),
        compiler_params=grant(4),
        name="tables",
    )(first_cell, other_cell, jnp.asarray(send_ids), jnp.asarray(got_ids), jnp.asarray(got_ids))
    angle = rim_angle[0]
    rim = (send_table, rim_base[0].T, rim_weight[0].T, jnp.cos(angle), jnp.sin(angle))
    factors = jnp.asarray(row_factors(rows, lat_count, loop.nth, loop.nph))
    radial = jnp.asarray(radial_factors(levels, loop.nth))

    east_first = lax.axis_index("lon") % 2 == 0
    head, tail = cells[:, :HALO], cells[:, cols - HALO :]
    own_even = jnp.where(east_first, tail, head).reshape(rows * HALO * fields, levels)
    own_odd = jnp.where(east_first, head, tail).reshape(rows * HALO * fields, levels)
    strip_even, strip_odd = pl.pallas_call(
        lambda *refs: strip_kernel(rows, cols, *refs),
        out_shape=[tile_array(tall * HALO)] * 2,
        in_specs=whole(4),
        out_specs=whole(2),
        compiler_params=grant(4),
        name="strips",
    )(own_even, own_odd, lat_even, lat_odd)
    lon_even = lax.ppermute(strip_even, ("panel", "lon"), swap_route(0, lon_count))
    lon_odd = lax.ppermute(strip_odd, ("panel", "lon"), swap_route(1, lon_count))

    packed_shapes = [tile_array(loop.column_slots)] * lon_count
    frame, *packed = pl.pallas_call(
        lambda *refs: frame_kernel(loop, *refs),
        out_shape=[tile_array(tall * wide)] + packed_shapes,
        in_specs=scalars(5) + whole(5),
        out_specs=whole(1 + lon_count),
        scratch_shapes=[pltpu.VMEM((entries * TILE, levels), f32)],
        compiler_params=grant(8),
        name="frame",
    )(*rim, block, lat_even, lat_odd, lon_even, lon_odd)

    def first_round(packed):
        got = [packed[0]] + [
            lax.ppermute(packed[step], "lon", lon_route(step, lon_count))
            for step in range(1, lon_count)
        ]
        return pl.pallas_call(
            lambda *refs: swap_kernel(loop, *refs),
            out_shape=[tile_array(lon_count * loop.slots)] * lat_count,
            in_specs=scalars(1) + whole(lon_count),
            out_specs=whole(lat_count),
            compiler_params=grant(4),
            name="swap",
        )(swap_table, *got)

    def second_round(turned):
        return [
            lax.ppermute(turned[step], ("panel", "lat"), lat_route(step, lat_count))
            for step in range(lat_count)
        ]

    planes = [
        jax.ShapeDtypeStruct((fields * tall * pitch, levels), f32),
        jax.ShapeDtypeStruct((13 * tall * pitch, levels), f32),
    ]
    rates = jax.ShapeDtypeStruct((fields, tall, wide, levels), f32)

    turned = first_round(packed)
    got = second_round(turned)
    frame, rate, plane, work = pl.pallas_call(
        lambda *refs: first_inner_kernel(loop, *refs),
        out_shape=[tile_array(tall * wide), rates] + planes,
        in_specs=scalars(1) + whole(3),
        out_specs=whole(4),
        compiler_params=grant(4),
        name="first_inner",
    )(factors, radial, frame, turned[-1])
    frame, rate, _, _, *packed = pl.pallas_call(
        lambda *refs: first_edge_kernel(loop, *refs),
        out_shape=[tile_array(tall * wide), rates] + planes + packed_shapes,
        in_specs=scalars(7) + whole(5 + lat_count),
        out_specs=whole(4 + lon_count),
        scratch_shapes=[pltpu.VMEM((entries * TILE, levels), f32)],
        input_output_aliases={8: 0, 9: 1, 10: 2, 11: 3},
        compiler_params=grant(4),
        name="first_edge",
    )(*rim, receive_table, factors, radial, frame, rate, plane, work, *got)

    turned = first_round(packed)
    got = second_round(turned)
    inner, plane, work = pl.pallas_call(
        lambda *refs: second_inner_kernel(loop, *refs),
        out_shape=[tile_array(rows * cols)] + planes,
        in_specs=scalars(1) + whole(4),
        out_specs=whole(3),
        compiler_params=grant(4),
        name="second_inner",
    )(factors, radial, frame, rate, turned[-1])
    _, _, change = pl.pallas_call(
        lambda *refs: second_edge_kernel(loop, *refs),
        out_shape=planes + [tile_array(rows * cols)],
        in_specs=scalars(2) + whole(5 + lat_count),
        out_specs=whole(3),
        input_output_aliases={5: 0, 6: 1},
        compiler_params=grant(4),
        name="second_edge",
    )(receive_table, factors, radial, rate, inner, plane, work, *got)
    return change.reshape(1, rows, cols, fields, levels)


def solution(mesh):
    return jax.shard_map(
        per_device,
        mesh=mesh,
        in_specs=(
            P("panel", "lat", "lon", None, None),
            P("panel", ("lat", "lon"), None),
            P("panel", ("lat", "lon"), None),
            P("panel", ("lat", "lon")),
            P("panel", None, None),
        ),
        out_specs=P("panel", "lat", "lon", None, None),
        check_vma=False,
    )
```

```python
import math

import jax
import jax.numpy as jnp
import numpy as np
from jax import lax
from jax.experimental import pallas as pl
from jax.experimental.pallas import tpu as pltpu
from jax.sharding import PartitionSpec as P

ETA_COEF = 0.2
NU_COEF = 0.2
KAPPA_COEF = 0.3
SOUND_SQ = 1.0
ARCHIMEDES_LIFT = 0.5
TIME_STEP = 0.2

HALO = 4
PAD = 8
TILE = 8


def is_power_of_two(count):
    return count & (count - 1) == 0


def to_device(index, step, count):
    return index ^ step if is_power_of_two(count) else (index + step) % count


def from_device(index, step, count):
    return index ^ step if is_power_of_two(count) else (index + count - step) % count


def swap_route(parity, lat_count, lon_count, along_lat):
    count, across = (lat_count, lon_count) if along_lat else (lon_count, lat_count)
    mate = list(range(count))
    for low in range(parity, count - 1, 2):
        mate[low], mate[low + 1] = low + 1, low
    route = []
    for side in range(2):
        for lat in range(lat_count):
            for lon in range(lon_count):
                here, other = (lat, lon) if along_lat else (lon, lat)
                there = mate[here]
                if there == here:
                    other = other ^ 1 if other ^ 1 < across else other
                target = (there, other) if along_lat else (other, there)
                route.append(
                    (
                        (side * lat_count + lat) * lon_count + lon,
                        (side * lat_count + target[0]) * lon_count + target[1],
                    )
                )
    return route


def lon_route(step, count):
    return [(i, to_device(i, step, count)) for i in range(count)]


def lat_route(step, count):
    return [
        (side * count + i, (1 - side) * count + to_device(i, step, count))
        for side in range(2)
        for i in range(count)
    ]


class Loop:
    def __init__(self, rows, cols, lat_count, lon_count, entries):
        self.rows, self.cols = rows, cols
        self.lat_count, self.lon_count = lat_count, lon_count
        self.nth, self.nph = rows * lat_count, cols * lon_count
        self.total = 4 * (self.nth + self.nph)
        self.blocks = lat_count * lon_count
        self.entries = entries
        one_row = 2 * (cols + 2 * HALO)
        one_col = 2 * (rows + 2 * HALO)
        corner = 2 * (rows + cols + 2 * HALO)
        self.slots = -(-max(corner, one_row, one_col) // self.blocks)
        self.half = -(-one_row // self.blocks)
        side = 4 * (cols + HALO) + 2 * self.nth
        self.column_slots = max(-(-side // self.blocks), 2 * self.half)

    def position(self, row, col):
        nth, nph = self.nth, self.nph
        top = 2 * col + row + 2
        right = 2 * nph + 2 * row + col - nph
        bottom = 2 * nph + 2 * nth + 2 * (nph - 1 - col) + row - nth
        left = 4 * nph + 2 * nth + 2 * (nth - 1 - row) + col + 2
        return jnp.where(
            row < 0, top, jnp.where(row >= nth, bottom, jnp.where(col >= nph, right, left))
        )

    def cell(self, place):
        nth, nph = self.nth, self.nph
        right = place - 2 * nph
        bottom = right - 2 * nth
        left = bottom - 2 * nph
        on_top, on_right, on_bottom = right < 0, bottom < 0, left < 0
        row = jnp.where(
            on_top,
            (place & 1) - 2,
            jnp.where(
                on_right,
                right >> 1,
                jnp.where(on_bottom, nth + (bottom & 1), nth - 1 - (left >> 1)),
            ),
        )
        col = jnp.where(
            on_top,
            place >> 1,
            jnp.where(
                on_right,
                nph + (right & 1),
                jnp.where(on_bottom, nph - 1 - (bottom >> 1), (left & 1) - 2),
            ),
        )
        return row, col

    def top_start(self, lon):
        return 2 * jnp.maximum(lon * self.cols - HALO, 0)

    def bottom_start(self, lon):
        high = jnp.minimum(lon * self.cols + self.cols + HALO, self.nph)
        return 2 * self.nph + 2 * self.nth + 2 * (self.nph - high)

    def stretch(self, lat, lon):
        nth, nph = self.nth, self.nph
        row_low = jnp.maximum(lat * self.rows - HALO, 0)
        row_high = jnp.minimum(lat * self.rows + self.rows + HALO, nth)
        col_low = jnp.maximum(lon * self.cols - HALO, 0)
        col_high = jnp.minimum(lon * self.cols + self.cols + HALO, nph)
        top, bottom = lat == 0, lat == self.lat_count - 1
        left, right = lon == 0, lon == self.lon_count - 1
        left_start = 4 * nph + 2 * nth + 2 * (nth - row_high)
        start = jnp.where(
            top & left,
            left_start,
            jnp.where(
                top,
                self.top_start(lon),
                jnp.where(
                    right,
                    2 * nph + 2 * row_low,
                    jnp.where(bottom, self.bottom_start(lon), left_start),
                ),
            ),
        )
        span = jnp.where(top | bottom, 2 * (col_high - col_low), 0) + jnp.where(
            left | right, 2 * (row_high - row_low), 0
        )
        return start, span

    def first_entry(self, start, donor, offset):
        lead = -(-2 * self.total // self.blocks)
        raised = start - donor - offset + lead * self.blocks + self.blocks - 1
        if is_power_of_two(self.blocks):
            return (raised >> (self.blocks.bit_length() - 1)) - lead
        return lax.div(raised, jnp.full_like(raised, self.blocks)) - lead

    def wrap(self, entry):
        for bound in (8, 4, 2, 1):
            entry = jnp.where(entry < 0, entry + self.entries * bound, entry)
        for bound in (8, 4, 2, 1):
            over = entry - self.entries * bound
            entry = jnp.where(over >= 0, over, entry)
        return entry

    def column_entry(self, lon, donor, offset, slot):
        side = (lon == 0) | (lon == self.lon_count - 1)
        top = self.first_entry(self.top_start(lon), donor, offset)
        bottom = self.first_entry(self.bottom_start(lon), donor, offset)
        lower = (lon == 0) | jnp.logical_not(side) & (slot >= self.half)
        skipped = jnp.where(jnp.logical_not(side) & (slot >= self.half), self.half, 0)
        return jnp.where(lower, bottom, top) + slot - skipped

    def column_slot(self, lat, lon, donor, offset):
        side = (lon == 0) | (lon == self.lon_count - 1)
        start, _ = self.stretch(lat, lon)
        ahead = self.first_entry(start, donor, offset) - self.first_entry(
            jnp.where(lon == 0, self.bottom_start(lon), self.top_start(lon)), donor, offset
        )
        middle = jnp.where(lat == self.lat_count - 1, self.half, 0)
        return jnp.where(side, jnp.maximum(ahead, 0), middle)


def padded_rows(count):
    return -(-count // 1024) * 8


def table_ids(outer, inner, slots):
    rows = padded_rows(outer * inner * slots)
    flat = np.minimum(np.arange(rows * 128), outer * inner * slots - 1)
    return np.stack(
        [flat // (inner * slots), flat // slots % inner, flat % slots]
    ).reshape(3, rows, 128).astype(np.int32)


def whole(count):
    return [pl.BlockSpec(memory_space=pltpu.VMEM)] * count


def scalars(count):
    return [pl.BlockSpec(memory_space=pltpu.SMEM)] * count


def lookup(table_ref, index):
    return table_ref[index // 128, index % 128]


def grant(mebibytes):
    return pltpu.CompilerParams(vmem_limit_bytes=mebibytes << 20)


def tiles(index, count):
    if isinstance(index, int):
        return pl.ds(index * TILE, count * TILE)
    return pl.ds(pl.multiple_of(index * TILE, TILE), count * TILE)


def table_kernel(
    loop, pitch, cell_ref, other_ref, send_id_ref, swap_id_ref, got_id_ref,
    base_ref, weight_ref, turn_ref, send_ref, swap_ref, receive_ref, corner_ref, spread_ref,
):
    entries = loop.entries
    diagonal = lax.broadcasted_iota(jnp.int32, (entries, entries), 0) == (
        lax.broadcasted_iota(jnp.int32, (entries, entries), 1)
    )
    for number in range(18):
        ref, row = (weight_ref, number) if number < 16 else (turn_ref, number - 16)
        column = jnp.sum(
            jnp.where(diagonal, ref[row : row + 1, :], 0.0), axis=1, keepdims=True
        )
        spread_ref[pl.ds(number * entries, entries), :] = jnp.broadcast_to(
            column, (entries, spread_ref.shape[1])
        )

    lat, lon = lax.axis_index("lat"), lax.axis_index("lon")
    lat_count, lon_count = loop.lat_count, loop.lon_count
    wide = loop.cols + 2 * HALO
    base = (base_ref[0:1, :] - lat * loop.rows + HALO - 1) * wide + (
        base_ref[1:2, :] - lon * loop.cols + HALO - 1
    )
    corner_ref[0:1, 0:entries] = base
    mine = loop.position(cell_ref[0], cell_ref[1])
    other = loop.position(other_ref[0], other_ref[1])

    step, _, slot = [send_id_ref[n] for n in range(3)]
    entry = loop.column_entry(
        to_device(lon, step, lon_count), lat * lon_count + lon, other, slot
    )
    send_ref[...] = loop.wrap(entry)

    lat_step, lon_step, slot = [swap_id_ref[n] for n in range(3)]
    donor = lat * lon_count + from_device(lon, lon_step, lon_count)
    here = jnp.full_like(slot, lon)
    ahead = loop.column_slot(to_device(lat, lat_step, lat_count), here, donor, other)
    swap_ref[...] = jnp.minimum(ahead + slot, loop.column_slots - 1)

    lat_step, lon_step, slot = [got_id_ref[n] for n in range(3)]
    donor = from_device(lat, lat_step, lat_count) * lon_count + from_device(
        lon, lon_step, lon_count
    )
    start, span = loop.stretch(jnp.full_like(slot, lat), jnp.full_like(slot, lon))
    entry = loop.first_entry(start, donor, mine) + slot
    place = entry * loop.blocks + donor + mine
    wrapped = jnp.where(place >= loop.total, place - loop.total, place)
    row, col = loop.cell(wrapped)
    spot = (row - lat * loop.rows + HALO) * pitch + PAD + (col - lon * loop.cols + HALO)
    receive_ref[...] = jnp.where(place < start + span, spot, 0)


def strip_kernel(rows, cols, own_even_ref, own_odd_ref, even_ref, odd_ref, *send_refs):
    lat_even = lax.rem(lax.axis_index("lat"), 2) == 0
    lon_even = lax.rem(lax.axis_index("lon"), 2) == 0
    high = cols - HALO
    lows = (jnp.where(lon_even, high, 0), jnp.where(lon_even, 0, high))

    def copy_halo(first, source):
        for send_ref, low in zip(send_refs, lows):
            for row in range(HALO):
                send_ref[tiles((first + row) * HALO, HALO), :] = source[
                    tiles(row * cols + low, HALO), :
                ]

    for send_ref, own_ref in zip(send_refs, (own_even_ref, own_odd_ref)):
        send_ref[tiles(HALO * HALO, rows * HALO), :] = own_ref[...]

    @pl.when(lat_even)
    def _():
        copy_halo(0, odd_ref)
        copy_halo(HALO + rows, even_ref)

    @pl.when(jnp.logical_not(lat_even))
    def _():
        copy_halo(0, even_ref)
        copy_halo(HALO + rows, odd_ref)


def mix_and_pack(loop, wide, rim, frame_ref, value_ref, send_refs):
    send_table_ref, corner_ref, spread_ref = rim
    entries = loop.entries
    field = lax.broadcasted_iota(jnp.int32, (TILE, 128), 0)
    takes_next = (field == 1) | (field == 4)
    turned = takes_next | (field == 2) | (field == 5)

    def one_entry(entry, carry):
        base = corner_ref[0, entry]

        def over_tile(number):
            return spread_ref[pl.ds(number * entries + entry, TILE, stride=0), :]

        total = None
        for a in range(4):
            for b in range(4):
                part = over_tile(4 * a + b) * frame_ref[tiles(base + a * wide + b, 1), :]
                total = part if total is None else total + part
        cosine, sine = over_tile(16), over_tile(17)
        other = jnp.where(
            takes_next, pltpu.roll(total, TILE - 1, 0), pltpu.roll(total, 1, 0)
        )
        mixed = cosine * total + jnp.where(takes_next, -sine, sine) * other
        value_ref[tiles(entry, 1), :] = jnp.where(turned, mixed, total)
        return carry

    lax.fori_loop(0, loop.entries, one_entry, 0, unroll=4)
    for step, send_ref in enumerate(send_refs):
        for slot in range(loop.column_slots):
            entry = lookup(send_table_ref, step * loop.column_slots + slot)
            send_ref[tiles(slot, 1), :] = value_ref[tiles(entry, 1), :]


def frame_kernel(loop, *refs):
    rim, refs = refs[:3], refs[3:]
    state_ref, lat_even_ref, lat_odd_ref, lon_even_ref, lon_odd_ref, frame_ref = refs[:6]
    send_refs, value_ref = refs[6:-1], refs[-1]
    rows, cols = loop.rows, loop.cols
    wide = cols + 2 * HALO
    lat_even = lax.rem(lax.axis_index("lat"), 2) == 0
    lon_even = lax.rem(lax.axis_index("lon"), 2) == 0

    def copy_rows(first, count, source, left, width):
        for row in range(count):
            frame_ref[tiles((first + row) * wide + left, width), :] = source[
                tiles(row * width, width), :
            ]

    copy_rows(HALO, rows, state_ref, HALO, cols)

    @pl.when(lat_even)
    def _():
        copy_rows(0, HALO, lat_odd_ref, HALO, cols)
        copy_rows(HALO + rows, HALO, lat_even_ref, HALO, cols)

    @pl.when(jnp.logical_not(lat_even))
    def _():
        copy_rows(0, HALO, lat_even_ref, HALO, cols)
        copy_rows(HALO + rows, HALO, lat_odd_ref, HALO, cols)

    @pl.when(lon_even)
    def _():
        copy_rows(0, rows + 2 * HALO, lon_odd_ref, 0, HALO)
        copy_rows(0, rows + 2 * HALO, lon_even_ref, HALO + cols, HALO)

    @pl.when(jnp.logical_not(lon_even))
    def _():
        copy_rows(0, rows + 2 * HALO, lon_even_ref, 0, HALO)
        copy_rows(0, rows + 2 * HALO, lon_odd_ref, HALO + cols, HALO)

    lat, lon = lax.axis_index("lat"), lax.axis_index("lon")
    zeros = jnp.zeros((HALO * TILE, frame_ref.shape[1]), jnp.float32)
    for at_row, top in ((lat == 0, 0), (lat == loop.lat_count - 1, HALO + rows)):
        for at_col, left in ((lon == 0, 0), (lon == loop.lon_count - 1, HALO + cols)):

            @pl.when(at_row & at_col)
            def _():
                for row in range(HALO):
                    frame_ref[tiles((top + row) * wide + left, HALO), :] = zeros

    mix_and_pack(loop, wide, rim, frame_ref, value_ref, send_refs)


def swap_kernel(loop, table_ref, *refs):
    got_refs, out_refs = refs[: loop.lon_count], refs[loop.lon_count :]
    for lat_step in range(loop.lat_count):
        for lon_step in range(loop.lon_count):
            for slot in range(loop.slots):
                place = lon_step * loop.slots + slot
                source = lookup(table_ref, lat_step * loop.lon_count * loop.slots + place)
                out_refs[lat_step][tiles(place, 1), :] = got_refs[lon_step][tiles(source, 1), :]


class Section:
    def __init__(self, loop, factor_ref, radial_ref, plane_ref, work_ref):
        self.loop = loop
        self.tall, self.wide = loop.rows + 2 * HALO, loop.cols + 2 * HALO
        self.pitch = self.wide + 2 * PAD
        self.factor_ref, self.radial_ref = factor_ref, radial_ref
        self.plane_ref, self.work_ref = plane_ref, work_ref
        lat, lon = lax.axis_index("lat"), lax.axis_index("lon")
        self.lat = lat
        self.at_top, self.at_left = lat == 0, lon == 0
        self.on_row_edge = self.at_top | (lat == loop.lat_count - 1)
        self.on_col_edge = self.at_left | (lon == loop.lon_count - 1)

    def spread(self, frame_ref, rows):
        def one_row(row, carry):
            for chunk in range(0, self.wide, 8):
                for f in range(TILE):
                    start = (row * self.wide + chunk) * TILE + f
                    self.plane_ref[self.at(f, row, chunk), :] = frame_ref[
                        pl.ds(start, 8, stride=TILE), :
                    ]
            return carry

        lax.fori_loop(*rows, one_row, 0)

    def scatter(self, receive_ref, got_refs):
        arrivals = self.loop.lon_count * self.loop.slots
        for lat_step in range(self.loop.lat_count):
            for place in range(arrivals):
                spot = lookup(receive_ref, lat_step * arrivals + place)
                self.plane_ref[pl.ds(spot, TILE, stride=self.tall * self.pitch), :] = got_refs[
                    lat_step
                ][tiles(place, 1), :]

    def at(self, number, row, col):
        return pl.ds((number * self.tall + row) * self.pitch + PAD + col, 8)

    def reader(self, ref, row, col):
        def read(number, row_step=0, col_step=0):
            return ref[self.at(number, row + row_step, col + col_step), :]

        return read

    def prepare(self, row):
        factors = [self.factor_ref[(self.lat * 3 + n) * self.tall + row] for n in range(3)]
        inverse_radius = self.radial_ref[0]
        with_theta = inverse_radius * (self.loop.nth / math.pi)
        return factors, inverse_radius * factors[2], with_theta

    def up(self, x):
        return pltpu.roll(x, x.shape[-1] - 1, 1)

    def down(self, x):
        return pltpu.roll(x, 1, 1)

    def curl(self, read, first, prepared):
        (tu, td, ph), with_phi, with_theta = prepared
        ru, rl = self.radial_ref[1], self.radial_ref[2]
        a, b, c = first, first + 1, first + 2
        mid_b, mid_c = read(b), read(c)
        radial = self.radial_ref[0] * (
            (tu * read(c, 1) - td * read(c, -1)) - ph * (read(b, 0, 1) - read(b, 0, -1))
        )
        polar = with_phi * (read(a, 0, 1) - read(a, 0, -1)) - (
            ru * self.up(mid_c) - rl * self.down(mid_c)
        )
        azimuth = (ru * self.up(mid_b) - rl * self.down(mid_b)) - with_theta * (
            read(a, 1) - read(a, -1)
        )
        return radial, polar, azimuth

    def slope(self, read, number, prepared):
        _, with_phi, with_theta = prepared
        mid = read(number)
        return (
            self.radial_ref[3] * self.up(mid) - self.radial_ref[4] * self.down(mid),
            with_theta * (read(number, 1) - read(number, -1)),
            with_phi * (read(number, 0, 1) - read(number, 0, -1)),
        )

    def outflow(self, read, first, prepared):
        (tu, td, ph), _, _ = prepared
        mid = read(first)
        return (
            self.radial_ref[5] * self.up(mid) - self.radial_ref[6] * self.down(mid)
        ) + self.radial_ref[0] * (
            (tu * read(first + 1, 1) - td * read(first + 1, -1))
            + ph * (read(first + 2, 0, 1) - read(first + 2, 0, -1))
        )

    def first_pass(self, row, chunk):
        prepared = self.prepare(row)
        read = self.reader(self.plane_ref, row, chunk)

        def put(number, value):
            self.work_ref[self.at(number, row, chunk), :] = value

        flow = [read(n) for n in range(3)]
        field = [read(n) for n in range(3, 6)]
        current = self.curl(read, 3, prepared)
        spin = self.curl(read, 0, prepared)
        induced = cross(flow, field)
        warm = self.slope(read, 6, prepared)
        for n in range(3):
            put(n, current[n])
            put(3 + n, spin[n])
            put(6 + n, induced[n] - ETA_COEF * current[n])
            put(9 + n, warm[n])
        put(12, read(7) + 0.5 * dot(flow, flow))

    def second_pass(self, row, chunk, emit):
        prepared = self.prepare(row)
        read = self.reader(self.plane_ref, row, chunk)
        work = self.reader(self.work_ref, row, chunk)
        flow = [read(n) for n in range(3)]
        field = [read(n) for n in range(3, 6)]
        current = [work(n) for n in range(3)]
        spin = [work(3 + n) for n in range(3)]
        warm = [work(9 + n) for n in range(3)]
        field_rate = self.curl(work, 6, prepared)
        spin_curl = self.curl(work, 3, prepared)
        head = self.slope(work, 12, prepared)
        lorentz = cross(current, field)
        advect = cross(flow, spin)
        speed = [advect[n] + lorentz[n] - head[n] - NU_COEF * spin_curl[n] for n in range(3)]
        speed[0] = speed[0] + ARCHIMEDES_LIFT * read(6)
        heat = KAPPA_COEF * self.outflow(work, 9, prepared) - dot(flow, warm)
        squeeze = -SOUND_SQ * self.outflow(read, 0, prepared)
        emit(row, chunk, read, speed + list(field_rate) + [heat, squeeze])

    def over(self, rows, one_row, unroll):
        def step(row, carry):
            one_row(row)
            return carry

        lax.fori_loop(*rows, step, 0, unroll=unroll)

    def everywhere(self, rows, chunks, emit):
        def first(row):
            for chunk in range(0, self.wide, 8):
                self.first_pass(row, chunk)

        def second(row):
            for chunk in chunks:
                self.second_pass(row, chunk, emit)

        self.over((rows[0] - 1, rows[1] + 1), first, 2)
        self.over(rows, second, 2)

    def along_edges(self, rows, chunks, emit):
        tall, wide = self.tall, self.wide
        low_chunk, high_chunk = chunks[0], chunks[-1]

        @pl.when(self.on_row_edge)
        def _():
            row = jnp.where(self.at_top, HALO - 1, tall - HALO - 1)
            for step in range(2):
                for chunk in range(0, wide, 8):
                    self.first_pass(row + step, chunk)

        @pl.when(self.on_col_edge)
        def _():
            chunk = pl.multiple_of(jnp.where(self.at_left, 0, wide - 8), 8)
            count = rows[1] - rows[0]
            self.over(
                (rows[0] - 1, rows[1] + 1), lambda row: self.first_pass(row, chunk), count // 2 + 1
            )

        @pl.when(self.on_row_edge)
        def _():
            row = jnp.where(self.at_top, HALO, tall - HALO - 2)
            for step in range(2):
                for chunk in chunks:
                    self.second_pass(row + step, chunk, emit)

        @pl.when(self.on_col_edge)
        def _():
            chunk = jnp.where(self.at_left, low_chunk, high_chunk)
            count = rows[1] - rows[0]
            self.over(rows, lambda row: self.second_pass(row, chunk, emit), count // 2)


def cross(x, y):
    return (
        x[1] * y[2] - x[2] * y[1],
        x[2] * y[0] - x[0] * y[2],
        x[0] * y[1] - x[1] * y[0],
    )


def dot(x, y):
    return x[0] * y[0] + x[1] * y[1] + x[2] * y[2]


def middle_state(loop, frame_ref, rate_ref):
    wide = loop.cols + 2 * HALO
    first_row = lax.axis_index("lat") * loop.rows - HALO
    first_col = lax.axis_index("lon") * loop.cols - HALO

    def emit(row, chunk, read, rate):
        in_row = (row + first_row >= 0) & (row + first_row < loop.nth)
        col = lax.broadcasted_iota(jnp.int32, (8, 128), 0) + (chunk + first_col)
        inside = (col >= jnp.where(in_row, 0, loop.nph)) & (col < loop.nph)
        for f in range(TILE):
            rate_ref[f, row, pl.ds(chunk, 8), :] = rate[f]
            start = (row * wide + chunk) * TILE + f
            frame_ref[pl.ds(start, 8, stride=TILE), :] = jnp.where(
                inside, read(f) + TIME_STEP * rate[f], 0.0
            )

    return emit


def total_change(loop, change_ref, rate_ref):
    def emit(row, chunk, read, rate):
        for f in range(TILE):
            start = ((row - HALO) * loop.cols + chunk - HALO) * TILE + f
            change_ref[pl.ds(start, 8, stride=TILE), :] = (0.5 * TIME_STEP) * (
                rate_ref[f, row, pl.ds(chunk, 8), :] + rate[f]
            )

    return emit


def first_inner_kernel(
    loop, factor_ref, radial_ref, frame_in_ref, after_ref, frame_ref, rate_ref, plane_ref, work_ref
):
    del after_ref
    part = Section(loop, factor_ref, radial_ref, plane_ref, work_ref)
    part.spread(frame_in_ref, (0, part.tall))
    part.everywhere(
        (2, part.tall - 2), range(0, part.wide, 8), middle_state(loop, frame_ref, rate_ref)
    )


def first_edge_kernel(loop, *refs):
    rim, refs = refs[:3], refs[3:]
    receive_ref, factor_ref, radial_ref = refs[:3]
    got_refs, refs = refs[7 : 7 + loop.lat_count], refs[7 + loop.lat_count :]
    frame_ref, rate_ref, plane_ref, work_ref = refs[:4]
    send_refs, value_ref = refs[4:-1], refs[-1]
    part = Section(loop, factor_ref, radial_ref, plane_ref, work_ref)
    part.scatter(receive_ref, got_refs)
    part.along_edges(
        (2, part.tall - 2), range(0, part.wide, 8), middle_state(loop, frame_ref, rate_ref)
    )
    mix_and_pack(loop, part.wide, rim, frame_ref, value_ref, send_refs)


def second_inner_kernel(
    loop, factor_ref, radial_ref, frame_ref, rate_ref, after_ref, change_ref, plane_ref, work_ref
):
    del after_ref
    part = Section(loop, factor_ref, radial_ref, plane_ref, work_ref)
    part.spread(frame_ref, (2, part.tall - 2))
    part.everywhere(
        (HALO, HALO + loop.rows),
        range(HALO, HALO + loop.cols, 8),
        total_change(loop, change_ref, rate_ref),
    )


def second_edge_kernel(loop, receive_ref, factor_ref, radial_ref, rate_ref, inner_ref, *refs):
    got_refs, refs = refs[2 : 2 + loop.lat_count], refs[2 + loop.lat_count :]
    plane_ref, work_ref, change_ref = refs
    part = Section(loop, factor_ref, radial_ref, plane_ref, work_ref)
    for row in range(loop.rows):
        here = tiles(row * loop.cols, loop.cols)
        change_ref[here, :] = inner_ref[here, :]
    part.scatter(receive_ref, got_refs)
    part.along_edges(
        (HALO, HALO + loop.rows),
        range(HALO, HALO + loop.cols, 8),
        total_change(loop, change_ref, rate_ref),
    )


def radial_factors(levels, theta_count):
    scale = 2.0 * theta_count / math.pi
    step = 0.65 * scale / levels
    radius = 0.35 * scale + (np.arange(levels) + 0.5) * step
    half = 0.5 / step
    above = np.append(radius[1:], 0.0)
    below = np.append(0.0, radius[:-1])
    ones_above = np.append(np.ones(levels - 1), 0.0)
    ones_below = np.append(0.0, np.ones(levels - 1))
    rows = np.stack(
        [
            1.0 / radius,
            half * above / radius,
            half * below / radius,
            half * ones_above,
            half * ones_below,
            half * above**2 / radius**2,
            half * below**2 / radius**2,
        ]
    )
    return np.repeat(rows[:, None, :], 8, axis=1).astype(np.float32)


def row_factors(rows, lat_count, nth, nph):
    polar_step, azimuth_step = math.pi / (2 * nth), 1.5 * math.pi / nph
    tall = rows + 2 * HALO
    parts = []
    for lat in range(lat_count):
        row = lat * rows - HALO - 1 + np.arange(tall + 2)
        sines = np.sin(math.pi / 4 + (row + 0.5) * polar_step)
        middle = sines[1:-1]
        parts += [
            sines[2:] / middle * (0.5 / polar_step),
            sines[:-2] / middle * (0.5 / polar_step),
            (0.5 / azimuth_step) / middle,
        ]
    return np.concatenate(parts).astype(np.float32)


def per_device(state, rim_base, rim_weight, rim_angle, rim_target):
    _, rows, cols, fields, levels = state.shape
    lat_count, lon_count = lax.axis_size("lat"), lax.axis_size("lon")
    entries = rim_base.shape[1]
    loop = Loop(rows, cols, lat_count, lon_count, entries)
    tall, wide = rows + 2 * HALO, cols + 2 * HALO
    pitch = wide + 2 * PAD
    block = state[0].reshape(rows * cols * fields, levels)
    f32 = jnp.float32

    def tile_array(count):
        return jax.ShapeDtypeStruct((count * TILE, levels), f32)

    first_cell = rim_target[0, 0]
    other_cell = lax.ppermute(first_cell, "panel", [(0, 1), (1, 0)])

    everyone = ("panel", "lat", "lon")
    cells = state[0]
    last_first = lax.axis_index("lat") % 2 == 0
    head, tail = cells[:HALO], cells[rows - HALO :]
    send_even = jnp.where(last_first, tail, head).reshape(HALO * cols * fields, levels)
    send_odd = jnp.where(last_first, head, tail).reshape(HALO * cols * fields, levels)
    lat_even = lax.ppermute(send_even, everyone, swap_route(0, lat_count, lon_count, True))
    lat_odd = lax.ppermute(send_odd, everyone, swap_route(1, lat_count, lon_count, True))

    send_ids = table_ids(1, lon_count, loop.column_slots)[[1, 0, 2]]
    got_ids = table_ids(lat_count, lon_count, loop.slots)
    angle = rim_angle[0]
    turn = jnp.stack([jnp.cos(angle), jnp.sin(angle)])
    send_table, swap_table, receive_table, corner_table, spread_weights = pl.pallas_call(
        lambda *refs: table_kernel(loop, pitch, *refs),
        out_shape=[
            jax.ShapeDtypeStruct(ids.shape[1:], jnp.int32) for ids in (send_ids, got_ids, got_ids)
        ]
        + [
            jax.ShapeDtypeStruct((8, -(-entries // 128) * 128), jnp.int32),
            jax.ShapeDtypeStruct((18 * entries + TILE, levels), f32),
        ],
        in_specs=scalars(2) + whole(6),
        out_specs=whole(5),
        compiler_params=grant(4),
        name="tables",
    )(
        first_cell,
        other_cell,
        jnp.asarray(send_ids),
        jnp.asarray(got_ids),
        jnp.asarray(got_ids),
        rim_base[0].T,
        rim_weight[0].T,
        turn,
    )
    rim = (send_table, corner_table, spread_weights)
    factors = jnp.asarray(row_factors(rows, lat_count, loop.nth, loop.nph))
    radial = jnp.asarray(radial_factors(levels, loop.nth))

    east_first = lax.axis_index("lon") % 2 == 0
    head, tail = cells[:, :HALO], cells[:, cols - HALO :]
    own_even = jnp.where(east_first, tail, head).reshape(rows * HALO * fields, levels)
    own_odd = jnp.where(east_first, head, tail).reshape(rows * HALO * fields, levels)
    strip_even, strip_odd = pl.pallas_call(
        lambda *refs: strip_kernel(rows, cols, *refs),
        out_shape=[tile_array(tall * HALO)] * 2,
        in_specs=whole(4),
        out_specs=whole(2),
        compiler_params=grant(4),
        name="strips",
    )(own_even, own_odd, lat_even, lat_odd)
    lon_even = lax.ppermute(strip_even, everyone, swap_route(0, lat_count, lon_count, False))
    lon_odd = lax.ppermute(strip_odd, everyone, swap_route(1, lat_count, lon_count, False))

    packed_shapes = [tile_array(loop.column_slots)] * lon_count
    frame, *packed = pl.pallas_call(
        lambda *refs: frame_kernel(loop, *refs),
        out_shape=[tile_array(tall * wide)] + packed_shapes,
        in_specs=scalars(2) + whole(6),
        out_specs=whole(1 + lon_count),
        scratch_shapes=[pltpu.VMEM((entries * TILE, levels), f32)],
        compiler_params=grant(8),
        name="frame",
    )(*rim, block, lat_even, lat_odd, lon_even, lon_odd)

    def first_round(packed):
        got = [packed[0]] + [
            lax.ppermute(packed[step], "lon", lon_route(step, lon_count))
            for step in range(1, lon_count)
        ]
        return pl.pallas_call(
            lambda *refs: swap_kernel(loop, *refs),
            out_shape=[tile_array(lon_count * loop.slots)] * lat_count,
            in_specs=scalars(1) + whole(lon_count),
            out_specs=whole(lat_count),
            compiler_params=grant(4),
            name="swap",
        )(swap_table, *got)

    def second_round(turned):
        return [
            lax.ppermute(turned[step], ("panel", "lat"), lat_route(step, lat_count))
            for step in range(lat_count)
        ]

    planes = [
        jax.ShapeDtypeStruct((fields * tall * pitch, levels), f32),
        jax.ShapeDtypeStruct((13 * tall * pitch, levels), f32),
    ]
    rates = jax.ShapeDtypeStruct((fields, tall, wide, levels), f32)

    turned = first_round(packed)
    got = second_round(turned)
    frame, rate, plane, work = pl.pallas_call(
        lambda *refs: first_inner_kernel(loop, *refs),
        out_shape=[tile_array(tall * wide), rates] + planes,
        in_specs=scalars(1) + whole(3),
        out_specs=whole(4),
        compiler_params=grant(4),
        name="first_inner",
    )(factors, radial, frame, turned[-1])
    frame, rate, _, _, *packed = pl.pallas_call(
        lambda *refs: first_edge_kernel(loop, *refs),
        out_shape=[tile_array(tall * wide), rates] + planes + packed_shapes,
        in_specs=scalars(2) + whole(1) + scalars(2) + whole(5 + lat_count),
        out_specs=whole(4 + lon_count),
        scratch_shapes=[pltpu.VMEM((entries * TILE, levels), f32)],
        input_output_aliases={6: 0, 7: 1, 8: 2, 9: 3},
        compiler_params=grant(4),
        name="first_edge",
    )(*rim, receive_table, factors, radial, frame, rate, plane, work, *got)

    turned = first_round(packed)
    got = second_round(turned)
    inner, plane, work = pl.pallas_call(
        lambda *refs: second_inner_kernel(loop, *refs),
        out_shape=[tile_array(rows * cols)] + planes,
        in_specs=scalars(1) + whole(4),
        out_specs=whole(3),
        compiler_params=grant(4),
        name="second_inner",
    )(factors, radial, frame, rate, turned[-1])
    _, _, change = pl.pallas_call(
        lambda *refs: second_edge_kernel(loop, *refs),
        out_shape=planes + [tile_array(rows * cols)],
        in_specs=scalars(2) + whole(5 + lat_count),
        out_specs=whole(3),
        input_output_aliases={5: 0, 6: 1},
        compiler_params=grant(4),
        name="second_edge",
    )(receive_table, factors, radial, rate, inner, plane, work, *got)
    return change.reshape(1, rows, cols, fields, levels)


def solution(mesh):
    return jax.shard_map(
        per_device,
        mesh=mesh,
        in_specs=(
            P("panel", "lat", "lon", None, None),
            P("panel", ("lat", "lon"), None),
            P("panel", ("lat", "lon"), None),
            P("panel", ("lat", "lon")),
            P("panel", None, None),
        ),
        out_specs=P("panel", "lat", "lon", None, None),
        check_vma=False,
    )
```

```python
import math

import jax
import jax.numpy as jnp
import numpy as np
from jax import lax
from jax.experimental import pallas as pl
from jax.experimental.pallas import tpu as pltpu
from jax.sharding import PartitionSpec as P

ETA_COEF = 0.2
NU_COEF = 0.2
KAPPA_COEF = 0.3
SOUND_SQ = 1.0
ARCHIMEDES_LIFT = 0.5
TIME_STEP = 0.2

HALO = 4
PAD = 8
TILE = 8


def hardest_first(step):
    return -step.bit_length(), step


def start_order(first, count):
    return sorted(range(first, count), key=hardest_first)


def by_step(first, refs):
    order = start_order(first, first + len(refs))
    return [refs[order.index(step)] for step in range(first, first + len(refs))]


def is_power_of_two(count):
    return count & (count - 1) == 0


def to_device(index, step, count):
    return index ^ step if is_power_of_two(count) else (index + step) % count


def from_device(index, step, count):
    return index ^ step if is_power_of_two(count) else (index + count - step) % count


def swap_route(parity, lat_count, lon_count, along_lat):
    count, across = (lat_count, lon_count) if along_lat else (lon_count, lat_count)
    mate = list(range(count))
    for low in range(parity, count - 1, 2):
        mate[low], mate[low + 1] = low + 1, low
    route = []
    for side in range(2):
        for lat in range(lat_count):
            for lon in range(lon_count):
                here, other = (lat, lon) if along_lat else (lon, lat)
                there = mate[here]
                if there == here:
                    other = other ^ 1 if other ^ 1 < across else other
                target = (there, other) if along_lat else (other, there)
                route.append(
                    (
                        (side * lat_count + lat) * lon_count + lon,
                        (side * lat_count + target[0]) * lon_count + target[1],
                    )
                )
    return route


def lon_route(step, count):
    return [(i, to_device(i, step, count)) for i in range(count)]


def lat_route(step, count):
    return [
        (side * count + i, (1 - side) * count + to_device(i, step, count))
        for side in range(2)
        for i in range(count)
    ]


class Loop:
    def __init__(self, rows, cols, lat_count, lon_count, entries):
        self.rows, self.cols = rows, cols
        self.lat_count, self.lon_count = lat_count, lon_count
        self.nth, self.nph = rows * lat_count, cols * lon_count
        self.total = 4 * (self.nth + self.nph)
        self.blocks = lat_count * lon_count
        self.entries = entries
        one_row = 2 * (cols + 2 * HALO)
        one_col = 2 * (rows + 2 * HALO)
        corner = 2 * (rows + cols + 2 * HALO)
        self.slots = -(-max(corner, one_row, one_col) // self.blocks)
        self.half = -(-one_row // self.blocks)
        side = 4 * (cols + HALO) + 2 * self.nth
        self.column_slots = max(-(-side // self.blocks), 2 * self.half)

    def position(self, row, col):
        nth, nph = self.nth, self.nph
        top = 2 * col + row + 2
        right = 2 * nph + 2 * row + col - nph
        bottom = 2 * nph + 2 * nth + 2 * (nph - 1 - col) + row - nth
        left = 4 * nph + 2 * nth + 2 * (nth - 1 - row) + col + 2
        return jnp.where(
            row < 0, top, jnp.where(row >= nth, bottom, jnp.where(col >= nph, right, left))
        )

    def cell(self, place):
        nth, nph = self.nth, self.nph
        right = place - 2 * nph
        bottom = right - 2 * nth
        left = bottom - 2 * nph
        on_top, on_right, on_bottom = right < 0, bottom < 0, left < 0
        row = jnp.where(
            on_top,
            (place & 1) - 2,
            jnp.where(
                on_right,
                right >> 1,
                jnp.where(on_bottom, nth + (bottom & 1), nth - 1 - (left >> 1)),
            ),
        )
        col = jnp.where(
            on_top,
            place >> 1,
            jnp.where(
                on_right,
                nph + (right & 1),
                jnp.where(on_bottom, nph - 1 - (bottom >> 1), (left & 1) - 2),
            ),
        )
        return row, col

    def top_start(self, lon):
        return 2 * jnp.maximum(lon * self.cols - HALO, 0)

    def bottom_start(self, lon):
        high = jnp.minimum(lon * self.cols + self.cols + HALO, self.nph)
        return 2 * self.nph + 2 * self.nth + 2 * (self.nph - high)

    def stretch(self, lat, lon):
        nth, nph = self.nth, self.nph
        row_low = jnp.maximum(lat * self.rows - HALO, 0)
        row_high = jnp.minimum(lat * self.rows + self.rows + HALO, nth)
        col_low = jnp.maximum(lon * self.cols - HALO, 0)
        col_high = jnp.minimum(lon * self.cols + self.cols + HALO, nph)
        top, bottom = lat == 0, lat == self.lat_count - 1
        left, right = lon == 0, lon == self.lon_count - 1
        left_start = 4 * nph + 2 * nth + 2 * (nth - row_high)
        start = jnp.where(
            top & left,
            left_start,
            jnp.where(
                top,
                self.top_start(lon),
                jnp.where(
                    right,
                    2 * nph + 2 * row_low,
                    jnp.where(bottom, self.bottom_start(lon), left_start),
                ),
            ),
        )
        span = jnp.where(top | bottom, 2 * (col_high - col_low), 0) + jnp.where(
            left | right, 2 * (row_high - row_low), 0
        )
        return start, span

    def first_entry(self, start, donor, offset):
        lead = -(-2 * self.total // self.blocks)
        raised = start - donor - offset + lead * self.blocks + self.blocks - 1
        if is_power_of_two(self.blocks):
            return (raised >> (self.blocks.bit_length() - 1)) - lead
        return lax.div(raised, jnp.full_like(raised, self.blocks)) - lead

    def wrap(self, entry):
        for bound in (8, 4, 2, 1):
            entry = jnp.where(entry < 0, entry + self.entries * bound, entry)
        for bound in (8, 4, 2, 1):
            over = entry - self.entries * bound
            entry = jnp.where(over >= 0, over, entry)
        return entry

    def column_entry(self, lon, donor, offset, slot):
        side = (lon == 0) | (lon == self.lon_count - 1)
        top = self.first_entry(self.top_start(lon), donor, offset)
        bottom = self.first_entry(self.bottom_start(lon), donor, offset)
        lower = (lon == 0) | jnp.logical_not(side) & (slot >= self.half)
        skipped = jnp.where(jnp.logical_not(side) & (slot >= self.half), self.half, 0)
        return jnp.where(lower, bottom, top) + slot - skipped

    def column_slot(self, lat, lon, donor, offset):
        side = (lon == 0) | (lon == self.lon_count - 1)
        start, _ = self.stretch(lat, lon)
        ahead = self.first_entry(start, donor, offset) - self.first_entry(
            jnp.where(lon == 0, self.bottom_start(lon), self.top_start(lon)), donor, offset
        )
        middle = jnp.where(lat == self.lat_count - 1, self.half, 0)
        return jnp.where(side, jnp.maximum(ahead, 0), middle)


def padded_rows(count):
    return -(-count // 1024) * 8


def whole(count):
    return [pl.BlockSpec(memory_space=pltpu.VMEM)] * count


def scalars(count):
    return [pl.BlockSpec(memory_space=pltpu.SMEM)] * count


def lookup(table_ref, index):
    return table_ref[index // 128, index % 128]


def grant(mebibytes):
    return pltpu.CompilerParams(vmem_limit_bytes=mebibytes << 20)


def tiles(index, count):
    if isinstance(index, int):
        return pl.ds(index * TILE, count * TILE)
    return pl.ds(pl.multiple_of(index * TILE, TILE), count * TILE)


def weight_kernel(loop, base_ref, weight_ref, turn_ref, corner_ref, spread_ref):
    entries = loop.entries
    diagonal = lax.broadcasted_iota(jnp.int32, (entries, entries), 0) == (
        lax.broadcasted_iota(jnp.int32, (entries, entries), 1)
    )
    for number in range(18):
        ref, row = (weight_ref, number) if number < 16 else (turn_ref, number - 16)
        column = jnp.sum(
            jnp.where(diagonal, ref[row : row + 1, :], 0.0), axis=1, keepdims=True
        )
        spread_ref[pl.ds(number * entries, entries), :] = jnp.broadcast_to(
            column, (entries, spread_ref.shape[1])
        )
    wide = loop.cols + 2 * HALO
    corner_ref[0:1, 0:entries] = (
        base_ref[0:1, :] - lax.axis_index("lat") * loop.rows + HALO - 1
    ) * wide + (base_ref[1:2, :] - lax.axis_index("lon") * loop.cols + HALO - 1)


def digits(shape, outer, inner, slots):
    flat = lax.broadcasted_iota(jnp.int32, shape, 0) * shape[1] + lax.broadcasted_iota(
        jnp.int32, shape, 1
    )
    high = jnp.zeros(shape, jnp.int32)
    for n in range(1, outer):
        high = high + jnp.where(flat >= n * inner * slots, 1, 0)
    rest = flat - high * (inner * slots)
    middle = jnp.zeros(shape, jnp.int32)
    for n in range(1, inner):
        middle = middle + jnp.where(rest >= n * slots, 1, 0)
    return high, middle, jnp.minimum(rest - middle * slots, slots - 1)


def table_kernel(loop, pitch, cell_ref, other_ref, send_ref, swap_ref, receive_ref):
    lat, lon = lax.axis_index("lat"), lax.axis_index("lon")
    lat_count, lon_count = loop.lat_count, loop.lon_count
    mine = loop.position(cell_ref[0], cell_ref[1])
    other = loop.position(other_ref[0], other_ref[1])

    _, step, slot = digits(send_ref.shape, 1, lon_count, loop.column_slots)
    entry = loop.column_entry(
        to_device(lon, step, lon_count), lat * lon_count + lon, other, slot
    )
    send_ref[...] = loop.wrap(entry)

    lat_step, lon_step, slot = digits(swap_ref.shape, lat_count, lon_count, loop.slots)
    donor = lat * lon_count + from_device(lon, lon_step, lon_count)
    here = jnp.full_like(slot, lon)
    ahead = loop.column_slot(to_device(lat, lat_step, lat_count), here, donor, other)
    swap_ref[...] = jnp.minimum(ahead + slot, loop.column_slots - 1)

    donor = from_device(lat, lat_step, lat_count) * lon_count + from_device(
        lon, lon_step, lon_count
    )
    start, span = loop.stretch(jnp.full_like(slot, lat), jnp.full_like(slot, lon))
    entry = loop.first_entry(start, donor, mine) + slot
    place = entry * loop.blocks + donor + mine
    wrapped = jnp.where(place >= loop.total, place - loop.total, place)
    row, col = loop.cell(wrapped)
    spot = (row - lat * loop.rows + HALO) * pitch + PAD + (col - lon * loop.cols + HALO)
    receive_ref[...] = jnp.where(place < start + span, spot, 0)


def strip_kernel(
    rows, cols, after_ref, own_even_ref, own_odd_ref, even_ref, odd_ref, *send_refs
):
    del after_ref
    lat_even = lax.rem(lax.axis_index("lat"), 2) == 0
    lon_even = lax.rem(lax.axis_index("lon"), 2) == 0
    high = cols - HALO
    lows = (jnp.where(lon_even, high, 0), jnp.where(lon_even, 0, high))

    def copy_halo(first, source):
        for send_ref, low in zip(send_refs, lows):
            for row in range(HALO):
                send_ref[tiles((first + row) * HALO, HALO), :] = source[
                    tiles(row * cols + low, HALO), :
                ]

    for send_ref, own_ref in zip(send_refs, (own_even_ref, own_odd_ref)):
        send_ref[tiles(HALO * HALO, rows * HALO), :] = own_ref[...]

    @pl.when(lat_even)
    def _():
        copy_halo(0, odd_ref)
        copy_halo(HALO + rows, even_ref)

    @pl.when(jnp.logical_not(lat_even))
    def _():
        copy_halo(0, even_ref)
        copy_halo(HALO + rows, odd_ref)


def mix_and_pack(loop, wide, rim, frame_ref, value_ref, send_refs):
    send_table_ref, corner_ref, spread_ref = rim
    entries = loop.entries
    field = lax.broadcasted_iota(jnp.int32, (TILE, 128), 0)
    takes_next = (field == 1) | (field == 4)
    turned = takes_next | (field == 2) | (field == 5)

    def one_entry(entry, carry):
        base = corner_ref[0, entry]

        def over_tile(number):
            return spread_ref[pl.ds(number * entries + entry, TILE, stride=0), :]

        total = None
        for a in range(4):
            for b in range(4):
                part = over_tile(4 * a + b) * frame_ref[tiles(base + a * wide + b, 1), :]
                total = part if total is None else total + part
        cosine, sine = over_tile(16), over_tile(17)
        other = jnp.where(
            takes_next, pltpu.roll(total, TILE - 1, 0), pltpu.roll(total, 1, 0)
        )
        mixed = cosine * total + jnp.where(takes_next, -sine, sine) * other
        value_ref[tiles(entry, 1), :] = jnp.where(turned, mixed, total)
        return carry

    lax.fori_loop(0, loop.entries, one_entry, 0, unroll=4)
    for step, send_ref in enumerate(send_refs):
        for slot in range(loop.column_slots):
            entry = lookup(send_table_ref, step * loop.column_slots + slot)
            send_ref[tiles(slot, 1), :] = value_ref[tiles(entry, 1), :]


def frame_kernel(loop, *refs):
    rim, refs = refs[:3], refs[3:]
    state_ref, lat_even_ref, lat_odd_ref, lon_odd_ref, lon_even_ref, frame_ref = refs[:6]
    send_refs, value_ref = refs[6:-1], refs[-1]
    rows, cols = loop.rows, loop.cols
    wide = cols + 2 * HALO
    lat_even = lax.rem(lax.axis_index("lat"), 2) == 0
    lon_even = lax.rem(lax.axis_index("lon"), 2) == 0

    def copy_rows(first, count, source, left, width):
        for row in range(count):
            frame_ref[tiles((first + row) * wide + left, width), :] = source[
                tiles(row * width, width), :
            ]

    copy_rows(HALO, rows, state_ref, HALO, cols)

    @pl.when(lat_even)
    def _():
        copy_rows(0, HALO, lat_odd_ref, HALO, cols)
        copy_rows(HALO + rows, HALO, lat_even_ref, HALO, cols)

    @pl.when(jnp.logical_not(lat_even))
    def _():
        copy_rows(0, HALO, lat_even_ref, HALO, cols)
        copy_rows(HALO + rows, HALO, lat_odd_ref, HALO, cols)

    @pl.when(lon_even)
    def _():
        copy_rows(0, rows + 2 * HALO, lon_odd_ref, 0, HALO)
        copy_rows(0, rows + 2 * HALO, lon_even_ref, HALO + cols, HALO)

    @pl.when(jnp.logical_not(lon_even))
    def _():
        copy_rows(0, rows + 2 * HALO, lon_even_ref, 0, HALO)
        copy_rows(0, rows + 2 * HALO, lon_odd_ref, HALO + cols, HALO)

    lat, lon = lax.axis_index("lat"), lax.axis_index("lon")
    zeros = jnp.zeros((HALO * TILE, frame_ref.shape[1]), jnp.float32)
    for at_row, top in ((lat == 0, 0), (lat == loop.lat_count - 1, HALO + rows)):
        for at_col, left in ((lon == 0, 0), (lon == loop.lon_count - 1, HALO + cols)):

            @pl.when(at_row & at_col)
            def _():
                for row in range(HALO):
                    frame_ref[tiles((top + row) * wide + left, HALO), :] = zeros

    mix_and_pack(loop, wide, rim, frame_ref, value_ref, send_refs)


def swap_kernel(loop, table_ref, *refs):
    got_refs = [refs[0]] + by_step(1, refs[1 : loop.lon_count])
    out_refs = refs[loop.lon_count :]
    for lat_step in range(loop.lat_count):
        for lon_step in range(loop.lon_count):
            for slot in range(loop.slots):
                place = lon_step * loop.slots + slot
                source = lookup(table_ref, lat_step * loop.lon_count * loop.slots + place)
                out_refs[lat_step][tiles(place, 1), :] = got_refs[lon_step][tiles(source, 1), :]


class Section:
    def __init__(self, loop, factor_ref, radial_ref, plane_ref, work_ref):
        self.loop = loop
        self.tall, self.wide = loop.rows + 2 * HALO, loop.cols + 2 * HALO
        self.pitch = self.wide + 2 * PAD
        self.factor_ref, self.radial_ref = factor_ref, radial_ref
        self.plane_ref, self.work_ref = plane_ref, work_ref
        lat, lon = lax.axis_index("lat"), lax.axis_index("lon")
        self.lat = lat
        self.at_top, self.at_left = lat == 0, lon == 0
        self.on_row_edge = self.at_top | (lat == loop.lat_count - 1)
        self.on_col_edge = self.at_left | (lon == loop.lon_count - 1)

    def spread(self, frame_ref, rows):
        def one_row(row, carry):
            for chunk in range(0, self.wide, 8):
                for f in range(TILE):
                    start = (row * self.wide + chunk) * TILE + f
                    self.plane_ref[self.at(f, row, chunk), :] = frame_ref[
                        pl.ds(start, 8, stride=TILE), :
                    ]
            return carry

        lax.fori_loop(*rows, one_row, 0)

    def scatter(self, receive_ref, got_refs):
        arrivals = self.loop.lon_count * self.loop.slots
        got_refs = by_step(0, got_refs)
        for lat_step in range(self.loop.lat_count):
            for place in range(arrivals):
                spot = lookup(receive_ref, lat_step * arrivals + place)
                self.plane_ref[pl.ds(spot, TILE, stride=self.tall * self.pitch), :] = got_refs[
                    lat_step
                ][tiles(place, 1), :]

    def at(self, number, row, col):
        return pl.ds((number * self.tall + row) * self.pitch + PAD + col, 8)

    def reader(self, ref, row, col):
        def read(number, row_step=0, col_step=0):
            return ref[self.at(number, row + row_step, col + col_step), :]

        return read

    def prepare(self, row):
        factors = [self.factor_ref[(self.lat * 3 + n) * self.tall + row] for n in range(3)]
        inverse_radius = self.radial_ref[0]
        with_theta = inverse_radius * (self.loop.nth / math.pi)
        return factors, inverse_radius * factors[2], with_theta

    def up(self, x):
        return pltpu.roll(x, x.shape[-1] - 1, 1)

    def down(self, x):
        return pltpu.roll(x, 1, 1)

    def curl(self, read, first, prepared):
        (tu, td, ph), with_phi, with_theta = prepared
        ru, rl = self.radial_ref[1], self.radial_ref[2]
        a, b, c = first, first + 1, first + 2
        mid_b, mid_c = read(b), read(c)
        radial = self.radial_ref[0] * (
            (tu * read(c, 1) - td * read(c, -1)) - ph * (read(b, 0, 1) - read(b, 0, -1))
        )
        polar = with_phi * (read(a, 0, 1) - read(a, 0, -1)) - (
            ru * self.up(mid_c) - rl * self.down(mid_c)
        )
        azimuth = (ru * self.up(mid_b) - rl * self.down(mid_b)) - with_theta * (
            read(a, 1) - read(a, -1)
        )
        return radial, polar, azimuth

    def slope(self, read, number, prepared):
        _, with_phi, with_theta = prepared
        mid = read(number)
        return (
            self.radial_ref[3] * self.up(mid) - self.radial_ref[4] * self.down(mid),
            with_theta * (read(number, 1) - read(number, -1)),
            with_phi * (read(number, 0, 1) - read(number, 0, -1)),
        )

    def outflow(self, read, first, prepared):
        (tu, td, ph), _, _ = prepared
        mid = read(first)
        return (
            self.radial_ref[5] * self.up(mid) - self.radial_ref[6] * self.down(mid)
        ) + self.radial_ref[0] * (
            (tu * read(first + 1, 1) - td * read(first + 1, -1))
            + ph * (read(first + 2, 0, 1) - read(first + 2, 0, -1))
        )

    def first_pass(self, row, chunk):
        prepared = self.prepare(row)
        read = self.reader(self.plane_ref, row, chunk)

        def put(number, value):
            self.work_ref[self.at(number, row, chunk), :] = value

        flow = [read(n) for n in range(3)]
        field = [read(n) for n in range(3, 6)]
        current = self.curl(read, 3, prepared)
        spin = self.curl(read, 0, prepared)
        induced = cross(flow, field)
        warm = self.slope(read, 6, prepared)
        for n in range(3):
            put(n, current[n])
            put(3 + n, spin[n])
            put(6 + n, induced[n] - ETA_COEF * current[n])
            put(9 + n, warm[n])
        put(12, read(7) + 0.5 * dot(flow, flow))

    def second_pass(self, row, chunk, emit):
        prepared = self.prepare(row)
        read = self.reader(self.plane_ref, row, chunk)
        work = self.reader(self.work_ref, row, chunk)
        flow = [read(n) for n in range(3)]
        field = [read(n) for n in range(3, 6)]
        current = [work(n) for n in range(3)]
        spin = [work(3 + n) for n in range(3)]
        warm = [work(9 + n) for n in range(3)]
        field_rate = self.curl(work, 6, prepared)
        spin_curl = self.curl(work, 3, prepared)
        head = self.slope(work, 12, prepared)
        lorentz = cross(current, field)
        advect = cross(flow, spin)
        speed = [advect[n] + lorentz[n] - head[n] - NU_COEF * spin_curl[n] for n in range(3)]
        speed[0] = speed[0] + ARCHIMEDES_LIFT * read(6)
        heat = KAPPA_COEF * self.outflow(work, 9, prepared) - dot(flow, warm)
        squeeze = -SOUND_SQ * self.outflow(read, 0, prepared)
        emit(row, chunk, read, speed + list(field_rate) + [heat, squeeze])

    def over(self, rows, one_row, unroll):
        def step(row, carry):
            one_row(row)
            return carry

        lax.fori_loop(*rows, step, 0, unroll=unroll)

    def everywhere(self, rows, chunks, emit):
        def first(row):
            for chunk in range(0, self.wide, 8):
                self.first_pass(row, chunk)

        def second(row):
            for chunk in chunks:
                self.second_pass(row, chunk, emit)

        self.over((rows[0] - 1, rows[1] + 1), first, 2)
        self.over(rows, second, 2)

    def along_edges(self, rows, chunks, emit):
        tall, wide = self.tall, self.wide
        low_chunk, high_chunk = chunks[0], chunks[-1]

        @pl.when(self.on_row_edge)
        def _():
            row = jnp.where(self.at_top, HALO - 1, tall - HALO - 1)
            for step in range(2):
                for chunk in range(0, wide, 8):
                    self.first_pass(row + step, chunk)

        @pl.when(self.on_col_edge)
        def _():
            chunk = pl.multiple_of(jnp.where(self.at_left, 0, wide - 8), 8)
            count = rows[1] - rows[0]
            self.over(
                (rows[0] - 1, rows[1] + 1), lambda row: self.first_pass(row, chunk), count // 2 + 1
            )

        @pl.when(self.on_row_edge)
        def _():
            row = jnp.where(self.at_top, HALO, tall - HALO - 2)
            for step in range(2):
                for chunk in chunks:
                    self.second_pass(row + step, chunk, emit)

        @pl.when(self.on_col_edge)
        def _():
            chunk = jnp.where(self.at_left, low_chunk, high_chunk)
            count = rows[1] - rows[0]
            self.over(rows, lambda row: self.second_pass(row, chunk, emit), count // 2)


def cross(x, y):
    return (
        x[1] * y[2] - x[2] * y[1],
        x[2] * y[0] - x[0] * y[2],
        x[0] * y[1] - x[1] * y[0],
    )


def dot(x, y):
    return x[0] * y[0] + x[1] * y[1] + x[2] * y[2]


def middle_state(loop, frame_ref, rate_ref):
    wide = loop.cols + 2 * HALO
    first_row = lax.axis_index("lat") * loop.rows - HALO
    first_col = lax.axis_index("lon") * loop.cols - HALO

    def emit(row, chunk, read, rate):
        in_row = (row + first_row >= 0) & (row + first_row < loop.nth)
        col = lax.broadcasted_iota(jnp.int32, (8, 128), 0) + (chunk + first_col)
        inside = (col >= jnp.where(in_row, 0, loop.nph)) & (col < loop.nph)
        for f in range(TILE):
            rate_ref[f, row, pl.ds(chunk, 8), :] = rate[f]
            start = (row * wide + chunk) * TILE + f
            frame_ref[pl.ds(start, 8, stride=TILE), :] = jnp.where(
                inside, read(f) + TIME_STEP * rate[f], 0.0
            )

    return emit


def total_change(loop, change_ref, rate_ref):
    def emit(row, chunk, read, rate):
        for f in range(TILE):
            start = ((row - HALO) * loop.cols + chunk - HALO) * TILE + f
            change_ref[pl.ds(start, 8, stride=TILE), :] = (0.5 * TIME_STEP) * (
                rate_ref[f, row, pl.ds(chunk, 8), :] + rate[f]
            )

    return emit


def first_inner_kernel(
    loop, factor_ref, radial_ref, frame_in_ref, after_ref, frame_ref, rate_ref, plane_ref, work_ref
):
    del after_ref
    part = Section(loop, factor_ref, radial_ref, plane_ref, work_ref)
    part.spread(frame_in_ref, (0, part.tall))
    part.everywhere(
        (2, part.tall - 2), range(0, part.wide, 8), middle_state(loop, frame_ref, rate_ref)
    )


def first_edge_kernel(loop, *refs):
    rim, refs = refs[:3], refs[3:]
    receive_ref, factor_ref, radial_ref = refs[:3]
    got_refs, refs = refs[7 : 7 + loop.lat_count], refs[7 + loop.lat_count :]
    frame_ref, rate_ref, plane_ref, work_ref = refs[:4]
    send_refs, value_ref = refs[4:-1], refs[-1]
    part = Section(loop, factor_ref, radial_ref, plane_ref, work_ref)
    part.scatter(receive_ref, got_refs)
    part.along_edges(
        (2, part.tall - 2), range(0, part.wide, 8), middle_state(loop, frame_ref, rate_ref)
    )
    mix_and_pack(loop, part.wide, rim, frame_ref, value_ref, send_refs)


def second_inner_kernel(
    loop, factor_ref, radial_ref, frame_ref, rate_ref, after_ref, change_ref, plane_ref, work_ref
):
    del after_ref
    part = Section(loop, factor_ref, radial_ref, plane_ref, work_ref)
    part.spread(frame_ref, (2, part.tall - 2))
    part.everywhere(
        (HALO, HALO + loop.rows),
        range(HALO, HALO + loop.cols, 8),
        total_change(loop, change_ref, rate_ref),
    )


def second_edge_kernel(loop, receive_ref, factor_ref, radial_ref, rate_ref, inner_ref, *refs):
    got_refs, refs = refs[2 : 2 + loop.lat_count], refs[2 + loop.lat_count :]
    plane_ref, work_ref, change_ref = refs
    part = Section(loop, factor_ref, radial_ref, plane_ref, work_ref)
    for row in range(loop.rows):
        here = tiles(row * loop.cols, loop.cols)
        change_ref[here, :] = inner_ref[here, :]
    part.scatter(receive_ref, got_refs)
    part.along_edges(
        (HALO, HALO + loop.rows),
        range(HALO, HALO + loop.cols, 8),
        total_change(loop, change_ref, rate_ref),
    )


def radial_factors(levels, theta_count):
    scale = 2.0 * theta_count / math.pi
    step = 0.65 * scale / levels
    radius = 0.35 * scale + (np.arange(levels) + 0.5) * step
    half = 0.5 / step
    above = np.append(radius[1:], 0.0)
    below = np.append(0.0, radius[:-1])
    ones_above = np.append(np.ones(levels - 1), 0.0)
    ones_below = np.append(0.0, np.ones(levels - 1))
    rows = np.stack(
        [
            1.0 / radius,
            half * above / radius,
            half * below / radius,
            half * ones_above,
            half * ones_below,
            half * above**2 / radius**2,
            half * below**2 / radius**2,
        ]
    )
    return np.repeat(rows[:, None, :], 8, axis=1).astype(np.float32)


def row_factors(rows, lat_count, nth, nph):
    polar_step, azimuth_step = math.pi / (2 * nth), 1.5 * math.pi / nph
    tall = rows + 2 * HALO
    parts = []
    for lat in range(lat_count):
        row = lat * rows - HALO - 1 + np.arange(tall + 2)
        sines = np.sin(math.pi / 4 + (row + 0.5) * polar_step)
        middle = sines[1:-1]
        parts += [
            sines[2:] / middle * (0.5 / polar_step),
            sines[:-2] / middle * (0.5 / polar_step),
            (0.5 / azimuth_step) / middle,
        ]
    return np.concatenate(parts).astype(np.float32)


def per_device(state, rim_base, rim_weight, rim_angle, rim_target):
    _, rows, cols, fields, levels = state.shape
    lat_count, lon_count = lax.axis_size("lat"), lax.axis_size("lon")
    entries = rim_base.shape[1]
    loop = Loop(rows, cols, lat_count, lon_count, entries)
    tall, wide = rows + 2 * HALO, cols + 2 * HALO
    pitch = wide + 2 * PAD
    block = state[0].reshape(rows * cols * fields, levels)
    f32 = jnp.float32

    def tile_array(count):
        return jax.ShapeDtypeStruct((count * TILE, levels), f32)

    first_cell = rim_target[0, 0]
    other_cell = lax.ppermute(first_cell, "panel", [(0, 1), (1, 0)])

    everyone = ("panel", "lat", "lon")
    cells = state[0]
    last_first = lax.axis_index("lat") % 2 == 0
    head, tail = cells[:HALO], cells[rows - HALO :]
    send_even = jnp.where(last_first, tail, head).reshape(HALO * cols * fields, levels)
    send_odd = jnp.where(last_first, head, tail).reshape(HALO * cols * fields, levels)
    lat_even = lax.ppermute(send_even, everyone, swap_route(0, lat_count, lon_count, True))
    lat_odd = lax.ppermute(send_odd, everyone, swap_route(1, lat_count, lon_count, True))

    angle = rim_angle[0]
    corner_table, spread_weights = pl.pallas_call(
        lambda *refs: weight_kernel(loop, *refs),
        out_shape=[
            jax.ShapeDtypeStruct((8, -(-entries // 128) * 128), jnp.int32),
            jax.ShapeDtypeStruct((18 * entries + TILE, levels), f32),
        ],
        in_specs=whole(3),
        out_specs=whole(2),
        compiler_params=grant(4),
        name="weights",
    )(rim_base[0].T, rim_weight[0].T, jnp.stack([jnp.cos(angle), jnp.sin(angle)]))
    send_count = lon_count * loop.column_slots
    got_count = lat_count * lon_count * loop.slots
    send_table, swap_table, receive_table = pl.pallas_call(
        lambda *refs: table_kernel(loop, pitch, *refs),
        out_shape=[
            jax.ShapeDtypeStruct((padded_rows(count), 128), jnp.int32)
            for count in (send_count, got_count, got_count)
        ],
        in_specs=scalars(2),
        out_specs=whole(3),
        compiler_params=grant(4),
        name="tables",
    )(first_cell, other_cell)
    rim = (send_table, corner_table, spread_weights)
    factors = jnp.asarray(row_factors(rows, lat_count, loop.nth, loop.nph))
    radial = jnp.asarray(radial_factors(levels, loop.nth))

    east_first = lax.axis_index("lon") % 2 == 0
    head, tail = cells[:, :HALO], cells[:, cols - HALO :]
    own_even = jnp.where(east_first, tail, head).reshape(rows * HALO * fields, levels)
    own_odd = jnp.where(east_first, head, tail).reshape(rows * HALO * fields, levels)
    strip_even, strip_odd = pl.pallas_call(
        lambda *refs: strip_kernel(rows, cols, *refs),
        out_shape=[tile_array(tall * HALO)] * 2,
        in_specs=whole(5),
        out_specs=whole(2),
        compiler_params=grant(4),
        name="strips",
    )(corner_table, own_even, own_odd, lat_even, lat_odd)
    lon_odd = lax.ppermute(strip_odd, everyone, swap_route(1, lat_count, lon_count, False))
    lon_even = lax.ppermute(strip_even, everyone, swap_route(0, lat_count, lon_count, False))

    packed_shapes = [tile_array(loop.column_slots)] * lon_count
    frame, *packed = pl.pallas_call(
        lambda *refs: frame_kernel(loop, *refs),
        out_shape=[tile_array(tall * wide)] + packed_shapes,
        in_specs=scalars(2) + whole(6),
        out_specs=whole(1 + lon_count),
        scratch_shapes=[pltpu.VMEM((entries * TILE, levels), f32)],
        compiler_params=grant(8),
        name="frame",
    )(*rim, block, lat_even, lat_odd, lon_odd, lon_even)

    def first_round(packed):
        got = [packed[0]] + [
            lax.ppermute(packed[step], "lon", lon_route(step, lon_count))
            for step in start_order(1, lon_count)
        ]
        return pl.pallas_call(
            lambda *refs: swap_kernel(loop, *refs),
            out_shape=[tile_array(lon_count * loop.slots)] * lat_count,
            in_specs=scalars(1) + whole(lon_count),
            out_specs=whole(lat_count),
            compiler_params=grant(4),
            name="swap",
        )(swap_table, *got)

    def second_round(turned):
        return [
            lax.ppermute(turned[step], ("panel", "lat"), lat_route(step, lat_count))
            for step in start_order(0, lat_count)
        ]

    planes = [
        jax.ShapeDtypeStruct((fields * tall * pitch, levels), f32),
        jax.ShapeDtypeStruct((13 * tall * pitch, levels), f32),
    ]
    rates = jax.ShapeDtypeStruct((fields, tall, wide, levels), f32)

    turned = first_round(packed)
    got = second_round(turned)
    frame, rate, plane, work = pl.pallas_call(
        lambda *refs: first_inner_kernel(loop, *refs),
        out_shape=[tile_array(tall * wide), rates] + planes,
        in_specs=scalars(1) + whole(3),
        out_specs=whole(4),
        compiler_params=grant(4),
        name="first_inner",
    )(factors, radial, frame, turned[0])
    frame, rate, _, _, *packed = pl.pallas_call(
        lambda *refs: first_edge_kernel(loop, *refs),
        out_shape=[tile_array(tall * wide), rates] + planes + packed_shapes,
        in_specs=scalars(2) + whole(1) + scalars(2) + whole(5 + lat_count),
        out_specs=whole(4 + lon_count),
        scratch_shapes=[pltpu.VMEM((entries * TILE, levels), f32)],
        input_output_aliases={6: 0, 7: 1, 8: 2, 9: 3},
        compiler_params=grant(4),
        name="first_edge",
    )(*rim, receive_table, factors, radial, frame, rate, plane, work, *got)

    turned = first_round(packed)
    got = second_round(turned)
    inner, plane, work = pl.pallas_call(
        lambda *refs: second_inner_kernel(loop, *refs),
        out_shape=[tile_array(rows * cols)] + planes,
        in_specs=scalars(1) + whole(4),
        out_specs=whole(3),
        compiler_params=grant(4),
        name="second_inner",
    )(factors, radial, frame, rate, turned[0])
    _, _, change = pl.pallas_call(
        lambda *refs: second_edge_kernel(loop, *refs),
        out_shape=planes + [tile_array(rows * cols)],
        in_specs=scalars(2) + whole(5 + lat_count),
        out_specs=whole(3),
        input_output_aliases={5: 0, 6: 1},
        compiler_params=grant(4),
        name="second_edge",
    )(receive_table, factors, radial, rate, inner, plane, work, *got)
    return change.reshape(1, rows, cols, fields, levels)


def solution(mesh):
    return jax.shard_map(
        per_device,
        mesh=mesh,
        in_specs=(
            P("panel", "lat", "lon", None, None),
            P("panel", ("lat", "lon"), None),
            P("panel", ("lat", "lon"), None),
            P("panel", ("lat", "lon")),
            P("panel", None, None),
        ),
        out_specs=P("panel", "lat", "lon", None, None),
        check_vma=False,
    )
```

```python
import math

import jax
import jax.numpy as jnp
import numpy as np
from jax import lax
from jax.experimental import pallas as pl
from jax.experimental.pallas import tpu as pltpu
from jax.sharding import PartitionSpec as P

ETA_COEF = 0.2
NU_COEF = 0.2
KAPPA_COEF = 0.3
SOUND_SQ = 1.0
ARCHIMEDES_LIFT = 0.5
TIME_STEP = 0.2

HALO = 4
PAD = 8
TILE = 8


def hardest_first(step):
    return -step.bit_length(), step


def start_order(first, count):
    return sorted(range(first, count), key=hardest_first)


def by_step(first, refs):
    order = start_order(first, first + len(refs))
    return [refs[order.index(step)] for step in range(first, first + len(refs))]


def is_power_of_two(count):
    return count & (count - 1) == 0


def to_device(index, step, count):
    return index ^ step if is_power_of_two(count) else (index + step) % count


def from_device(index, step, count):
    return index ^ step if is_power_of_two(count) else (index + count - step) % count


def swap_route(parity, lat_count, lon_count, along_lat):
    count, across = (lat_count, lon_count) if along_lat else (lon_count, lat_count)
    mate = list(range(count))
    for low in range(parity, count - 1, 2):
        mate[low], mate[low + 1] = low + 1, low
    route = []
    for side in range(2):
        for lat in range(lat_count):
            for lon in range(lon_count):
                here, other = (lat, lon) if along_lat else (lon, lat)
                there = mate[here]
                if there == here:
                    other = other ^ 1 if other ^ 1 < across else other
                target = (there, other) if along_lat else (other, there)
                route.append(
                    (
                        (side * lat_count + lat) * lon_count + lon,
                        (side * lat_count + target[0]) * lon_count + target[1],
                    )
                )
    return route


def lon_route(step, count):
    return [(i, to_device(i, step, count)) for i in range(count)]


def lat_route(step, count):
    return [
        (side * count + i, (1 - side) * count + to_device(i, step, count))
        for side in range(2)
        for i in range(count)
    ]


class Loop:
    def __init__(self, rows, cols, lat_count, lon_count, entries):
        self.rows, self.cols = rows, cols
        self.lat_count, self.lon_count = lat_count, lon_count
        self.nth, self.nph = rows * lat_count, cols * lon_count
        self.total = 4 * (self.nth + self.nph)
        self.blocks = lat_count * lon_count
        self.entries = entries
        one_row = 2 * (cols + 2 * HALO)
        one_col = 2 * (rows + 2 * HALO)
        corner = 2 * (rows + cols + 2 * HALO)
        self.slots = -(-max(corner, one_row, one_col) // self.blocks)
        self.half = -(-one_row // self.blocks)
        side = 4 * (cols + HALO) + 2 * self.nth
        leads = [2 * (cols + HALO) + 2 * (n * rows - HALO) for n in range(1, lat_count)]
        self.even_leads = all(lead % self.blocks == 0 for lead in leads)
        self.column_slots = max(-(-side // self.blocks), 2 * self.half)

    def position(self, row, col):
        nth, nph = self.nth, self.nph
        top = 2 * col + row + 2
        right = 2 * nph + 2 * row + col - nph
        bottom = 2 * nph + 2 * nth + 2 * (nph - 1 - col) + row - nth
        left = 4 * nph + 2 * nth + 2 * (nth - 1 - row) + col + 2
        return jnp.where(
            row < 0, top, jnp.where(row >= nth, bottom, jnp.where(col >= nph, right, left))
        )

    def cell(self, place):
        nth, nph = self.nth, self.nph
        right = place - 2 * nph
        bottom = right - 2 * nth
        left = bottom - 2 * nph
        on_top, on_right, on_bottom = right < 0, bottom < 0, left < 0
        row = jnp.where(
            on_top,
            (place & 1) - 2,
            jnp.where(
                on_right,
                right >> 1,
                jnp.where(on_bottom, nth + (bottom & 1), nth - 1 - (left >> 1)),
            ),
        )
        col = jnp.where(
            on_top,
            place >> 1,
            jnp.where(
                on_right,
                nph + (right & 1),
                jnp.where(on_bottom, nph - 1 - (bottom >> 1), (left & 1) - 2),
            ),
        )
        return row, col

    def top_start(self, lon):
        return 2 * jnp.maximum(lon * self.cols - HALO, 0)

    def bottom_start(self, lon):
        high = jnp.minimum(lon * self.cols + self.cols + HALO, self.nph)
        return 2 * self.nph + 2 * self.nth + 2 * (self.nph - high)

    def stretch(self, lat, lon):
        nth, nph = self.nth, self.nph
        row_low = jnp.maximum(lat * self.rows - HALO, 0)
        row_high = jnp.minimum(lat * self.rows + self.rows + HALO, nth)
        col_low = jnp.maximum(lon * self.cols - HALO, 0)
        col_high = jnp.minimum(lon * self.cols + self.cols + HALO, nph)
        top, bottom = lat == 0, lat == self.lat_count - 1
        left, right = lon == 0, lon == self.lon_count - 1
        left_start = 4 * nph + 2 * nth + 2 * (nth - row_high)
        start = jnp.where(
            top & left,
            left_start,
            jnp.where(
                top,
                self.top_start(lon),
                jnp.where(
                    right,
                    2 * nph + 2 * row_low,
                    jnp.where(bottom, self.bottom_start(lon), left_start),
                ),
            ),
        )
        span = jnp.where(top | bottom, 2 * (col_high - col_low), 0) + jnp.where(
            left | right, 2 * (row_high - row_low), 0
        )
        return start, span

    def first_entry(self, start, donor, offset):
        lead = -(-2 * self.total // self.blocks)
        raised = start - donor - offset + lead * self.blocks + self.blocks - 1
        if is_power_of_two(self.blocks):
            return (raised >> (self.blocks.bit_length() - 1)) - lead
        return lax.div(raised, jnp.full_like(raised, self.blocks)) - lead

    def wrap(self, entry):
        for bound in (8, 4, 2, 1):
            entry = jnp.where(entry < 0, entry + self.entries * bound, entry)
        for bound in (8, 4, 2, 1):
            over = entry - self.entries * bound
            entry = jnp.where(over >= 0, over, entry)
        return entry

    def column_entry(self, lon, donor, offset, slot):
        side = (lon == 0) | (lon == self.lon_count - 1)
        top = self.first_entry(self.top_start(lon), donor, offset)
        bottom = self.first_entry(self.bottom_start(lon), donor, offset)
        lower = (lon == 0) | jnp.logical_not(side) & (slot >= self.half)
        skipped = jnp.where(jnp.logical_not(side) & (slot >= self.half), self.half, 0)
        return jnp.where(lower, bottom, top) + slot - skipped

    def column_slot(self, lat, lon, donor=None, offset=None):
        side = (lon == 0) | (lon == self.lon_count - 1)
        start, _ = self.stretch(lat, lon)
        column = jnp.where(lon == 0, self.bottom_start(lon), self.top_start(lon))
        if donor is None:
            ahead = lax.div(start - column, jnp.int32(self.blocks))
        else:
            ahead = self.first_entry(start, donor, offset) - self.first_entry(
                column, donor, offset
            )
        middle = jnp.where(lat == self.lat_count - 1, self.half, 0)
        return jnp.where(side, jnp.maximum(ahead, 0), middle)


def padded_rows(count):
    return -(-count // 1024) * 8


def whole(count):
    return [pl.BlockSpec(memory_space=pltpu.VMEM)] * count


def scalars(count):
    return [pl.BlockSpec(memory_space=pltpu.SMEM)] * count


def lookup(table_ref, index):
    return table_ref[index // 128, index % 128]


def grant(mebibytes):
    return pltpu.CompilerParams(vmem_limit_bytes=mebibytes << 20)


def tiles(index, count):
    if isinstance(index, int):
        return pl.ds(index * TILE, count * TILE)
    return pl.ds(pl.multiple_of(index * TILE, TILE), count * TILE)


def weight_kernel(loop, base_ref, weight_ref, turn_ref, corner_ref, spread_ref):
    entries = loop.entries
    diagonal = lax.broadcasted_iota(jnp.int32, (entries, entries), 0) == (
        lax.broadcasted_iota(jnp.int32, (entries, entries), 1)
    )
    for number in range(18):
        ref, row = (weight_ref, number) if number < 16 else (turn_ref, number - 16)
        column = jnp.sum(
            jnp.where(diagonal, ref[row : row + 1, :], 0.0), axis=1, keepdims=True
        )
        spread_ref[pl.ds(number * entries, entries), :] = jnp.broadcast_to(
            column, (entries, spread_ref.shape[1])
        )
    wide = loop.cols + 2 * HALO
    corner_ref[0:1, 0:entries] = (
        base_ref[0:1, :] - lax.axis_index("lat") * loop.rows + HALO - 1
    ) * wide + (base_ref[1:2, :] - lax.axis_index("lon") * loop.cols + HALO - 1)


def digits(shape, outer, inner, slots):
    flat = lax.broadcasted_iota(jnp.int32, shape, 0) * shape[1] + lax.broadcasted_iota(
        jnp.int32, shape, 1
    )
    high = jnp.zeros(shape, jnp.int32)
    for n in range(1, outer):
        high = high + jnp.where(flat >= n * inner * slots, 1, 0)
    rest = flat - high * (inner * slots)
    middle = jnp.zeros(shape, jnp.int32)
    for n in range(1, inner):
        middle = middle + jnp.where(rest >= n * slots, 1, 0)
    return high, middle, jnp.minimum(rest - middle * slots, slots - 1)


def table_kernel(loop, pitch, cell_ref, other_ref, send_ref, swap_ref, receive_ref):
    lat, lon = lax.axis_index("lat"), lax.axis_index("lon")
    lat_count, lon_count = loop.lat_count, loop.lon_count
    mine = loop.position(cell_ref[0], cell_ref[1])
    other = loop.position(other_ref[0], other_ref[1])

    _, step, slot = digits(send_ref.shape, 1, lon_count, loop.column_slots)
    entry = loop.column_entry(
        to_device(lon, step, lon_count), lat * lon_count + lon, other, slot
    )
    send_ref[...] = loop.wrap(entry)

    lat_step, lon_step, slot = digits(swap_ref.shape, lat_count, lon_count, loop.slots)
    donor = lat * lon_count + from_device(lon, lon_step, lon_count)
    here = jnp.full_like(slot, lon)
    ahead = loop.column_slot(to_device(lat, lat_step, lat_count), here, donor, other)
    swap_ref[...] = jnp.minimum(ahead + slot, loop.column_slots - 1)

    donor = from_device(lat, lat_step, lat_count) * lon_count + from_device(
        lon, lon_step, lon_count
    )
    start, span = loop.stretch(jnp.full_like(slot, lat), jnp.full_like(slot, lon))
    entry = loop.first_entry(start, donor, mine) + slot
    place = entry * loop.blocks + donor + mine
    wrapped = jnp.where(place >= loop.total, place - loop.total, place)
    row, col = loop.cell(wrapped)
    spot = (row - lat * loop.rows + HALO) * pitch + PAD + (col - lon * loop.cols + HALO)
    receive_ref[...] = jnp.where(place < start + span, spot, 0)


def strip_kernel(
    rows, cols, after_ref, own_even_ref, own_odd_ref, even_ref, odd_ref, *send_refs
):
    del after_ref
    lat_even = lax.rem(lax.axis_index("lat"), 2) == 0
    lon_even = lax.rem(lax.axis_index("lon"), 2) == 0
    high = cols - HALO
    lows = (jnp.where(lon_even, high, 0), jnp.where(lon_even, 0, high))

    def copy_halo(first, source):
        for send_ref, low in zip(send_refs, lows):
            for row in range(HALO):
                send_ref[tiles((first + row) * HALO, HALO), :] = source[
                    tiles(row * cols + low, HALO), :
                ]

    for send_ref, own_ref in zip(send_refs, (own_even_ref, own_odd_ref)):
        send_ref[tiles(HALO * HALO, rows * HALO), :] = own_ref[...]

    @pl.when(lat_even)
    def _():
        copy_halo(0, odd_ref)
        copy_halo(HALO + rows, even_ref)

    @pl.when(jnp.logical_not(lat_even))
    def _():
        copy_halo(0, even_ref)
        copy_halo(HALO + rows, odd_ref)


def mix_and_pack(loop, wide, rim, frame_ref, value_ref, send_refs):
    send_table_ref, corner_ref, spread_ref = rim
    entries = loop.entries
    field = lax.broadcasted_iota(jnp.int32, (TILE, 128), 0)
    takes_next = (field == 1) | (field == 4)
    turned = takes_next | (field == 2) | (field == 5)

    def one_entry(entry, carry):
        base = corner_ref[0, entry]

        def over_tile(number):
            return spread_ref[pl.ds(number * entries + entry, TILE, stride=0), :]

        total = None
        for a in range(4):
            for b in range(4):
                part = over_tile(4 * a + b) * frame_ref[tiles(base + a * wide + b, 1), :]
                total = part if total is None else total + part
        cosine, sine = over_tile(16), over_tile(17)
        other = jnp.where(
            takes_next, pltpu.roll(total, TILE - 1, 0), pltpu.roll(total, 1, 0)
        )
        mixed = cosine * total + jnp.where(takes_next, -sine, sine) * other
        value_ref[tiles(entry, 1), :] = jnp.where(turned, mixed, total)
        return carry

    lax.fori_loop(0, loop.entries, one_entry, 0, unroll=4)
    for step, send_ref in enumerate(send_refs):
        for slot in range(loop.column_slots):
            entry = lookup(send_table_ref, step * loop.column_slots + slot)
            send_ref[tiles(slot, 1), :] = value_ref[tiles(entry, 1), :]


def middle_kernel(rows, cols, state_ref, lat_even_ref, lat_odd_ref, frame_ref):
    wide = cols + 2 * HALO
    lat_even = lax.rem(lax.axis_index("lat"), 2) == 0

    def copy_rows(first, count, source):
        for row in range(count):
            frame_ref[tiles((first + row) * wide + HALO, cols), :] = source[
                tiles(row * cols, cols), :
            ]

    copy_rows(HALO, rows, state_ref)

    @pl.when(lat_even)
    def _():
        copy_rows(0, HALO, lat_odd_ref)
        copy_rows(HALO + rows, HALO, lat_even_ref)

    @pl.when(jnp.logical_not(lat_even))
    def _():
        copy_rows(0, HALO, lat_even_ref)
        copy_rows(HALO + rows, HALO, lat_odd_ref)


def frame_kernel(loop, *refs):
    rim, refs = refs[:3], refs[3:]
    lon_odd_ref, lon_even_ref, _, frame_ref = refs[:4]
    send_refs, value_ref = refs[4:-1], refs[-1]
    rows, cols = loop.rows, loop.cols
    wide = cols + 2 * HALO
    lat, lon = lax.axis_index("lat"), lax.axis_index("lon")
    lon_even = lax.rem(lon, 2) == 0

    def copy_columns(source, left):
        for row in range(rows + 2 * HALO):
            frame_ref[tiles(row * wide + left, HALO), :] = source[tiles(row * HALO, HALO), :]

    @pl.when(lon_even)
    def _():
        copy_columns(lon_odd_ref, 0)
        copy_columns(lon_even_ref, HALO + cols)

    @pl.when(jnp.logical_not(lon_even))
    def _():
        copy_columns(lon_even_ref, 0)
        copy_columns(lon_odd_ref, HALO + cols)

    zeros = jnp.zeros((HALO * TILE, frame_ref.shape[1]), jnp.float32)
    for at_row, top in ((lat == 0, 0), (lat == loop.lat_count - 1, HALO + rows)):
        for at_col, left in ((lon == 0, 0), (lon == loop.lon_count - 1, HALO + cols)):

            @pl.when(at_row & at_col)
            def _():
                for row in range(HALO):
                    frame_ref[tiles((top + row) * wide + left, HALO), :] = zeros

    mix_and_pack(loop, wide, rim, frame_ref, value_ref, send_refs)


def swap_kernel(loop, *refs):
    table_ref = None
    if not loop.even_leads:
        table_ref, refs = refs[0], refs[1:]
    got_refs = [refs[0]] + by_step(1, refs[1 : loop.lon_count])
    out_refs = refs[loop.lon_count :]
    lat, lon = lax.axis_index("lat"), lax.axis_index("lon")
    for lat_step in range(loop.lat_count):
        if loop.even_leads:
            lead = loop.column_slot(to_device(lat, lat_step, loop.lat_count), lon)
            lead = jnp.minimum(lead, loop.column_slots - loop.slots)
        for lon_step in range(loop.lon_count):
            for slot in range(loop.slots):
                place = lon_step * loop.slots + slot
                if loop.even_leads:
                    source = lead + slot
                else:
                    source = lookup(table_ref, lat_step * loop.lon_count * loop.slots + place)
                out_refs[lat_step][tiles(place, 1), :] = got_refs[lon_step][tiles(source, 1), :]


class Section:
    def __init__(self, loop, factor_ref, radial_ref, plane_ref, work_ref):
        self.loop = loop
        self.tall, self.wide = loop.rows + 2 * HALO, loop.cols + 2 * HALO
        self.pitch = self.wide + 2 * PAD
        self.factor_ref, self.radial_ref = factor_ref, radial_ref
        self.plane_ref, self.work_ref = plane_ref, work_ref
        lat, lon = lax.axis_index("lat"), lax.axis_index("lon")
        self.lat = lat
        self.at_top, self.at_left = lat == 0, lon == 0
        self.on_row_edge = self.at_top | (lat == loop.lat_count - 1)
        self.on_col_edge = self.at_left | (lon == loop.lon_count - 1)

    def spread(self, frame_ref, rows):
        def one_row(row, carry):
            for chunk in range(0, self.wide, 8):
                for f in range(TILE):
                    start = (row * self.wide + chunk) * TILE + f
                    self.plane_ref[self.at(f, row, chunk), :] = frame_ref[
                        pl.ds(start, 8, stride=TILE), :
                    ]
            return carry

        lax.fori_loop(*rows, one_row, 0)

    def scatter(self, receive_ref, got_refs):
        arrivals = self.loop.lon_count * self.loop.slots
        got_refs = by_step(0, got_refs)
        for lat_step in range(self.loop.lat_count):
            for place in range(arrivals):
                spot = lookup(receive_ref, lat_step * arrivals + place)
                self.plane_ref[pl.ds(spot, TILE, stride=self.tall * self.pitch), :] = got_refs[
                    lat_step
                ][tiles(place, 1), :]

    def at(self, number, row, col):
        return pl.ds((number * self.tall + row) * self.pitch + PAD + col, 8)

    def reader(self, ref, row, col):
        def read(number, row_step=0, col_step=0):
            return ref[self.at(number, row + row_step, col + col_step), :]

        return read

    def prepare(self, row):
        factors = [self.factor_ref[(self.lat * 3 + n) * self.tall + row] for n in range(3)]
        inverse_radius = self.radial_ref[0]
        with_theta = inverse_radius * (self.loop.nth / math.pi)
        return factors, inverse_radius * factors[2], with_theta

    def up(self, x):
        return pltpu.roll(x, x.shape[-1] - 1, 1)

    def down(self, x):
        return pltpu.roll(x, 1, 1)

    def curl(self, read, first, prepared):
        (tu, td, ph), with_phi, with_theta = prepared
        ru, rl = self.radial_ref[1], self.radial_ref[2]
        a, b, c = first, first + 1, first + 2
        mid_b, mid_c = read(b), read(c)
        radial = self.radial_ref[0] * (
            (tu * read(c, 1) - td * read(c, -1)) - ph * (read(b, 0, 1) - read(b, 0, -1))
        )
        polar = with_phi * (read(a, 0, 1) - read(a, 0, -1)) - (
            ru * self.up(mid_c) - rl * self.down(mid_c)
        )
        azimuth = (ru * self.up(mid_b) - rl * self.down(mid_b)) - with_theta * (
            read(a, 1) - read(a, -1)
        )
        return radial, polar, azimuth

    def slope(self, read, number, prepared):
        _, with_phi, with_theta = prepared
        mid = read(number)
        return (
            self.radial_ref[3] * self.up(mid) - self.radial_ref[4] * self.down(mid),
            with_theta * (read(number, 1) - read(number, -1)),
            with_phi * (read(number, 0, 1) - read(number, 0, -1)),
        )

    def outflow(self, read, first, prepared):
        (tu, td, ph), _, _ = prepared
        mid = read(first)
        return (
            self.radial_ref[5] * self.up(mid) - self.radial_ref[6] * self.down(mid)
        ) + self.radial_ref[0] * (
            (tu * read(first + 1, 1) - td * read(first + 1, -1))
            + ph * (read(first + 2, 0, 1) - read(first + 2, 0, -1))
        )

    def first_pass(self, row, chunk):
        prepared = self.prepare(row)
        read = self.reader(self.plane_ref, row, chunk)

        def put(number, value):
            self.work_ref[self.at(number, row, chunk), :] = value

        flow = [read(n) for n in range(3)]
        field = [read(n) for n in range(3, 6)]
        current = self.curl(read, 3, prepared)
        spin = self.curl(read, 0, prepared)
        induced = cross(flow, field)
        warm = self.slope(read, 6, prepared)
        for n in range(3):
            put(n, current[n])
            put(3 + n, spin[n])
            put(6 + n, induced[n] - ETA_COEF * current[n])
            put(9 + n, warm[n])
        put(12, read(7) + 0.5 * dot(flow, flow))

    def second_pass(self, row, chunk, emit):
        prepared = self.prepare(row)
        read = self.reader(self.plane_ref, row, chunk)
        work = self.reader(self.work_ref, row, chunk)
        flow = [read(n) for n in range(3)]
        field = [read(n) for n in range(3, 6)]
        current = [work(n) for n in range(3)]
        spin = [work(3 + n) for n in range(3)]
        warm = [work(9 + n) for n in range(3)]
        field_rate = self.curl(work, 6, prepared)
        spin_curl = self.curl(work, 3, prepared)
        head = self.slope(work, 12, prepared)
        lorentz = cross(current, field)
        advect = cross(flow, spin)
        speed = [advect[n] + lorentz[n] - head[n] - NU_COEF * spin_curl[n] for n in range(3)]
        speed[0] = speed[0] + ARCHIMEDES_LIFT * read(6)
        heat = KAPPA_COEF * self.outflow(work, 9, prepared) - dot(flow, warm)
        squeeze = -SOUND_SQ * self.outflow(read, 0, prepared)
        emit(row, chunk, read, speed + list(field_rate) + [heat, squeeze])

    def over(self, rows, one_row, unroll):
        def step(row, carry):
            one_row(row)
            return carry

        lax.fori_loop(*rows, step, 0, unroll=unroll)

    def everywhere(self, rows, chunks, emit):
        def first(row):
            for chunk in range(0, self.wide, 8):
                self.first_pass(row, chunk)

        def second(row):
            for chunk in chunks:
                self.second_pass(row, chunk, emit)

        self.over((rows[0] - 1, rows[1] + 1), first, 2)
        self.over(rows, second, 2)

    def along_edges(self, rows, chunks, emit):
        tall, wide = self.tall, self.wide
        low_chunk, high_chunk = chunks[0], chunks[-1]

        @pl.when(self.on_row_edge)
        def _():
            row = jnp.where(self.at_top, HALO - 1, tall - HALO - 1)
            for step in range(2):
                for chunk in range(0, wide, 8):
                    self.first_pass(row + step, chunk)

        @pl.when(self.on_col_edge)
        def _():
            chunk = pl.multiple_of(jnp.where(self.at_left, 0, wide - 8), 8)
            count = rows[1] - rows[0]
            self.over(
                (rows[0] - 1, rows[1] + 1), lambda row: self.first_pass(row, chunk), count // 2 + 1
            )

        @pl.when(self.on_row_edge)
        def _():
            row = jnp.where(self.at_top, HALO, tall - HALO - 2)
            for step in range(2):
                for chunk in chunks:
                    self.second_pass(row + step, chunk, emit)

        @pl.when(self.on_col_edge)
        def _():
            chunk = jnp.where(self.at_left, low_chunk, high_chunk)
            count = rows[1] - rows[0]
            self.over(rows, lambda row: self.second_pass(row, chunk, emit), count // 2)


def cross(x, y):
    return (
        x[1] * y[2] - x[2] * y[1],
        x[2] * y[0] - x[0] * y[2],
        x[0] * y[1] - x[1] * y[0],
    )


def dot(x, y):
    return x[0] * y[0] + x[1] * y[1] + x[2] * y[2]


def middle_state(loop, frame_ref, rate_ref):
    wide = loop.cols + 2 * HALO
    first_row = lax.axis_index("lat") * loop.rows - HALO
    first_col = lax.axis_index("lon") * loop.cols - HALO

    def emit(row, chunk, read, rate):
        in_row = (row + first_row >= 0) & (row + first_row < loop.nth)
        col = lax.broadcasted_iota(jnp.int32, (8, 128), 0) + (chunk + first_col)
        inside = (col >= jnp.where(in_row, 0, loop.nph)) & (col < loop.nph)
        for f in range(TILE):
            rate_ref[f, row, pl.ds(chunk, 8), :] = rate[f]
            start = (row * wide + chunk) * TILE + f
            frame_ref[pl.ds(start, 8, stride=TILE), :] = jnp.where(
                inside, read(f) + TIME_STEP * rate[f], 0.0
            )

    return emit


def total_change(loop, change_ref, rate_ref):
    def emit(row, chunk, read, rate):
        for f in range(TILE):
            start = ((row - HALO) * loop.cols + chunk - HALO) * TILE + f
            change_ref[pl.ds(start, 8, stride=TILE), :] = (0.5 * TIME_STEP) * (
                rate_ref[f, row, pl.ds(chunk, 8), :] + rate[f]
            )

    return emit


def first_inner_kernel(
    loop, factor_ref, radial_ref, frame_in_ref, after_ref, frame_ref, rate_ref, plane_ref, work_ref
):
    del after_ref
    part = Section(loop, factor_ref, radial_ref, plane_ref, work_ref)
    part.spread(frame_in_ref, (0, part.tall))
    part.everywhere(
        (2, part.tall - 2), range(0, part.wide, 8), middle_state(loop, frame_ref, rate_ref)
    )


def first_edge_kernel(loop, *refs):
    rim, refs = refs[:3], refs[3:]
    receive_ref, factor_ref, radial_ref = refs[:3]
    got_refs, refs = refs[7 : 7 + loop.lat_count], refs[7 + loop.lat_count :]
    frame_ref, rate_ref, plane_ref, work_ref = refs[:4]
    send_refs, value_ref = refs[4:-1], refs[-1]
    part = Section(loop, factor_ref, radial_ref, plane_ref, work_ref)
    part.scatter(receive_ref, got_refs)
    part.along_edges(
        (2, part.tall - 2), range(0, part.wide, 8), middle_state(loop, frame_ref, rate_ref)
    )
    mix_and_pack(loop, part.wide, rim, frame_ref, value_ref, send_refs)


def second_inner_kernel(
    loop, factor_ref, radial_ref, frame_ref, rate_ref, after_ref, change_ref, plane_ref, work_ref
):
    del after_ref
    part = Section(loop, factor_ref, radial_ref, plane_ref, work_ref)
    part.spread(frame_ref, (2, part.tall - 2))
    part.everywhere(
        (HALO, HALO + loop.rows),
        range(HALO, HALO + loop.cols, 8),
        total_change(loop, change_ref, rate_ref),
    )


def second_edge_kernel(loop, receive_ref, factor_ref, radial_ref, rate_ref, inner_ref, *refs):
    got_refs, refs = refs[2 : 2 + loop.lat_count], refs[2 + loop.lat_count :]
    plane_ref, work_ref, change_ref = refs
    part = Section(loop, factor_ref, radial_ref, plane_ref, work_ref)
    for row in range(loop.rows):
        here = tiles(row * loop.cols, loop.cols)
        change_ref[here, :] = inner_ref[here, :]
    part.scatter(receive_ref, got_refs)
    part.along_edges(
        (HALO, HALO + loop.rows),
        range(HALO, HALO + loop.cols, 8),
        total_change(loop, change_ref, rate_ref),
    )


def radial_factors(levels, theta_count):
    scale = 2.0 * theta_count / math.pi
    step = 0.65 * scale / levels
    radius = 0.35 * scale + (np.arange(levels) + 0.5) * step
    half = 0.5 / step
    above = np.append(radius[1:], 0.0)
    below = np.append(0.0, radius[:-1])
    ones_above = np.append(np.ones(levels - 1), 0.0)
    ones_below = np.append(0.0, np.ones(levels - 1))
    rows = np.stack(
        [
            1.0 / radius,
            half * above / radius,
            half * below / radius,
            half * ones_above,
            half * ones_below,
            half * above**2 / radius**2,
            half * below**2 / radius**2,
        ]
    )
    return np.repeat(rows[:, None, :], 8, axis=1).astype(np.float32)


def row_factors(rows, lat_count, nth, nph):
    polar_step, azimuth_step = math.pi / (2 * nth), 1.5 * math.pi / nph
    tall = rows + 2 * HALO
    parts = []
    for lat in range(lat_count):
        row = lat * rows - HALO - 1 + np.arange(tall + 2)
        sines = np.sin(math.pi / 4 + (row + 0.5) * polar_step)
        middle = sines[1:-1]
        parts += [
            sines[2:] / middle * (0.5 / polar_step),
            sines[:-2] / middle * (0.5 / polar_step),
            (0.5 / azimuth_step) / middle,
        ]
    return np.concatenate(parts).astype(np.float32)


def per_device(state, rim_base, rim_weight, rim_angle, rim_target):
    _, rows, cols, fields, levels = state.shape
    lat_count, lon_count = lax.axis_size("lat"), lax.axis_size("lon")
    entries = rim_base.shape[1]
    loop = Loop(rows, cols, lat_count, lon_count, entries)
    tall, wide = rows + 2 * HALO, cols + 2 * HALO
    pitch = wide + 2 * PAD
    block = state[0].reshape(rows * cols * fields, levels)
    f32 = jnp.float32

    def tile_array(count):
        return jax.ShapeDtypeStruct((count * TILE, levels), f32)

    first_cell = rim_target[0, 0]
    other_cell = lax.ppermute(first_cell, "panel", [(0, 1), (1, 0)])

    everyone = ("panel", "lat", "lon")
    cells = state[0]
    last_first = lax.axis_index("lat") % 2 == 0
    head, tail = cells[:HALO], cells[rows - HALO :]
    send_even = jnp.where(last_first, tail, head).reshape(HALO * cols * fields, levels)
    send_odd = jnp.where(last_first, head, tail).reshape(HALO * cols * fields, levels)
    lat_even = lax.ppermute(send_even, everyone, swap_route(0, lat_count, lon_count, True))
    lat_odd = lax.ppermute(send_odd, everyone, swap_route(1, lat_count, lon_count, True))

    angle = rim_angle[0]
    corner_table, spread_weights = pl.pallas_call(
        lambda *refs: weight_kernel(loop, *refs),
        out_shape=[
            jax.ShapeDtypeStruct((8, -(-entries // 128) * 128), jnp.int32),
            jax.ShapeDtypeStruct((18 * entries + TILE, levels), f32),
        ],
        in_specs=whole(3),
        out_specs=whole(2),
        compiler_params=grant(4),
        name="weights",
    )(rim_base[0].T, rim_weight[0].T, jnp.stack([jnp.cos(angle), jnp.sin(angle)]))
    send_count = lon_count * loop.column_slots
    got_count = lat_count * lon_count * loop.slots
    send_table, swap_table, receive_table = pl.pallas_call(
        lambda *refs: table_kernel(loop, pitch, *refs),
        out_shape=[
            jax.ShapeDtypeStruct((padded_rows(count), 128), jnp.int32)
            for count in (send_count, got_count, got_count)
        ],
        in_specs=scalars(2),
        out_specs=whole(3),
        compiler_params=grant(4),
        name="tables",
    )(first_cell, other_cell)
    rim = (send_table, corner_table, spread_weights)
    swap_tables = () if loop.even_leads else (swap_table,)
    factors = jnp.asarray(row_factors(rows, lat_count, loop.nth, loop.nph))
    radial = jnp.asarray(radial_factors(levels, loop.nth))

    east_first = lax.axis_index("lon") % 2 == 0
    head, tail = cells[:, :HALO], cells[:, cols - HALO :]
    own_even = jnp.where(east_first, tail, head).reshape(rows * HALO * fields, levels)
    own_odd = jnp.where(east_first, head, tail).reshape(rows * HALO * fields, levels)
    strip_even, strip_odd = pl.pallas_call(
        lambda *refs: strip_kernel(rows, cols, *refs),
        out_shape=[tile_array(tall * HALO)] * 2,
        in_specs=whole(5),
        out_specs=whole(2),
        compiler_params=grant(4),
        name="strips",
    )(corner_table, own_even, own_odd, lat_even, lat_odd)
    lon_odd = lax.ppermute(strip_odd, everyone, swap_route(1, lat_count, lon_count, False))
    lon_even = lax.ppermute(strip_even, everyone, swap_route(0, lat_count, lon_count, False))

    frame = pl.pallas_call(
        lambda *refs: middle_kernel(rows, cols, *refs[1:]),
        out_shape=tile_array(tall * wide),
        in_specs=whole(4),
        out_specs=whole(1)[0],
        compiler_params=grant(4),
        name="middle",
    )(strip_even, block, lat_even, lat_odd)
    packed_shapes = [tile_array(loop.column_slots)] * lon_count
    frame, *packed = pl.pallas_call(
        lambda *refs: frame_kernel(loop, *refs),
        out_shape=[tile_array(tall * wide)] + packed_shapes,
        in_specs=scalars(2) + whole(4),
        out_specs=whole(1 + lon_count),
        scratch_shapes=[pltpu.VMEM((entries * TILE, levels), f32)],
        input_output_aliases={5: 0},
        compiler_params=grant(4),
        name="frame",
    )(*rim, lon_odd, lon_even, frame)

    def first_round(packed):
        got = [packed[0]] + [
            lax.ppermute(packed[step], "lon", lon_route(step, lon_count))
            for step in start_order(1, lon_count)
        ]
        return pl.pallas_call(
            lambda *refs: swap_kernel(loop, *refs),
            out_shape=[tile_array(lon_count * loop.slots)] * lat_count,
            in_specs=scalars(len(swap_tables)) + whole(lon_count),
            out_specs=whole(lat_count),
            compiler_params=grant(4),
            name="swap",
        )(*swap_tables, *got)

    def second_round(turned):
        return [
            lax.ppermute(turned[step], ("panel", "lat"), lat_route(step, lat_count))
            for step in start_order(0, lat_count)
        ]

    planes = [
        jax.ShapeDtypeStruct((fields * tall * pitch, levels), f32),
        jax.ShapeDtypeStruct((13 * tall * pitch, levels), f32),
    ]
    rates = jax.ShapeDtypeStruct((fields, tall, wide, levels), f32)

    turned = first_round(packed)
    got = second_round(turned)
    frame, rate, plane, work = pl.pallas_call(
        lambda *refs: first_inner_kernel(loop, *refs),
        out_shape=[tile_array(tall * wide), rates] + planes,
        in_specs=scalars(1) + whole(3),
        out_specs=whole(4),
        compiler_params=grant(4),
        name="first_inner",
    )(factors, radial, frame, turned[0])
    frame, rate, _, _, *packed = pl.pallas_call(
        lambda *refs: first_edge_kernel(loop, *refs),
        out_shape=[tile_array(tall * wide), rates] + planes + packed_shapes,
        in_specs=scalars(2) + whole(1) + scalars(2) + whole(5 + lat_count),
        out_specs=whole(4 + lon_count),
        scratch_shapes=[pltpu.VMEM((entries * TILE, levels), f32)],
        input_output_aliases={6: 0, 7: 1, 8: 2, 9: 3},
        compiler_params=grant(4),
        name="first_edge",
    )(*rim, receive_table, factors, radial, frame, rate, plane, work, *got)

    turned = first_round(packed)
    got = second_round(turned)
    inner, plane, work = pl.pallas_call(
        lambda *refs: second_inner_kernel(loop, *refs),
        out_shape=[tile_array(rows * cols)] + planes,
        in_specs=scalars(1) + whole(4),
        out_specs=whole(3),
        compiler_params=grant(4),
        name="second_inner",
    )(factors, radial, frame, rate, turned[0])
    _, _, change = pl.pallas_call(
        lambda *refs: second_edge_kernel(loop, *refs),
        out_shape=planes + [tile_array(rows * cols)],
        in_specs=scalars(2) + whole(5 + lat_count),
        out_specs=whole(3),
        input_output_aliases={5: 0, 6: 1},
        compiler_params=grant(4),
        name="second_edge",
    )(receive_table, factors, radial, rate, inner, plane, work, *got)
    return change.reshape(1, rows, cols, fields, levels)


def solution(mesh):
    return jax.shard_map(
        per_device,
        mesh=mesh,
        in_specs=(
            P("panel", "lat", "lon", None, None),
            P("panel", ("lat", "lon"), None),
            P("panel", ("lat", "lon"), None),
            P("panel", ("lat", "lon")),
            P("panel", None, None),
        ),
        out_specs=P("panel", "lat", "lon", None, None),
        check_vma=False,
    )
```

```python
import math

import jax
import jax.numpy as jnp
import numpy as np
from jax import lax
from jax.experimental import pallas as pl
from jax.experimental.pallas import tpu as pltpu
from jax.sharding import PartitionSpec as P

ETA_COEF = 0.2
NU_COEF = 0.2
KAPPA_COEF = 0.3
SOUND_SQ = 1.0
ARCHIMEDES_LIFT = 0.5
TIME_STEP = 0.2

HALO = 4
PAD = 8
TILE = 8


def hardest_first(step):
    return -step.bit_length(), step


def start_order(first, count):
    return sorted(range(first, count), key=hardest_first)


def by_step(first, refs):
    order = start_order(first, first + len(refs))
    return [refs[order.index(step)] for step in range(first, first + len(refs))]


def is_power_of_two(count):
    return count & (count - 1) == 0


def to_device(index, step, count):
    return index ^ step if is_power_of_two(count) else (index + step) % count


def from_device(index, step, count):
    return index ^ step if is_power_of_two(count) else (index + count - step) % count


def swap_route(parity, lat_count, lon_count, along_lat):
    count, across = (lat_count, lon_count) if along_lat else (lon_count, lat_count)
    mate = list(range(count))
    for low in range(parity, count - 1, 2):
        mate[low], mate[low + 1] = low + 1, low
    route = []
    for side in range(2):
        for lat in range(lat_count):
            for lon in range(lon_count):
                here, other = (lat, lon) if along_lat else (lon, lat)
                there = mate[here]
                if there == here:
                    other = other ^ 1 if other ^ 1 < across else other
                target = (there, other) if along_lat else (other, there)
                route.append(
                    (
                        (side * lat_count + lat) * lon_count + lon,
                        (side * lat_count + target[0]) * lon_count + target[1],
                    )
                )
    return route


def lon_route(step, count):
    return [(i, to_device(i, step, count)) for i in range(count)]


def lat_route(step, count):
    return [
        (side * count + i, (1 - side) * count + to_device(i, step, count))
        for side in range(2)
        for i in range(count)
    ]


class Loop:
    def __init__(self, rows, cols, lat_count, lon_count, entries):
        self.rows, self.cols = rows, cols
        self.lat_count, self.lon_count = lat_count, lon_count
        self.nth, self.nph = rows * lat_count, cols * lon_count
        self.total = 4 * (self.nth + self.nph)
        self.blocks = lat_count * lon_count
        self.entries = entries
        one_row = 2 * (cols + 2 * HALO)
        one_col = 2 * (rows + 2 * HALO)
        corner = 2 * (rows + cols + 2 * HALO)
        self.slots = -(-max(corner, one_row, one_col) // self.blocks)
        self.half = -(-one_row // self.blocks)
        side = 4 * (cols + HALO) + 2 * self.nth
        leads = [2 * (cols + HALO) + 2 * (n * rows - HALO) for n in range(1, lat_count)]
        self.even_leads = all(lead % self.blocks == 0 for lead in leads)
        self.column_slots = max(-(-side // self.blocks), 2 * self.half)

    def position(self, row, col):
        nth, nph = self.nth, self.nph
        top = 2 * col + row + 2
        right = 2 * nph + 2 * row + col - nph
        bottom = 2 * nph + 2 * nth + 2 * (nph - 1 - col) + row - nth
        left = 4 * nph + 2 * nth + 2 * (nth - 1 - row) + col + 2
        return jnp.where(
            row < 0, top, jnp.where(row >= nth, bottom, jnp.where(col >= nph, right, left))
        )

    def cell(self, place):
        nth, nph = self.nth, self.nph
        right = place - 2 * nph
        bottom = right - 2 * nth
        left = bottom - 2 * nph
        on_top, on_right, on_bottom = right < 0, bottom < 0, left < 0
        row = jnp.where(
            on_top,
            (place & 1) - 2,
            jnp.where(
                on_right,
                right >> 1,
                jnp.where(on_bottom, nth + (bottom & 1), nth - 1 - (left >> 1)),
            ),
        )
        col = jnp.where(
            on_top,
            place >> 1,
            jnp.where(
                on_right,
                nph + (right & 1),
                jnp.where(on_bottom, nph - 1 - (bottom >> 1), (left & 1) - 2),
            ),
        )
        return row, col

    def top_start(self, lon):
        return 2 * jnp.maximum(lon * self.cols - HALO, 0)

    def bottom_start(self, lon):
        high = jnp.minimum(lon * self.cols + self.cols + HALO, self.nph)
        return 2 * self.nph + 2 * self.nth + 2 * (self.nph - high)

    def stretch(self, lat, lon):
        nth, nph = self.nth, self.nph
        row_low = jnp.maximum(lat * self.rows - HALO, 0)
        row_high = jnp.minimum(lat * self.rows + self.rows + HALO, nth)
        col_low = jnp.maximum(lon * self.cols - HALO, 0)
        col_high = jnp.minimum(lon * self.cols + self.cols + HALO, nph)
        top, bottom = lat == 0, lat == self.lat_count - 1
        left, right = lon == 0, lon == self.lon_count - 1
        left_start = 4 * nph + 2 * nth + 2 * (nth - row_high)
        start = jnp.where(
            top & left,
            left_start,
            jnp.where(
                top,
                self.top_start(lon),
                jnp.where(
                    right,
                    2 * nph + 2 * row_low,
                    jnp.where(bottom, self.bottom_start(lon), left_start),
                ),
            ),
        )
        span = jnp.where(top | bottom, 2 * (col_high - col_low), 0) + jnp.where(
            left | right, 2 * (row_high - row_low), 0
        )
        return start, span

    def first_entry(self, start, donor, offset):
        lead = -(-2 * self.total // self.blocks)
        raised = start - donor - offset + lead * self.blocks + self.blocks - 1
        if is_power_of_two(self.blocks):
            return (raised >> (self.blocks.bit_length() - 1)) - lead
        return lax.div(raised, jnp.full_like(raised, self.blocks)) - lead

    def wrap(self, entry):
        for bound in (8, 4, 2, 1):
            entry = jnp.where(entry < 0, entry + self.entries * bound, entry)
        for bound in (8, 4, 2, 1):
            over = entry - self.entries * bound
            entry = jnp.where(over >= 0, over, entry)
        return entry

    def column_entry(self, lon, donor, offset, slot):
        side = (lon == 0) | (lon == self.lon_count - 1)
        top = self.first_entry(self.top_start(lon), donor, offset)
        bottom = self.first_entry(self.bottom_start(lon), donor, offset)
        lower = (lon == 0) | jnp.logical_not(side) & (slot >= self.half)
        skipped = jnp.where(jnp.logical_not(side) & (slot >= self.half), self.half, 0)
        return jnp.where(lower, bottom, top) + slot - skipped

    def column_slot(self, lat, lon, donor=None, offset=None):
        side = (lon == 0) | (lon == self.lon_count - 1)
        start, _ = self.stretch(lat, lon)
        column = jnp.where(lon == 0, self.bottom_start(lon), self.top_start(lon))
        if donor is None:
            ahead = lax.div(start - column, jnp.int32(self.blocks))
        else:
            ahead = self.first_entry(start, donor, offset) - self.first_entry(
                column, donor, offset
            )
        middle = jnp.where(lat == self.lat_count - 1, self.half, 0)
        return jnp.where(side, jnp.maximum(ahead, 0), middle)


def padded_rows(count):
    return -(-count // 8) * 8


def whole(count):
    return [pl.BlockSpec(memory_space=pltpu.VMEM)] * count


def scalars(count):
    return [pl.BlockSpec(memory_space=pltpu.SMEM)] * count


def lookup(table_ref, index):
    return table_ref[index, 0]


def grant(mebibytes):
    return pltpu.CompilerParams(vmem_limit_bytes=mebibytes << 20)


def tiles(index, count):
    if isinstance(index, int):
        return pl.ds(index * TILE, count * TILE)
    return pl.ds(pl.multiple_of(index * TILE, TILE), count * TILE)


def weight_kernel(loop, base_ref, weight_ref, turn_ref, corner_ref, spread_ref):
    entries = loop.entries
    diagonal = lax.broadcasted_iota(jnp.int32, (entries, entries), 0) == (
        lax.broadcasted_iota(jnp.int32, (entries, entries), 1)
    )
    for number in range(18):
        ref, row = (weight_ref, number) if number < 16 else (turn_ref, number - 16)
        column = jnp.sum(
            jnp.where(diagonal, ref[row : row + 1, :], 0.0), axis=1, keepdims=True
        )
        spread_ref[pl.ds(number * entries, entries), :] = jnp.broadcast_to(
            column, (entries, spread_ref.shape[1])
        )
    wide = loop.cols + 2 * HALO
    base = (base_ref[0:1, :] - lax.axis_index("lat") * loop.rows + HALO - 1) * wide + (
        base_ref[1:2, :] - lax.axis_index("lon") * loop.cols + HALO - 1
    )
    column = jnp.sum(
        jnp.where(diagonal, base.astype(jnp.float32), 0.0), axis=1, keepdims=True
    )
    corner_ref[pl.ds(0, entries), :] = jnp.broadcast_to(
        column, (entries, corner_ref.shape[1])
    ).astype(jnp.int32)


def digits(shape, outer, inner, slots):
    flat = lax.broadcasted_iota(jnp.int32, shape, 0)
    high = jnp.zeros(shape, jnp.int32)
    for n in range(1, outer):
        high = high + jnp.where(flat >= n * inner * slots, 1, 0)
    rest = flat - high * (inner * slots)
    middle = jnp.zeros(shape, jnp.int32)
    for n in range(1, inner):
        middle = middle + jnp.where(rest >= n * slots, 1, 0)
    return high, middle, jnp.minimum(rest - middle * slots, slots - 1)


def table_kernel(loop, pitch, cell_ref, other_ref, send_ref, receive_ref, swap_ref=None):
    lat, lon = lax.axis_index("lat"), lax.axis_index("lon")
    lat_count, lon_count = loop.lat_count, loop.lon_count
    mine = loop.position(cell_ref[0], cell_ref[1])
    other = loop.position(other_ref[0], other_ref[1])

    _, step, slot = digits(send_ref.shape, 1, lon_count, loop.column_slots)
    entry = loop.column_entry(
        to_device(lon, step, lon_count), lat * lon_count + lon, other, slot
    )
    send_ref[...] = loop.wrap(entry)

    lat_step, lon_step, slot = digits(receive_ref.shape, lat_count, lon_count, loop.slots)
    if swap_ref is not None:
        donor = lat * lon_count + from_device(lon, lon_step, lon_count)
        here = jnp.full_like(slot, lon)
        ahead = loop.column_slot(to_device(lat, lat_step, lat_count), here, donor, other)
        swap_ref[...] = jnp.minimum(ahead + slot, loop.column_slots - 1)

    donor = from_device(lat, lat_step, lat_count) * lon_count + from_device(
        lon, lon_step, lon_count
    )
    start, span = loop.stretch(jnp.full_like(slot, lat), jnp.full_like(slot, lon))
    entry = loop.first_entry(start, donor, mine) + slot
    place = entry * loop.blocks + donor + mine
    wrapped = jnp.where(place >= loop.total, place - loop.total, place)
    row, col = loop.cell(wrapped)
    spot = (row - lat * loop.rows + HALO) * pitch + PAD + (col - lon * loop.cols + HALO)
    receive_ref[...] = jnp.where(place < start + span, spot, 0)


def strip_kernel(
    rows, cols, after_ref, own_even_ref, own_odd_ref, even_ref, odd_ref, *send_refs
):
    del after_ref
    lat_even = lax.rem(lax.axis_index("lat"), 2) == 0
    lon_even = lax.rem(lax.axis_index("lon"), 2) == 0
    high = cols - HALO
    lows = (jnp.where(lon_even, high, 0), jnp.where(lon_even, 0, high))

    def copy_halo(first, source):
        for send_ref, low in zip(send_refs, lows):
            for row in range(HALO):
                send_ref[tiles((first + row) * HALO, HALO), :] = source[
                    tiles(row * cols + low, HALO), :
                ]

    for send_ref, own_ref in zip(send_refs, (own_even_ref, own_odd_ref)):
        send_ref[tiles(HALO * HALO, rows * HALO), :] = own_ref[...]

    @pl.when(lat_even)
    def _():
        copy_halo(0, odd_ref)
        copy_halo(HALO + rows, even_ref)

    @pl.when(jnp.logical_not(lat_even))
    def _():
        copy_halo(0, even_ref)
        copy_halo(HALO + rows, odd_ref)


def mix_and_pack(loop, wide, rim, frame_ref, value_ref, send_refs):
    send_table_ref, corner_ref, spread_ref = rim
    entries = loop.entries
    field = lax.broadcasted_iota(jnp.int32, (TILE, 128), 0)
    takes_next = (field == 1) | (field == 4)
    turned = takes_next | (field == 2) | (field == 5)

    def one_entry(entry, carry):
        base = lookup(corner_ref, entry)

        def over_tile(number):
            return spread_ref[pl.ds(number * entries + entry, TILE, stride=0), :]

        total = None
        for a in range(4):
            for b in range(4):
                part = over_tile(4 * a + b) * frame_ref[tiles(base + a * wide + b, 1), :]
                total = part if total is None else total + part
        cosine, sine = over_tile(16), over_tile(17)
        other = jnp.where(
            takes_next, pltpu.roll(total, TILE - 1, 0), pltpu.roll(total, 1, 0)
        )
        mixed = cosine * total + jnp.where(takes_next, -sine, sine) * other
        value_ref[tiles(entry, 1), :] = jnp.where(turned, mixed, total)
        return carry

    lax.fori_loop(0, loop.entries, one_entry, 0, unroll=4)
    for step, send_ref in enumerate(send_refs):
        for slot in range(loop.column_slots):
            entry = lookup(send_table_ref, step * loop.column_slots + slot)
            send_ref[tiles(slot, 1), :] = value_ref[tiles(entry, 1), :]


def middle_kernel(rows, cols, state_ref, lat_even_ref, lat_odd_ref, frame_ref):
    wide = cols + 2 * HALO
    lat_even = lax.rem(lax.axis_index("lat"), 2) == 0

    def copy_rows(first, count, source):
        for row in range(count):
            frame_ref[tiles((first + row) * wide + HALO, cols), :] = source[
                tiles(row * cols, cols), :
            ]

    copy_rows(HALO, rows, state_ref)

    @pl.when(lat_even)
    def _():
        copy_rows(0, HALO, lat_odd_ref)
        copy_rows(HALO + rows, HALO, lat_even_ref)

    @pl.when(jnp.logical_not(lat_even))
    def _():
        copy_rows(0, HALO, lat_even_ref)
        copy_rows(HALO + rows, HALO, lat_odd_ref)


def frame_kernel(loop, *refs):
    rim, refs = refs[:3], refs[3:]
    lon_odd_ref, lon_even_ref, _, frame_ref = refs[:4]
    send_refs, value_ref = refs[4:-1], refs[-1]
    rows, cols = loop.rows, loop.cols
    wide = cols + 2 * HALO
    lat, lon = lax.axis_index("lat"), lax.axis_index("lon")
    lon_even = lax.rem(lon, 2) == 0

    def copy_columns(source, left):
        for row in range(rows + 2 * HALO):
            frame_ref[tiles(row * wide + left, HALO), :] = source[tiles(row * HALO, HALO), :]

    @pl.when(lon_even)
    def _():
        copy_columns(lon_odd_ref, 0)
        copy_columns(lon_even_ref, HALO + cols)

    @pl.when(jnp.logical_not(lon_even))
    def _():
        copy_columns(lon_even_ref, 0)
        copy_columns(lon_odd_ref, HALO + cols)

    zeros = jnp.zeros((HALO * TILE, frame_ref.shape[1]), jnp.float32)
    for at_row, top in ((lat == 0, 0), (lat == loop.lat_count - 1, HALO + rows)):
        for at_col, left in ((lon == 0, 0), (lon == loop.lon_count - 1, HALO + cols)):

            @pl.when(at_row & at_col)
            def _():
                for row in range(HALO):
                    frame_ref[tiles((top + row) * wide + left, HALO), :] = zeros

    mix_and_pack(loop, wide, rim, frame_ref, value_ref, send_refs)


def swap_kernel(loop, *refs):
    table_ref = None
    if not loop.even_leads:
        table_ref, refs = refs[0], refs[1:]
    got_refs = [refs[0]] + by_step(1, refs[1 : loop.lon_count])
    out_refs = refs[loop.lon_count :]
    lat, lon = lax.axis_index("lat"), lax.axis_index("lon")
    for lat_step in range(loop.lat_count):
        if loop.even_leads:
            lead = loop.column_slot(to_device(lat, lat_step, loop.lat_count), lon)
            lead = jnp.minimum(lead, loop.column_slots - loop.slots)
        for lon_step in range(loop.lon_count):
            for slot in range(loop.slots):
                place = lon_step * loop.slots + slot
                if loop.even_leads:
                    source = lead + slot
                else:
                    source = lookup(table_ref, lat_step * loop.lon_count * loop.slots + place)
                out_refs[lat_step][tiles(place, 1), :] = got_refs[lon_step][tiles(source, 1), :]


class Section:
    def __init__(self, loop, factor_ref, radial_ref, plane_ref, work_ref):
        self.loop = loop
        self.tall, self.wide = loop.rows + 2 * HALO, loop.cols + 2 * HALO
        self.pitch = self.wide + 2 * PAD
        self.factor_ref, self.radial_ref = factor_ref, radial_ref
        self.plane_ref, self.work_ref = plane_ref, work_ref
        lat, lon = lax.axis_index("lat"), lax.axis_index("lon")
        self.lat = lat
        self.at_top, self.at_left = lat == 0, lon == 0
        self.on_row_edge = self.at_top | (lat == loop.lat_count - 1)
        self.on_col_edge = self.at_left | (lon == loop.lon_count - 1)

    def spread(self, frame_ref, rows):
        def one_row(row, carry):
            for chunk in range(0, self.wide, 8):
                for f in range(TILE):
                    start = (row * self.wide + chunk) * TILE + f
                    self.plane_ref[self.at(f, row, chunk), :] = frame_ref[
                        pl.ds(start, 8, stride=TILE), :
                    ]
            return carry

        lax.fori_loop(*rows, one_row, 0)

    def scatter(self, receive_ref, got_refs):
        arrivals = self.loop.lon_count * self.loop.slots
        got_refs = by_step(0, got_refs)
        for lat_step in range(self.loop.lat_count):
            for place in range(arrivals):
                spot = lookup(receive_ref, lat_step * arrivals + place)
                self.plane_ref[pl.ds(spot, TILE, stride=self.tall * self.pitch), :] = got_refs[
                    lat_step
                ][tiles(place, 1), :]

    def at(self, number, row, col):
        return pl.ds((number * self.tall + row) * self.pitch + PAD + col, 8)

    def reader(self, ref, row, col):
        def read(number, row_step=0, col_step=0):
            return ref[self.at(number, row + row_step, col + col_step), :]

        return read

    def prepare(self, row):
        factors = [
            self.factor_ref[pl.ds((self.lat * 3 + n) * self.tall + row, 8, stride=0), :]
            for n in range(3)
        ]
        inverse_radius = self.radial_ref[0]
        with_theta = inverse_radius * (self.loop.nth / math.pi)
        return factors, inverse_radius * factors[2], with_theta

    def up(self, x):
        return pltpu.roll(x, x.shape[-1] - 1, 1)

    def down(self, x):
        return pltpu.roll(x, 1, 1)

    def curl(self, read, first, prepared):
        (tu, td, ph), with_phi, with_theta = prepared
        ru, rl = self.radial_ref[1], self.radial_ref[2]
        a, b, c = first, first + 1, first + 2
        mid_b, mid_c = read(b), read(c)
        radial = self.radial_ref[0] * (
            (tu * read(c, 1) - td * read(c, -1)) - ph * (read(b, 0, 1) - read(b, 0, -1))
        )
        polar = with_phi * (read(a, 0, 1) - read(a, 0, -1)) - (
            ru * self.up(mid_c) - rl * self.down(mid_c)
        )
        azimuth = (ru * self.up(mid_b) - rl * self.down(mid_b)) - with_theta * (
            read(a, 1) - read(a, -1)
        )
        return radial, polar, azimuth

    def slope(self, read, number, prepared):
        _, with_phi, with_theta = prepared
        mid = read(number)
        return (
            self.radial_ref[3] * self.up(mid) - self.radial_ref[4] * self.down(mid),
            with_theta * (read(number, 1) - read(number, -1)),
            with_phi * (read(number, 0, 1) - read(number, 0, -1)),
        )

    def outflow(self, read, first, prepared):
        (tu, td, ph), _, _ = prepared
        mid = read(first)
        return (
            self.radial_ref[5] * self.up(mid) - self.radial_ref[6] * self.down(mid)
        ) + self.radial_ref[0] * (
            (tu * read(first + 1, 1) - td * read(first + 1, -1))
            + ph * (read(first + 2, 0, 1) - read(first + 2, 0, -1))
        )

    def first_pass(self, row, chunk):
        prepared = self.prepare(row)
        read = self.reader(self.plane_ref, row, chunk)

        def put(number, value):
            self.work_ref[self.at(number, row, chunk), :] = value

        flow = [read(n) for n in range(3)]
        field = [read(n) for n in range(3, 6)]
        current = self.curl(read, 3, prepared)
        spin = self.curl(read, 0, prepared)
        induced = cross(flow, field)
        warm = self.slope(read, 6, prepared)
        for n in range(3):
            put(n, current[n])
            put(3 + n, spin[n])
            put(6 + n, induced[n] - ETA_COEF * current[n])
            put(9 + n, warm[n])
        put(12, read(7) + 0.5 * dot(flow, flow))

    def second_pass(self, row, chunk, emit):
        prepared = self.prepare(row)
        read = self.reader(self.plane_ref, row, chunk)
        work = self.reader(self.work_ref, row, chunk)
        flow = [read(n) for n in range(3)]
        field = [read(n) for n in range(3, 6)]
        current = [work(n) for n in range(3)]
        spin = [work(3 + n) for n in range(3)]
        warm = [work(9 + n) for n in range(3)]
        field_rate = self.curl(work, 6, prepared)
        spin_curl = self.curl(work, 3, prepared)
        head = self.slope(work, 12, prepared)
        lorentz = cross(current, field)
        advect = cross(flow, spin)
        speed = [advect[n] + lorentz[n] - head[n] - NU_COEF * spin_curl[n] for n in range(3)]
        speed[0] = speed[0] + ARCHIMEDES_LIFT * read(6)
        heat = KAPPA_COEF * self.outflow(work, 9, prepared) - dot(flow, warm)
        squeeze = -SOUND_SQ * self.outflow(read, 0, prepared)
        emit(row, chunk, read, speed + list(field_rate) + [heat, squeeze])

    def over(self, rows, one_row, unroll):
        def step(row, carry):
            one_row(row)
            return carry

        lax.fori_loop(*rows, step, 0, unroll=unroll)

    def everywhere(self, rows, chunks, emit):
        def first(row):
            for chunk in range(0, self.wide, 8):
                self.first_pass(row, chunk)

        def second(row):
            for chunk in chunks:
                self.second_pass(row, chunk, emit)

        self.over((rows[0] - 1, rows[1] + 1), first, 2)
        self.over(rows, second, 2)

    def along_edges(self, rows, chunks, emit):
        tall, wide = self.tall, self.wide
        low_chunk, high_chunk = chunks[0], chunks[-1]

        @pl.when(self.on_row_edge)
        def _():
            row = jnp.where(self.at_top, HALO - 1, tall - HALO - 1)
            for step in range(2):
                for chunk in range(0, wide, 8):
                    self.first_pass(row + step, chunk)

        @pl.when(self.on_col_edge)
        def _():
            chunk = pl.multiple_of(jnp.where(self.at_left, 0, wide - 8), 8)
            count = rows[1] - rows[0]
            self.over(
                (rows[0] - 1, rows[1] + 1), lambda row: self.first_pass(row, chunk), count // 2 + 1
            )

        @pl.when(self.on_row_edge)
        def _():
            row = jnp.where(self.at_top, HALO, tall - HALO - 2)
            for step in range(2):
                for chunk in chunks:
                    self.second_pass(row + step, chunk, emit)

        @pl.when(self.on_col_edge)
        def _():
            chunk = jnp.where(self.at_left, low_chunk, high_chunk)
            count = rows[1] - rows[0]
            self.over(rows, lambda row: self.second_pass(row, chunk, emit), count // 2)


def cross(x, y):
    return (
        x[1] * y[2] - x[2] * y[1],
        x[2] * y[0] - x[0] * y[2],
        x[0] * y[1] - x[1] * y[0],
    )


def dot(x, y):
    return x[0] * y[0] + x[1] * y[1] + x[2] * y[2]


def middle_state(loop, frame_ref, rate_ref):
    wide = loop.cols + 2 * HALO
    first_row = lax.axis_index("lat") * loop.rows - HALO
    first_col = lax.axis_index("lon") * loop.cols - HALO

    def emit(row, chunk, read, rate):
        in_row = (row + first_row >= 0) & (row + first_row < loop.nth)
        col = lax.broadcasted_iota(jnp.int32, (8, 128), 0) + (chunk + first_col)
        inside = (col >= jnp.where(in_row, 0, loop.nph)) & (col < loop.nph)
        for f in range(TILE):
            rate_ref[f, row, pl.ds(chunk, 8), :] = rate[f]
            start = (row * wide + chunk) * TILE + f
            frame_ref[pl.ds(start, 8, stride=TILE), :] = jnp.where(
                inside, read(f) + TIME_STEP * rate[f], 0.0
            )

    return emit


def total_change(loop, change_ref, rate_ref):
    def emit(row, chunk, read, rate):
        for f in range(TILE):
            start = ((row - HALO) * loop.cols + chunk - HALO) * TILE + f
            change_ref[pl.ds(start, 8, stride=TILE), :] = (0.5 * TIME_STEP) * (
                rate_ref[f, row, pl.ds(chunk, 8), :] + rate[f]
            )

    return emit


def first_inner_kernel(
    loop, factor_ref, radial_ref, frame_in_ref, after_ref, frame_ref, rate_ref, plane_ref, work_ref
):
    del after_ref
    part = Section(loop, factor_ref, radial_ref, plane_ref, work_ref)
    part.spread(frame_in_ref, (0, part.tall))
    part.everywhere(
        (2, part.tall - 2), range(0, part.wide, 8), middle_state(loop, frame_ref, rate_ref)
    )


def first_edge_kernel(loop, *refs):
    rim, refs = refs[:3], refs[3:]
    receive_ref, factor_ref, radial_ref = refs[:3]
    got_refs, refs = refs[7 : 7 + loop.lat_count], refs[7 + loop.lat_count :]
    frame_ref, rate_ref, plane_ref, work_ref = refs[:4]
    send_refs, value_ref = refs[4:-1], refs[-1]
    part = Section(loop, factor_ref, radial_ref, plane_ref, work_ref)
    part.scatter(receive_ref, got_refs)
    part.along_edges(
        (2, part.tall - 2), range(0, part.wide, 8), middle_state(loop, frame_ref, rate_ref)
    )
    mix_and_pack(loop, part.wide, rim, frame_ref, value_ref, send_refs)


def second_inner_kernel(
    loop, factor_ref, radial_ref, frame_ref, rate_ref, after_ref, change_ref, plane_ref, work_ref
):
    del after_ref
    part = Section(loop, factor_ref, radial_ref, plane_ref, work_ref)
    part.spread(frame_ref, (2, part.tall - 2))
    part.everywhere(
        (HALO, HALO + loop.rows),
        range(HALO, HALO + loop.cols, 8),
        total_change(loop, change_ref, rate_ref),
    )


def second_edge_kernel(loop, receive_ref, factor_ref, radial_ref, rate_ref, inner_ref, *refs):
    got_refs, refs = refs[2 : 2 + loop.lat_count], refs[2 + loop.lat_count :]
    plane_ref, work_ref, change_ref = refs
    part = Section(loop, factor_ref, radial_ref, plane_ref, work_ref)
    for row in range(loop.rows):
        here = tiles(row * loop.cols, loop.cols)
        change_ref[here, :] = inner_ref[here, :]
    part.scatter(receive_ref, got_refs)
    part.along_edges(
        (HALO, HALO + loop.rows),
        range(HALO, HALO + loop.cols, 8),
        total_change(loop, change_ref, rate_ref),
    )


def radial_factors(levels, theta_count):
    scale = 2.0 * theta_count / math.pi
    step = 0.65 * scale / levels
    radius = 0.35 * scale + (np.arange(levels) + 0.5) * step
    half = 0.5 / step
    above = np.append(radius[1:], 0.0)
    below = np.append(0.0, radius[:-1])
    ones_above = np.append(np.ones(levels - 1), 0.0)
    ones_below = np.append(0.0, np.ones(levels - 1))
    rows = np.stack(
        [
            1.0 / radius,
            half * above / radius,
            half * below / radius,
            half * ones_above,
            half * ones_below,
            half * above**2 / radius**2,
            half * below**2 / radius**2,
        ]
    )
    return np.repeat(rows[:, None, :], 8, axis=1).astype(np.float32)


def row_factors(rows, lat_count, nth, nph, levels):
    polar_step, azimuth_step = math.pi / (2 * nth), 1.5 * math.pi / nph
    tall = rows + 2 * HALO
    parts = []
    for lat in range(lat_count):
        row = lat * rows - HALO - 1 + np.arange(tall + 2)
        sines = np.sin(math.pi / 4 + (row + 0.5) * polar_step)
        middle = sines[1:-1]
        parts += [
            sines[2:] / middle * (0.5 / polar_step),
            sines[:-2] / middle * (0.5 / polar_step),
            (0.5 / azimuth_step) / middle,
        ]
    flat = np.concatenate(parts + [np.zeros(8)]).astype(np.float32)
    return np.repeat(flat[:, None], levels, axis=1)


def per_device(state, rim_base, rim_weight, rim_angle, rim_target):
    _, rows, cols, fields, levels = state.shape
    lat_count, lon_count = lax.axis_size("lat"), lax.axis_size("lon")
    entries = rim_base.shape[1]
    loop = Loop(rows, cols, lat_count, lon_count, entries)
    tall, wide = rows + 2 * HALO, cols + 2 * HALO
    pitch = wide + 2 * PAD
    block = state[0].reshape(rows * cols * fields, levels)
    f32 = jnp.float32

    def tile_array(count):
        return jax.ShapeDtypeStruct((count * TILE, levels), f32)

    first_cell = rim_target[0, 0]
    other_cell = lax.ppermute(first_cell, "panel", [(0, 1), (1, 0)])

    everyone = ("panel", "lat", "lon")
    cells = state[0]
    last_first = lax.axis_index("lat") % 2 == 0
    head, tail = cells[:HALO], cells[rows - HALO :]
    send_even = jnp.where(last_first, tail, head).reshape(HALO * cols * fields, levels)
    send_odd = jnp.where(last_first, head, tail).reshape(HALO * cols * fields, levels)
    lat_even = lax.ppermute(send_even, everyone, swap_route(0, lat_count, lon_count, True))
    lat_odd = lax.ppermute(send_odd, everyone, swap_route(1, lat_count, lon_count, True))

    angle = rim_angle[0]
    corner_table, spread_weights = pl.pallas_call(
        lambda *refs: weight_kernel(loop, *refs),
        out_shape=[
            jax.ShapeDtypeStruct((padded_rows(entries), 128), jnp.int32),
            jax.ShapeDtypeStruct((18 * entries + TILE, levels), f32),
        ],
        in_specs=whole(3),
        out_specs=whole(2),
        compiler_params=grant(4),
        name="weights",
    )(rim_base[0].T, rim_weight[0].T, jnp.stack([jnp.cos(angle), jnp.sin(angle)]))
    send_count = lon_count * loop.column_slots
    got_count = lat_count * lon_count * loop.slots
    counts = [send_count, got_count] + [got_count] * (not loop.even_leads)
    send_table, receive_table, *swap_tables = pl.pallas_call(
        lambda *refs: table_kernel(loop, pitch, *refs),
        out_shape=[
            jax.ShapeDtypeStruct((padded_rows(count), 128), jnp.int32) for count in counts
        ],
        in_specs=scalars(2),
        out_specs=whole(len(counts)),
        compiler_params=grant(4),
        name="tables",
    )(first_cell, other_cell)
    rim = (send_table, corner_table, spread_weights)
    factors = jnp.asarray(row_factors(rows, lat_count, loop.nth, loop.nph, levels))
    radial = jnp.asarray(radial_factors(levels, loop.nth))

    east_first = lax.axis_index("lon") % 2 == 0
    head, tail = cells[:, :HALO], cells[:, cols - HALO :]
    own_even = jnp.where(east_first, tail, head).reshape(rows * HALO * fields, levels)
    own_odd = jnp.where(east_first, head, tail).reshape(rows * HALO * fields, levels)
    strip_even, strip_odd = pl.pallas_call(
        lambda *refs: strip_kernel(rows, cols, *refs),
        out_shape=[tile_array(tall * HALO)] * 2,
        in_specs=whole(5),
        out_specs=whole(2),
        compiler_params=grant(4),
        name="strips",
    )(corner_table, own_even, own_odd, lat_even, lat_odd)
    lon_odd = lax.ppermute(strip_odd, everyone, swap_route(1, lat_count, lon_count, False))
    lon_even = lax.ppermute(strip_even, everyone, swap_route(0, lat_count, lon_count, False))

    frame = pl.pallas_call(
        lambda *refs: middle_kernel(rows, cols, *refs[1:]),
        out_shape=tile_array(tall * wide),
        in_specs=whole(4),
        out_specs=whole(1)[0],
        compiler_params=grant(4),
        name="middle",
    )(strip_even, block, lat_even, lat_odd)
    packed_shapes = [tile_array(loop.column_slots)] * lon_count
    frame, *packed = pl.pallas_call(
        lambda *refs: frame_kernel(loop, *refs),
        out_shape=[tile_array(tall * wide)] + packed_shapes,
        in_specs=whole(6),
        out_specs=whole(1 + lon_count),
        scratch_shapes=[pltpu.VMEM((entries * TILE, levels), f32)],
        input_output_aliases={5: 0},
        compiler_params=grant(4),
        name="frame",
    )(*rim, lon_odd, lon_even, frame)

    def first_round(packed):
        got = [packed[0]] + [
            lax.ppermute(packed[step], "lon", lon_route(step, lon_count))
            for step in start_order(1, lon_count)
        ]
        return pl.pallas_call(
            lambda *refs: swap_kernel(loop, *refs),
            out_shape=[tile_array(lon_count * loop.slots)] * lat_count,
            in_specs=whole(len(swap_tables) + lon_count),
            out_specs=whole(lat_count),
            compiler_params=grant(4),
            name="swap",
        )(*swap_tables, *got)

    def second_round(turned):
        return [
            lax.ppermute(turned[step], ("panel", "lat"), lat_route(step, lat_count))
            for step in start_order(0, lat_count)
        ]

    planes = [
        jax.ShapeDtypeStruct((fields * tall * pitch, levels), f32),
        jax.ShapeDtypeStruct((13 * tall * pitch, levels), f32),
    ]
    rates = jax.ShapeDtypeStruct((fields, tall, wide, levels), f32)

    turned = first_round(packed)
    got = second_round(turned)
    frame, rate, plane, work = pl.pallas_call(
        lambda *refs: first_inner_kernel(loop, *refs),
        out_shape=[tile_array(tall * wide), rates] + planes,
        in_specs=whole(4),
        out_specs=whole(4),
        compiler_params=grant(4),
        name="first_inner",
    )(factors, radial, frame, turned[0])
    frame, rate, _, _, *packed = pl.pallas_call(
        lambda *refs: first_edge_kernel(loop, *refs),
        out_shape=[tile_array(tall * wide), rates] + planes + packed_shapes,
        in_specs=whole(10 + lat_count),
        out_specs=whole(4 + lon_count),
        scratch_shapes=[pltpu.VMEM((entries * TILE, levels), f32)],
        input_output_aliases={6: 0, 7: 1, 8: 2, 9: 3},
        compiler_params=grant(4),
        name="first_edge",
    )(*rim, receive_table, factors, radial, frame, rate, plane, work, *got)

    turned = first_round(packed)
    got = second_round(turned)
    inner, plane, work = pl.pallas_call(
        lambda *refs: second_inner_kernel(loop, *refs),
        out_shape=[tile_array(rows * cols)] + planes,
        in_specs=whole(5),
        out_specs=whole(3),
        compiler_params=grant(4),
        name="second_inner",
    )(factors, radial, frame, rate, turned[0])
    _, _, change = pl.pallas_call(
        lambda *refs: second_edge_kernel(loop, *refs),
        out_shape=planes + [tile_array(rows * cols)],
        in_specs=whole(7 + lat_count),
        out_specs=whole(3),
        input_output_aliases={5: 0, 6: 1},
        compiler_params=grant(4),
        name="second_edge",
    )(receive_table, factors, radial, rate, inner, plane, work, *got)
    return change.reshape(1, rows, cols, fields, levels)


def solution(mesh):
    return jax.shard_map(
        per_device,
        mesh=mesh,
        in_specs=(
            P("panel", "lat", "lon", None, None),
            P("panel", ("lat", "lon"), None),
            P("panel", ("lat", "lon"), None),
            P("panel", ("lat", "lon")),
            P("panel", None, None),
        ),
        out_specs=P("panel", "lat", "lon", None, None),
        check_vma=False,
    )
```

```python
import math

import jax
import jax.numpy as jnp
import numpy as np
from jax import lax
from jax.experimental import pallas as pl
from jax.experimental.pallas import tpu as pltpu
from jax.sharding import PartitionSpec as P

ETA_COEF = 0.2
NU_COEF = 0.2
KAPPA_COEF = 0.3
SOUND_SQ = 1.0
ARCHIMEDES_LIFT = 0.5
TIME_STEP = 0.2

HALO = 4
PAD = 8
TILE = 8


def hardest_first(step):
    return -step.bit_length(), step


def start_order(first, count):
    return sorted(range(first, count), key=hardest_first)


def by_step(first, refs):
    order = start_order(first, first + len(refs))
    return [refs[order.index(step)] for step in range(first, first + len(refs))]


def is_power_of_two(count):
    return count & (count - 1) == 0


def to_device(index, step, count):
    return index ^ step if is_power_of_two(count) else (index + step) % count


def from_device(index, step, count):
    return index ^ step if is_power_of_two(count) else (index + count - step) % count


def swap_route(parity, lat_count, lon_count, along_lat):
    count, across = (lat_count, lon_count) if along_lat else (lon_count, lat_count)
    mate = list(range(count))
    for low in range(parity, count - 1, 2):
        mate[low], mate[low + 1] = low + 1, low
    route = []
    for side in range(2):
        for lat in range(lat_count):
            for lon in range(lon_count):
                here, other = (lat, lon) if along_lat else (lon, lat)
                there = mate[here]
                if there == here:
                    other = other ^ 1 if other ^ 1 < across else other
                target = (there, other) if along_lat else (other, there)
                route.append(
                    (
                        (side * lat_count + lat) * lon_count + lon,
                        (side * lat_count + target[0]) * lon_count + target[1],
                    )
                )
    return route


def lon_route(step, count):
    return [(i, to_device(i, step, count)) for i in range(count)]


def lat_route(step, lat_count, lon_count):
    route = []
    inner = set(range(1, lat_count - 1))
    for side in range(2):
        for lon in range(lon_count):
            target = {lat: (1 - side, to_device(lat, step, lat_count), lon) for lat in range(lat_count)}
            if 0 < lon < lon_count - 1 and lon_count % 2 == 0:
                idle = {lat for lat in target if target[lat][1] in inner}
                mate = (lon - 1 ^ 1) + 1
                for lat in idle & inner:
                    target[lat] = (side, lat, mate)
                for lat, free in zip(sorted(idle - inner), sorted(inner - idle)):
                    target[lat] = (side, free, lon)
            for lat, (there, row, col) in target.items():
                route.append(
                    (
                        (side * lat_count + lat) * lon_count + lon,
                        (there * lat_count + row) * lon_count + col,
                    )
                )
    assert len({there for _, there in route}) == len(route)
    return route


class Loop:
    def __init__(self, rows, cols, lat_count, lon_count, entries):
        self.rows, self.cols = rows, cols
        self.lat_count, self.lon_count = lat_count, lon_count
        self.nth, self.nph = rows * lat_count, cols * lon_count
        self.total = 4 * (self.nth + self.nph)
        self.blocks = lat_count * lon_count
        self.entries = entries
        one_row = 2 * (cols + 2 * HALO)
        one_col = 2 * (rows + 2 * HALO)
        corner = 2 * (rows + cols + 2 * HALO)
        self.slots = -(-max(corner, one_row, one_col) // self.blocks)
        self.half = -(-one_row // self.blocks)
        side = 4 * (cols + HALO) + 2 * self.nth
        leads = [2 * (cols + HALO) + 2 * (n * rows - HALO) for n in range(1, lat_count)]
        self.even_leads = all(lead % self.blocks == 0 for lead in leads)
        self.column_slots = max(-(-side // self.blocks), 2 * self.half)

    def position(self, row, col):
        nth, nph = self.nth, self.nph
        top = 2 * col + row + 2
        right = 2 * nph + 2 * row + col - nph
        bottom = 2 * nph + 2 * nth + 2 * (nph - 1 - col) + row - nth
        left = 4 * nph + 2 * nth + 2 * (nth - 1 - row) + col + 2
        return jnp.where(
            row < 0, top, jnp.where(row >= nth, bottom, jnp.where(col >= nph, right, left))
        )

    def cell(self, place):
        nth, nph = self.nth, self.nph
        right = place - 2 * nph
        bottom = right - 2 * nth
        left = bottom - 2 * nph
        on_top, on_right, on_bottom = right < 0, bottom < 0, left < 0
        row = jnp.where(
            on_top,
            (place & 1) - 2,
            jnp.where(
                on_right,
                right >> 1,
                jnp.where(on_bottom, nth + (bottom & 1), nth - 1 - (left >> 1)),
            ),
        )
        col = jnp.where(
            on_top,
            place >> 1,
            jnp.where(
                on_right,
                nph + (right & 1),
                jnp.where(on_bottom, nph - 1 - (bottom >> 1), (left & 1) - 2),
            ),
        )
        return row, col

    def top_start(self, lon):
        return 2 * jnp.maximum(lon * self.cols - HALO, 0)

    def bottom_start(self, lon):
        high = jnp.minimum(lon * self.cols + self.cols + HALO, self.nph)
        return 2 * self.nph + 2 * self.nth + 2 * (self.nph - high)

    def stretch(self, lat, lon):
        nth, nph = self.nth, self.nph
        row_low = jnp.maximum(lat * self.rows - HALO, 0)
        row_high = jnp.minimum(lat * self.rows + self.rows + HALO, nth)
        col_low = jnp.maximum(lon * self.cols - HALO, 0)
        col_high = jnp.minimum(lon * self.cols + self.cols + HALO, nph)
        top, bottom = lat == 0, lat == self.lat_count - 1
        left, right = lon == 0, lon == self.lon_count - 1
        left_start = 4 * nph + 2 * nth + 2 * (nth - row_high)
        start = jnp.where(
            top & left,
            left_start,
            jnp.where(
                top,
                self.top_start(lon),
                jnp.where(
                    right,
                    2 * nph + 2 * row_low,
                    jnp.where(bottom, self.bottom_start(lon), left_start),
                ),
            ),
        )
        span = jnp.where(top | bottom, 2 * (col_high - col_low), 0) + jnp.where(
            left | right, 2 * (row_high - row_low), 0
        )
        return start, span

    def first_entry(self, start, donor, offset):
        lead = -(-2 * self.total // self.blocks)
        raised = start - donor - offset + lead * self.blocks + self.blocks - 1
        if is_power_of_two(self.blocks):
            return (raised >> (self.blocks.bit_length() - 1)) - lead
        return lax.div(raised, jnp.full_like(raised, self.blocks)) - lead

    def wrap(self, entry):
        for bound in (8, 4, 2, 1):
            entry = jnp.where(entry < 0, entry + self.entries * bound, entry)
        for bound in (8, 4, 2, 1):
            over = entry - self.entries * bound
            entry = jnp.where(over >= 0, over, entry)
        return entry

    def column_entry(self, lon, donor, offset, slot):
        side = (lon == 0) | (lon == self.lon_count - 1)
        top = self.first_entry(self.top_start(lon), donor, offset)
        bottom = self.first_entry(self.bottom_start(lon), donor, offset)
        lower = (lon == 0) | jnp.logical_not(side) & (slot >= self.half)
        skipped = jnp.where(jnp.logical_not(side) & (slot >= self.half), self.half, 0)
        return jnp.where(lower, bottom, top) + slot - skipped

    def column_slot(self, lat, lon, donor=None, offset=None):
        side = (lon == 0) | (lon == self.lon_count - 1)
        start, _ = self.stretch(lat, lon)
        column = jnp.where(lon == 0, self.bottom_start(lon), self.top_start(lon))
        if donor is None:
            ahead = lax.div(start - column, jnp.int32(self.blocks))
        else:
            ahead = self.first_entry(start, donor, offset) - self.first_entry(
                column, donor, offset
            )
        middle = jnp.where(lat == self.lat_count - 1, self.half, 0)
        return jnp.where(side, jnp.maximum(ahead, 0), middle)


def padded_rows(count):
    return -(-count // 8) * 8


def whole(count):
    return [pl.BlockSpec(memory_space=pltpu.VMEM)] * count


def scalars(count):
    return [pl.BlockSpec(memory_space=pltpu.SMEM)] * count


def lookup(table_ref, index):
    return table_ref[index, 0]


def grant(mebibytes):
    return pltpu.CompilerParams(vmem_limit_bytes=mebibytes << 20)


def tiles(index, count):
    if isinstance(index, int):
        return pl.ds(index * TILE, count * TILE)
    return pl.ds(pl.multiple_of(index * TILE, TILE), count * TILE)


def weight_kernel(loop, base_ref, weight_ref, turn_ref, corner_ref, spread_ref):
    entries = loop.entries
    diagonal = lax.broadcasted_iota(jnp.int32, (entries, entries), 0) == (
        lax.broadcasted_iota(jnp.int32, (entries, entries), 1)
    )
    for number in range(18):
        ref, row = (weight_ref, number) if number < 16 else (turn_ref, number - 16)
        column = jnp.sum(
            jnp.where(diagonal, ref[row : row + 1, :], 0.0), axis=1, keepdims=True
        )
        spread_ref[pl.ds(number * entries, entries), :] = jnp.broadcast_to(
            column, (entries, spread_ref.shape[1])
        )
    wide = loop.cols + 2 * HALO
    base = (base_ref[0:1, :] - lax.axis_index("lat") * loop.rows + HALO - 1) * wide + (
        base_ref[1:2, :] - lax.axis_index("lon") * loop.cols + HALO - 1
    )
    column = jnp.sum(
        jnp.where(diagonal, base.astype(jnp.float32), 0.0), axis=1, keepdims=True
    )
    corner_ref[pl.ds(0, entries), :] = jnp.broadcast_to(
        column, (entries, corner_ref.shape[1])
    ).astype(jnp.int32)


def digits(shape, outer, inner, slots):
    flat = lax.broadcasted_iota(jnp.int32, shape, 0)
    high = jnp.zeros(shape, jnp.int32)
    for n in range(1, outer):
        high = high + jnp.where(flat >= n * inner * slots, 1, 0)
    rest = flat - high * (inner * slots)
    middle = jnp.zeros(shape, jnp.int32)
    for n in range(1, inner):
        middle = middle + jnp.where(rest >= n * slots, 1, 0)
    return high, middle, jnp.minimum(rest - middle * slots, slots - 1)


def table_kernel(loop, pitch, cell_ref, other_ref, send_ref, receive_ref, swap_ref=None):
    lat, lon = lax.axis_index("lat"), lax.axis_index("lon")
    lat_count, lon_count = loop.lat_count, loop.lon_count
    mine = loop.position(cell_ref[0], cell_ref[1])
    other = loop.position(other_ref[0], other_ref[1])

    _, step, slot = digits(send_ref.shape, 1, lon_count, loop.column_slots)
    entry = loop.column_entry(
        to_device(lon, step, lon_count), lat * lon_count + lon, other, slot
    )
    send_ref[...] = loop.wrap(entry)

    lat_step, lon_step, slot = digits(receive_ref.shape, lat_count, lon_count, loop.slots)
    if swap_ref is not None:
        donor = lat * lon_count + from_device(lon, lon_step, lon_count)
        here = jnp.full_like(slot, lon)
        ahead = loop.column_slot(to_device(lat, lat_step, lat_count), here, donor, other)
        swap_ref[...] = jnp.minimum(ahead + slot, loop.column_slots - 1)

    donor = from_device(lat, lat_step, lat_count) * lon_count + from_device(
        lon, lon_step, lon_count
    )
    start, span = loop.stretch(jnp.full_like(slot, lat), jnp.full_like(slot, lon))
    entry = loop.first_entry(start, donor, mine) + slot
    place = entry * loop.blocks + donor + mine
    wrapped = jnp.where(place >= loop.total, place - loop.total, place)
    row, col = loop.cell(wrapped)
    spot = (row - lat * loop.rows + HALO) * pitch + PAD + (col - lon * loop.cols + HALO)
    receive_ref[...] = jnp.where(place < start + span, spot, 0)


def strip_kernel(
    rows, cols, after_ref, own_even_ref, own_odd_ref, even_ref, odd_ref, *send_refs
):
    del after_ref
    lat_even = lax.rem(lax.axis_index("lat"), 2) == 0
    lon_even = lax.rem(lax.axis_index("lon"), 2) == 0
    high = cols - HALO
    lows = (jnp.where(lon_even, high, 0), jnp.where(lon_even, 0, high))

    def copy_halo(first, source):
        for send_ref, low in zip(send_refs, lows):
            for row in range(HALO):
                send_ref[tiles((first + row) * HALO, HALO), :] = source[
                    tiles(row * cols + low, HALO), :
                ]

    for send_ref, own_ref in zip(send_refs, (own_even_ref, own_odd_ref)):
        send_ref[tiles(HALO * HALO, rows * HALO), :] = own_ref[...]

    @pl.when(lat_even)
    def _():
        copy_halo(0, odd_ref)
        copy_halo(HALO + rows, even_ref)

    @pl.when(jnp.logical_not(lat_even))
    def _():
        copy_halo(0, even_ref)
        copy_halo(HALO + rows, odd_ref)


def mix_and_pack(loop, wide, rim, frame_ref, value_ref, send_refs):
    send_table_ref, corner_ref, spread_ref = rim
    entries = loop.entries
    field = lax.broadcasted_iota(jnp.int32, (TILE, 128), 0)
    takes_next = (field == 1) | (field == 4)
    turned = takes_next | (field == 2) | (field == 5)

    def one_entry(entry, carry):
        base = lookup(corner_ref, entry)

        def over_tile(number):
            return spread_ref[pl.ds(number * entries + entry, TILE, stride=0), :]

        total = None
        for a in range(4):
            for b in range(4):
                part = over_tile(4 * a + b) * frame_ref[tiles(base + a * wide + b, 1), :]
                total = part if total is None else total + part
        cosine, sine = over_tile(16), over_tile(17)
        other = jnp.where(
            takes_next, pltpu.roll(total, TILE - 1, 0), pltpu.roll(total, 1, 0)
        )
        mixed = cosine * total + jnp.where(takes_next, -sine, sine) * other
        value_ref[tiles(entry, 1), :] = jnp.where(turned, mixed, total)
        return carry

    lax.fori_loop(0, loop.entries, one_entry, 0, unroll=4)
    for step, send_ref in enumerate(send_refs):
        for slot in range(loop.column_slots):
            entry = lookup(send_table_ref, step * loop.column_slots + slot)
            send_ref[tiles(slot, 1), :] = value_ref[tiles(entry, 1), :]


def middle_kernel(rows, cols, state_ref, lat_even_ref, lat_odd_ref, frame_ref):
    wide = cols + 2 * HALO
    lat_even = lax.rem(lax.axis_index("lat"), 2) == 0

    def copy_rows(first, count, source):
        for row in range(count):
            frame_ref[tiles((first + row) * wide + HALO, cols), :] = source[
                tiles(row * cols, cols), :
            ]

    copy_rows(HALO, rows, state_ref)

    @pl.when(lat_even)
    def _():
        copy_rows(0, HALO, lat_odd_ref)
        copy_rows(HALO + rows, HALO, lat_even_ref)

    @pl.when(jnp.logical_not(lat_even))
    def _():
        copy_rows(0, HALO, lat_even_ref)
        copy_rows(HALO + rows, HALO, lat_odd_ref)


def frame_kernel(loop, *refs):
    rim, refs = refs[:3], refs[3:]
    lon_odd_ref, lon_even_ref, _, frame_ref = refs[:4]
    send_refs, value_ref = refs[4:-1], refs[-1]
    rows, cols = loop.rows, loop.cols
    wide = cols + 2 * HALO
    lat, lon = lax.axis_index("lat"), lax.axis_index("lon")
    lon_even = lax.rem(lon, 2) == 0

    def copy_columns(source, left):
        for row in range(rows + 2 * HALO):
            frame_ref[tiles(row * wide + left, HALO), :] = source[tiles(row * HALO, HALO), :]

    @pl.when(lon_even)
    def _():
        copy_columns(lon_odd_ref, 0)
        copy_columns(lon_even_ref, HALO + cols)

    @pl.when(jnp.logical_not(lon_even))
    def _():
        copy_columns(lon_even_ref, 0)
        copy_columns(lon_odd_ref, HALO + cols)

    zeros = jnp.zeros((HALO * TILE, frame_ref.shape[1]), jnp.float32)
    for at_row, top in ((lat == 0, 0), (lat == loop.lat_count - 1, HALO + rows)):
        for at_col, left in ((lon == 0, 0), (lon == loop.lon_count - 1, HALO + cols)):

            @pl.when(at_row & at_col)
            def _():
                for row in range(HALO):
                    frame_ref[tiles((top + row) * wide + left, HALO), :] = zeros

    mix_and_pack(loop, wide, rim, frame_ref, value_ref, send_refs)


def swap_kernel(loop, *refs):
    table_ref = None
    if not loop.even_leads:
        table_ref, refs = refs[0], refs[1:]
    got_refs = [refs[0]] + by_step(1, refs[1 : loop.lon_count])
    out_refs = refs[loop.lon_count :]
    lat, lon = lax.axis_index("lat"), lax.axis_index("lon")
    for lat_step in range(loop.lat_count):
        if loop.even_leads:
            lead = loop.column_slot(to_device(lat, lat_step, loop.lat_count), lon)
            lead = jnp.minimum(lead, loop.column_slots - loop.slots)
        for lon_step in range(loop.lon_count):
            for slot in range(loop.slots):
                place = lon_step * loop.slots + slot
                if loop.even_leads:
                    source = lead + slot
                else:
                    source = lookup(table_ref, lat_step * loop.lon_count * loop.slots + place)
                out_refs[lat_step][tiles(place, 1), :] = got_refs[lon_step][tiles(source, 1), :]


class Section:
    def __init__(self, loop, factor_ref, radial_ref, plane_ref, work_ref):
        self.loop = loop
        self.tall, self.wide = loop.rows + 2 * HALO, loop.cols + 2 * HALO
        self.pitch = self.wide + 2 * PAD
        self.factor_ref, self.radial_ref = factor_ref, radial_ref
        self.plane_ref, self.work_ref = plane_ref, work_ref
        lat, lon = lax.axis_index("lat"), lax.axis_index("lon")
        self.lat = lat
        self.at_top, self.at_left = lat == 0, lon == 0
        self.on_row_edge = self.at_top | (lat == loop.lat_count - 1)
        self.on_col_edge = self.at_left | (lon == loop.lon_count - 1)

    def spread(self, frame_ref, rows):
        def one_row(row, carry):
            for chunk in range(0, self.wide, 8):
                for f in range(TILE):
                    start = (row * self.wide + chunk) * TILE + f
                    self.plane_ref[self.at(f, row, chunk), :] = frame_ref[
                        pl.ds(start, 8, stride=TILE), :
                    ]
            return carry

        lax.fori_loop(*rows, one_row, 0)

    def scatter(self, receive_ref, got_refs):
        arrivals = self.loop.lon_count * self.loop.slots
        got_refs = by_step(0, got_refs)
        for lat_step in range(self.loop.lat_count):
            for place in range(arrivals):
                spot = lookup(receive_ref, lat_step * arrivals + place)
                self.plane_ref[pl.ds(spot, TILE, stride=self.tall * self.pitch), :] = got_refs[
                    lat_step
                ][tiles(place, 1), :]

    def at(self, number, row, col):
        return pl.ds((number * self.tall + row) * self.pitch + PAD + col, 8)

    def reader(self, ref, row, col):
        def read(number, row_step=0, col_step=0):
            return ref[self.at(number, row + row_step, col + col_step), :]

        return read

    def prepare(self, row):
        factors = [
            self.factor_ref[pl.ds((self.lat * 3 + n) * self.tall + row, 8, stride=0), :]
            for n in range(3)
        ]
        inverse_radius = self.radial_ref[0]
        with_theta = inverse_radius * (self.loop.nth / math.pi)
        return factors, inverse_radius * factors[2], with_theta

    def up(self, x):
        return pltpu.roll(x, x.shape[-1] - 1, 1)

    def down(self, x):
        return pltpu.roll(x, 1, 1)

    def curl(self, read, first, prepared):
        (tu, td, ph), with_phi, with_theta = prepared
        ru, rl = self.radial_ref[1], self.radial_ref[2]
        a, b, c = first, first + 1, first + 2
        mid_b, mid_c = read(b), read(c)
        radial = self.radial_ref[0] * (
            (tu * read(c, 1) - td * read(c, -1)) - ph * (read(b, 0, 1) - read(b, 0, -1))
        )
        polar = with_phi * (read(a, 0, 1) - read(a, 0, -1)) - (
            ru * self.up(mid_c) - rl * self.down(mid_c)
        )
        azimuth = (ru * self.up(mid_b) - rl * self.down(mid_b)) - with_theta * (
            read(a, 1) - read(a, -1)
        )
        return radial, polar, azimuth

    def slope(self, read, number, prepared):
        _, with_phi, with_theta = prepared
        mid = read(number)
        return (
            self.radial_ref[3] * self.up(mid) - self.radial_ref[4] * self.down(mid),
            with_theta * (read(number, 1) - read(number, -1)),
            with_phi * (read(number, 0, 1) - read(number, 0, -1)),
        )

    def outflow(self, read, first, prepared):
        (tu, td, ph), _, _ = prepared
        mid = read(first)
        return (
            self.radial_ref[5] * self.up(mid) - self.radial_ref[6] * self.down(mid)
        ) + self.radial_ref[0] * (
            (tu * read(first + 1, 1) - td * read(first + 1, -1))
            + ph * (read(first + 2, 0, 1) - read(first + 2, 0, -1))
        )

    def first_pass(self, row, chunk):
        prepared = self.prepare(row)
        read = self.reader(self.plane_ref, row, chunk)

        def put(number, value):
            self.work_ref[self.at(number, row, chunk), :] = value

        flow = [read(n) for n in range(3)]
        field = [read(n) for n in range(3, 6)]
        current = self.curl(read, 3, prepared)
        spin = self.curl(read, 0, prepared)
        induced = cross(flow, field)
        warm = self.slope(read, 6, prepared)
        for n in range(3):
            put(n, current[n])
            put(3 + n, spin[n])
            put(6 + n, induced[n] - ETA_COEF * current[n])
            put(9 + n, warm[n])
        put(12, read(7) + 0.5 * dot(flow, flow))

    def second_pass(self, row, chunk, emit):
        prepared = self.prepare(row)
        read = self.reader(self.plane_ref, row, chunk)
        work = self.reader(self.work_ref, row, chunk)
        flow = [read(n) for n in range(3)]
        field = [read(n) for n in range(3, 6)]
        current = [work(n) for n in range(3)]
        spin = [work(3 + n) for n in range(3)]
        warm = [work(9 + n) for n in range(3)]
        field_rate = self.curl(work, 6, prepared)
        spin_curl = self.curl(work, 3, prepared)
        head = self.slope(work, 12, prepared)
        lorentz = cross(current, field)
        advect = cross(flow, spin)
        speed = [advect[n] + lorentz[n] - head[n] - NU_COEF * spin_curl[n] for n in range(3)]
        speed[0] = speed[0] + ARCHIMEDES_LIFT * read(6)
        heat = KAPPA_COEF * self.outflow(work, 9, prepared) - dot(flow, warm)
        squeeze = -SOUND_SQ * self.outflow(read, 0, prepared)
        emit(row, chunk, read, speed + list(field_rate) + [heat, squeeze])

    def over(self, rows, one_row, unroll):
        def step(row, carry):
            one_row(row)
            return carry

        lax.fori_loop(*rows, step, 0, unroll=unroll)

    def everywhere(self, rows, chunks, emit):
        def first(row):
            for chunk in range(0, self.wide, 8):
                self.first_pass(row, chunk)

        def second(row):
            for chunk in chunks:
                self.second_pass(row, chunk, emit)

        self.over((rows[0] - 1, rows[1] + 1), first, 2)
        self.over(rows, second, 2)

    def along_edges(self, rows, chunks, emit):
        tall, wide = self.tall, self.wide
        low_chunk, high_chunk = chunks[0], chunks[-1]

        @pl.when(self.on_row_edge)
        def _():
            row = jnp.where(self.at_top, HALO - 1, tall - HALO - 1)
            for step in range(2):
                for chunk in range(0, wide, 8):
                    self.first_pass(row + step, chunk)

        @pl.when(self.on_col_edge)
        def _():
            chunk = pl.multiple_of(jnp.where(self.at_left, 0, wide - 8), 8)
            count = rows[1] - rows[0]
            self.over(
                (rows[0] - 1, rows[1] + 1), lambda row: self.first_pass(row, chunk), count // 2 + 1
            )

        @pl.when(self.on_row_edge)
        def _():
            row = jnp.where(self.at_top, HALO, tall - HALO - 2)
            for step in range(2):
                for chunk in chunks:
                    self.second_pass(row + step, chunk, emit)

        @pl.when(self.on_col_edge)
        def _():
            chunk = jnp.where(self.at_left, low_chunk, high_chunk)
            count = rows[1] - rows[0]
            self.over(rows, lambda row: self.second_pass(row, chunk, emit), count // 2)


def cross(x, y):
    return (
        x[1] * y[2] - x[2] * y[1],
        x[2] * y[0] - x[0] * y[2],
        x[0] * y[1] - x[1] * y[0],
    )


def dot(x, y):
    return x[0] * y[0] + x[1] * y[1] + x[2] * y[2]


def middle_state(loop, frame_ref, rate_ref):
    wide = loop.cols + 2 * HALO
    first_row = lax.axis_index("lat") * loop.rows - HALO
    first_col = lax.axis_index("lon") * loop.cols - HALO

    def emit(row, chunk, read, rate):
        in_row = (row + first_row >= 0) & (row + first_row < loop.nth)
        col = lax.broadcasted_iota(jnp.int32, (8, 128), 0) + (chunk + first_col)
        inside = (col >= jnp.where(in_row, 0, loop.nph)) & (col < loop.nph)
        for f in range(TILE):
            rate_ref[f, row, pl.ds(chunk, 8), :] = rate[f]
            start = (row * wide + chunk) * TILE + f
            frame_ref[pl.ds(start, 8, stride=TILE), :] = jnp.where(
                inside, read(f) + TIME_STEP * rate[f], 0.0
            )

    return emit


def total_change(loop, change_ref, rate_ref):
    def emit(row, chunk, read, rate):
        for f in range(TILE):
            start = ((row - HALO) * loop.cols + chunk - HALO) * TILE + f
            change_ref[pl.ds(start, 8, stride=TILE), :] = (0.5 * TIME_STEP) * (
                rate_ref[f, row, pl.ds(chunk, 8), :] + rate[f]
            )

    return emit


def first_inner_kernel(
    loop, factor_ref, radial_ref, frame_in_ref, after_ref, frame_ref, rate_ref, plane_ref, work_ref
):
    del after_ref
    part = Section(loop, factor_ref, radial_ref, plane_ref, work_ref)
    part.spread(frame_in_ref, (0, part.tall))
    part.everywhere(
        (2, part.tall - 2), range(0, part.wide, 8), middle_state(loop, frame_ref, rate_ref)
    )


def first_edge_kernel(loop, *refs):
    rim, refs = refs[:3], refs[3:]
    receive_ref, factor_ref, radial_ref = refs[:3]
    got_refs, refs = refs[7 : 7 + loop.lat_count], refs[7 + loop.lat_count :]
    frame_ref, rate_ref, plane_ref, work_ref = refs[:4]
    send_refs, value_ref = refs[4:-1], refs[-1]
    part = Section(loop, factor_ref, radial_ref, plane_ref, work_ref)
    part.scatter(receive_ref, got_refs)
    part.along_edges(
        (2, part.tall - 2), range(0, part.wide, 8), middle_state(loop, frame_ref, rate_ref)
    )
    mix_and_pack(loop, part.wide, rim, frame_ref, value_ref, send_refs)


def second_inner_kernel(
    loop, factor_ref, radial_ref, frame_ref, rate_ref, after_ref, change_ref, plane_ref, work_ref
):
    del after_ref
    part = Section(loop, factor_ref, radial_ref, plane_ref, work_ref)
    part.spread(frame_ref, (2, part.tall - 2))
    part.everywhere(
        (HALO, HALO + loop.rows),
        range(HALO, HALO + loop.cols, 8),
        total_change(loop, change_ref, rate_ref),
    )


def second_edge_kernel(loop, receive_ref, factor_ref, radial_ref, rate_ref, inner_ref, *refs):
    got_refs, refs = refs[2 : 2 + loop.lat_count], refs[2 + loop.lat_count :]
    plane_ref, work_ref, change_ref = refs
    part = Section(loop, factor_ref, radial_ref, plane_ref, work_ref)
    for row in range(loop.rows):
        here = tiles(row * loop.cols, loop.cols)
        change_ref[here, :] = inner_ref[here, :]
    part.scatter(receive_ref, got_refs)
    part.along_edges(
        (HALO, HALO + loop.rows),
        range(HALO, HALO + loop.cols, 8),
        total_change(loop, change_ref, rate_ref),
    )


def radial_factors(levels, theta_count):
    scale = 2.0 * theta_count / math.pi
    step = 0.65 * scale / levels
    radius = 0.35 * scale + (np.arange(levels) + 0.5) * step
    half = 0.5 / step
    above = np.append(radius[1:], 0.0)
    below = np.append(0.0, radius[:-1])
    ones_above = np.append(np.ones(levels - 1), 0.0)
    ones_below = np.append(0.0, np.ones(levels - 1))
    rows = np.stack(
        [
            1.0 / radius,
            half * above / radius,
            half * below / radius,
            half * ones_above,
            half * ones_below,
            half * above**2 / radius**2,
            half * below**2 / radius**2,
        ]
    )
    return np.repeat(rows[:, None, :], 8, axis=1).astype(np.float32)


def row_factors(rows, lat_count, nth, nph, levels):
    polar_step, azimuth_step = math.pi / (2 * nth), 1.5 * math.pi / nph
    tall = rows + 2 * HALO
    parts = []
    for lat in range(lat_count):
        row = lat * rows - HALO - 1 + np.arange(tall + 2)
        sines = np.sin(math.pi / 4 + (row + 0.5) * polar_step)
        middle = sines[1:-1]
        parts += [
            sines[2:] / middle * (0.5 / polar_step),
            sines[:-2] / middle * (0.5 / polar_step),
            (0.5 / azimuth_step) / middle,
        ]
    flat = np.concatenate(parts + [np.zeros(8)]).astype(np.float32)
    return np.repeat(flat[:, None], levels, axis=1)


def per_device(state, rim_base, rim_weight, rim_angle, rim_target):
    _, rows, cols, fields, levels = state.shape
    lat_count, lon_count = lax.axis_size("lat"), lax.axis_size("lon")
    entries = rim_base.shape[1]
    loop = Loop(rows, cols, lat_count, lon_count, entries)
    tall, wide = rows + 2 * HALO, cols + 2 * HALO
    pitch = wide + 2 * PAD
    block = state[0].reshape(rows * cols * fields, levels)
    f32 = jnp.float32

    def tile_array(count):
        return jax.ShapeDtypeStruct((count * TILE, levels), f32)

    first_cell = rim_target[0, 0]
    other_cell = lax.ppermute(first_cell, "panel", [(0, 1), (1, 0)])

    everyone = ("panel", "lat", "lon")
    cells = state[0]
    last_first = lax.axis_index("lat") % 2 == 0
    head, tail = cells[:HALO], cells[rows - HALO :]
    send_even = jnp.where(last_first, tail, head).reshape(HALO * cols * fields, levels)
    send_odd = jnp.where(last_first, head, tail).reshape(HALO * cols * fields, levels)
    lat_even = lax.ppermute(send_even, everyone, swap_route(0, lat_count, lon_count, True))
    lat_odd = lax.ppermute(send_odd, everyone, swap_route(1, lat_count, lon_count, True))

    angle = rim_angle[0]
    corner_table, spread_weights = pl.pallas_call(
        lambda *refs: weight_kernel(loop, *refs),
        out_shape=[
            jax.ShapeDtypeStruct((padded_rows(entries), 128), jnp.int32),
            jax.ShapeDtypeStruct((18 * entries + TILE, levels), f32),
        ],
        in_specs=whole(3),
        out_specs=whole(2),
        compiler_params=grant(4),
        name="weights",
    )(rim_base[0].T, rim_weight[0].T, jnp.stack([jnp.cos(angle), jnp.sin(angle)]))
    send_count = lon_count * loop.column_slots
    got_count = lat_count * lon_count * loop.slots
    counts = [send_count, got_count] + [got_count] * (not loop.even_leads)
    send_table, receive_table, *swap_tables = pl.pallas_call(
        lambda *refs: table_kernel(loop, pitch, *refs),
        out_shape=[
            jax.ShapeDtypeStruct((padded_rows(count), 128), jnp.int32) for count in counts
        ],
        in_specs=scalars(2),
        out_specs=whole(len(counts)),
        compiler_params=grant(4),
        name="tables",
    )(first_cell, other_cell)
    rim = (send_table, corner_table, spread_weights)
    factors = jnp.asarray(row_factors(rows, lat_count, loop.nth, loop.nph, levels))
    radial = jnp.asarray(radial_factors(levels, loop.nth))

    east_first = lax.axis_index("lon") % 2 == 0
    head, tail = cells[:, :HALO], cells[:, cols - HALO :]
    own_even = jnp.where(east_first, tail, head).reshape(rows * HALO * fields, levels)
    own_odd = jnp.where(east_first, head, tail).reshape(rows * HALO * fields, levels)
    strip_even, strip_odd = pl.pallas_call(
        lambda *refs: strip_kernel(rows, cols, *refs),
        out_shape=[tile_array(tall * HALO)] * 2,
        in_specs=whole(5),
        out_specs=whole(2),
        compiler_params=grant(4),
        name="strips",
    )(corner_table, own_even, own_odd, lat_even, lat_odd)
    lon_odd = lax.ppermute(strip_odd, everyone, swap_route(1, lat_count, lon_count, False))
    lon_even = lax.ppermute(strip_even, everyone, swap_route(0, lat_count, lon_count, False))

    frame = pl.pallas_call(
        lambda *refs: middle_kernel(rows, cols, *refs[1:]),
        out_shape=tile_array(tall * wide),
        in_specs=whole(4),
        out_specs=whole(1)[0],
        compiler_params=grant(4),
        name="middle",
    )(strip_even, block, lat_even, lat_odd)
    packed_shapes = [tile_array(loop.column_slots)] * lon_count
    frame, *packed = pl.pallas_call(
        lambda *refs: frame_kernel(loop, *refs),
        out_shape=[tile_array(tall * wide)] + packed_shapes,
        in_specs=whole(6),
        out_specs=whole(1 + lon_count),
        scratch_shapes=[pltpu.VMEM((entries * TILE, levels), f32)],
        input_output_aliases={5: 0},
        compiler_params=grant(4),
        name="frame",
    )(*rim, lon_odd, lon_even, frame)

    def first_round(packed):
        got = [packed[0]] + [
            lax.ppermute(packed[step], "lon", lon_route(step, lon_count))
            for step in start_order(1, lon_count)
        ]
        return pl.pallas_call(
            lambda *refs: swap_kernel(loop, *refs),
            out_shape=[tile_array(lon_count * loop.slots)] * lat_count,
            in_specs=whole(len(swap_tables) + lon_count),
            out_specs=whole(lat_count),
            compiler_params=grant(4),
            name="swap",
        )(*swap_tables, *got)

    def second_round(turned):
        return [
            lax.ppermute(turned[step], everyone, lat_route(step, lat_count, lon_count))
            for step in start_order(0, lat_count)
        ]

    planes = [
        jax.ShapeDtypeStruct((fields * tall * pitch, levels), f32),
        jax.ShapeDtypeStruct((13 * tall * pitch, levels), f32),
    ]
    rates = jax.ShapeDtypeStruct((fields, tall, wide, levels), f32)

    turned = first_round(packed)
    got = second_round(turned)
    frame, rate, plane, work = pl.pallas_call(
        lambda *refs: first_inner_kernel(loop, *refs),
        out_shape=[tile_array(tall * wide), rates] + planes,
        in_specs=whole(4),
        out_specs=whole(4),
        compiler_params=grant(4),
        name="first_inner",
    )(factors, radial, frame, turned[0])
    frame, rate, _, _, *packed = pl.pallas_call(
        lambda *refs: first_edge_kernel(loop, *refs),
        out_shape=[tile_array(tall * wide), rates] + planes + packed_shapes,
        in_specs=whole(10 + lat_count),
        out_specs=whole(4 + lon_count),
        scratch_shapes=[pltpu.VMEM((entries * TILE, levels), f32)],
        input_output_aliases={6: 0, 7: 1, 8: 2, 9: 3},
        compiler_params=grant(4),
        name="first_edge",
    )(*rim, receive_table, factors, radial, frame, rate, plane, work, *got)

    turned = first_round(packed)
    got = second_round(turned)
    inner, plane, work = pl.pallas_call(
        lambda *refs: second_inner_kernel(loop, *refs),
        out_shape=[tile_array(rows * cols)] + planes,
        in_specs=whole(5),
        out_specs=whole(3),
        compiler_params=grant(4),
        name="second_inner",
    )(factors, radial, frame, rate, turned[0])
    _, _, change = pl.pallas_call(
        lambda *refs: second_edge_kernel(loop, *refs),
        out_shape=planes + [tile_array(rows * cols)],
        in_specs=whole(7 + lat_count),
        out_specs=whole(3),
        input_output_aliases={5: 0, 6: 1},
        compiler_params=grant(4),
        name="second_edge",
    )(receive_table, factors, radial, rate, inner, plane, work, *got)
    return change.reshape(1, rows, cols, fields, levels)


def solution(mesh):
    return jax.shard_map(
        per_device,
        mesh=mesh,
        in_specs=(
            P("panel", "lat", "lon", None, None),
            P("panel", ("lat", "lon"), None),
            P("panel", ("lat", "lon"), None),
            P("panel", ("lat", "lon")),
            P("panel", None, None),
        ),
        out_specs=P("panel", "lat", "lon", None, None),
        check_vma=False,
    )
```

```python
import math

import jax
import jax.numpy as jnp
import numpy as np
from jax import lax
from jax.experimental import pallas as pl
from jax.experimental.pallas import tpu as pltpu
from jax.sharding import PartitionSpec as P

ETA_COEF = 0.2
NU_COEF = 0.2
KAPPA_COEF = 0.3
SOUND_SQ = 1.0
ARCHIMEDES_LIFT = 0.5
TIME_STEP = 0.2

HALO = 4
PAD = 8
TILE = 8


def start_order(first, count):
    down = first == 1
    odd = sorted((n for n in range(first, count) if n % 2), reverse=down)
    even = sorted((n for n in range(first, count) if n % 2 == 0), reverse=not down)
    return odd + even


def by_step(first, refs):
    order = start_order(first, first + len(refs))
    return [refs[order.index(step)] for step in range(first, first + len(refs))]


def is_power_of_two(count):
    return count & (count - 1) == 0


def to_device(index, step, count):
    return index ^ step if is_power_of_two(count) else (index + step) % count


def from_device(index, step, count):
    return index ^ step if is_power_of_two(count) else (index + count - step) % count


def swap_route(parity, lat_count, lon_count, along_lat):
    count, across = (lat_count, lon_count) if along_lat else (lon_count, lat_count)
    mate = list(range(count))
    for low in range(parity, count - 1, 2):
        mate[low], mate[low + 1] = low + 1, low
    route = []
    for side in range(2):
        for lat in range(lat_count):
            for lon in range(lon_count):
                here, other = (lat, lon) if along_lat else (lon, lat)
                there = mate[here]
                if there == here:
                    other = other ^ 1 if other ^ 1 < across else other
                target = (there, other) if along_lat else (other, there)
                route.append(
                    (
                        (side * lat_count + lat) * lon_count + lon,
                        (side * lat_count + target[0]) * lon_count + target[1],
                    )
                )
    return route


def lon_route(step, count):
    return [(i, to_device(i, step, count)) for i in range(count)]


def lat_route(step, lat_count, lon_count):
    route = []
    inner = set(range(1, lat_count - 1))
    for side in range(2):
        for lon in range(lon_count):
            target = {lat: (1 - side, to_device(lat, step, lat_count), lon) for lat in range(lat_count)}
            if 0 < lon < lon_count - 1 and lon_count % 2 == 0:
                idle = {lat for lat in target if target[lat][1] in inner}
                mate = (lon - 1 ^ 1) + 1
                for lat in idle & inner:
                    target[lat] = (side, lat, mate)
                for lat, free in zip(sorted(idle - inner), sorted(inner - idle)):
                    target[lat] = (side, free, lon)
            for lat, (there, row, col) in target.items():
                route.append(
                    (
                        (side * lat_count + lat) * lon_count + lon,
                        (there * lat_count + row) * lon_count + col,
                    )
                )
    assert len({there for _, there in route}) == len(route)
    return route


class Loop:
    def __init__(self, rows, cols, lat_count, lon_count, entries):
        self.rows, self.cols = rows, cols
        self.lat_count, self.lon_count = lat_count, lon_count
        self.nth, self.nph = rows * lat_count, cols * lon_count
        self.total = 4 * (self.nth + self.nph)
        self.blocks = lat_count * lon_count
        self.entries = entries
        one_row = 2 * (cols + 2 * HALO)
        one_col = 2 * (rows + 2 * HALO)
        corner = 2 * (rows + cols + 2 * HALO)
        self.slots = -(-max(corner, one_row, one_col) // self.blocks)
        self.half = -(-one_row // self.blocks)
        side = 4 * (cols + HALO) + 2 * self.nth
        leads = [2 * (cols + HALO) + 2 * (n * rows - HALO) for n in range(1, lat_count)]
        self.even_leads = all(lead % self.blocks == 0 for lead in leads)
        self.column_slots = max(-(-side // self.blocks), 2 * self.half)

    def position(self, row, col):
        nth, nph = self.nth, self.nph
        top = 2 * col + row + 2
        right = 2 * nph + 2 * row + col - nph
        bottom = 2 * nph + 2 * nth + 2 * (nph - 1 - col) + row - nth
        left = 4 * nph + 2 * nth + 2 * (nth - 1 - row) + col + 2
        return jnp.where(
            row < 0, top, jnp.where(row >= nth, bottom, jnp.where(col >= nph, right, left))
        )

    def cell(self, place):
        nth, nph = self.nth, self.nph
        right = place - 2 * nph
        bottom = right - 2 * nth
        left = bottom - 2 * nph
        on_top, on_right, on_bottom = right < 0, bottom < 0, left < 0
        row = jnp.where(
            on_top,
            (place & 1) - 2,
            jnp.where(
                on_right,
                right >> 1,
                jnp.where(on_bottom, nth + (bottom & 1), nth - 1 - (left >> 1)),
            ),
        )
        col = jnp.where(
            on_top,
            place >> 1,
            jnp.where(
                on_right,
                nph + (right & 1),
                jnp.where(on_bottom, nph - 1 - (bottom >> 1), (left & 1) - 2),
            ),
        )
        return row, col

    def top_start(self, lon):
        return 2 * jnp.maximum(lon * self.cols - HALO, 0)

    def bottom_start(self, lon):
        high = jnp.minimum(lon * self.cols + self.cols + HALO, self.nph)
        return 2 * self.nph + 2 * self.nth + 2 * (self.nph - high)

    def stretch(self, lat, lon):
        nth, nph = self.nth, self.nph
        row_low = jnp.maximum(lat * self.rows - HALO, 0)
        row_high = jnp.minimum(lat * self.rows + self.rows + HALO, nth)
        col_low = jnp.maximum(lon * self.cols - HALO, 0)
        col_high = jnp.minimum(lon * self.cols + self.cols + HALO, nph)
        top, bottom = lat == 0, lat == self.lat_count - 1
        left, right = lon == 0, lon == self.lon_count - 1
        left_start = 4 * nph + 2 * nth + 2 * (nth - row_high)
        start = jnp.where(
            top & left,
            left_start,
            jnp.where(
                top,
                self.top_start(lon),
                jnp.where(
                    right,
                    2 * nph + 2 * row_low,
                    jnp.where(bottom, self.bottom_start(lon), left_start),
                ),
            ),
        )
        span = jnp.where(top | bottom, 2 * (col_high - col_low), 0) + jnp.where(
            left | right, 2 * (row_high - row_low), 0
        )
        return start, span

    def first_entry(self, start, donor, offset):
        lead = -(-2 * self.total // self.blocks)
        raised = start - donor - offset + lead * self.blocks + self.blocks - 1
        if is_power_of_two(self.blocks):
            return (raised >> (self.blocks.bit_length() - 1)) - lead
        return lax.div(raised, jnp.full_like(raised, self.blocks)) - lead

    def wrap(self, entry):
        for bound in (8, 4, 2, 1):
            entry = jnp.where(entry < 0, entry + self.entries * bound, entry)
        for bound in (8, 4, 2, 1):
            over = entry - self.entries * bound
            entry = jnp.where(over >= 0, over, entry)
        return entry

    def column_entry(self, lon, donor, offset, slot):
        side = (lon == 0) | (lon == self.lon_count - 1)
        top = self.first_entry(self.top_start(lon), donor, offset)
        bottom = self.first_entry(self.bottom_start(lon), donor, offset)
        lower = (lon == 0) | jnp.logical_not(side) & (slot >= self.half)
        skipped = jnp.where(jnp.logical_not(side) & (slot >= self.half), self.half, 0)
        return jnp.where(lower, bottom, top) + slot - skipped

    def column_slot(self, lat, lon, donor=None, offset=None):
        side = (lon == 0) | (lon == self.lon_count - 1)
        start, _ = self.stretch(lat, lon)
        column = jnp.where(lon == 0, self.bottom_start(lon), self.top_start(lon))
        if donor is None:
            ahead = lax.div(start - column, jnp.int32(self.blocks))
        else:
            ahead = self.first_entry(start, donor, offset) - self.first_entry(
                column, donor, offset
            )
        middle = jnp.where(lat == self.lat_count - 1, self.half, 0)
        return jnp.where(side, jnp.maximum(ahead, 0), middle)


def padded_rows(count):
    return -(-count // 8) * 8


def whole(count):
    return [pl.BlockSpec(memory_space=pltpu.VMEM)] * count


def scalars(count):
    return [pl.BlockSpec(memory_space=pltpu.SMEM)] * count


def lookup(table_ref, index):
    return table_ref[index, 0]


def grant(mebibytes):
    return pltpu.CompilerParams(vmem_limit_bytes=mebibytes << 20)


def tiles(index, count):
    if isinstance(index, int):
        return pl.ds(index * TILE, count * TILE)
    return pl.ds(pl.multiple_of(index * TILE, TILE), count * TILE)


def weight_kernel(loop, base_ref, weight_ref, turn_ref, corner_ref, spread_ref):
    entries = loop.entries
    diagonal = lax.broadcasted_iota(jnp.int32, (entries, entries), 0) == (
        lax.broadcasted_iota(jnp.int32, (entries, entries), 1)
    )
    for number in range(18):
        ref, row = (weight_ref, number) if number < 16 else (turn_ref, number - 16)
        column = jnp.sum(
            jnp.where(diagonal, ref[row : row + 1, :], 0.0), axis=1, keepdims=True
        )
        spread_ref[pl.ds(number * entries, entries), :] = jnp.broadcast_to(
            column, (entries, spread_ref.shape[1])
        )
    wide = loop.cols + 2 * HALO
    base = (base_ref[0:1, :] - lax.axis_index("lat") * loop.rows + HALO - 1) * wide + (
        base_ref[1:2, :] - lax.axis_index("lon") * loop.cols + HALO - 1
    )
    column = jnp.sum(
        jnp.where(diagonal, base.astype(jnp.float32), 0.0), axis=1, keepdims=True
    )
    corner_ref[pl.ds(0, entries), :] = jnp.broadcast_to(
        column, (entries, corner_ref.shape[1])
    ).astype(jnp.int32)


def digits(shape, outer, inner, slots):
    flat = lax.broadcasted_iota(jnp.int32, shape, 0)
    high = jnp.zeros(shape, jnp.int32)
    for n in range(1, outer):
        high = high + jnp.where(flat >= n * inner * slots, 1, 0)
    rest = flat - high * (inner * slots)
    middle = jnp.zeros(shape, jnp.int32)
    for n in range(1, inner):
        middle = middle + jnp.where(rest >= n * slots, 1, 0)
    return high, middle, jnp.minimum(rest - middle * slots, slots - 1)


def table_kernel(loop, pitch, cell_ref, other_ref, send_ref, receive_ref, swap_ref=None):
    lat, lon = lax.axis_index("lat"), lax.axis_index("lon")
    lat_count, lon_count = loop.lat_count, loop.lon_count
    mine = loop.position(cell_ref[0], cell_ref[1])
    other = loop.position(other_ref[0], other_ref[1])

    _, step, slot = digits(send_ref.shape, 1, lon_count, loop.column_slots)
    entry = loop.column_entry(
        to_device(lon, step, lon_count), lat * lon_count + lon, other, slot
    )
    send_ref[...] = loop.wrap(entry)

    lat_step, lon_step, slot = digits(receive_ref.shape, lat_count, lon_count, loop.slots)
    if swap_ref is not None:
        donor = lat * lon_count + from_device(lon, lon_step, lon_count)
        here = jnp.full_like(slot, lon)
        ahead = loop.column_slot(to_device(lat, lat_step, lat_count), here, donor, other)
        swap_ref[...] = jnp.minimum(ahead + slot, loop.column_slots - 1)

    donor = from_device(lat, lat_step, lat_count) * lon_count + from_device(
        lon, lon_step, lon_count
    )
    start, span = loop.stretch(jnp.full_like(slot, lat), jnp.full_like(slot, lon))
    entry = loop.first_entry(start, donor, mine) + slot
    place = entry * loop.blocks + donor + mine
    wrapped = jnp.where(place >= loop.total, place - loop.total, place)
    row, col = loop.cell(wrapped)
    spot = (row - lat * loop.rows + HALO) * pitch + PAD + (col - lon * loop.cols + HALO)
    receive_ref[...] = jnp.where(place < start + span, spot, 0)


def strip_kernel(
    rows, cols, after_ref, own_even_ref, own_odd_ref, even_ref, odd_ref, *send_refs
):
    del after_ref
    lat_even = lax.rem(lax.axis_index("lat"), 2) == 0
    lon_even = lax.rem(lax.axis_index("lon"), 2) == 0
    high = cols - HALO
    lows = (jnp.where(lon_even, high, 0), jnp.where(lon_even, 0, high))

    def copy_halo(first, source):
        for send_ref, low in zip(send_refs, lows):
            for row in range(HALO):
                send_ref[tiles((first + row) * HALO, HALO), :] = source[
                    tiles(row * cols + low, HALO), :
                ]

    for send_ref, own_ref in zip(send_refs, (own_even_ref, own_odd_ref)):
        send_ref[tiles(HALO * HALO, rows * HALO), :] = own_ref[...]

    @pl.when(lat_even)
    def _():
        copy_halo(0, odd_ref)
        copy_halo(HALO + rows, even_ref)

    @pl.when(jnp.logical_not(lat_even))
    def _():
        copy_halo(0, even_ref)
        copy_halo(HALO + rows, odd_ref)


def mix_and_pack(loop, wide, rim, frame_ref, value_ref, send_refs):
    send_table_ref, corner_ref, spread_ref = rim
    entries = loop.entries
    field = lax.broadcasted_iota(jnp.int32, (TILE, 128), 0)
    takes_next = (field == 1) | (field == 4)
    turned = takes_next | (field == 2) | (field == 5)

    def one_entry(entry, carry):
        base = lookup(corner_ref, entry)

        def over_tile(number):
            return spread_ref[pl.ds(number * entries + entry, TILE, stride=0), :]

        total = None
        for a in range(4):
            for b in range(4):
                part = over_tile(4 * a + b) * frame_ref[tiles(base + a * wide + b, 1), :]
                total = part if total is None else total + part
        cosine, sine = over_tile(16), over_tile(17)
        other = jnp.where(
            takes_next, pltpu.roll(total, TILE - 1, 0), pltpu.roll(total, 1, 0)
        )
        mixed = cosine * total + jnp.where(takes_next, -sine, sine) * other
        value_ref[tiles(entry, 1), :] = jnp.where(turned, mixed, total)
        return carry

    lax.fori_loop(0, loop.entries, one_entry, 0, unroll=4)
    for step, send_ref in enumerate(send_refs):
        for slot in range(loop.column_slots):
            entry = lookup(send_table_ref, step * loop.column_slots + slot)
            send_ref[tiles(slot, 1), :] = value_ref[tiles(entry, 1), :]


def middle_kernel(rows, cols, state_ref, lat_even_ref, lat_odd_ref, frame_ref):
    wide = cols + 2 * HALO
    lat_even = lax.rem(lax.axis_index("lat"), 2) == 0

    def copy_rows(first, count, source):
        for row in range(count):
            frame_ref[tiles((first + row) * wide + HALO, cols), :] = source[
                tiles(row * cols, cols), :
            ]

    copy_rows(HALO, rows, state_ref)

    @pl.when(lat_even)
    def _():
        copy_rows(0, HALO, lat_odd_ref)
        copy_rows(HALO + rows, HALO, lat_even_ref)

    @pl.when(jnp.logical_not(lat_even))
    def _():
        copy_rows(0, HALO, lat_even_ref)
        copy_rows(HALO + rows, HALO, lat_odd_ref)


def frame_kernel(loop, *refs):
    rim, refs = refs[:3], refs[3:]
    lon_odd_ref, lon_even_ref, _, frame_ref = refs[:4]
    send_refs, value_ref = refs[4:-1], refs[-1]
    rows, cols = loop.rows, loop.cols
    wide = cols + 2 * HALO
    lat, lon = lax.axis_index("lat"), lax.axis_index("lon")
    lon_even = lax.rem(lon, 2) == 0

    def copy_columns(source, left):
        for row in range(rows + 2 * HALO):
            frame_ref[tiles(row * wide + left, HALO), :] = source[tiles(row * HALO, HALO), :]

    @pl.when(lon_even)
    def _():
        copy_columns(lon_odd_ref, 0)
        copy_columns(lon_even_ref, HALO + cols)

    @pl.when(jnp.logical_not(lon_even))
    def _():
        copy_columns(lon_even_ref, 0)
        copy_columns(lon_odd_ref, HALO + cols)

    zeros = jnp.zeros((HALO * TILE, frame_ref.shape[1]), jnp.float32)
    for at_row, top in ((lat == 0, 0), (lat == loop.lat_count - 1, HALO + rows)):
        for at_col, left in ((lon == 0, 0), (lon == loop.lon_count - 1, HALO + cols)):

            @pl.when(at_row & at_col)
            def _():
                for row in range(HALO):
                    frame_ref[tiles((top + row) * wide + left, HALO), :] = zeros

    mix_and_pack(loop, wide, rim, frame_ref, value_ref, send_refs)


def swap_kernel(loop, *refs):
    table_ref = None
    if not loop.even_leads:
        table_ref, refs = refs[0], refs[1:]
    got_refs = [refs[0]] + by_step(1, refs[1 : loop.lon_count])
    out_refs = refs[loop.lon_count :]
    lat, lon = lax.axis_index("lat"), lax.axis_index("lon")
    for lat_step in range(loop.lat_count):
        if loop.even_leads:
            lead = loop.column_slot(to_device(lat, lat_step, loop.lat_count), lon)
            lead = jnp.minimum(lead, loop.column_slots - loop.slots)
        for lon_step in range(loop.lon_count):
            for slot in range(loop.slots):
                place = lon_step * loop.slots + slot
                if loop.even_leads:
                    source = lead + slot
                else:
                    source = lookup(table_ref, lat_step * loop.lon_count * loop.slots + place)
                out_refs[lat_step][tiles(place, 1), :] = got_refs[lon_step][tiles(source, 1), :]


class Section:
    def __init__(self, loop, factor_ref, radial_ref, plane_ref, work_ref):
        self.loop = loop
        self.tall, self.wide = loop.rows + 2 * HALO, loop.cols + 2 * HALO
        self.pitch = self.wide + 2 * PAD
        self.factor_ref, self.radial_ref = factor_ref, radial_ref
        self.plane_ref, self.work_ref = plane_ref, work_ref
        lat, lon = lax.axis_index("lat"), lax.axis_index("lon")
        self.lat = lat
        self.at_top, self.at_left = lat == 0, lon == 0
        self.on_row_edge = self.at_top | (lat == loop.lat_count - 1)
        self.on_col_edge = self.at_left | (lon == loop.lon_count - 1)

    def spread(self, frame_ref, rows):
        def one_row(row, carry):
            for chunk in range(0, self.wide, 8):
                for f in range(TILE):
                    start = (row * self.wide + chunk) * TILE + f
                    self.plane_ref[self.at(f, row, chunk), :] = frame_ref[
                        pl.ds(start, 8, stride=TILE), :
                    ]
            return carry

        lax.fori_loop(*rows, one_row, 0)

    def scatter(self, receive_ref, got_refs):
        arrivals = self.loop.lon_count * self.loop.slots
        got_refs = by_step(0, got_refs)
        for lat_step in range(self.loop.lat_count):
            for place in range(arrivals):
                spot = lookup(receive_ref, lat_step * arrivals + place)
                self.plane_ref[pl.ds(spot, TILE, stride=self.tall * self.pitch), :] = got_refs[
                    lat_step
                ][tiles(place, 1), :]

    def at(self, number, row, col):
        return pl.ds((number * self.tall + row) * self.pitch + PAD + col, 8)

    def reader(self, ref, row, col):
        def read(number, row_step=0, col_step=0):
            return ref[self.at(number, row + row_step, col + col_step), :]

        return read

    def prepare(self, row):
        factors = [
            self.factor_ref[pl.ds((self.lat * 3 + n) * self.tall + row, 8, stride=0), :]
            for n in range(3)
        ]
        inverse_radius = self.radial_ref[0]
        with_theta = inverse_radius * (self.loop.nth / math.pi)
        return factors, inverse_radius * factors[2], with_theta

    def up(self, x):
        return pltpu.roll(x, x.shape[-1] - 1, 1)

    def down(self, x):
        return pltpu.roll(x, 1, 1)

    def curl(self, read, first, prepared):
        (tu, td, ph), with_phi, with_theta = prepared
        ru, rl = self.radial_ref[1], self.radial_ref[2]
        a, b, c = first, first + 1, first + 2
        mid_b, mid_c = read(b), read(c)
        radial = self.radial_ref[0] * (
            (tu * read(c, 1) - td * read(c, -1)) - ph * (read(b, 0, 1) - read(b, 0, -1))
        )
        polar = with_phi * (read(a, 0, 1) - read(a, 0, -1)) - (
            ru * self.up(mid_c) - rl * self.down(mid_c)
        )
        azimuth = (ru * self.up(mid_b) - rl * self.down(mid_b)) - with_theta * (
            read(a, 1) - read(a, -1)
        )
        return radial, polar, azimuth

    def slope(self, read, number, prepared):
        _, with_phi, with_theta = prepared
        mid = read(number)
        return (
            self.radial_ref[3] * self.up(mid) - self.radial_ref[4] * self.down(mid),
            with_theta * (read(number, 1) - read(number, -1)),
            with_phi * (read(number, 0, 1) - read(number, 0, -1)),
        )

    def outflow(self, read, first, prepared):
        (tu, td, ph), _, _ = prepared
        mid = read(first)
        return (
            self.radial_ref[5] * self.up(mid) - self.radial_ref[6] * self.down(mid)
        ) + self.radial_ref[0] * (
            (tu * read(first + 1, 1) - td * read(first + 1, -1))
            + ph * (read(first + 2, 0, 1) - read(first + 2, 0, -1))
        )

    def first_pass(self, row, chunk):
        prepared = self.prepare(row)
        read = self.reader(self.plane_ref, row, chunk)

        def put(number, value):
            self.work_ref[self.at(number, row, chunk), :] = value

        flow = [read(n) for n in range(3)]
        field = [read(n) for n in range(3, 6)]
        current = self.curl(read, 3, prepared)
        spin = self.curl(read, 0, prepared)
        induced = cross(flow, field)
        warm = self.slope(read, 6, prepared)
        for n in range(3):
            put(n, current[n])
            put(3 + n, spin[n])
            put(6 + n, induced[n] - ETA_COEF * current[n])
            put(9 + n, warm[n])
        put(12, read(7) + 0.5 * dot(flow, flow))

    def second_pass(self, row, chunk, emit):
        prepared = self.prepare(row)
        read = self.reader(self.plane_ref, row, chunk)
        work = self.reader(self.work_ref, row, chunk)
        flow = [read(n) for n in range(3)]
        field = [read(n) for n in range(3, 6)]
        current = [work(n) for n in range(3)]
        spin = [work(3 + n) for n in range(3)]
        warm = [work(9 + n) for n in range(3)]
        field_rate = self.curl(work, 6, prepared)
        spin_curl = self.curl(work, 3, prepared)
        head = self.slope(work, 12, prepared)
        lorentz = cross(current, field)
        advect = cross(flow, spin)
        speed = [advect[n] + lorentz[n] - head[n] - NU_COEF * spin_curl[n] for n in range(3)]
        speed[0] = speed[0] + ARCHIMEDES_LIFT * read(6)
        heat = KAPPA_COEF * self.outflow(work, 9, prepared) - dot(flow, warm)
        squeeze = -SOUND_SQ * self.outflow(read, 0, prepared)
        emit(row, chunk, read, speed + list(field_rate) + [heat, squeeze])

    def over(self, rows, one_row, unroll):
        def step(row, carry):
            one_row(row)
            return carry

        lax.fori_loop(*rows, step, 0, unroll=unroll)

    def everywhere(self, rows, chunks, emit):
        def first(row):
            for chunk in range(0, self.wide, 8):
                self.first_pass(row, chunk)

        def second(row):
            for chunk in chunks:
                self.second_pass(row, chunk, emit)

        self.over((rows[0] - 1, rows[1] + 1), first, 2)
        self.over(rows, second, 2)

    def along_edges(self, rows, chunks, emit):
        tall, wide = self.tall, self.wide
        low_chunk, high_chunk = chunks[0], chunks[-1]

        @pl.when(self.on_row_edge)
        def _():
            row = jnp.where(self.at_top, HALO - 1, tall - HALO - 1)
            for step in range(2):
                for chunk in range(0, wide, 8):
                    self.first_pass(row + step, chunk)

        @pl.when(self.on_col_edge)
        def _():
            chunk = pl.multiple_of(jnp.where(self.at_left, 0, wide - 8), 8)
            count = rows[1] - rows[0]
            self.over(
                (rows[0] - 1, rows[1] + 1), lambda row: self.first_pass(row, chunk), count // 2 + 1
            )

        @pl.when(self.on_row_edge)
        def _():
            row = jnp.where(self.at_top, HALO, tall - HALO - 2)
            for step in range(2):
                for chunk in chunks:
                    self.second_pass(row + step, chunk, emit)

        @pl.when(self.on_col_edge)
        def _():
            chunk = jnp.where(self.at_left, low_chunk, high_chunk)
            count = rows[1] - rows[0]
            self.over(rows, lambda row: self.second_pass(row, chunk, emit), count // 2)


def cross(x, y):
    return (
        x[1] * y[2] - x[2] * y[1],
        x[2] * y[0] - x[0] * y[2],
        x[0] * y[1] - x[1] * y[0],
    )


def dot(x, y):
    return x[0] * y[0] + x[1] * y[1] + x[2] * y[2]


def middle_state(loop, frame_ref, rate_ref):
    wide = loop.cols + 2 * HALO
    first_row = lax.axis_index("lat") * loop.rows - HALO
    first_col = lax.axis_index("lon") * loop.cols - HALO

    def emit(row, chunk, read, rate):
        in_row = (row + first_row >= 0) & (row + first_row < loop.nth)
        col = lax.broadcasted_iota(jnp.int32, (8, 128), 0) + (chunk + first_col)
        inside = (col >= jnp.where(in_row, 0, loop.nph)) & (col < loop.nph)
        for f in range(TILE):
            rate_ref[f, row, pl.ds(chunk, 8), :] = rate[f]
            start = (row * wide + chunk) * TILE + f
            frame_ref[pl.ds(start, 8, stride=TILE), :] = jnp.where(
                inside, read(f) + TIME_STEP * rate[f], 0.0
            )

    return emit


def total_change(loop, change_ref, rate_ref):
    def emit(row, chunk, read, rate):
        for f in range(TILE):
            start = ((row - HALO) * loop.cols + chunk - HALO) * TILE + f
            change_ref[pl.ds(start, 8, stride=TILE), :] = (0.5 * TIME_STEP) * (
                rate_ref[f, row, pl.ds(chunk, 8), :] + rate[f]
            )

    return emit


def first_inner_kernel(
    loop, factor_ref, radial_ref, frame_in_ref, after_ref, frame_ref, rate_ref, plane_ref, work_ref
):
    del after_ref
    part = Section(loop, factor_ref, radial_ref, plane_ref, work_ref)
    part.spread(frame_in_ref, (0, part.tall))
    part.everywhere(
        (2, part.tall - 2), range(0, part.wide, 8), middle_state(loop, frame_ref, rate_ref)
    )


def first_edge_kernel(loop, *refs):
    rim, refs = refs[:3], refs[3:]
    receive_ref, factor_ref, radial_ref = refs[:3]
    got_refs, refs = refs[7 : 7 + loop.lat_count], refs[7 + loop.lat_count :]
    frame_ref, rate_ref, plane_ref, work_ref = refs[:4]
    send_refs, value_ref = refs[4:-1], refs[-1]
    part = Section(loop, factor_ref, radial_ref, plane_ref, work_ref)
    part.scatter(receive_ref, got_refs)
    part.along_edges(
        (2, part.tall - 2), range(0, part.wide, 8), middle_state(loop, frame_ref, rate_ref)
    )
    mix_and_pack(loop, part.wide, rim, frame_ref, value_ref, send_refs)


def second_inner_kernel(
    loop, factor_ref, radial_ref, frame_ref, rate_ref, after_ref, change_ref, plane_ref, work_ref
):
    del after_ref
    part = Section(loop, factor_ref, radial_ref, plane_ref, work_ref)
    part.spread(frame_ref, (2, part.tall - 2))
    part.everywhere(
        (HALO, HALO + loop.rows),
        range(HALO, HALO + loop.cols, 8),
        total_change(loop, change_ref, rate_ref),
    )


def second_edge_kernel(loop, receive_ref, factor_ref, radial_ref, rate_ref, inner_ref, *refs):
    got_refs, refs = refs[2 : 2 + loop.lat_count], refs[2 + loop.lat_count :]
    plane_ref, work_ref, change_ref = refs
    part = Section(loop, factor_ref, radial_ref, plane_ref, work_ref)
    for row in range(loop.rows):
        here = tiles(row * loop.cols, loop.cols)
        change_ref[here, :] = inner_ref[here, :]
    part.scatter(receive_ref, got_refs)
    part.along_edges(
        (HALO, HALO + loop.rows),
        range(HALO, HALO + loop.cols, 8),
        total_change(loop, change_ref, rate_ref),
    )


def radial_factors(levels, theta_count):
    scale = 2.0 * theta_count / math.pi
    step = 0.65 * scale / levels
    radius = 0.35 * scale + (np.arange(levels) + 0.5) * step
    half = 0.5 / step
    above = np.append(radius[1:], 0.0)
    below = np.append(0.0, radius[:-1])
    ones_above = np.append(np.ones(levels - 1), 0.0)
    ones_below = np.append(0.0, np.ones(levels - 1))
    rows = np.stack(
        [
            1.0 / radius,
            half * above / radius,
            half * below / radius,
            half * ones_above,
            half * ones_below,
            half * above**2 / radius**2,
            half * below**2 / radius**2,
        ]
    )
    return np.repeat(rows[:, None, :], 8, axis=1).astype(np.float32)


def row_factors(rows, lat_count, nth, nph, levels):
    polar_step, azimuth_step = math.pi / (2 * nth), 1.5 * math.pi / nph
    tall = rows + 2 * HALO
    parts = []
    for lat in range(lat_count):
        row = lat * rows - HALO - 1 + np.arange(tall + 2)
        sines = np.sin(math.pi / 4 + (row + 0.5) * polar_step)
        middle = sines[1:-1]
        parts += [
            sines[2:] / middle * (0.5 / polar_step),
            sines[:-2] / middle * (0.5 / polar_step),
            (0.5 / azimuth_step) / middle,
        ]
    flat = np.concatenate(parts + [np.zeros(8)]).astype(np.float32)
    return np.repeat(flat[:, None], levels, axis=1)


def per_device(state, rim_base, rim_weight, rim_angle, rim_target):
    _, rows, cols, fields, levels = state.shape
    lat_count, lon_count = lax.axis_size("lat"), lax.axis_size("lon")
    entries = rim_base.shape[1]
    loop = Loop(rows, cols, lat_count, lon_count, entries)
    tall, wide = rows + 2 * HALO, cols + 2 * HALO
    pitch = wide + 2 * PAD
    block = state[0].reshape(rows * cols * fields, levels)
    f32 = jnp.float32

    def tile_array(count):
        return jax.ShapeDtypeStruct((count * TILE, levels), f32)

    first_cell = rim_target[0, 0]
    other_cell = lax.ppermute(first_cell, "panel", [(0, 1), (1, 0)])

    everyone = ("panel", "lat", "lon")
    cells = state[0]
    last_first = lax.axis_index("lat") % 2 == 0
    head, tail = cells[:HALO], cells[rows - HALO :]
    send_even = jnp.where(last_first, tail, head).reshape(HALO * cols * fields, levels)
    send_odd = jnp.where(last_first, head, tail).reshape(HALO * cols * fields, levels)
    lat_even = lax.ppermute(send_even, everyone, swap_route(0, lat_count, lon_count, True))
    lat_odd = lax.ppermute(send_odd, everyone, swap_route(1, lat_count, lon_count, True))

    angle = rim_angle[0]
    corner_table, spread_weights = pl.pallas_call(
        lambda *refs: weight_kernel(loop, *refs),
        out_shape=[
            jax.ShapeDtypeStruct((padded_rows(entries), 128), jnp.int32),
            jax.ShapeDtypeStruct((18 * entries + TILE, levels), f32),
        ],
        in_specs=whole(3),
        out_specs=whole(2),
        compiler_params=grant(4),
        name="weights",
    )(rim_base[0].T, rim_weight[0].T, jnp.stack([jnp.cos(angle), jnp.sin(angle)]))
    send_count = lon_count * loop.column_slots
    got_count = lat_count * lon_count * loop.slots
    counts = [send_count, got_count] + [got_count] * (not loop.even_leads)
    send_table, receive_table, *swap_tables = pl.pallas_call(
        lambda *refs: table_kernel(loop, pitch, *refs),
        out_shape=[
            jax.ShapeDtypeStruct((padded_rows(count), 128), jnp.int32) for count in counts
        ],
        in_specs=scalars(2),
        out_specs=whole(len(counts)),
        compiler_params=grant(4),
        name="tables",
    )(first_cell, other_cell)
    rim = (send_table, corner_table, spread_weights)
    factors = jnp.asarray(row_factors(rows, lat_count, loop.nth, loop.nph, levels))
    radial = jnp.asarray(radial_factors(levels, loop.nth))

    east_first = lax.axis_index("lon") % 2 == 0
    head, tail = cells[:, :HALO], cells[:, cols - HALO :]
    own_even = jnp.where(east_first, tail, head).reshape(rows * HALO * fields, levels)
    own_odd = jnp.where(east_first, head, tail).reshape(rows * HALO * fields, levels)
    strip_even, strip_odd = pl.pallas_call(
        lambda *refs: strip_kernel(rows, cols, *refs),
        out_shape=[tile_array(tall * HALO)] * 2,
        in_specs=whole(5),
        out_specs=whole(2),
        compiler_params=grant(4),
        name="strips",
    )(corner_table, own_even, own_odd, lat_even, lat_odd)
    lon_odd = lax.ppermute(strip_odd, everyone, swap_route(1, lat_count, lon_count, False))
    lon_even = lax.ppermute(strip_even, everyone, swap_route(0, lat_count, lon_count, False))

    frame = pl.pallas_call(
        lambda *refs: middle_kernel(rows, cols, *refs[1:]),
        out_shape=tile_array(tall * wide),
        in_specs=whole(4),
        out_specs=whole(1)[0],
        compiler_params=grant(4),
        name="middle",
    )(strip_even, block, lat_even, lat_odd)
    packed_shapes = [tile_array(loop.column_slots)] * lon_count
    frame, *packed = pl.pallas_call(
        lambda *refs: frame_kernel(loop, *refs),
        out_shape=[tile_array(tall * wide)] + packed_shapes,
        in_specs=whole(6),
        out_specs=whole(1 + lon_count),
        scratch_shapes=[pltpu.VMEM((entries * TILE, levels), f32)],
        input_output_aliases={5: 0},
        compiler_params=grant(4),
        name="frame",
    )(*rim, lon_odd, lon_even, frame)

    def first_round(packed):
        got = [packed[0]] + [
            lax.ppermute(packed[step], "lon", lon_route(step, lon_count))
            for step in start_order(1, lon_count)
        ]
        return pl.pallas_call(
            lambda *refs: swap_kernel(loop, *refs),
            out_shape=[tile_array(lon_count * loop.slots)] * lat_count,
            in_specs=whole(len(swap_tables) + lon_count),
            out_specs=whole(lat_count),
            compiler_params=grant(4),
            name="swap",
        )(*swap_tables, *got)

    def second_round(turned):
        return [
            lax.ppermute(turned[step], everyone, lat_route(step, lat_count, lon_count))
            for step in start_order(0, lat_count)
        ]

    planes = [
        jax.ShapeDtypeStruct((fields * tall * pitch, levels), f32),
        jax.ShapeDtypeStruct((13 * tall * pitch, levels), f32),
    ]
    rates = jax.ShapeDtypeStruct((fields, tall, wide, levels), f32)

    turned = first_round(packed)
    got = second_round(turned)
    frame, rate, plane, work = pl.pallas_call(
        lambda *refs: first_inner_kernel(loop, *refs),
        out_shape=[tile_array(tall * wide), rates] + planes,
        in_specs=whole(4),
        out_specs=whole(4),
        compiler_params=grant(4),
        name="first_inner",
    )(factors, radial, frame, turned[0])
    frame, rate, _, _, *packed = pl.pallas_call(
        lambda *refs: first_edge_kernel(loop, *refs),
        out_shape=[tile_array(tall * wide), rates] + planes + packed_shapes,
        in_specs=whole(10 + lat_count),
        out_specs=whole(4 + lon_count),
        scratch_shapes=[pltpu.VMEM((entries * TILE, levels), f32)],
        input_output_aliases={6: 0, 7: 1, 8: 2, 9: 3},
        compiler_params=grant(4),
        name="first_edge",
    )(*rim, receive_table, factors, radial, frame, rate, plane, work, *got)

    turned = first_round(packed)
    got = second_round(turned)
    inner, plane, work = pl.pallas_call(
        lambda *refs: second_inner_kernel(loop, *refs),
        out_shape=[tile_array(rows * cols)] + planes,
        in_specs=whole(5),
        out_specs=whole(3),
        compiler_params=grant(4),
        name="second_inner",
    )(factors, radial, frame, rate, turned[0])
    _, _, change = pl.pallas_call(
        lambda *refs: second_edge_kernel(loop, *refs),
        out_shape=planes + [tile_array(rows * cols)],
        in_specs=whole(7 + lat_count),
        out_specs=whole(3),
        input_output_aliases={5: 0, 6: 1},
        compiler_params=grant(4),
        name="second_edge",
    )(receive_table, factors, radial, rate, inner, plane, work, *got)
    return change.reshape(1, rows, cols, fields, levels)


def solution(mesh):
    return jax.shard_map(
        per_device,
        mesh=mesh,
        in_specs=(
            P("panel", "lat", "lon", None, None),
            P("panel", ("lat", "lon"), None),
            P("panel", ("lat", "lon"), None),
            P("panel", ("lat", "lon")),
            P("panel", None, None),
        ),
        out_specs=P("panel", "lat", "lon", None, None),
        check_vma=False,
    )
```

```python
import math

import jax
import jax.numpy as jnp
import numpy as np
from jax import lax
from jax.experimental import pallas as pl
from jax.experimental.pallas import tpu as pltpu
from jax.sharding import PartitionSpec as P

ETA_COEF = 0.2
NU_COEF = 0.2
KAPPA_COEF = 0.3
SOUND_SQ = 1.0
ARCHIMEDES_LIFT = 0.5
TIME_STEP = 0.2

HALO = 4
PAD = 8
TILE = 8


def start_order(first, count):
    down = first == 1
    odd = sorted((n for n in range(first, count) if n % 2), reverse=down)
    even = sorted((n for n in range(first, count) if n % 2 == 0), reverse=not down)
    return odd + even


def by_step(first, refs):
    order = start_order(first, first + len(refs))
    return [refs[order.index(step)] for step in range(first, first + len(refs))]


def is_power_of_two(count):
    return count & (count - 1) == 0


def to_device(index, step, count):
    return index ^ step if is_power_of_two(count) else (index + step) % count


def from_device(index, step, count):
    return index ^ step if is_power_of_two(count) else (index + count - step) % count


def swap_route(parity, lat_count, lon_count, along_lat):
    count, across = (lat_count, lon_count) if along_lat else (lon_count, lat_count)
    mate = list(range(count))
    for low in range(parity, count - 1, 2):
        mate[low], mate[low + 1] = low + 1, low
    route = []
    for side in range(2):
        for lat in range(lat_count):
            for lon in range(lon_count):
                here, other = (lat, lon) if along_lat else (lon, lat)
                there = mate[here]
                if there == here:
                    other = other ^ 1 if other ^ 1 < across else other
                target = (there, other) if along_lat else (other, there)
                route.append(
                    (
                        (side * lat_count + lat) * lon_count + lon,
                        (side * lat_count + target[0]) * lon_count + target[1],
                    )
                )
    return route


def lon_route(step, count):
    return [(i, to_device(i, step, count)) for i in range(count)]


def lat_route(step, lat_count, lon_count):
    route = []
    inner = set(range(1, lat_count - 1))
    for side in range(2):
        for lon in range(lon_count):
            target = {lat: (1 - side, to_device(lat, step, lat_count), lon) for lat in range(lat_count)}
            if 0 < lon < lon_count - 1 and lon_count % 2 == 0:
                idle = {lat for lat in target if target[lat][1] in inner}
                mate = (lon - 1 ^ 1) + 1
                for lat in idle & inner:
                    target[lat] = (side, lat, mate)
                for lat, free in zip(sorted(idle - inner), sorted(inner - idle)):
                    target[lat] = (side, free, lon)
            for lat, (there, row, col) in target.items():
                route.append(
                    (
                        (side * lat_count + lat) * lon_count + lon,
                        (there * lat_count + row) * lon_count + col,
                    )
                )
    assert len({there for _, there in route}) == len(route)
    return route


class Loop:
    def __init__(self, rows, cols, lat_count, lon_count, entries):
        self.rows, self.cols = rows, cols
        self.lat_count, self.lon_count = lat_count, lon_count
        self.nth, self.nph = rows * lat_count, cols * lon_count
        self.total = 4 * (self.nth + self.nph)
        self.blocks = lat_count * lon_count
        self.entries = entries
        one_row = 2 * (cols + 2 * HALO)
        one_col = 2 * (rows + 2 * HALO)
        corner = 2 * (rows + cols + 2 * HALO)
        self.slots = -(-max(corner, one_row, one_col) // self.blocks)
        self.half = -(-one_row // self.blocks)
        side = 4 * (cols + HALO) + 2 * self.nth
        leads = [2 * (cols + HALO) + 2 * (n * rows - HALO) for n in range(1, lat_count)]
        self.even_leads = all(lead % self.blocks == 0 for lead in leads)
        self.column_slots = max(-(-side // self.blocks), 2 * self.half)

    def position(self, row, col):
        nth, nph = self.nth, self.nph
        top = 2 * col + row + 2
        right = 2 * nph + 2 * row + col - nph
        bottom = 2 * nph + 2 * nth + 2 * (nph - 1 - col) + row - nth
        left = 4 * nph + 2 * nth + 2 * (nth - 1 - row) + col + 2
        return jnp.where(
            row < 0, top, jnp.where(row >= nth, bottom, jnp.where(col >= nph, right, left))
        )

    def cell(self, place):
        nth, nph = self.nth, self.nph
        right = place - 2 * nph
        bottom = right - 2 * nth
        left = bottom - 2 * nph
        on_top, on_right, on_bottom = right < 0, bottom < 0, left < 0
        row = jnp.where(
            on_top,
            (place & 1) - 2,
            jnp.where(
                on_right,
                right >> 1,
                jnp.where(on_bottom, nth + (bottom & 1), nth - 1 - (left >> 1)),
            ),
        )
        col = jnp.where(
            on_top,
            place >> 1,
            jnp.where(
                on_right,
                nph + (right & 1),
                jnp.where(on_bottom, nph - 1 - (bottom >> 1), (left & 1) - 2),
            ),
        )
        return row, col

    def top_start(self, lon):
        return 2 * jnp.maximum(lon * self.cols - HALO, 0)

    def bottom_start(self, lon):
        high = jnp.minimum(lon * self.cols + self.cols + HALO, self.nph)
        return 2 * self.nph + 2 * self.nth + 2 * (self.nph - high)

    def stretch(self, lat, lon):
        nth, nph = self.nth, self.nph
        row_low = jnp.maximum(lat * self.rows - HALO, 0)
        row_high = jnp.minimum(lat * self.rows + self.rows + HALO, nth)
        col_low = jnp.maximum(lon * self.cols - HALO, 0)
        col_high = jnp.minimum(lon * self.cols + self.cols + HALO, nph)
        top, bottom = lat == 0, lat == self.lat_count - 1
        left, right = lon == 0, lon == self.lon_count - 1
        left_start = 4 * nph + 2 * nth + 2 * (nth - row_high)
        start = jnp.where(
            top & left,
            left_start,
            jnp.where(
                top,
                self.top_start(lon),
                jnp.where(
                    right,
                    2 * nph + 2 * row_low,
                    jnp.where(bottom, self.bottom_start(lon), left_start),
                ),
            ),
        )
        span = jnp.where(top | bottom, 2 * (col_high - col_low), 0) + jnp.where(
            left | right, 2 * (row_high - row_low), 0
        )
        return start, span

    def first_entry(self, start, donor, offset):
        lead = -(-2 * self.total // self.blocks)
        raised = start - donor - offset + lead * self.blocks + self.blocks - 1
        if is_power_of_two(self.blocks):
            return (raised >> (self.blocks.bit_length() - 1)) - lead
        return lax.div(raised, jnp.full_like(raised, self.blocks)) - lead

    def wrap(self, entry):
        for bound in (8, 4, 2, 1):
            entry = jnp.where(entry < 0, entry + self.entries * bound, entry)
        for bound in (8, 4, 2, 1):
            over = entry - self.entries * bound
            entry = jnp.where(over >= 0, over, entry)
        return entry

    def column_entry(self, lon, donor, offset, slot):
        side = (lon == 0) | (lon == self.lon_count - 1)
        top = self.first_entry(self.top_start(lon), donor, offset)
        bottom = self.first_entry(self.bottom_start(lon), donor, offset)
        lower = (lon == 0) | jnp.logical_not(side) & (slot >= self.half)
        skipped = jnp.where(jnp.logical_not(side) & (slot >= self.half), self.half, 0)
        return jnp.where(lower, bottom, top) + slot - skipped

    def column_slot(self, lat, lon, donor=None, offset=None):
        side = (lon == 0) | (lon == self.lon_count - 1)
        start, _ = self.stretch(lat, lon)
        column = jnp.where(lon == 0, self.bottom_start(lon), self.top_start(lon))
        if donor is None:
            ahead = lax.div(start - column, jnp.int32(self.blocks))
        else:
            ahead = self.first_entry(start, donor, offset) - self.first_entry(
                column, donor, offset
            )
        middle = jnp.where(lat == self.lat_count - 1, self.half, 0)
        return jnp.where(side, jnp.maximum(ahead, 0), middle)


def padded_rows(count):
    return -(-count // 8) * 8


def whole(count):
    return [pl.BlockSpec(memory_space=pltpu.VMEM)] * count


def scalars(count):
    return [pl.BlockSpec(memory_space=pltpu.SMEM)] * count


def lookup(table_ref, index):
    return table_ref[index, 0]


def grant(mebibytes):
    return pltpu.CompilerParams(vmem_limit_bytes=mebibytes << 20)


def tiles(index, count):
    if isinstance(index, int):
        return pl.ds(index * TILE, count * TILE)
    return pl.ds(pl.multiple_of(index * TILE, TILE), count * TILE)


def weight_kernel(loop, base_ref, weight_ref, turn_ref, corner_ref, spread_ref):
    entries = loop.entries
    diagonal = lax.broadcasted_iota(jnp.int32, (entries, entries), 0) == (
        lax.broadcasted_iota(jnp.int32, (entries, entries), 1)
    )
    for number in range(18):
        ref, row = (weight_ref, number) if number < 16 else (turn_ref, number - 16)
        column = jnp.sum(
            jnp.where(diagonal, ref[row : row + 1, :], 0.0), axis=1, keepdims=True
        )
        spread_ref[pl.ds(number * entries, entries), :] = jnp.broadcast_to(
            column, (entries, spread_ref.shape[1])
        )
    wide = loop.cols + 2 * HALO
    base = (base_ref[0:1, :] - lax.axis_index("lat") * loop.rows + HALO - 1) * wide + (
        base_ref[1:2, :] - lax.axis_index("lon") * loop.cols + HALO - 1
    )
    column = jnp.sum(
        jnp.where(diagonal, base.astype(jnp.float32), 0.0), axis=1, keepdims=True
    )
    corner_ref[pl.ds(0, entries), :] = jnp.broadcast_to(
        column, (entries, corner_ref.shape[1])
    ).astype(jnp.int32)


def digits(shape, outer, inner, slots):
    flat = lax.broadcasted_iota(jnp.int32, shape, 0)
    high = jnp.zeros(shape, jnp.int32)
    for n in range(1, outer):
        high = high + jnp.where(flat >= n * inner * slots, 1, 0)
    rest = flat - high * (inner * slots)
    middle = jnp.zeros(shape, jnp.int32)
    for n in range(1, inner):
        middle = middle + jnp.where(rest >= n * slots, 1, 0)
    return high, middle, jnp.minimum(rest - middle * slots, slots - 1)


def table_kernel(loop, pitch, cell_ref, other_ref, send_ref, receive_ref, swap_ref=None):
    lat, lon = lax.axis_index("lat"), lax.axis_index("lon")
    lat_count, lon_count = loop.lat_count, loop.lon_count
    mine = loop.position(cell_ref[0], cell_ref[1])
    other = loop.position(other_ref[0], other_ref[1])

    _, step, slot = digits(send_ref.shape, 1, lon_count, loop.column_slots)
    entry = loop.column_entry(
        to_device(lon, step, lon_count), lat * lon_count + lon, other, slot
    )
    send_ref[...] = loop.wrap(entry)

    lat_step, lon_step, slot = digits(receive_ref.shape, lat_count, lon_count, loop.slots)
    if swap_ref is not None:
        donor = lat * lon_count + from_device(lon, lon_step, lon_count)
        here = jnp.full_like(slot, lon)
        ahead = loop.column_slot(to_device(lat, lat_step, lat_count), here, donor, other)
        swap_ref[...] = jnp.minimum(ahead + slot, loop.column_slots - 1)

    donor = from_device(lat, lat_step, lat_count) * lon_count + from_device(
        lon, lon_step, lon_count
    )
    start, span = loop.stretch(jnp.full_like(slot, lat), jnp.full_like(slot, lon))
    entry = loop.first_entry(start, donor, mine) + slot
    place = entry * loop.blocks + donor + mine
    wrapped = jnp.where(place >= loop.total, place - loop.total, place)
    row, col = loop.cell(wrapped)
    spot = (row - lat * loop.rows + HALO) * pitch + PAD + (col - lon * loop.cols + HALO)
    receive_ref[...] = jnp.where(place < start + span, spot, 0)


def strip_kernel(
    rows, cols, after_ref, own_even_ref, own_odd_ref, even_ref, odd_ref, *send_refs
):
    del after_ref
    lat_even = lax.rem(lax.axis_index("lat"), 2) == 0
    lon_even = lax.rem(lax.axis_index("lon"), 2) == 0
    high = cols - HALO
    lows = (jnp.where(lon_even, high, 0), jnp.where(lon_even, 0, high))

    def copy_halo(first, source):
        for send_ref, low in zip(send_refs, lows):
            for row in range(HALO):
                send_ref[tiles((first + row) * HALO, HALO), :] = source[
                    tiles(row * cols + low, HALO), :
                ]

    for send_ref, own_ref in zip(send_refs, (own_even_ref, own_odd_ref)):
        send_ref[tiles(HALO * HALO, rows * HALO), :] = own_ref[...]

    @pl.when(lat_even)
    def _():
        copy_halo(0, odd_ref)
        copy_halo(HALO + rows, even_ref)

    @pl.when(jnp.logical_not(lat_even))
    def _():
        copy_halo(0, even_ref)
        copy_halo(HALO + rows, odd_ref)


def mix_and_pack(loop, wide, rim, frame_ref, value_ref, send_refs):
    send_table_ref, corner_ref, spread_ref = rim
    entries = loop.entries
    field = lax.broadcasted_iota(jnp.int32, (TILE, 128), 0)
    takes_next = (field == 1) | (field == 4)
    turned = takes_next | (field == 2) | (field == 5)

    def one_entry(entry, carry):
        base = lookup(corner_ref, entry)

        def over_tile(number):
            return spread_ref[pl.ds(number * entries + entry, TILE, stride=0), :]

        total = None
        for a in range(4):
            for b in range(4):
                part = over_tile(4 * a + b) * frame_ref[tiles(base + a * wide + b, 1), :]
                total = part if total is None else total + part
        cosine, sine = over_tile(16), over_tile(17)
        other = jnp.where(
            takes_next, pltpu.roll(total, TILE - 1, 0), pltpu.roll(total, 1, 0)
        )
        mixed = cosine * total + jnp.where(takes_next, -sine, sine) * other
        value_ref[tiles(entry, 1), :] = jnp.where(turned, mixed, total)
        return carry

    lax.fori_loop(0, loop.entries, one_entry, 0, unroll=8 if loop.entries % 8 == 0 else 4)
    for step, send_ref in enumerate(send_refs):
        for slot in range(loop.column_slots):
            entry = lookup(send_table_ref, step * loop.column_slots + slot)
            send_ref[tiles(slot, 1), :] = value_ref[tiles(entry, 1), :]


def middle_kernel(rows, cols, state_ref, lat_even_ref, lat_odd_ref, frame_ref):
    wide = cols + 2 * HALO
    lat_even = lax.rem(lax.axis_index("lat"), 2) == 0

    def copy_rows(first, count, source):
        for row in range(count):
            frame_ref[tiles((first + row) * wide + HALO, cols), :] = source[
                tiles(row * cols, cols), :
            ]

    copy_rows(HALO, rows, state_ref)

    @pl.when(lat_even)
    def _():
        copy_rows(0, HALO, lat_odd_ref)
        copy_rows(HALO + rows, HALO, lat_even_ref)

    @pl.when(jnp.logical_not(lat_even))
    def _():
        copy_rows(0, HALO, lat_even_ref)
        copy_rows(HALO + rows, HALO, lat_odd_ref)


def frame_kernel(loop, *refs):
    rim, refs = refs[:3], refs[3:]
    lon_odd_ref, lon_even_ref, _, frame_ref = refs[:4]
    send_refs, value_ref = refs[4:-1], refs[-1]
    rows, cols = loop.rows, loop.cols
    wide = cols + 2 * HALO
    lat, lon = lax.axis_index("lat"), lax.axis_index("lon")
    lon_even = lax.rem(lon, 2) == 0

    def copy_columns(source, left):
        for row in range(rows + 2 * HALO):
            frame_ref[tiles(row * wide + left, HALO), :] = source[tiles(row * HALO, HALO), :]

    @pl.when(lon_even)
    def _():
        copy_columns(lon_odd_ref, 0)
        copy_columns(lon_even_ref, HALO + cols)

    @pl.when(jnp.logical_not(lon_even))
    def _():
        copy_columns(lon_even_ref, 0)
        copy_columns(lon_odd_ref, HALO + cols)

    zeros = jnp.zeros((HALO * TILE, frame_ref.shape[1]), jnp.float32)
    for at_row, top in ((lat == 0, 0), (lat == loop.lat_count - 1, HALO + rows)):
        for at_col, left in ((lon == 0, 0), (lon == loop.lon_count - 1, HALO + cols)):

            @pl.when(at_row & at_col)
            def _():
                for row in range(HALO):
                    frame_ref[tiles((top + row) * wide + left, HALO), :] = zeros

    mix_and_pack(loop, wide, rim, frame_ref, value_ref, send_refs)


def swap_kernel(loop, *refs):
    table_ref = None
    if not loop.even_leads:
        table_ref, refs = refs[0], refs[1:]
    got_refs = [refs[0]] + by_step(1, refs[1 : loop.lon_count])
    out_refs = refs[loop.lon_count :]
    lat, lon = lax.axis_index("lat"), lax.axis_index("lon")
    for lat_step in range(loop.lat_count):
        if loop.even_leads:
            lead = loop.column_slot(to_device(lat, lat_step, loop.lat_count), lon)
            lead = jnp.minimum(lead, loop.column_slots - loop.slots)
        for lon_step in range(loop.lon_count):
            for slot in range(loop.slots):
                place = lon_step * loop.slots + slot
                if loop.even_leads:
                    source = lead + slot
                else:
                    source = lookup(table_ref, lat_step * loop.lon_count * loop.slots + place)
                out_refs[lat_step][tiles(place, 1), :] = got_refs[lon_step][tiles(source, 1), :]


class Section:
    def __init__(self, loop, factor_ref, radial_ref, plane_ref, work_ref):
        self.loop = loop
        self.tall, self.wide = loop.rows + 2 * HALO, loop.cols + 2 * HALO
        self.pitch = self.wide + 2 * PAD
        self.factor_ref, self.radial_ref = factor_ref, radial_ref
        self.plane_ref, self.work_ref = plane_ref, work_ref
        lat, lon = lax.axis_index("lat"), lax.axis_index("lon")
        self.lat = lat
        self.at_top, self.at_left = lat == 0, lon == 0
        self.on_row_edge = self.at_top | (lat == loop.lat_count - 1)
        self.on_col_edge = self.at_left | (lon == loop.lon_count - 1)

    def spread(self, frame_ref, rows):
        def one_row(row, carry):
            for chunk in range(0, self.wide, 8):
                for f in range(TILE):
                    start = (row * self.wide + chunk) * TILE + f
                    self.plane_ref[self.at(f, row, chunk), :] = frame_ref[
                        pl.ds(start, 8, stride=TILE), :
                    ]
            return carry

        lax.fori_loop(*rows, one_row, 0)

    def scatter(self, receive_ref, got_refs):
        arrivals = self.loop.lon_count * self.loop.slots
        got_refs = by_step(0, got_refs)
        for lat_step in range(self.loop.lat_count):
            for place in range(arrivals):
                spot = lookup(receive_ref, lat_step * arrivals + place)
                self.plane_ref[pl.ds(spot, TILE, stride=self.tall * self.pitch), :] = got_refs[
                    lat_step
                ][tiles(place, 1), :]

    def at(self, number, row, col):
        return pl.ds((number * self.tall + row) * self.pitch + PAD + col, 8)

    def reader(self, ref, row, col):
        def read(number, row_step=0, col_step=0):
            return ref[self.at(number, row + row_step, col + col_step), :]

        return read

    def prepare(self, row):
        factors = [
            self.factor_ref[pl.ds((self.lat * 3 + n) * self.tall + row, 8, stride=0), :]
            for n in range(3)
        ]
        inverse_radius = self.radial_ref[0]
        with_theta = inverse_radius * (self.loop.nth / math.pi)
        return factors, inverse_radius * factors[2], with_theta

    def up(self, x):
        return pltpu.roll(x, x.shape[-1] - 1, 1)

    def down(self, x):
        return pltpu.roll(x, 1, 1)

    def curl(self, read, first, prepared):
        (tu, td, ph), with_phi, with_theta = prepared
        ru, rl = self.radial_ref[1], self.radial_ref[2]
        a, b, c = first, first + 1, first + 2
        mid_b, mid_c = read(b), read(c)
        radial = self.radial_ref[0] * (
            (tu * read(c, 1) - td * read(c, -1)) - ph * (read(b, 0, 1) - read(b, 0, -1))
        )
        polar = with_phi * (read(a, 0, 1) - read(a, 0, -1)) - (
            ru * self.up(mid_c) - rl * self.down(mid_c)
        )
        azimuth = (ru * self.up(mid_b) - rl * self.down(mid_b)) - with_theta * (
            read(a, 1) - read(a, -1)
        )
        return radial, polar, azimuth

    def slope(self, read, number, prepared):
        _, with_phi, with_theta = prepared
        mid = read(number)
        return (
            self.radial_ref[3] * self.up(mid) - self.radial_ref[4] * self.down(mid),
            with_theta * (read(number, 1) - read(number, -1)),
            with_phi * (read(number, 0, 1) - read(number, 0, -1)),
        )

    def outflow(self, read, first, prepared):
        (tu, td, ph), _, _ = prepared
        mid = read(first)
        return (
            self.radial_ref[5] * self.up(mid) - self.radial_ref[6] * self.down(mid)
        ) + self.radial_ref[0] * (
            (tu * read(first + 1, 1) - td * read(first + 1, -1))
            + ph * (read(first + 2, 0, 1) - read(first + 2, 0, -1))
        )

    def first_pass(self, row, chunk):
        prepared = self.prepare(row)
        read = self.reader(self.plane_ref, row, chunk)

        def put(number, value):
            self.work_ref[self.at(number, row, chunk), :] = value

        flow = [read(n) for n in range(3)]
        field = [read(n) for n in range(3, 6)]
        current = self.curl(read, 3, prepared)
        spin = self.curl(read, 0, prepared)
        induced = cross(flow, field)
        warm = self.slope(read, 6, prepared)
        for n in range(3):
            put(n, current[n])
            put(3 + n, spin[n])
            put(6 + n, induced[n] - ETA_COEF * current[n])
            put(9 + n, warm[n])
        put(12, read(7) + 0.5 * dot(flow, flow))

    def second_pass(self, row, chunk, emit):
        prepared = self.prepare(row)
        read = self.reader(self.plane_ref, row, chunk)
        work = self.reader(self.work_ref, row, chunk)
        flow = [read(n) for n in range(3)]
        field = [read(n) for n in range(3, 6)]
        current = [work(n) for n in range(3)]
        spin = [work(3 + n) for n in range(3)]
        warm = [work(9 + n) for n in range(3)]
        field_rate = self.curl(work, 6, prepared)
        spin_curl = self.curl(work, 3, prepared)
        head = self.slope(work, 12, prepared)
        lorentz = cross(current, field)
        advect = cross(flow, spin)
        speed = [advect[n] + lorentz[n] - head[n] - NU_COEF * spin_curl[n] for n in range(3)]
        speed[0] = speed[0] + ARCHIMEDES_LIFT * read(6)
        heat = KAPPA_COEF * self.outflow(work, 9, prepared) - dot(flow, warm)
        squeeze = -SOUND_SQ * self.outflow(read, 0, prepared)
        emit(row, chunk, read, speed + list(field_rate) + [heat, squeeze])

    def over(self, rows, one_row, unroll):
        def step(row, carry):
            one_row(row)
            return carry

        lax.fori_loop(*rows, step, 0, unroll=unroll)

    def everywhere(self, rows, chunks, emit):
        def first(row):
            for chunk in range(0, self.wide, 8):
                self.first_pass(row, chunk)

        def second(row):
            for chunk in chunks:
                self.second_pass(row, chunk, emit)

        self.over((rows[0] - 1, rows[1] + 1), first, 2)
        self.over(rows, second, 2)

    def along_edges(self, rows, chunks, emit):
        tall, wide = self.tall, self.wide
        low_chunk, high_chunk = chunks[0], chunks[-1]

        @pl.when(self.on_row_edge)
        def _():
            row = jnp.where(self.at_top, HALO - 1, tall - HALO - 1)
            for step in range(2):
                for chunk in range(0, wide, 8):
                    self.first_pass(row + step, chunk)

        @pl.when(self.on_col_edge)
        def _():
            chunk = pl.multiple_of(jnp.where(self.at_left, 0, wide - 8), 8)
            count = rows[1] - rows[0]
            self.over(
                (rows[0] - 1, rows[1] + 1), lambda row: self.first_pass(row, chunk), count // 2 + 1
            )

        @pl.when(self.on_row_edge)
        def _():
            row = jnp.where(self.at_top, HALO, tall - HALO - 2)
            for step in range(2):
                for chunk in chunks:
                    self.second_pass(row + step, chunk, emit)

        @pl.when(self.on_col_edge)
        def _():
            chunk = jnp.where(self.at_left, low_chunk, high_chunk)
            count = rows[1] - rows[0]
            self.over(rows, lambda row: self.second_pass(row, chunk, emit), count // 2)


def cross(x, y):
    return (
        x[1] * y[2] - x[2] * y[1],
        x[2] * y[0] - x[0] * y[2],
        x[0] * y[1] - x[1] * y[0],
    )


def dot(x, y):
    return x[0] * y[0] + x[1] * y[1] + x[2] * y[2]


def middle_state(loop, frame_ref, rate_ref):
    wide = loop.cols + 2 * HALO
    first_row = lax.axis_index("lat") * loop.rows - HALO
    first_col = lax.axis_index("lon") * loop.cols - HALO

    def emit(row, chunk, read, rate):
        in_row = (row + first_row >= 0) & (row + first_row < loop.nth)
        col = lax.broadcasted_iota(jnp.int32, (8, 128), 0) + (chunk + first_col)
        inside = (col >= jnp.where(in_row, 0, loop.nph)) & (col < loop.nph)
        for f in range(TILE):
            rate_ref[f, row, pl.ds(chunk, 8), :] = rate[f]
            start = (row * wide + chunk) * TILE + f
            frame_ref[pl.ds(start, 8, stride=TILE), :] = jnp.where(
                inside, read(f) + TIME_STEP * rate[f], 0.0
            )

    return emit


def total_change(loop, change_ref, rate_ref):
    def emit(row, chunk, read, rate):
        for f in range(TILE):
            start = ((row - HALO) * loop.cols + chunk - HALO) * TILE + f
            change_ref[pl.ds(start, 8, stride=TILE), :] = (0.5 * TIME_STEP) * (
                rate_ref[f, row, pl.ds(chunk, 8), :] + rate[f]
            )

    return emit


def first_inner_kernel(
    loop, factor_ref, radial_ref, frame_in_ref, after_ref, frame_ref, rate_ref, plane_ref, work_ref
):
    del after_ref
    part = Section(loop, factor_ref, radial_ref, plane_ref, work_ref)
    part.spread(frame_in_ref, (0, part.tall))
    part.everywhere(
        (2, part.tall - 2), range(0, part.wide, 8), middle_state(loop, frame_ref, rate_ref)
    )


def first_edge_kernel(loop, *refs):
    rim, refs = refs[:3], refs[3:]
    receive_ref, factor_ref, radial_ref = refs[:3]
    got_refs, refs = refs[7 : 7 + loop.lat_count], refs[7 + loop.lat_count :]
    frame_ref, rate_ref, plane_ref, work_ref = refs[:4]
    send_refs, value_ref = refs[4:-1], refs[-1]
    part = Section(loop, factor_ref, radial_ref, plane_ref, work_ref)
    part.scatter(receive_ref, got_refs)
    part.along_edges(
        (2, part.tall - 2), range(0, part.wide, 8), middle_state(loop, frame_ref, rate_ref)
    )
    mix_and_pack(loop, part.wide, rim, frame_ref, value_ref, send_refs)


def second_inner_kernel(
    loop, factor_ref, radial_ref, frame_ref, rate_ref, after_ref, change_ref, plane_ref, work_ref
):
    del after_ref
    part = Section(loop, factor_ref, radial_ref, plane_ref, work_ref)
    part.spread(frame_ref, (2, part.tall - 2))
    part.everywhere(
        (HALO, HALO + loop.rows),
        range(HALO, HALO + loop.cols, 8),
        total_change(loop, change_ref, rate_ref),
    )


def second_edge_kernel(loop, receive_ref, factor_ref, radial_ref, rate_ref, inner_ref, *refs):
    got_refs, refs = refs[2 : 2 + loop.lat_count], refs[2 + loop.lat_count :]
    plane_ref, work_ref, change_ref = refs
    part = Section(loop, factor_ref, radial_ref, plane_ref, work_ref)
    for row in range(loop.rows):
        here = tiles(row * loop.cols, loop.cols)
        change_ref[here, :] = inner_ref[here, :]
    part.scatter(receive_ref, got_refs)
    part.along_edges(
        (HALO, HALO + loop.rows),
        range(HALO, HALO + loop.cols, 8),
        total_change(loop, change_ref, rate_ref),
    )


def radial_factors(levels, theta_count):
    scale = 2.0 * theta_count / math.pi
    step = 0.65 * scale / levels
    radius = 0.35 * scale + (np.arange(levels) + 0.5) * step
    half = 0.5 / step
    above = np.append(radius[1:], 0.0)
    below = np.append(0.0, radius[:-1])
    ones_above = np.append(np.ones(levels - 1), 0.0)
    ones_below = np.append(0.0, np.ones(levels - 1))
    rows = np.stack(
        [
            1.0 / radius,
            half * above / radius,
            half * below / radius,
            half * ones_above,
            half * ones_below,
            half * above**2 / radius**2,
            half * below**2 / radius**2,
        ]
    )
    return np.repeat(rows[:, None, :], 8, axis=1).astype(np.float32)


def row_factors(rows, lat_count, nth, nph, levels):
    polar_step, azimuth_step = math.pi / (2 * nth), 1.5 * math.pi / nph
    tall = rows + 2 * HALO
    parts = []
    for lat in range(lat_count):
        row = lat * rows - HALO - 1 + np.arange(tall + 2)
        sines = np.sin(math.pi / 4 + (row + 0.5) * polar_step)
        middle = sines[1:-1]
        parts += [
            sines[2:] / middle * (0.5 / polar_step),
            sines[:-2] / middle * (0.5 / polar_step),
            (0.5 / azimuth_step) / middle,
        ]
    flat = np.concatenate(parts + [np.zeros(8)]).astype(np.float32)
    return np.repeat(flat[:, None], levels, axis=1)


def per_device(state, rim_base, rim_weight, rim_angle, rim_target):
    _, rows, cols, fields, levels = state.shape
    lat_count, lon_count = lax.axis_size("lat"), lax.axis_size("lon")
    entries = rim_base.shape[1]
    loop = Loop(rows, cols, lat_count, lon_count, entries)
    tall, wide = rows + 2 * HALO, cols + 2 * HALO
    pitch = wide + 2 * PAD
    block = state[0].reshape(rows * cols * fields, levels)
    f32 = jnp.float32

    def tile_array(count):
        return jax.ShapeDtypeStruct((count * TILE, levels), f32)

    first_cell = rim_target[0, 0]
    other_cell = lax.ppermute(first_cell, "panel", [(0, 1), (1, 0)])

    everyone = ("panel", "lat", "lon")
    cells = state[0]
    last_first = lax.axis_index("lat") % 2 == 0
    head, tail = cells[:HALO], cells[rows - HALO :]
    send_even = jnp.where(last_first, tail, head).reshape(HALO * cols * fields, levels)
    send_odd = jnp.where(last_first, head, tail).reshape(HALO * cols * fields, levels)
    lat_even = lax.ppermute(send_even, everyone, swap_route(0, lat_count, lon_count, True))
    lat_odd = lax.ppermute(send_odd, everyone, swap_route(1, lat_count, lon_count, True))

    angle = rim_angle[0]
    corner_table, spread_weights = pl.pallas_call(
        lambda *refs: weight_kernel(loop, *refs),
        out_shape=[
            jax.ShapeDtypeStruct((padded_rows(entries), 128), jnp.int32),
            jax.ShapeDtypeStruct((18 * entries + TILE, levels), f32),
        ],
        in_specs=whole(3),
        out_specs=whole(2),
        compiler_params=grant(4),
        name="weights",
    )(rim_base[0].T, rim_weight[0].T, jnp.stack([jnp.cos(angle), jnp.sin(angle)]))
    send_count = lon_count * loop.column_slots
    got_count = lat_count * lon_count * loop.slots
    counts = [send_count, got_count] + [got_count] * (not loop.even_leads)
    send_table, receive_table, *swap_tables = pl.pallas_call(
        lambda *refs: table_kernel(loop, pitch, *refs),
        out_shape=[
            jax.ShapeDtypeStruct((padded_rows(count), 128), jnp.int32) for count in counts
        ],
        in_specs=scalars(2),
        out_specs=whole(len(counts)),
        compiler_params=grant(4),
        name="tables",
    )(first_cell, other_cell)
    rim = (send_table, corner_table, spread_weights)
    factors = jnp.asarray(row_factors(rows, lat_count, loop.nth, loop.nph, levels))
    radial = jnp.asarray(radial_factors(levels, loop.nth))

    east_first = lax.axis_index("lon") % 2 == 0
    head, tail = cells[:, :HALO], cells[:, cols - HALO :]
    own_even = jnp.where(east_first, tail, head).reshape(rows * HALO * fields, levels)
    own_odd = jnp.where(east_first, head, tail).reshape(rows * HALO * fields, levels)
    strip_even, strip_odd = pl.pallas_call(
        lambda *refs: strip_kernel(rows, cols, *refs),
        out_shape=[tile_array(tall * HALO)] * 2,
        in_specs=whole(5),
        out_specs=whole(2),
        compiler_params=grant(4),
        name="strips",
    )(corner_table, own_even, own_odd, lat_even, lat_odd)
    lon_odd = lax.ppermute(strip_odd, everyone, swap_route(1, lat_count, lon_count, False))
    lon_even = lax.ppermute(strip_even, everyone, swap_route(0, lat_count, lon_count, False))

    frame = pl.pallas_call(
        lambda *refs: middle_kernel(rows, cols, *refs[1:]),
        out_shape=tile_array(tall * wide),
        in_specs=whole(4),
        out_specs=whole(1)[0],
        compiler_params=grant(4),
        name="middle",
    )(strip_even, block, lat_even, lat_odd)
    packed_shapes = [tile_array(loop.column_slots)] * lon_count
    frame, *packed = pl.pallas_call(
        lambda *refs: frame_kernel(loop, *refs),
        out_shape=[tile_array(tall * wide)] + packed_shapes,
        in_specs=whole(6),
        out_specs=whole(1 + lon_count),
        scratch_shapes=[pltpu.VMEM((entries * TILE, levels), f32)],
        input_output_aliases={5: 0},
        compiler_params=grant(4),
        name="frame",
    )(*rim, lon_odd, lon_even, frame)

    def first_round(packed):
        got = [packed[0]] + [
            lax.ppermute(packed[step], "lon", lon_route(step, lon_count))
            for step in start_order(1, lon_count)
        ]
        return pl.pallas_call(
            lambda *refs: swap_kernel(loop, *refs),
            out_shape=[tile_array(lon_count * loop.slots)] * lat_count,
            in_specs=whole(len(swap_tables) + lon_count),
            out_specs=whole(lat_count),
            compiler_params=grant(4),
            name="swap",
        )(*swap_tables, *got)

    def second_round(turned):
        return [
            lax.ppermute(turned[step], everyone, lat_route(step, lat_count, lon_count))
            for step in start_order(0, lat_count)
        ]

    planes = [
        jax.ShapeDtypeStruct((fields * tall * pitch, levels), f32),
        jax.ShapeDtypeStruct((13 * tall * pitch, levels), f32),
    ]
    rates = jax.ShapeDtypeStruct((fields, tall, wide, levels), f32)

    turned = first_round(packed)
    got = second_round(turned)
    frame, rate, plane, work = pl.pallas_call(
        lambda *refs: first_inner_kernel(loop, *refs),
        out_shape=[tile_array(tall * wide), rates] + planes,
        in_specs=whole(4),
        out_specs=whole(4),
        compiler_params=grant(4),
        name="first_inner",
    )(factors, radial, frame, turned[0])
    frame, rate, _, _, *packed = pl.pallas_call(
        lambda *refs: first_edge_kernel(loop, *refs),
        out_shape=[tile_array(tall * wide), rates] + planes + packed_shapes,
        in_specs=whole(10 + lat_count),
        out_specs=whole(4 + lon_count),
        scratch_shapes=[pltpu.VMEM((entries * TILE, levels), f32)],
        input_output_aliases={6: 0, 7: 1, 8: 2, 9: 3},
        compiler_params=grant(4),
        name="first_edge",
    )(*rim, receive_table, factors, radial, frame, rate, plane, work, *got)

    turned = first_round(packed)
    got = second_round(turned)
    inner, plane, work = pl.pallas_call(
        lambda *refs: second_inner_kernel(loop, *refs),
        out_shape=[tile_array(rows * cols)] + planes,
        in_specs=whole(5),
        out_specs=whole(3),
        compiler_params=grant(4),
        name="second_inner",
    )(factors, radial, frame, rate, turned[0])
    _, _, change = pl.pallas_call(
        lambda *refs: second_edge_kernel(loop, *refs),
        out_shape=planes + [tile_array(rows * cols)],
        in_specs=whole(7 + lat_count),
        out_specs=whole(3),
        input_output_aliases={5: 0, 6: 1},
        compiler_params=grant(4),
        name="second_edge",
    )(receive_table, factors, radial, rate, inner, plane, work, *got)
    return change.reshape(1, rows, cols, fields, levels)


def solution(mesh):
    return jax.shard_map(
        per_device,
        mesh=mesh,
        in_specs=(
            P("panel", "lat", "lon", None, None),
            P("panel", ("lat", "lon"), None),
            P("panel", ("lat", "lon"), None),
            P("panel", ("lat", "lon")),
            P("panel", None, None),
        ),
        out_specs=P("panel", "lat", "lon", None, None),
        check_vma=False,
    )
```
